128 devices in a mesh: gx: 16 (over x, z_hi, core), gy: 8 (over y, z_lo).
Axes of the slice: x: 4, y: 4, z: 4 (z_hi: 2, z_lo: 2; z = z_hi * 2 + z_lo), core: 2. Of those that a mesh axis runs over, the one named last changes fastest.
Arguments:
- disc_pos: float32 [2, 64, 256, 128], P(None, 'gy', 'gx'), may hold values from 0 to 1
- disc_vel: float32 [2, 64, 256, 128], P(None, 'gy', 'gx'), may hold values from -3 to 3
- radius: float32 [64, 256, 128], P('gy', 'gx'), may hold values from 0.04 to 0.08
- bond_list: int32 [4, 64, 256, 128], P(None, 'gy', 'gx'), may hold values from 0 to 127
- contact_mask: int32 [8, 64, 256], P(None, 'gy', 'gx'), may hold values 0 or 1
- remap_block: int32 [128, 128, 2], P(('gx', 'gy')), may hold values from -1 to 127, as said below
- ocean_state: float32 [4, 48, 256, 2048], P(None, None, 'gy', 'gx'), may hold values from -6 to 6
- mix_coef: float32 [48, 256, 2048], P(None, 'gy', 'gx'), may hold values from 0.02 to 0.2
- remap_cell: int32 [128, 128, 2], P(('gx', 'gy')), may hold values from 0 to 4095
- fold_perm: int32 [2048], P('gx'), may hold values from 0 to 2047, as said below
Outputs:
- pos_next: float32 [2, 64, 256, 128], P(None, 'gy', 'gx')
- vel_next: float32 [2, 64, 256, 128], P(None, 'gy', 'gx')
- ocean_next: float32 [4, 48, 256, 2048], P(None, None, 'gy', 'gx')
The draws below stay inside these ranges and needn't reach their ends.
Inputs may be any that keep to these rules, and one draw needn't show every extreme that they name: `remap_block`: for each ice tile, every one of its 128 local blocks stands in exactly one slot and the other slots hold -1; in every draw some ocean tile gets all 2 of its slots filled by every ice tile. `fold_perm`: A permutation of the 2048 columns.
All inputs are finite; a program needn't handle non-finite values. No bound on the sum of `contact_mask` on one device may be relied on, other than what follows from the above.
Results may differ from the reference program's by a relative error of at most 0.0003.
Values sent between devices are 32-bit elements; how exact they have to be, the bound alone decides.
A program may use at most 128 MiB of HBM per device.

```python
import math
import jax
import jax.numpy as jnp
from jax import lax

DISCS = 128
BONDS = 4
SUB = 3
KL = 48
BGX = 16
BGY = 8
OX = 128
OY = 32
NBX = 256
NBY = 64
TILES = 128
CAP = 2
NXO = 2048
NYO = 256
OCELLS = 4096
N_GX = 16
N_GY = 8


def draw_remap_block(key, part):
    blocks = BGX * BGY
    slots = TILES * CAP
    full_tile = jax.random.randint(jax.random.fold_in(key, 11), (), 0, TILES)
    slot_ids = jnp.arange(slots, dtype=jnp.int32)

    def one_source(source):
        scores = jax.random.permutation(jax.random.fold_in(key, 1000 + source), slots).astype(jnp.int32)
        scores = jnp.where(slot_ids // CAP == full_tile, slot_ids % CAP - CAP, scores)
        order = jnp.argsort(scores, stable=True)
        table = jnp.full((slots,), -1, jnp.int32).at[order[:blocks]].set(jnp.arange(blocks, dtype=jnp.int32))
        return table.reshape(TILES, CAP)
    return jax.vmap(one_source)(jnp.arange(TILES, dtype=jnp.int32))


def draw_fold_perm(key, part):
    return jax.random.permutation(jax.random.fold_in(key, 23), NXO).astype(jnp.int32)


def set_ends(values, own_key, low, top_value):
    shape = values.shape
    spot = [jax.random.randint(jax.random.fold_in(own_key, axis), (), 0, shape[axis]) for axis in range(len(shape))]
    values = values.at[tuple(spot)].set(low)
    longest = shape.index(max(shape))
    spot[longest] = (spot[longest] + 1) % shape[longest]
    return values.at[tuple(spot)].set(top_value)


def block_levels(own_key, dims, shards, smallest, high):
    loudness = 1.0
    for dim, shards_of in shards:
        heights = jax.random.uniform(jax.random.fold_in(jax.random.fold_in(own_key, 6), dim), (shards_of,), jnp.float32, smallest / len(shards), high / len(shards))
        loudness = loudness * jnp.repeat(jnp.exp(heights), dims[dim] // shards_of).reshape((-1,) + (1,) * (len(dims) - 1 - dim))
    return loudness


def normal_values(own_key, extent, scale, most, pieces=(), kind=jnp.bfloat16):
    values = jax.random.normal(own_key, extent, jnp.float32) * scale
    if len(pieces) > 0:
        values = block_levels(own_key, extent, pieces, -0.22, 0.18) * values
    return jnp.clip(values, min=-most, max=most).astype(kind)


def setup_inputs(seed: int = 0) -> dict:
    key_list = jax.random.split(jax.random.key(seed), 11)
    disc_pos = jnp.clip(1.0 * jax.random.uniform(key_list[0], (2, NBY, NBX, DISCS), jnp.float32) ** block_levels(key_list[0], (2, NBY, NBX, DISCS), ((1, 8), (2, 16)), -0.2, 0.2), 0.0, 1.0)
    disc_vel = normal_values(key_list[1], (2, NBY, NBX, DISCS), 0.5, 3.0, ((1, 8), (2, 16)), jnp.float32)
    radius = jnp.clip(0.04 + 0.04 * jax.random.uniform(key_list[2], (NBY, NBX, DISCS), jnp.float32) ** block_levels(key_list[2], (NBY, NBX, DISCS), ((0, 8), (1, 16)), -0.2, 0.2), 0.04, 0.08)
    bond_list = set_ends(jax.random.randint(key_list[3], (BONDS, NBY, NBX, DISCS), 0, DISCS), jax.random.fold_in(key_list[3], 1), 0, DISCS - 1).astype(jnp.int32)
    contact_mask = set_ends((jax.random.randint(key_list[4], (8, NBY, NBX), 0, 2) < 1).astype(jnp.int32), jax.random.fold_in(key_list[4], 1), 0, 1)
    remap_block = draw_remap_block(jax.random.fold_in(key_list[10], 71), 0)
    ocean_state = normal_values(key_list[6], (4, KL, NYO, NXO), 1.0, 6.0, ((2, 8), (3, 16)), jnp.float32)
    mix_coef = jnp.clip(jnp.exp(math.log(0.2) - 2.3025851 * jax.random.uniform(key_list[7], (KL, NYO, NXO), jnp.float32) ** block_levels(key_list[7], (KL, NYO, NXO), ((1, 8), (2, 16)), -0.2, 0.2)), 0.02, 0.2)
    remap_cell = set_ends(jax.random.randint(key_list[8], (TILES, TILES, CAP), 0, OCELLS), jax.random.fold_in(key_list[8], 1), 0, OCELLS - 1).astype(jnp.int32)
    fold_perm = draw_fold_perm(jax.random.fold_in(key_list[10], 71), 0)
    return dict(disc_pos=disc_pos, disc_vel=disc_vel, radius=radius, bond_list=bond_list, contact_mask=contact_mask, remap_block=remap_block, ocean_state=ocean_state, mix_coef=mix_coef, remap_cell=remap_cell, fold_perm=fold_perm)


SOFTEN = 0.0001
STIFFNESS = 2.0
BOND_STIFF = 0.1
TIME_STEP = 0.05
DRAG_ICE = 15.0
DRAG_BACK = 0.5
VERT_MIX = 0.1
SPIN_RATE = 0.3
ALL_SHIFTS = ((-1, -1), (-1, 0), (-1, 1), (0, -1), (0, 0), (0, 1), (1, -1), (1, 0), (1, 1))

def pair_force(own, other, shift_y, shift_x):
    sep_x = other[0][..., None, :] + shift_x - own[0][..., :, None]
    sep_y = other[1][..., None, :] + shift_y - own[1][..., :, None]
    distance = jnp.sqrt(sep_x * sep_x + sep_y * sep_y + SOFTEN)
    push = STIFFNESS * jnp.maximum(own[2][..., :, None] + other[2][..., None, :] - distance, 0.0) / distance
    return jnp.stack([-lax.optimization_barrier(jnp.sum(push * sep_x, axis=-1)), -lax.optimization_barrier(jnp.sum(push * sep_y, axis=-1))])

def make_weights(contact_mask):
    rows = jnp.arange(NBY, dtype=jnp.int32)
    masked = contact_mask.astype(jnp.float32)
    weights = []
    counter = 0
    for shift_y, shift_x in ALL_SHIFTS:
        if shift_y == 0 and shift_x == 0:
            weights.append(jnp.ones((NBY, NBX), jnp.float32))
        else:
            inside = ((rows + shift_y >= 0) & (rows + shift_y < NBY)).astype(jnp.float32)
            weights.append(masked[counter] * inside[:, None])
            counter = counter + 1
    return jnp.stack(weights)

def contact_all(state, weights):
    wide = jnp.concatenate([state[:, :, -1:], state, state[:, :, :1]], axis=2)
    wide = jnp.pad(wide, ((0, 0), (1, 1), (0, 0), (0, 0)))

    def one_row(inputs):
        row, weight_row = inputs
        band = lax.dynamic_slice_in_dim(wide, row, 3, axis=1)
        own = band[:, 1, 1:NBX + 1]
        total = jnp.zeros((2, NBX, own.shape[2]), jnp.float32)
        for index, (shift_y, shift_x) in enumerate(ALL_SHIFTS):
            other = band[:, 1 + shift_y, 1 + shift_x:1 + shift_x + NBX]
            total = total + pair_force(own, other, float(shift_y), float(shift_x)) * weight_row[index][None, :, None]
        return total
    rows = jnp.arange(NBY, dtype=jnp.int32)
    result = lax.map(one_row, (rows, jnp.moveaxis(weights, 1, 0)))
    return jnp.moveaxis(result, 0, 1)

def to_tiles(field):
    lead = field.shape[0]
    shaped = field.reshape(lead, N_GY, BGY, N_GX, BGX).transpose(0, 3, 1, 2, 4)
    return shaped.reshape(lead, TILES, BGY * BGX)

def from_tiles(field):
    lead = field.shape[0]
    shaped = field.reshape(lead, N_GX, N_GY, BGY, BGX).transpose(0, 2, 3, 1, 4)
    return shaped.reshape(lead, NBY, NBX)

def ocean_step(ocean_state, mix_coef, forcing, fold_perm):
    east = jnp.roll(ocean_state, -1, axis=3)
    west = jnp.roll(ocean_state, 1, axis=3)
    south = jnp.concatenate([jnp.zeros_like(ocean_state[:, :, :1]), ocean_state[:, :, :-1]], axis=2)
    signs = jnp.array([-1.0, -1.0, 1.0, 1.0], jnp.float32)[:, None, None]
    mirrored = signs * jnp.take(ocean_state[:, :, -1], fold_perm, axis=2)
    north = jnp.concatenate([ocean_state[:, :, 1:], mirrored[:, :, None]], axis=2)
    laplace = east + west + north + south - 4.0 * ocean_state
    above = jnp.concatenate([ocean_state[:, :1], ocean_state[:, :-1]], axis=1)
    below = jnp.concatenate([ocean_state[:, 1:], ocean_state[:, -1:]], axis=1)
    vertical = above + below - 2.0 * ocean_state
    updated = ocean_state + mix_coef[None] * laplace + VERT_MIX * vertical
    latitude = jnp.arange(NYO, dtype=jnp.float32)
    coriolis = (SPIN_RATE * (2.0 * (latitude + 0.5) / NYO - 1.0))[None, :, None]
    updated = updated.at[0].add(coriolis * ocean_state[1])
    updated = updated.at[1].add(-coriolis * ocean_state[0])
    updated = updated.at[0:2, 0].add(forcing)
    return updated

def reference(disc_pos, disc_vel, radius, bond_list, contact_mask, remap_block, ocean_state, mix_coef, remap_cell, fold_perm):
    mass = (radius / 0.06) ** 2
    weights = make_weights(contact_mask)
    position, velocity = (disc_pos, disc_vel)
    for substep in range(SUB):
        state = jnp.concatenate([position, radius[None]], axis=0)
        contact = contact_all(state, weights)
        bonded = jnp.stack([reduce_value(lambda left, right: left + right, [jnp.take_along_axis(position[comp], bond_list[partner], axis=-1) for partner in range(BONDS)]) for comp in range(2)])
        force = contact + BOND_STIFF * (bonded - BONDS * position)
        velocity = velocity + force / mass
        position = position + TIME_STEP * velocity
    impulse = DRAG_ICE * lax.optimization_barrier(jnp.sum(radius * radius * velocity, axis=-1))
    blocks = BGX * BGY
    tile_impulse = to_tiles(impulse)
    chosen = jnp.clip(remap_block, 0, blocks - 1).reshape(1, TILES, TILES * CAP)
    values = jnp.take_along_axis(tile_impulse, chosen, axis=2).reshape(2, TILES, TILES, CAP)
    values = jnp.where(remap_block[None] >= 0, values, 0.0).transpose(0, 2, 1, 3)
    tile_ids = jnp.arange(TILES, dtype=jnp.int32)
    segment_ids = (tile_ids[:, None, None] * OCELLS + remap_cell).reshape(-1)
    forcing = jax.ops.segment_sum(values.reshape(2, -1).T, segment_ids, num_segments=TILES * OCELLS).T
    forcing = forcing.reshape(2, N_GX, N_GY, OY, OX).transpose(0, 2, 3, 1, 4).reshape(2, NYO, NXO)
    ocean_next = ocean_step(ocean_state, mix_coef, forcing, fold_perm)
    surface = ocean_next[0:2, 0].reshape(2, N_GY, OY, N_GX, OX).transpose(0, 3, 1, 2, 4).reshape(2, TILES, OCELLS)
    current = jnp.take_along_axis(surface, remap_cell.reshape(1, TILES, TILES * CAP), axis=2)
    current = current.reshape(2, TILES, TILES, CAP).transpose(0, 2, 1, 3)
    block_ids = jnp.where(remap_block >= 0, tile_ids[:, None, None] * blocks + remap_block, TILES * blocks).reshape(-1)
    per_block = jax.ops.segment_sum(current.reshape(2, -1).T, block_ids, num_segments=TILES * blocks + 1)[:TILES * blocks].T
    per_block = from_tiles(per_block.reshape(2, TILES, blocks))
    vel_next = velocity + DRAG_BACK * (per_block[..., None] - velocity)
    return (position, vel_next, ocean_next)

def reduce_value(function, items):
    total = items[0]
    for item in items[1:]:
        total = function(total, item)
    return total
```

```python
import jax
import jax.numpy as jnp
from jax import lax
from jax.experimental import pallas as pl
from jax.experimental.pallas import tpu as pltpu
from jax.sharding import PartitionSpec as P

BONDS = 4
SUB = 3


SOFTEN = 0.0001
STIFFNESS = 2.0
BOND_STIFF = 0.1
TIME_STEP = 0.05
DRAG_ICE = 15.0
DRAG_BACK = 0.5
VERT_MIX = 0.1
SPIN_RATE = 0.3


def with_halo(block, sides, width, periodic):
    for axis, dim in sides:
        count = lax.axis_size(axis)
        forward = [(i, i + 1) for i in range(count - 1)]
        if periodic:
            forward.append((count - 1, 0))
        backward = [(target, source) for source, target in forward]
        low = lax.ppermute(
            lax.slice_in_dim(block, block.shape[dim] - width, None, axis=dim), axis, forward
        )
        high = lax.ppermute(lax.slice_in_dim(block, 0, width, axis=dim), axis, backward)
        block = jnp.concatenate([low, block, high], axis=dim)
    return block


NEIGHBOURS = ((-1, -1), (-1, 0), (-1, 1), (0, -1), (0, 1), (1, -1), (1, 0), (1, 1))


def lane_take(rows, index):
    return jnp.take_along_axis(rows, index, axis=1, mode="promise_in_bounds")


def pair_terms(acc_x, acc_y, own_x, own_y, own_r, other_x, other_y, other_r):
    sep_x = other_x - own_x
    sep_y = other_y - own_y
    inverse = lax.rsqrt(sep_x * sep_x + sep_y * sep_y + SOFTEN)
    push = jnp.maximum((other_r + own_r) * inverse - 1.0, 0.0)
    return acc_x + push * sep_x, acc_y + push * sep_y


def contact_kernel(
    wide, pos, vel, rad, bonds, mask, pos_out, vel_out, columns, found, found_t, force, tally, counts, sem
):
    rows_dev, cols_dev = wide.shape[1] - 2, pos.shape[1] // (wide.shape[1] - 2)
    blocks, discs = rad.shape
    lane = lax.broadcasted_iota(jnp.int32, (8, discs), 1)
    lane_f = lane.astype(jnp.float32)
    tri_row = lax.broadcasted_iota(jnp.int32, (discs, 2 * discs), 0)
    tri_col = lax.broadcasted_iota(jnp.int32, (discs, 2 * discs), 1)
    triangle = (tri_row <= tri_col).astype(jnp.bfloat16)
    for comp in range(2):
        columns[comp] = pos[comp].T
    columns[2] = rad[...].T

    def collect(start):
        def one_row(y, carry):
            for half in range(cols_dev // 8):
                x0 = half * 8
                at = pl.multiple_of(y * cols_dev + x0, 8)
                own = [pos[0, pl.ds(at, 8), :], pos[1, pl.ds(at, 8), :], rad[pl.ds(at, 8), :]]
                reach = jnp.max(own[2], axis=1, keepdims=True)
                low = [jnp.min(own[c], axis=1, keepdims=True) - reach for c in range(2)]
                high = [jnp.max(own[c], axis=1, keepdims=True) + reach for c in range(2)]
                weights = mask[pl.ds(at, 8), :]
                near = []
                for k, (sy, sx) in enumerate(NEIGHBOURS):
                    where = (y + 1 + sy, pl.ds(x0 + 1 + sx, 8), slice(None))
                    nx = wide[(0,) + where] + float(sx)
                    ny = wide[(1,) + where] + float(sy)
                    nr = wide[(2,) + where]
                    close = (nx - nr < high[0]) & (nx + nr > low[0])
                    close = close & (ny - nr < high[1]) & (ny + nr > low[1])
                    close = close & (weights[:, k : k + 1] > 0.5)
                    near.append((nx, ny, nr, close))
                flags = jnp.concatenate([n[3].astype(jnp.float32) for n in near], axis=0)
                ranks = jnp.dot(
                    flags.astype(jnp.bfloat16), triangle, preferred_element_type=jnp.float32
                )
                base = jnp.zeros((8, discs), jnp.float32) - start
                gx = jnp.zeros((8, discs), jnp.float32)
                gy = jnp.zeros((8, discs), jnp.float32)
                gr = jnp.full((8, discs), -1.0, jnp.float32)
                for k in range(8):
                    nx, ny, nr, _ = near[k]
                    rank = ranks[8 * k : 8 * k + 8, :discs]
                    total = ranks[8 * k : 8 * k + 8, discs:]
                    want = lane_f - base
                    source = jnp.zeros((8, discs), jnp.int32)
                    step = discs // 2
                    while step >= 1:
                        probe = lane_take(rank, source + (step - 1))
                        source = jnp.where(probe <= want, source + step, source)
                        step //= 2
                    valid = (want >= 0.0) & (want < total)
                    gx = jnp.where(valid, lane_take(nx, source), gx)
                    gy = jnp.where(valid, lane_take(ny, source), gy)
                    gr = jnp.where(valid, lane_take(nr, source), gr)
                    base = base + total
                found[0, pl.ds(at, 8), :] = gx
                found[1, pl.ds(at, 8), :] = gy
                found[2, pl.ds(at, 8), :] = gr
                found[3, pl.ds(at, 8), :] = base
            return carry

        lax.fori_loop(0, rows_dev, one_row, 0)
        for comp in range(3):
            found_t[comp] = found[comp].T
        left = found[3].T[0:8]
        groups = jnp.clip(jnp.ceil(left * (1.0 / 32.0)), 0.0, 4.0).astype(jnp.int32)
        passes = jnp.ceil(jnp.max(left, axis=1, keepdims=True) * (1.0 / discs)).astype(jnp.int32)
        tally[0:8] = groups
        tally[8:16] = jnp.broadcast_to(passes, (8, discs))
        copy = pltpu.make_async_copy(tally, counts, sem)
        copy.start()
        copy.wait()

    def own_rows(b):
        return pos[0, pl.ds(b, 1), :], pos[1, pl.ds(b, 1), :], rad[pl.ds(b, 1), :]

    def ghosts(b, own, index, acc):
        def group(g, acc):
            for c in range(4):
                at = pl.ds(pl.multiple_of(g * 32 + c * 8, 8), 8)
                acc = pair_terms(*acc, *own, *[lane_take(found_t[k, at, :], index) for k in range(3)])
            return acc

        return lax.fori_loop(0, counts[0, b], group, acc)

    zero = jnp.zeros((8, discs), jnp.float32)
    collect(0.0)

    def target(b, carry):
        own = own_rows(b)
        index = jnp.full((8, discs), b, jnp.int32)
        acc = (zero, zero)
        for c in range(discs // 8):
            at = pl.ds(c * 8, 8)
            acc = pair_terms(*acc, *own, *[lane_take(columns[k, at, :], index) for k in range(3)])
        acc = ghosts(b, own, index, acc)
        for k in range(2):
            force[k, pl.ds(b, 1), :] = jnp.sum(acc[k], axis=0, keepdims=True)
        return carry

    lax.fori_loop(0, blocks, target, 0)

    def more(p, carry):
        collect(p.astype(jnp.float32) * discs)

        def again(b, carry):
            own = own_rows(b)
            index = jnp.full((8, discs), b, jnp.int32)
            acc = ghosts(b, own, index, (zero, zero))
            for k in range(2):
                force[k, pl.ds(b, 1), :] += jnp.sum(acc[k], axis=0, keepdims=True)
            return carry

        return lax.fori_loop(0, blocks, again, carry)

    lax.fori_loop(1, counts[8, 0], more, 0)

    def update(g, carry):
        at = pl.ds(pl.multiple_of(g * 8, 8), 8)
        scale = 0.06 / rad[at, :]
        scale = scale * scale
        for k in range(2):
            here = pos[k, at, :]
            bonded = lane_take(here, bonds[0, at, :])
            for p in range(1, 4):
                bonded = bonded + lane_take(here, bonds[p, at, :])
            total = 0.1 * (bonded - 4.0 * here) - 2.0 * force[k, at, :]
            speed = vel[k, at, :] + total * scale
            vel_out[k, at, :] = speed
            pos_out[k, at, :] = here + 0.05 * speed
        return carry

    lax.fori_loop(0, blocks // 8, update, 0)


def contact_step(wide, pos, vel, rad, bonds, mask):
    blocks, discs = rad.shape
    square = jax.ShapeDtypeStruct((2, blocks, discs), jnp.float32)
    vmem = pl.BlockSpec(memory_space=pltpu.VMEM)
    return pl.pallas_call(
        contact_kernel,
        out_shape=(square, square),
        in_specs=[vmem] * 6,
        out_specs=(vmem, vmem),
        scratch_shapes=[
            pltpu.VMEM((3, discs, blocks), jnp.float32),
            pltpu.VMEM((4, blocks, discs), jnp.float32),
            pltpu.VMEM((3, discs, blocks), jnp.float32),
            pltpu.VMEM((2, blocks, discs), jnp.float32),
            pltpu.VMEM((16, blocks), jnp.int32),
            pltpu.SMEM((16, blocks), jnp.int32),
            pltpu.SemaphoreType.DMA,
        ],
        compiler_params=pltpu.CompilerParams(vmem_limit_bytes=24 << 20),
        name="contact",
    )(wide, pos, vel, rad, bonds, mask)


def send_slots(values):
    return lax.all_to_all(values, ("gx", "gy"), split_axis=1, concat_axis=1, tiled=True)


def return_slots(values):
    return lax.all_to_all(values, ("gx", "gy"), split_axis=1, concat_axis=1, tiled=True)


def body(
    disc_pos,
    disc_vel,
    radius,
    bond_list,
    contact_mask,
    remap_block,
    ocean_state,
    mix_coef,
    remap_cell,
    fold_perm,
):
    rows_dev, cols_dev, disc_count = radius.shape
    block_count = rows_dev * cols_dev
    lat_tiles = lax.axis_size("gy")
    total_rows = rows_dev * lat_tiles
    global_rows = lax.axis_index("gy") * rows_dev + jnp.arange(rows_dev, dtype=jnp.int32)
    weights = []
    for index, (shift_y, shift_x) in enumerate(NEIGHBOURS):
        inside = (global_rows + shift_y >= 0) & (global_rows + shift_y < total_rows)
        weights.append(jnp.where(inside[:, None], contact_mask[index], 0).astype(jnp.float32))
    mask = jnp.stack(weights, axis=-1).reshape(block_count, 8)
    position, velocity = (disc_pos, disc_vel)
    for substep in range(SUB):
        state = jnp.concatenate([position, radius[None]], axis=0)
        wide = with_halo(state, (("gx", 2),), 1, True)
        wide = with_halo(wide, (("gy", 1),), 1, False)
        position, velocity = contact_step(
            wide,
            position.reshape(2, block_count, disc_count),
            velocity.reshape(2, block_count, disc_count),
            radius.reshape(block_count, disc_count),
            bond_list.reshape(BONDS, block_count, disc_count),
            mask,
        )
        position = position.reshape(disc_pos.shape)
        velocity = velocity.reshape(disc_pos.shape)
    impulse = (DRAG_ICE * jnp.sum(radius * radius * velocity, axis=-1)).reshape(2, block_count)
    source_count, tile_count, capacity = remap_block.shape
    selector = (
        remap_block[0].reshape(-1)[:, None] == jnp.arange(block_count, dtype=jnp.int32)[None]
    ).astype(jnp.float32)
    outgoing = jnp.dot(impulse, selector.T, precision=lax.Precision.HIGHEST).reshape(
        2, tile_count, capacity
    )
    arrived = send_slots(outgoing)
    layers, tile_rows, tile_cols = mix_coef.shape
    cells = remap_cell[0].reshape(-1)
    forcing = jax.ops.segment_sum(
        arrived.reshape(2, -1).T, cells, num_segments=tile_rows * tile_cols
    ).T
    forcing = forcing.reshape(2, tile_rows, tile_cols)
    lon_wide = with_halo(ocean_state, (("gx", 3),), 1, True)
    lat_wide = with_halo(ocean_state, (("gy", 2),), 1, False)
    top_row = ocean_state[:, :, tile_rows - 1]
    piece = lax.all_gather(top_row, "gx", axis=2, tiled=True)
    width = piece.shape[2]
    column_ids = jnp.arange(width, dtype=jnp.int32)
    picker = (column_ids[:, None] == fold_perm[None, :]).astype(jnp.float32)
    mirrored = jnp.einsum("fkw,wx->fkx", piece, picker, precision=lax.Precision.HIGHEST)
    signs = jnp.array([-1.0, -1.0, 1.0, 1.0], jnp.float32)[:, None, None]
    mirrored = signs * mirrored
    north = lat_wide[:, :, 2:]
    is_top = lax.axis_index("gy") == lat_tiles - 1
    last_row = jnp.where(is_top, mirrored, north[:, :, tile_rows - 1])
    north = jnp.concatenate([north[:, :, : tile_rows - 1], last_row[:, :, None]], axis=2)
    south = lat_wide[:, :, :tile_rows]
    east = lon_wide[..., 2:]
    west = lon_wide[..., :tile_cols]
    laplace = east + west + north + south - 4.0 * ocean_state
    above = jnp.concatenate([ocean_state[:, :1], ocean_state[:, :-1]], axis=1)
    below = jnp.concatenate([ocean_state[:, 1:], ocean_state[:, -1:]], axis=1)
    vertical = above + below - 2.0 * ocean_state
    updated = ocean_state + mix_coef[None] * laplace + VERT_MIX * vertical
    latitude = (lax.axis_index("gy") * tile_rows + jnp.arange(tile_rows, dtype=jnp.int32)).astype(
        jnp.float32
    )
    coriolis = (SPIN_RATE * (2.0 * (latitude + 0.5) / (tile_rows * lat_tiles) - 1.0))[None, :, None]
    updated = updated.at[0].add(coriolis * ocean_state[1])
    updated = updated.at[1].add(-coriolis * ocean_state[0])
    updated = updated.at[0:2, 0].add(forcing)
    surface = updated[0:2, 0].reshape(2, tile_rows * tile_cols)
    picked = jnp.take(surface, cells, axis=1).reshape(2, tile_count, capacity)
    returned = return_slots(picked)
    per_block = jnp.dot(returned.reshape(2, -1), selector, precision=lax.Precision.HIGHEST)
    per_block = per_block.reshape(2, rows_dev, cols_dev)
    vel_next = velocity + DRAG_BACK * (per_block[..., None] - velocity)
    return (position, vel_next, updated)


def solution(mesh):
    in_specs = (
        P(None, "gy", "gx", None),
        P(None, "gy", "gx", None),
        P("gy", "gx", None),
        P(None, "gy", "gx", None),
        P(None, "gy", "gx"),
        P(("gx", "gy"), None, None),
        P(None, None, "gy", "gx"),
        P(None, "gy", "gx"),
        P(("gx", "gy"), None, None),
        P("gx"),
    )
    out_specs = (P(None, "gy", "gx", None), P(None, "gy", "gx", None), P(None, None, "gy", "gx"))
    return jax.shard_map(body, mesh=mesh, in_specs=in_specs, out_specs=out_specs, check_vma=False)
```

```python
import functools

import jax
import jax.numpy as jnp
from jax import lax
from jax.experimental import pallas as pl
from jax.experimental.pallas import tpu as pltpu
from jax.sharding import PartitionSpec as P

BONDS = 4
SUB = 3
SOFTEN = 0.0001
STIFFNESS = 2.0
BOND_STIFF = 0.1
TIME_STEP = 0.05
DRAG_ICE = 15.0
DRAG_BACK = 0.5
VERT_MIX = 0.1
SPIN_RATE = 0.3
NEIGHBOURS = ((-1, -1), (-1, 0), (-1, 1), (0, -1), (0, 1), (1, -1), (1, 0), (1, 1))
TOGETHER = 4
STATIC = 2
ROWS = 2
CHUNK = 8
MESH = pl.DeviceIdType.MESH
VMEM = pl.BlockSpec(memory_space=pltpu.VMEM)
ANY = pl.BlockSpec(memory_space=pl.ANY)


def shape(*dims):
    return jax.ShapeDtypeStruct(dims, jnp.float32)


def split(value):
    high = value.astype(jnp.bfloat16)
    rest = value - high.astype(jnp.float32)
    middle = rest.astype(jnp.bfloat16)
    low = (rest - middle.astype(jnp.float32)).astype(jnp.bfloat16)
    return jnp.concatenate([high, middle, low], axis=0)


def joined(value):
    rows = value.shape[0] // 3
    return value[:rows] + value[rows : 2 * rows] + value[2 * rows :]


def lane_take(rows, index):
    return jnp.take_along_axis(rows, index, axis=1, mode="promise_in_bounds")


def pair_terms(acc_x, acc_y, own_x, own_y, own_r, other_x, other_y, other_r):
    sep_x = other_x - own_x
    sep_y = other_y - own_y
    inverse = lax.rsqrt(sep_x * sep_x + sep_y * sep_y + SOFTEN)
    push = jnp.maximum((other_r + own_r) * inverse - 1.0, 0.0)
    return acc_x + push * sep_x, acc_y + push * sep_y


def contact_kernel(last, pos, vel, rad, bonds, mask, halo, halo_first, *refs):
    if last:
        slots, pos_out, vel_out, sent, *scratch = refs
    else:
        pos_out, vel_out, edges, *scratch = refs
    wide, columns, found, found_t, force, tally, counts, sem = scratch
    rows_dev, cols_dev = wide.shape[1] - 2, pos.shape[1] // (wide.shape[1] - 2)
    for comp in range(3):
        source = pos.at[comp] if comp < 2 else rad
        frame = halo if comp < 2 else halo_first
        for y in range(rows_dev):
            wide[comp, y + 1, pl.ds(1, cols_dev), :] = source[pl.ds(y * cols_dev, cols_dev), :]
            wide[comp, y + 1, pl.ds(0, 1), :] = frame[3, comp, pl.ds(y, 1), :]
            wide[comp, y + 1, pl.ds(cols_dev + 1, 1), :] = frame[4, comp, pl.ds(y, 1), :]
        for side, y in ((0, 0), (5, rows_dev + 1)):
            wide[comp, y, pl.ds(0, 1), :] = frame[side, comp, pl.ds(7, 1), :]
            wide[comp, y, pl.ds(1, cols_dev), :] = frame[side + 1, comp]
            wide[comp, y, pl.ds(cols_dev + 1, 1), :] = frame[side + 2, comp, pl.ds(0, 1), :]
    blocks, discs = rad.shape
    lane = lax.broadcasted_iota(jnp.int32, (8, discs), 1)
    lane_f = lane.astype(jnp.float32)
    tri_row = lax.broadcasted_iota(jnp.int32, (discs, 2 * discs), 0)
    tri_col = lax.broadcasted_iota(jnp.int32, (discs, 2 * discs), 1)
    triangle = (tri_row <= tri_col).astype(jnp.bfloat16)
    for comp in range(2):
        columns[comp] = pos[comp].T
    columns[2] = rad[...].T

    def collect(start):
        def one_row(step_y, carry):
            for half in range(ROWS * cols_dev // 8):
                y = step_y * ROWS + half // (cols_dev // 8)
                x0 = half % (cols_dev // 8) * 8
                at = pl.multiple_of(y * cols_dev + x0, 8)
                own = [pos[0, pl.ds(at, 8), :], pos[1, pl.ds(at, 8), :], rad[pl.ds(at, 8), :]]
                reach = jnp.max(own[2], axis=1, keepdims=True)
                low = [jnp.min(own[c], axis=1, keepdims=True) - reach for c in range(2)]
                high = [jnp.max(own[c], axis=1, keepdims=True) + reach for c in range(2)]
                weights = mask[pl.ds(at, 8), :]
                near = []
                for k, (sy, sx) in enumerate(NEIGHBOURS):
                    where = (y + 1 + sy, pl.ds(x0 + 1 + sx, 8), slice(None))
                    nx = wide[(0,) + where] + float(sx)
                    ny = wide[(1,) + where] + float(sy)
                    nr = wide[(2,) + where]
                    close = (nx - nr < high[0]) & (nx + nr > low[0])
                    close = close & (ny - nr < high[1]) & (ny + nr > low[1])
                    close = close & (weights[:, k : k + 1] > 0.5)
                    near.append((nx, ny, nr, close))
                flags = jnp.concatenate([n[3].astype(jnp.float32) for n in near], axis=0)
                ranks = jnp.dot(
                    flags.astype(jnp.bfloat16), triangle, preferred_element_type=jnp.float32
                )
                base = jnp.zeros((8, discs), jnp.float32) - start
                gx = jnp.zeros((8, discs), jnp.float32)
                gy = jnp.zeros((8, discs), jnp.float32)
                gr = jnp.full((8, discs), -1.0, jnp.float32)
                for k in range(8):
                    nx, ny, nr, _ = near[k]
                    rank = ranks[8 * k : 8 * k + 8, :discs]
                    total = ranks[8 * k : 8 * k + 8, discs:]
                    want = lane_f - base
                    source = jnp.zeros((8, discs), jnp.int32)
                    step = discs // 2
                    while step >= 1:
                        probe = lane_take(rank, source + (step - 1))
                        source = jnp.where(probe <= want, source + step, source)
                        step //= 2
                    valid = (want >= 0.0) & (want < total)
                    gx = jnp.where(valid, lane_take(nx, source), gx)
                    gy = jnp.where(valid, lane_take(ny, source), gy)
                    gr = jnp.where(valid, lane_take(nr, source), gr)
                    base = base + total
                found[0, pl.ds(at, 8), :] = gx
                found[1, pl.ds(at, 8), :] = gy
                found[2, pl.ds(at, 8), :] = gr
                found[3, pl.ds(at, 8), :] = base
            return carry

        lax.fori_loop(0, rows_dev // ROWS, one_row, 0)
        for comp in range(3):
            found_t[comp] = found[comp].T
        left = found[3].T[0:8]
        groups = jnp.clip(jnp.ceil(left * (1.0 / 32.0)), 0.0, 4.0).astype(jnp.int32)
        passes = jnp.ceil(jnp.max(left, axis=1, keepdims=True) * (1.0 / discs)).astype(jnp.int32)
        tally[0:8] = groups
        tally[8:16] = jnp.broadcast_to(passes, (8, discs))
        copy = pltpu.make_async_copy(tally, counts, sem)
        copy.start()
        copy.wait()

    def gather_own(b):
        own = (pos[0, pl.ds(b, 1), :], pos[1, pl.ds(b, 1), :], rad[pl.ds(b, 1), :])
        return own, jnp.full((8, discs), b, jnp.int32)

    def visit(source, at, target, acc):
        own, index = target
        return pair_terms(*acc, *own, *[lane_take(source[k, at, :], index) for k in range(3)])

    zero = jnp.zeros((8, discs), jnp.float32)

    def sweep(first, static_groups):
        def some(t, carry):
            blocks_here = [t * TOGETHER + u for u in range(TOGETHER)]
            targets = [gather_own(b) for b in blocks_here]
            accs = [(zero, zero)] * TOGETHER
            for u in range(TOGETHER):
                if first:
                    for c in range(discs // 8):
                        accs[u] = visit(columns, pl.ds(c * 8, 8), targets[u], accs[u])
                for c in range(4 * static_groups):
                    accs[u] = visit(found_t, pl.ds(c * 8, 8), targets[u], accs[u])

            def group(g, accs):
                accs = list(accs)
                for u in range(TOGETHER):
                    for c in range(4):
                        at = pl.ds(pl.multiple_of(g * 32 + c * 8, 8), 8)
                        accs[u] = visit(found_t, at, targets[u], accs[u])
                return tuple(accs)

            most = counts[0, blocks_here[0]]
            for b in blocks_here[1:]:
                most = jnp.maximum(most, counts[0, b])
            accs = lax.fori_loop(static_groups, most, group, tuple(accs))
            for u in range(TOGETHER):
                for k in range(2):
                    total = jnp.sum(accs[u][k], axis=0, keepdims=True)
                    if first:
                        force[k, pl.ds(blocks_here[u], 1), :] = total
                    else:
                        force[k, pl.ds(blocks_here[u], 1), :] += total
            return carry

        lax.fori_loop(0, blocks // TOGETHER, some, 0)

    collect(0.0)
    sweep(True, STATIC)

    def more(p, carry):
        collect(p.astype(jnp.float32) * discs)
        sweep(False, 0)
        return carry

    lax.fori_loop(1, counts[8, 0], more, 0)

    def update(g, carry):
        at = pl.ds(pl.multiple_of(g * 8, 8), 8)
        scale = 0.06 / rad[at, :]
        scale = scale * scale
        for k in range(2):
            here = pos[k, at, :]
            bonded = lane_take(here, bonds[0, at, :])
            for p in range(1, BONDS):
                bonded = bonded + lane_take(here, bonds[p, at, :])
            total = BOND_STIFF * (bonded - BONDS * here) - STIFFNESS * force[k, at, :]
            speed = vel[k, at, :] + total * scale
            vel_out[k, at, :] = speed
            pos_out[k, at, :] = here + TIME_STEP * speed
        return carry

    lax.fori_loop(0, blocks // 8, update, 0)
    if last:
        spot = slots[...]
        for comp in range(2):
            drag = rad[...] * rad[...] * vel_out[comp]
            total = DRAG_ICE * jnp.sum(drag.T, axis=0, keepdims=True)
            total = jnp.broadcast_to(total, (8, blocks))
            moved = jnp.where(spot >= 0, lane_take(total, jnp.maximum(spot, 0)), 0.0)
            tally_f = found.at[comp]
            tally_f[pl.ds(0, 8), :] = moved
        both = [found[c, pl.ds(0, 8), :] for c in range(2)]
        rows = [both[0][0:1], both[0][1:2], both[1][0:1], both[1][1:2]]
        rows.append(jnp.zeros((blocks - 4, blocks), jnp.float32))
        sent[:, 0, :] = jnp.concatenate(rows, axis=0).T
    else:
        for side in range(2):
            for comp in range(2):
                at = pl.ds(side * (cols_dev - 1), rows_dev, stride=cols_dev)
                edges[side, comp] = pos_out[comp, at, :]


def contact_step(last, pos, vel, rad, bonds, mask, halo, halo_first, slots=None):
    blocks, discs = rad.shape
    rows_dev = blocks // 16
    square = shape(2, blocks, discs)
    tail = shape(blocks, 1, discs) if last else shape(2, 2, rows_dev, discs)
    args = (pos, vel, rad, bonds, mask, halo, halo_first) + ((slots,) if last else ())
    return pl.pallas_call(
        functools.partial(contact_kernel, last),
        out_shape=(square, square, tail),
        in_specs=[VMEM] * len(args),
        out_specs=(VMEM,) * 3,
        scratch_shapes=[
            pltpu.VMEM((3, rows_dev + 2, 24, discs), jnp.float32),
            pltpu.VMEM((3, discs, blocks), jnp.float32),
            pltpu.VMEM((4, blocks, discs), jnp.float32),
            pltpu.VMEM((3, discs, blocks), jnp.float32),
            pltpu.VMEM((2, blocks, discs), jnp.float32),
            pltpu.VMEM((16, blocks), jnp.int32),
            pltpu.SMEM((16, blocks), jnp.int32),
            pltpu.SemaphoreType.DMA,
        ],
        compiler_params=pltpu.CompilerParams(vmem_limit_bytes=16 << 20),
        name="contact_last" if last else "contact",
    )(*args)


def pack_kernel(ocean, pos, rad, columns, bottom, top, state, edges):
    rows = ocean.shape[2]
    lane = lax.broadcasted_iota(jnp.int32, (8, 128), 1)
    packed = [jnp.zeros((8, 128), jnp.float32)] * 2
    for field in range(4):
        for layer in range(CHUNK):
            for v in range(rows // 8):
                g = (field * CHUNK + layer) * (rows // 8) + v
                place = g % 64
                turned = pltpu.roll(ocean[field, layer, pl.ds(8 * v, 8), :], 2 * place + 1, 1)
                packed[g // 64] = jnp.where(lane // 2 == place, turned, packed[g // 64])
    columns[0] = jnp.concatenate(packed, axis=0)
    bottom[...] = ocean[:, :, 0, :]
    top[...] = ocean[:, :, rows - 1, :]

    @pl.when(pl.program_id(0) == 0)
    def _():
        for comp in range(3):
            source = pos.at[comp] if comp < 2 else rad
            state[comp] = source[...]
            for side in range(2):
                edges[side, comp] = source[pl.ds(side * 15, 8, stride=16), :]


def pack(ocean, pos, rad):
    fields, layers, rows, lanes = ocean.shape
    steps = layers // CHUNK
    whole = lambda *dims: pl.BlockSpec(dims, lambda i: (0,) * len(dims))
    row = pl.BlockSpec((fields, CHUNK, lanes), lambda i: (0, i, 0))
    return pl.pallas_call(
        pack_kernel,
        grid=(steps,),
        out_shape=(
            shape(steps, 16, lanes),
            shape(fields, layers, lanes),
            shape(fields, layers, lanes),
            shape(3, *rad.shape),
            shape(2, 3, 8, lanes),
        ),
        in_specs=[
            pl.BlockSpec((fields, CHUNK, rows, lanes), lambda i: (0, i, 0, 0)),
            whole(*pos.shape),
            whole(*rad.shape),
        ],
        out_specs=(
            pl.BlockSpec((1, 16, lanes), lambda i: (i, 0, 0)),
            row,
            row,
            whole(3, *rad.shape),
            whole(2, 3, 8, lanes),
        ),
        name="pack",
    )(ocean, pos, rad)


def exchange_kernel(which, n_gx, n_gy, *refs):
    if which == 0:
        state, edges, top, bottom, columns, halo, fold, lon, lat, *sems = refs
        send_sem, recv_sem, fold_send, fold_recv, sea_send, sea_recv = sems
    else:
        state, edges, top, halo, fold, send_sem, recv_sem, fold_send, fold_recv = refs
    gx, gy = lax.axis_index("gx"), lax.axis_index("gy")
    offsets = [5 * which + 1 + j for j in range(5)]
    is_top = gy == n_gy - 1

    def at(dx, dy):
        return lax.rem(gx + dx + n_gx, n_gx), lax.rem(gy + dy + n_gy, n_gy)

    barrier = pltpu.get_barrier_semaphore()
    for dy, dx in NEIGHBOURS:
        pl.semaphore_signal(barrier, inc=1, device_id=at(dx, dy), device_id_type=MESH)

    @pl.when(is_top)
    def _():
        for d in offsets:
            pl.semaphore_signal(barrier, inc=1, device_id=at(-d, 0), device_id_type=MESH)
        pl.semaphore_wait(barrier, len(NEIGHBOURS) + len(offsets))

    @pl.when(jnp.logical_not(is_top))
    def _():
        pl.semaphore_wait(barrier, len(NEIGHBOURS))

    def send(source, target, sems, index, device):
        return pltpu.make_async_remote_copy(
            src_ref=source,
            dst_ref=target,
            send_sem=sems[0].at[index],
            recv_sem=sems[1].at[index],
            device_id=device,
            device_id_type=MESH,
        )

    blocks = state.shape[1]
    copies = []
    for k, (sy, sx) in enumerate(NEIGHBOURS):
        device = at(-sx, -sy)
        first = 0 if sy == 1 else blocks - 16
        if sy == 0:
            source, target = edges.at[0 if sx == 1 else 1], halo.at[k, :, pl.ds(0, 8), :]
        elif sx == 0:
            source, target = state.at[:, pl.ds(first, 16), :], halo.at[k]
        else:
            first = first if sx == 1 else first + 8
            source, target = state.at[:, pl.ds(first, 8), :], halo.at[k, :, pl.ds(0, 8), :]
        copies.append(send(source, target, (send_sem, recv_sem), k, device))
    if which == 0:
        sea = (sea_send, sea_recv)
        copies.append(send(columns, lon.at[0], sea, 0, at(1, 0)))
        copies.append(send(columns, lon.at[1], sea, 1, at(-1, 0)))
        copies.append(send(top, lat.at[0], sea, 2, at(0, 1)))
        copies.append(send(bottom, lat.at[1], sea, 3, at(0, -1)))
    far = [
        send(top, fold.at[j], (fold_send, fold_recv), j, at(d, 0)) for j, d in enumerate(offsets)
    ]
    for copy in copies:
        copy.start()

    @pl.when(is_top)
    def _():
        for copy in far:
            copy.start()
        for copy in far:
            copy.wait()

    for copy in copies:
        copy.wait()


def exchange(which, n_gx, n_gy, state, edges, top, bottom=None, columns=None):
    comps = state.shape[0]
    lanes = state.shape[2]
    args = (state, edges, top) + ((bottom, columns) if which == 0 else ())
    outs = [shape(8, comps, 16, lanes), shape(5, *top.shape)]
    dma = pltpu.SemaphoreType.DMA
    scratch = [dma((8,)), dma((8,)), dma((5,)), dma((5,))]
    if which == 0:
        outs += [shape(2, *columns.shape), shape(2, *top.shape)]
        scratch += [dma((4,)), dma((4,))]
    return pl.pallas_call(
        functools.partial(exchange_kernel, which, n_gx, n_gy),
        out_shape=tuple(outs),
        in_specs=[VMEM, VMEM] + [ANY] * (len(args) - 2),
        out_specs=tuple([VMEM] + [ANY] * (len(outs) - 1)),
        scratch_shapes=scratch,
        compiler_params=pltpu.CompilerParams(collective_id=which, has_side_effects=True),
        name="exchange_first" if which == 0 else "exchange",
    )(*args)


def ocean_kernel(n_gx, n_gy, ocean, above, below, mix, lon, lat, f0, f1, f2, perm, place, out, skin):
    step = pl.program_id(0)
    steps = pl.num_programs(0)
    rows, lanes = ocean.shape[2], ocean.shape[3]
    gx, gy = place[0], place[1]
    lane = lax.broadcasted_iota(jnp.int32, (rows, lanes), 1)
    sub = lax.broadcasted_iota(jnp.int32, (rows, lanes), 0)
    lane8 = lax.broadcasted_iota(jnp.int32, (8, lanes), 1)
    wanted = jnp.broadcast_to(perm[...], (8, lanes))
    owner, column = wanted // lanes, wanted % lanes
    bands = []
    for half in range(2):
        at = pl.ds(8 * half, 8)
        west, east = pltpu.roll(lon[0, 0, at, :], 1, 1), pltpu.roll(lon[1, 0, at, :], lanes - 1, 1)
        bands.append(jnp.where(lane8 % 2 == 1, west, east))
    spin = 2.0 * ((gy * rows + sub).astype(jnp.float32) + 0.5) / (rows * n_gy) - 1.0
    spin = SPIN_RATE * spin
    is_top, is_low = gy == n_gy - 1, gy == 0
    for field in range(4):
        folded = lane_take(ocean[field, :, rows - 1, :], column)
        for group, part in enumerate((f0, f1, f2)):
            for j in range(5):
                source = lax.rem(gx - (5 * group + j + 1) + n_gx, n_gx)
                folded = jnp.where(owner == source, lane_take(part[j, field], column), folded)
        folded = -folded if field < 2 else folded
        upper = jnp.where(is_top, folded, lat[1, field])
        lower = jnp.where(is_low, 0.0, lat[0, field])
        for layer in range(CHUNK):
            here = ocean[field, layer]
            up = ocean[field, layer - 1] if layer > 0 else above[field, 0]
            down = ocean[field, layer + 1] if layer < CHUNK - 1 else below[field, 0]
            sides = []
            for v in range(rows // 8):
                g = (field * CHUNK + layer) * (rows // 8) + v
                sides.append(pltpu.roll(bands[g // 64], lanes - 1 - 2 * (g % 64), 1))
            sides = jnp.concatenate(sides, axis=0)
            west = jnp.where(lane == 0, sides, pltpu.roll(here, 1, 1))
            east = jnp.where(lane == lanes - 1, sides, pltpu.roll(here, lanes - 1, 1))
            south = jnp.where(sub == 0, lower[layer : layer + 1], pltpu.roll(here, 1, 0))
            north = jnp.where(sub == rows - 1, upper[layer : layer + 1], pltpu.roll(here, rows - 1, 0))
            laplace = east + west + north + south - 4.0 * here
            value = here + mix[layer] * laplace + VERT_MIX * (up + down - 2.0 * here)
            if field == 0:
                value = value + spin * ocean[1, layer]
            if field == 1:
                value = value - spin * ocean[0, layer]
            out[field, layer] = value
            if field < 2 and layer == 0:

                @pl.when(step == 0)
                def _():
                    skin[field] = value


def ocean_step(n_gx, n_gy, ocean, mix, lon, lat, folds, perm, place):
    fields, layers, rows, lanes = ocean.shape
    steps = layers // CHUNK
    block = pl.BlockSpec((fields, CHUNK, rows, lanes), lambda i: (0, i, 0, 0))
    one = (fields, 1, rows, lanes)
    fold = pl.BlockSpec((5, fields, CHUNK, lanes), lambda i: (0, 0, i, 0))
    return pl.pallas_call(
        functools.partial(ocean_kernel, n_gx, n_gy),
        grid=(steps,),
        out_shape=(shape(*ocean.shape), shape(2, rows, lanes)),
        in_specs=[
            block,
            pl.BlockSpec(one, lambda i: (0, jnp.maximum(i * CHUNK - 1, 0), 0, 0)),
            pl.BlockSpec(one, lambda i: (0, jnp.minimum(i * CHUNK + CHUNK, layers - 1), 0, 0)),
            pl.BlockSpec((CHUNK, rows, lanes), lambda i: (i, 0, 0)),
            pl.BlockSpec((2, 1, 16, lanes), lambda i: (0, i, 0, 0)),
            pl.BlockSpec((2, fields, CHUNK, lanes), lambda i: (0, 0, i, 0)),
            fold,
            fold,
            fold,
            pl.BlockSpec((1, lanes), lambda i: (0, 0)),
            pl.BlockSpec(memory_space=pltpu.SMEM),
        ],
        out_specs=(block, pl.BlockSpec((2, rows, lanes), lambda i: (0, 0, 0))),
        name="ocean",
    )(ocean, ocean, ocean, mix, lon, lat, *folds, perm, place)


def couple_kernel(n_gx, n_gy, sent, skin, cell, surface, current, *refs):
    here, there, back, home, *sems = refs
    gx, gy = lax.axis_index("gx"), lax.axis_index("gy")
    tiles, lanes = n_gx * n_gy, skin.shape[2]
    rows = skin.shape[1]
    barrier = pltpu.get_barrier_semaphore()
    for d in range(1, n_gx):
        peer = (lax.rem(gx + d, n_gx), gy)
        pl.semaphore_signal(barrier, inc=1, device_id=peer, device_id_type=MESH)
    for d in range(1, n_gy):
        peer = (gx, lax.rem(gy + d, n_gy))
        pl.semaphore_signal(barrier, inc=1, device_id=peer, device_id_type=MESH)
    pl.semaphore_wait(barrier, n_gx + n_gy - 2)

    def swap(source, middle, target, sems):
        send_x, recv_x, send_y, recv_y, local = sems
        own = pltpu.make_async_copy(source.at[gx], middle.at[gx], local)
        own.start()
        copies = []
        for d in range(1, n_gx):
            peer = lax.rem(gx + d, n_gx)
            copies.append(
                pltpu.make_async_remote_copy(
                    src_ref=source.at[peer],
                    dst_ref=middle.at[gx],
                    send_sem=send_x.at[d - 1],
                    recv_sem=recv_x.at[d - 1],
                    device_id=(peer, gy),
                    device_id_type=MESH,
                )
            )
        for copy in copies:
            copy.start()
        own.wait()
        for copy in copies:
            copy.wait()
        own = pltpu.make_async_copy(middle.at[:, gy], target.at[:, gy], local)
        own.start()
        copies = []
        for d in range(1, n_gy):
            peer = lax.rem(gy + d, n_gy)
            copies.append(
                pltpu.make_async_remote_copy(
                    src_ref=middle.at[:, peer],
                    dst_ref=target.at[:, gy],
                    send_sem=send_y.at[d - 1],
                    recv_sem=recv_y.at[d - 1],
                    device_id=(gx, peer),
                    device_id_type=MESH,
                )
            )
        for copy in copies:
            copy.start()
        own.wait()
        for copy in copies:
            copy.wait()

    swap(sent, here, there, sems[0:5])
    cells = jnp.concatenate([cell[0:1], cell[1:2]], axis=1)
    cell_row, cell_col = cells // lanes, cells % lanes
    pick = (lax.broadcasted_iota(jnp.int32, (lanes, 2 * tiles), 0) == cell_col).astype(jnp.bfloat16)
    in_row = lax.broadcasted_iota(jnp.int32, (rows, 2 * tiles), 0) == cell_row
    arrived = there[...].reshape(tiles, lanes).T
    spread = []
    for comp in range(2):
        values = jnp.concatenate([arrived[2 * comp : 2 * comp + 1], arrived[2 * comp + 1 : 2 * comp + 2]], axis=1)
        spread.append(jnp.where(in_row, values, 0.0))
    forcing = lax.dot_general(
        split(jnp.concatenate(spread, axis=0)),
        pick,
        (((1,), (1,)), ((), ())),
        preferred_element_type=jnp.float32,
    )
    level = skin[...].reshape(2 * rows, lanes) + joined(forcing)
    surface[...] = level.reshape(2, rows, lanes)
    found = joined(jnp.dot(split(level), pick, preferred_element_type=jnp.float32))
    replies = []
    for comp in range(2):
        values = jnp.where(in_row, found[comp * rows : (comp + 1) * rows], 0.0)
        values = jnp.sum(values, axis=0, keepdims=True)
        replies += [values[:, :tiles], values[:, tiles:]]
    replies.append(jnp.zeros((lanes - 4, tiles), jnp.float32))
    back[...] = jnp.concatenate(replies, axis=0).T.reshape(back.shape)
    swap(back, home, current, sems[5:10])


def couple(n_gx, n_gy, sent, skin, cell):
    tiles, lanes = n_gx * n_gy, skin.shape[2]
    box = (n_gx, n_gy, 1, lanes)
    dma = pltpu.SemaphoreType.DMA
    sems = [dma((n_gx - 1,)), dma((n_gx - 1,)), dma((n_gy - 1,)), dma((n_gy - 1,)), dma]
    return pl.pallas_call(
        functools.partial(couple_kernel, n_gx, n_gy),
        out_shape=(shape(*skin.shape), shape(*box)),
        in_specs=[VMEM] * 3,
        out_specs=(VMEM,) * 2,
        scratch_shapes=[pltpu.VMEM(box, jnp.float32)] * 4 + sems + sems,
        compiler_params=pltpu.CompilerParams(collective_id=SUB, has_side_effects=True),
        name="couple",
    )(sent.reshape(box), skin, cell)


def finish_kernel(ocean, surface, current, slots, vel, vel_out, ocean_out, sem):
    copy = pltpu.make_async_copy(surface, ocean_out.at[pl.ds(0, 2), 0], sem)
    copy.start()
    blocks, discs = vel.shape[1], vel.shape[2]
    tiles = current.shape[0]
    got = current[...].reshape(tiles, discs).T
    spots = jnp.concatenate([slots[0:1], slots[1:2]], axis=1)
    place = lax.broadcasted_iota(jnp.int32, (blocks, 2 * tiles), 0) == spots
    for comp in range(2):
        values = jnp.concatenate([got[2 * comp : 2 * comp + 1], got[2 * comp + 1 : 2 * comp + 2]], axis=1)
        values = jnp.sum(jnp.where(place, values, 0.0), axis=1, keepdims=True)
        speed = vel[comp]
        vel_out[comp] = speed + DRAG_BACK * (values - speed)
    copy.wait()


def finish(ocean, surface, current, slots, vel):
    tiles = current.shape[0] * current.shape[1]
    return pl.pallas_call(
        finish_kernel,
        out_shape=(shape(*vel.shape), shape(*ocean.shape)),
        in_specs=[ANY, VMEM, VMEM, VMEM, VMEM],
        out_specs=(VMEM, ANY),
        scratch_shapes=[pltpu.SemaphoreType.DMA],
        input_output_aliases={0: 1},
        name="finish",
    )(ocean, surface, current.reshape(tiles, 1, current.shape[3]), slots, vel)


def body(
    disc_pos,
    disc_vel,
    radius,
    bond_list,
    contact_mask,
    remap_block,
    ocean_state,
    mix_coef,
    remap_cell,
    fold_perm,
):
    n_gx, n_gy = lax.axis_size("gx"), lax.axis_size("gy")
    rows_dev, cols_dev, discs = radius.shape
    blocks = rows_dev * cols_dev
    total_rows = rows_dev * n_gy
    global_rows = lax.axis_index("gy") * rows_dev + jnp.arange(rows_dev, dtype=jnp.int32)
    weights = []
    for index, (shift_y, shift_x) in enumerate(NEIGHBOURS):
        inside = (global_rows + shift_y >= 0) & (global_rows + shift_y < total_rows)
        weights.append(jnp.where(inside[:, None], contact_mask[index], 0).astype(jnp.float32))
    mask = jnp.stack(weights, axis=-1).reshape(blocks, 8)
    slots = jnp.full((8, remap_block.shape[1]), -1, jnp.int32).at[0:2].set(remap_block[0].T)
    cell = jnp.zeros((8, remap_cell.shape[1]), jnp.int32).at[0:2].set(remap_cell[0].T)
    place = jnp.stack([lax.axis_index("gx"), lax.axis_index("gy")]).astype(jnp.int32)
    position = disc_pos.reshape(2, blocks, discs)
    velocity = disc_vel.reshape(2, blocks, discs)
    rad = radius.reshape(blocks, discs)
    bonds = bond_list.reshape(BONDS, blocks, discs)
    columns, bottom, top, state, edges = pack(ocean_state, position, rad)
    folds = []
    for substep in range(SUB):
        if substep == 0:
            halo, fold, lon, lat = exchange(0, n_gx, n_gy, state, edges, top, bottom, columns)
            halo_first = halo
        else:
            halo, fold = exchange(substep, n_gx, n_gy, position, edges, top)
        folds.append(fold)
        last = substep == SUB - 1
        extra = (slots,) if last else ()
        position, velocity, edges = contact_step(
            last, position, velocity, rad, bonds, mask, halo, halo_first, *extra
        )
    ocean, skin = ocean_step(
        n_gx, n_gy, ocean_state, mix_coef, lon, lat, folds, fold_perm.reshape(1, -1), place
    )
    surface, current = couple(n_gx, n_gy, edges, skin, cell)
    vel_next, ocean_next = finish(ocean, surface, current, slots, velocity)
    return (position.reshape(disc_pos.shape), vel_next.reshape(disc_vel.shape), ocean_next)


def solution(mesh):
    in_specs = (
        P(None, "gy", "gx", None),
        P(None, "gy", "gx", None),
        P("gy", "gx", None),
        P(None, "gy", "gx", None),
        P(None, "gy", "gx"),
        P(("gx", "gy"), None, None),
        P(None, None, "gy", "gx"),
        P(None, "gy", "gx"),
        P(("gx", "gy"), None, None),
        P("gx"),
    )
    out_specs = (P(None, "gy", "gx", None), P(None, "gy", "gx", None), P(None, None, "gy", "gx"))
    return jax.shard_map(body, mesh=mesh, in_specs=in_specs, out_specs=out_specs, check_vma=False)
```

```python
import functools

import jax
import jax.numpy as jnp
from jax import lax
from jax.experimental import pallas as pl
from jax.experimental.pallas import tpu as pltpu
from jax.sharding import PartitionSpec as P

BONDS = 4
SUB = 3
SOFTEN = 0.0001
STIFFNESS = 2.0
BOND_STIFF = 0.1
TIME_STEP = 0.05
DRAG_ICE = 15.0
DRAG_BACK = 0.5
VERT_MIX = 0.1
SPIN_RATE = 0.3
NEIGHBOURS = ((-1, -1), (-1, 0), (-1, 1), (0, -1), (0, 1), (1, -1), (1, 0), (1, 1))
TOGETHER = 4
STATIC = 2
ROWS = 2
CHUNK = 8
TURNERS = 12
TURN_ROWS = 16
MESH = pl.DeviceIdType.MESH
VMEM = pl.BlockSpec(memory_space=pltpu.VMEM)
ANY = pl.BlockSpec(memory_space=pl.ANY)


def grant(mib, **more):
    return pltpu.CompilerParams(vmem_limit_bytes=mib << 20, **more)


def shape(*dims):
    return jax.ShapeDtypeStruct(dims, jnp.float32)


def split(value):
    high = value.astype(jnp.bfloat16)
    rest = value - high.astype(jnp.float32)
    middle = rest.astype(jnp.bfloat16)
    low = (rest - middle.astype(jnp.float32)).astype(jnp.bfloat16)
    return jnp.concatenate([high, middle, low], axis=0)


def joined(value):
    rows = value.shape[0] // 3
    return value[:rows] + value[rows : 2 * rows] + value[2 * rows :]


def lane_take(rows, index):
    return jnp.take_along_axis(rows, index, axis=1, mode="promise_in_bounds")


def pair_terms(acc_x, acc_y, own_x, own_y, own_r, other_x, other_y, other_r):
    sep_x = other_x - own_x
    sep_y = other_y - own_y
    inverse = lax.rsqrt(sep_x * sep_x + sep_y * sep_y + SOFTEN)
    push = jnp.maximum((other_r + own_r) * inverse - 1.0, 0.0)
    return acc_x + push * sep_x, acc_y + push * sep_y


def turn(rows, perms, turned):
    lanes = rows.shape[2]

    def one(h, carry):
        wanted = jnp.broadcast_to(perms[h], (8, lanes))
        owner, column = wanted // lanes, wanted % lanes
        for half in range(TURN_ROWS // 8):
            at = pl.ds(8 * half, 8)
            got = jnp.zeros((8, lanes), jnp.float32)
            for source in range(rows.shape[0]):
                got = jnp.where(owner == source, lane_take(rows[source, at, :], column), got)
            turned[h, at, :] = got
        return carry

    lax.fori_loop(0, perms.shape[0], one, 0)


def contact_kernel(which, n_gy, pos, vel, rad, bonds, mask, halo, halo_first, *refs):
    last = which == SUB - 1
    if last:
        slots, pos_out, vel_out, sent, *scratch = refs
    elif which == 0:
        rows, perms, pos_out, vel_out, edges, turned, *scratch = refs

        @pl.when(lax.axis_index("gy") == n_gy - 1)
        def _():
            turn(rows, perms, turned)

    else:
        pos_out, vel_out, edges, *scratch = refs
    wide, columns, found, found_t, force, tally, counts, sem = scratch
    rows_dev, cols_dev = wide.shape[1] - 2, pos.shape[1] // (wide.shape[1] - 2)
    for comp in range(3):
        source = pos.at[comp] if comp < 2 else rad
        frame = halo if comp < 2 else halo_first
        for y in range(rows_dev):
            wide[comp, y + 1, pl.ds(1, cols_dev), :] = source[pl.ds(y * cols_dev, cols_dev), :]
            wide[comp, y + 1, pl.ds(0, 1), :] = frame[3, comp, pl.ds(y, 1), :]
            wide[comp, y + 1, pl.ds(cols_dev + 1, 1), :] = frame[4, comp, pl.ds(y, 1), :]
        for side, y in ((0, 0), (5, rows_dev + 1)):
            wide[comp, y, pl.ds(0, 1), :] = frame[side, comp, pl.ds(7, 1), :]
            wide[comp, y, pl.ds(1, cols_dev), :] = frame[side + 1, comp]
            wide[comp, y, pl.ds(cols_dev + 1, 1), :] = frame[side + 2, comp, pl.ds(0, 1), :]
    blocks, discs = rad.shape
    lane = lax.broadcasted_iota(jnp.int32, (8, discs), 1)
    lane_f = lane.astype(jnp.float32)
    tri_row = lax.broadcasted_iota(jnp.int32, (discs, 2 * discs), 0)
    tri_col = lax.broadcasted_iota(jnp.int32, (discs, 2 * discs), 1)
    triangle = (tri_row <= tri_col).astype(jnp.bfloat16)
    for comp in range(2):
        columns[comp] = pos[comp].T
    columns[2] = rad[...].T

    def collect(start):
        def one_row(step_y, carry):
            for half in range(ROWS * cols_dev // 8):
                y = step_y * ROWS + half // (cols_dev // 8)
                x0 = half % (cols_dev // 8) * 8
                at = pl.multiple_of(y * cols_dev + x0, 8)
                own = [pos[0, pl.ds(at, 8), :], pos[1, pl.ds(at, 8), :], rad[pl.ds(at, 8), :]]
                reach = jnp.max(own[2], axis=1, keepdims=True)
                low = [jnp.min(own[c], axis=1, keepdims=True) - reach for c in range(2)]
                high = [jnp.max(own[c], axis=1, keepdims=True) + reach for c in range(2)]
                weights = mask[pl.ds(at, 8), :]
                near = []
                for k, (sy, sx) in enumerate(NEIGHBOURS):
                    where = (y + 1 + sy, pl.ds(x0 + 1 + sx, 8), slice(None))
                    nx = wide[(0,) + where] + float(sx)
                    ny = wide[(1,) + where] + float(sy)
                    nr = wide[(2,) + where]
                    close = (nx - nr < high[0]) & (nx + nr > low[0])
                    close = close & (ny - nr < high[1]) & (ny + nr > low[1])
                    close = close & (weights[:, k : k + 1] > 0.5)
                    near.append((nx, ny, nr, close))
                flags = jnp.concatenate([n[3].astype(jnp.float32) for n in near], axis=0)
                ranks = jnp.dot(
                    flags.astype(jnp.bfloat16), triangle, preferred_element_type=jnp.float32
                )
                base = jnp.zeros((8, discs), jnp.float32) - start
                gx = jnp.zeros((8, discs), jnp.float32)
                gy = jnp.zeros((8, discs), jnp.float32)
                gr = jnp.full((8, discs), -1.0, jnp.float32)
                for k in range(8):
                    nx, ny, nr, _ = near[k]
                    rank = ranks[8 * k : 8 * k + 8, :discs]
                    total = ranks[8 * k : 8 * k + 8, discs:]
                    want = lane_f - base
                    source = jnp.zeros((8, discs), jnp.int32)
                    step = discs // 2
                    while step >= 1:
                        probe = lane_take(rank, source + (step - 1))
                        source = jnp.where(probe <= want, source + step, source)
                        step //= 2
                    valid = (want >= 0.0) & (want < total)
                    gx = jnp.where(valid, lane_take(nx, source), gx)
                    gy = jnp.where(valid, lane_take(ny, source), gy)
                    gr = jnp.where(valid, lane_take(nr, source), gr)
                    base = base + total
                found[0, pl.ds(at, 8), :] = gx
                found[1, pl.ds(at, 8), :] = gy
                found[2, pl.ds(at, 8), :] = gr
                found[3, pl.ds(at, 8), :] = base
            return carry

        lax.fori_loop(0, rows_dev // ROWS, one_row, 0)
        for comp in range(3):
            found_t[comp] = found[comp].T
        left = found[3].T[0:8]
        groups = jnp.clip(jnp.ceil(left * (1.0 / 32.0)), 0.0, 4.0).astype(jnp.int32)
        passes = jnp.ceil(jnp.max(left, axis=1, keepdims=True) * (1.0 / discs)).astype(jnp.int32)
        tally[0:8] = groups
        tally[8:16] = jnp.broadcast_to(passes, (8, discs))
        copy = pltpu.make_async_copy(tally, counts, sem)
        copy.start()
        copy.wait()

    def gather_own(b):
        own = (pos[0, pl.ds(b, 1), :], pos[1, pl.ds(b, 1), :], rad[pl.ds(b, 1), :])
        return own, jnp.full((8, discs), b, jnp.int32)

    def visit(source, at, target, acc):
        own, index = target
        return pair_terms(*acc, *own, *[lane_take(source[k, at, :], index) for k in range(3)])

    zero = jnp.zeros((8, discs), jnp.float32)

    def sweep(first, static_groups):
        def some(t, carry):
            blocks_here = [t * TOGETHER + u for u in range(TOGETHER)]
            targets = [gather_own(b) for b in blocks_here]
            accs = [(zero, zero)] * TOGETHER
            for u in range(TOGETHER):
                if first:
                    for c in range(discs // 8):
                        accs[u] = visit(columns, pl.ds(c * 8, 8), targets[u], accs[u])
                for c in range(4 * static_groups):
                    accs[u] = visit(found_t, pl.ds(c * 8, 8), targets[u], accs[u])

            def group(g, accs):
                accs = list(accs)
                for u in range(TOGETHER):
                    for c in range(4):
                        at = pl.ds(pl.multiple_of(g * 32 + c * 8, 8), 8)
                        accs[u] = visit(found_t, at, targets[u], accs[u])
                return tuple(accs)

            most = counts[0, blocks_here[0]]
            for b in blocks_here[1:]:
                most = jnp.maximum(most, counts[0, b])
            accs = lax.fori_loop(static_groups, most, group, tuple(accs))
            for u in range(TOGETHER):
                for k in range(2):
                    total = jnp.sum(accs[u][k], axis=0, keepdims=True)
                    if first:
                        force[k, pl.ds(blocks_here[u], 1), :] = total
                    else:
                        force[k, pl.ds(blocks_here[u], 1), :] += total
            return carry

        lax.fori_loop(0, blocks // TOGETHER, some, 0)

    collect(0.0)
    sweep(True, STATIC)

    def more(p, carry):
        collect(p.astype(jnp.float32) * discs)
        sweep(False, 0)
        return carry

    lax.fori_loop(1, counts[8, 0], more, 0)

    def update(g, carry):
        at = pl.ds(pl.multiple_of(g * 8, 8), 8)
        scale = 0.06 / rad[at, :]
        scale = scale * scale
        for k in range(2):
            here = pos[k, at, :]
            bonded = lane_take(here, bonds[0, at, :])
            for p in range(1, BONDS):
                bonded = bonded + lane_take(here, bonds[p, at, :])
            total = BOND_STIFF * (bonded - BONDS * here) - STIFFNESS * force[k, at, :]
            speed = vel[k, at, :] + total * scale
            vel_out[k, at, :] = speed
            pos_out[k, at, :] = here + TIME_STEP * speed
        return carry

    lax.fori_loop(0, blocks // 8, update, 0)
    if last:
        spots = [jnp.broadcast_to(slots[k : k + 1], (8, blocks)) for k in range(2)]
        rows = []
        for comp in range(2):
            drag = rad[...] * rad[...] * vel_out[comp]
            total = DRAG_ICE * jnp.sum(drag.T, axis=0, keepdims=True)
            total = jnp.broadcast_to(total, (8, blocks))
            for spot in spots:
                moved = lane_take(total, jnp.maximum(spot, 0))
                rows.append(jnp.where(spot >= 0, moved, 0.0)[0:1])
        rows.append(jnp.zeros((blocks - 4, blocks), jnp.float32))
        sent[:, 0, :] = jnp.concatenate(rows, axis=0).T
    else:
        for side in range(2):
            for comp in range(2):
                at = pl.ds(side * (cols_dev - 1), rows_dev, stride=cols_dev)
                edges[side, comp] = pos_out[comp, at, :]


def contact_step(which, n_gy, pos, vel, rad, bonds, mask, halo, halo_first, *extra):
    blocks, discs = rad.shape
    rows_dev = blocks // 16
    square = shape(2, blocks, discs)
    tail = shape(blocks, 1, discs) if which == SUB - 1 else shape(2, 2, rows_dev, discs)
    outs = (square, square, tail)
    if which == 0:
        outs += (shape(*extra[0].shape),)
    args = (pos, vel, rad, bonds, mask, halo, halo_first) + extra
    return pl.pallas_call(
        functools.partial(contact_kernel, which, n_gy),
        out_shape=outs,
        in_specs=[VMEM] * len(args),
        out_specs=(VMEM,) * len(outs),
        scratch_shapes=[
            pltpu.VMEM((3, rows_dev + 2, 24, discs), jnp.float32),
            pltpu.VMEM((3, discs, blocks), jnp.float32),
            pltpu.VMEM((4, blocks, discs), jnp.float32),
            pltpu.VMEM((3, discs, blocks), jnp.float32),
            pltpu.VMEM((2, blocks, discs), jnp.float32),
            pltpu.VMEM((16, blocks), jnp.int32),
            pltpu.SMEM((16, blocks), jnp.int32),
            pltpu.SemaphoreType.DMA,
        ],
        compiler_params=grant(16),
        name=("contact_first", "contact", "contact_last")[which],
    )(*args)


def pack_kernel(n_gy, ocean, pos, rad, allowed, columns, bottom, top, state, edges, mask):
    rows = ocean.shape[2]
    lane = lax.broadcasted_iota(jnp.int32, (8, 128), 1)
    packed = [jnp.zeros((8, 128), jnp.float32)] * 2
    for field in range(4):
        for layer in range(CHUNK):
            for v in range(rows // 8):
                g = (field * CHUNK + layer) * (rows // 8) + v
                place = g % 64
                turned = pltpu.roll(ocean[field, layer, pl.ds(8 * v, 8), :], 2 * place + 1, 1)
                packed[g // 64] = jnp.where(lane // 2 == place, turned, packed[g // 64])
    columns[0] = jnp.concatenate(packed, axis=0)
    bottom[...] = ocean[:, :, 0, :]
    top[...] = ocean[:, :, rows - 1, :]

    @pl.when(pl.program_id(0) == 0)
    def _():
        for comp in range(3):
            source = pos.at[comp] if comp < 2 else rad
            state[comp] = source[...]
            for side in range(2):
                edges[side, comp] = source[pl.ds(side * 15, 8, stride=16), :]
        _, rows_dev, cols_dev = allowed.shape
        spread = jnp.zeros((8, 128), jnp.float32)
        for y in range(rows_dev):
            part = allowed[:, y, :].astype(jnp.float32)
            part = jnp.concatenate([part, jnp.zeros((8, 128 - cols_dev), jnp.float32)], axis=1)
            spread = spread + (pltpu.roll(part, y * cols_dev, 1) if y else part)
        which = lax.broadcasted_iota(jnp.int32, (8, 128), 0)
        shift_y = jnp.where(which < 3, -1, jnp.where(which < 5, 0, 1))
        row = lax.axis_index("gy") * rows_dev + lane // cols_dev + shift_y
        spread = jnp.where((row >= 0) & (row < n_gy * rows_dev), spread, 0.0)
        mask[...] = jnp.concatenate([spread, jnp.zeros((120, 128), jnp.float32)], axis=0).T


def pack(n_gy, ocean, pos, rad, allowed):
    fields, layers, rows, lanes = ocean.shape
    steps = layers // CHUNK
    whole = lambda *dims: pl.BlockSpec(dims, lambda i: (0,) * len(dims))
    row = pl.BlockSpec((fields, CHUNK, lanes), lambda i: (0, i, 0))
    return pl.pallas_call(
        functools.partial(pack_kernel, n_gy),
        grid=(steps,),
        out_shape=(
            shape(steps, 16, lanes),
            shape(fields, layers, lanes),
            shape(fields, layers, lanes),
            shape(3, *rad.shape),
            shape(2, 3, 8, lanes),
            shape(*rad.shape),
        ),
        in_specs=[
            pl.BlockSpec((fields, CHUNK, rows, lanes), lambda i: (0, i, 0, 0)),
            whole(*pos.shape),
            whole(*rad.shape),
            whole(*allowed.shape),
        ],
        out_specs=(
            pl.BlockSpec((1, 16, lanes), lambda i: (i, 0, 0)),
            row,
            row,
            whole(3, *rad.shape),
            whole(2, 3, 8, lanes),
            whole(*rad.shape),
        ),
        compiler_params=grant(8),
        name="pack",
    )(ocean, pos, rad, allowed)


def exchange_kernel(which, n_gx, n_gy, *refs):
    if which == 0:
        state, edges, top, bottom, columns, perm, halo, lon, lat, rows, perms, *sems = refs
        send_sem, recv_sem, sea_send, sea_recv, far_send, far_recv, perm_send, perm_recv, own = sems
    elif which == 1:
        state, edges, turned, halo, mirror, send_sem, recv_sem, far_send, far_recv, own = refs
    else:
        state, edges, halo, send_sem, recv_sem = refs
    gx, gy = lax.axis_index("gx"), lax.axis_index("gy")
    is_top = gy == n_gy - 1

    def at(dx, dy):
        return lax.rem(gx + dx + n_gx, n_gx), lax.rem(gy + dy + n_gy, n_gy)

    barrier = pltpu.get_barrier_semaphore()
    for dy, dx in NEIGHBOURS:
        pl.semaphore_signal(barrier, inc=1, device_id=at(dx, dy), device_id_type=MESH)
    if which < 2:

        @pl.when(is_top)
        def _():
            for d in range(1, n_gx):
                pl.semaphore_signal(barrier, inc=1, device_id=at(d, 0), device_id_type=MESH)
            pl.semaphore_wait(barrier, len(NEIGHBOURS) + n_gx - 1)

        @pl.when(jnp.logical_not(is_top))
        def _():
            pl.semaphore_wait(barrier, len(NEIGHBOURS))

    else:
        pl.semaphore_wait(barrier, len(NEIGHBOURS))

    def send(source, target, sems, index, device):
        return pltpu.make_async_remote_copy(
            src_ref=source,
            dst_ref=target,
            send_sem=sems[0].at[index],
            recv_sem=sems[1].at[index],
            device_id=device,
            device_id_type=MESH,
        )

    blocks = state.shape[1]
    copies = []
    for k, (sy, sx) in enumerate(NEIGHBOURS):
        device = at(-sx, -sy)
        first = 0 if sy == 1 else blocks - 16
        if sy == 0:
            source, target = edges.at[0 if sx == 1 else 1], halo.at[k, :, pl.ds(0, 8), :]
        elif sx == 0:
            source, target = state.at[:, pl.ds(first, 16), :], halo.at[k]
        else:
            first = first if sx == 1 else first + 8
            source, target = state.at[:, pl.ds(first, 8), :], halo.at[k, :, pl.ds(0, 8), :]
        copies.append(send(source, target, (send_sem, recv_sem), k, device))
    for copy in copies:
        copy.start()
    if which == 0:
        sea = (sea_send, sea_recv)
        later = [
            send(columns, lon.at[0], sea, 0, at(1, 0)),
            send(columns, lon.at[1], sea, 1, at(-1, 0)),
            send(top, lat.at[0], sea, 2, at(0, 1)),
            send(bottom, lat.at[1], sea, 3, at(0, -1)),
        ]
        copies += later

    if which == 0:

        @pl.when(is_top)
        def _():
            kept = pltpu.make_async_copy(perm, perms.at[gx], own.at[0])
            kept.start()
            notes = [
                send(perm, perms.at[gx], (perm_send, perm_recv), d - 1, at(d, 0))
                for d in range(1, n_gx)
            ]
            for note in notes:
                note.start()
            far = []
            for d in range(1, n_gx):
                peer = lax.rem(gx + d, n_gx)
                first = pl.multiple_of(jnp.minimum(peer, TURNERS - 1) * TURN_ROWS, TURN_ROWS)
                source = top.at[pl.ds(first, TURN_ROWS), :]
                far.append(send(source, rows.at[gx], (far_send, far_recv), d - 1, at(d, 0)))

                @pl.when(peer < TURNERS)
                def _(copy=far[-1]):
                    copy.start()

            @pl.when(gx < TURNERS)
            def _():
                first = pl.multiple_of(jnp.minimum(gx, TURNERS - 1) * TURN_ROWS, TURN_ROWS)
                mine = pltpu.make_async_copy(top.at[pl.ds(first, TURN_ROWS), :], rows.at[gx], own.at[1])
                mine.start()
                mine.wait()
                for copy in far:
                    copy.wait_recv()

            for d in range(1, n_gx):

                @pl.when(lax.rem(gx + d, n_gx) < TURNERS)
                def _(copy=far[d - 1]):
                    copy.wait_send()

            kept.wait()
            for note in notes:
                note.wait()

        for copy in later:
            copy.start()

    if which == 1:

        @pl.when(is_top)
        def _():
            me = jnp.minimum(gx, TURNERS - 1)
            far = [
                send(turned.at[lax.rem(gx + d, n_gx)], mirror.at[me], (far_send, far_recv), d - 1, at(d, 0))
                for d in range(1, n_gx)
            ]

            @pl.when(gx < TURNERS)
            def _():
                mine = pltpu.make_async_copy(turned.at[gx], mirror.at[me], own)
                mine.start()
                for copy in far:
                    copy.start()
                mine.wait()
                for copy in far:
                    copy.wait_send()

            for d in range(1, n_gx):

                @pl.when(lax.rem(gx - d + n_gx, n_gx) < TURNERS)
                def _(copy=far[d - 1]):
                    copy.wait_recv()

    for copy in copies:
        copy.wait()


def exchange(which, n_gx, n_gy, state, edges, *args):
    comps = state.shape[0]
    lanes = state.shape[2]
    outs = [shape(8, comps, 16, lanes)]
    dma = pltpu.SemaphoreType.DMA
    scratch = [dma((8,)), dma((8,))]
    far = [dma((n_gx - 1,)), dma((n_gx - 1,))]
    if which == 0:
        top, bottom, columns, perm = args
        outs += [shape(2, *columns.shape), shape(2, *top.shape)]
        outs += [shape(n_gx, TURN_ROWS, lanes), jax.ShapeDtypeStruct((n_gx, 1, lanes), jnp.int32)]
        scratch += [dma((4,)), dma((4,))] + far + far + [dma((2,))]
    if which == 1:
        outs += [shape(TURNERS, TURN_ROWS, lanes)]
        scratch += far + [dma]
    return pl.pallas_call(
        functools.partial(exchange_kernel, which, n_gx, n_gy),
        out_shape=tuple(outs),
        in_specs=[VMEM] * (2 + len(args)),
        out_specs=(VMEM,) * len(outs),
        scratch_shapes=scratch,
        compiler_params=grant(4, collective_id=which, has_side_effects=True),
        name=("exchange_first", "exchange_second", "exchange_third")[which],
    )(state, edges, *args)


def ocean_kernel(n_gy, ocean, above, below, mix, lon, lat, mirror, out, skin):
    step = pl.program_id(0)
    rows, lanes = ocean.shape[2], ocean.shape[3]
    gy = lax.axis_index("gy")
    lane = lax.broadcasted_iota(jnp.int32, (rows, lanes), 1)
    sub = lax.broadcasted_iota(jnp.int32, (rows, lanes), 0)
    lane8 = lax.broadcasted_iota(jnp.int32, (8, lanes), 1)
    bands = []
    for half in range(2):
        at = pl.ds(8 * half, 8)
        west, east = pltpu.roll(lon[0, 0, at, :], 1, 1), pltpu.roll(lon[1, 0, at, :], lanes - 1, 1)
        bands.append(jnp.where(lane8 % 2 == 1, west, east))
    spin = 2.0 * ((gy * rows + sub).astype(jnp.float32) + 0.5) / (rows * n_gy) - 1.0
    spin = SPIN_RATE * spin
    is_top, is_low = gy == n_gy - 1, gy == 0
    for field in range(4):
        folded = -mirror[field] if field < 2 else mirror[field]
        upper = jnp.where(is_top, folded, lat[1, field])
        lower = jnp.where(is_low, 0.0, lat[0, field])
        for layer in range(CHUNK):
            here = ocean[field, layer]
            up = ocean[field, layer - 1] if layer > 0 else above[field, 0]
            down = ocean[field, layer + 1] if layer < CHUNK - 1 else below[field, 0]
            sides = []
            for v in range(rows // 8):
                g = (field * CHUNK + layer) * (rows // 8) + v
                sides.append(pltpu.roll(bands[g // 64], lanes - 1 - 2 * (g % 64), 1))
            sides = jnp.concatenate(sides, axis=0)
            west = jnp.where(lane == 0, sides, pltpu.roll(here, 1, 1))
            east = jnp.where(lane == lanes - 1, sides, pltpu.roll(here, lanes - 1, 1))
            south = jnp.where(sub == 0, lower[layer : layer + 1], pltpu.roll(here, 1, 0))
            north = jnp.where(sub == rows - 1, upper[layer : layer + 1], pltpu.roll(here, rows - 1, 0))
            laplace = east + west + north + south - 4.0 * here
            value = here + mix[layer] * laplace + VERT_MIX * (up + down - 2.0 * here)
            if field == 0:
                value = value + spin * ocean[1, layer]
            if field == 1:
                value = value - spin * ocean[0, layer]
            out[field, layer] = value
            if field < 2 and layer == 0:

                @pl.when(step == 0)
                def _():
                    skin[field] = value


def ocean_step(n_gy, ocean, mix, lon, lat, mirror):
    fields, layers, rows, lanes = ocean.shape
    steps = layers // CHUNK
    block = pl.BlockSpec((fields, CHUNK, rows, lanes), lambda i: (0, i, 0, 0))
    one = (fields, 1, rows, lanes)
    return pl.pallas_call(
        functools.partial(ocean_kernel, n_gy),
        grid=(steps,),
        out_shape=(shape(*ocean.shape), shape(2, rows, lanes)),
        in_specs=[
            block,
            pl.BlockSpec(one, lambda i: (0, jnp.maximum(i * CHUNK - 1, 0), 0, 0)),
            pl.BlockSpec(one, lambda i: (0, jnp.minimum(i * CHUNK + CHUNK, layers - 1), 0, 0)),
            pl.BlockSpec((CHUNK, rows, lanes), lambda i: (i, 0, 0)),
            pl.BlockSpec((2, 1, 16, lanes), lambda i: (0, i, 0, 0)),
            pl.BlockSpec((2, fields, CHUNK, lanes), lambda i: (0, 0, i, 0)),
            pl.BlockSpec((fields, CHUNK, lanes), lambda i: (0, i, 0)),
        ],
        out_specs=(block, pl.BlockSpec((2, rows, lanes), lambda i: (0, 0, 0))),
        compiler_params=grant(24),
        name="ocean",
    )(ocean, ocean, ocean, mix, lon, lat, mirror)


def couple_kernel(n_gx, n_gy, sent, skin, cell, surface, current, *refs):
    here, there, back, home, *sems = refs
    gx, gy = lax.axis_index("gx"), lax.axis_index("gy")
    tiles, lanes = n_gx * n_gy, skin.shape[2]
    rows = skin.shape[1]
    barrier = pltpu.get_barrier_semaphore()
    for d in range(1, n_gx):
        peer = (lax.rem(gx + d, n_gx), gy)
        pl.semaphore_signal(barrier, inc=1, device_id=peer, device_id_type=MESH)
    for d in range(1, n_gy):
        peer = (gx, lax.rem(gy + d, n_gy))
        pl.semaphore_signal(barrier, inc=1, device_id=peer, device_id_type=MESH)
    pl.semaphore_wait(barrier, n_gx + n_gy - 2)

    def swap(source, middle, target, sems):
        send_x, recv_x, send_y, recv_y, local = sems
        own = pltpu.make_async_copy(source.at[gx], middle.at[gx], local)
        own.start()
        copies = []
        for d in range(1, n_gx):
            peer = lax.rem(gx + d, n_gx)
            copies.append(
                pltpu.make_async_remote_copy(
                    src_ref=source.at[peer],
                    dst_ref=middle.at[gx],
                    send_sem=send_x.at[d - 1],
                    recv_sem=recv_x.at[d - 1],
                    device_id=(peer, gy),
                    device_id_type=MESH,
                )
            )
        for copy in copies:
            copy.start()
        own.wait()
        for copy in copies:
            copy.wait()
        own = pltpu.make_async_copy(middle.at[:, gy], target.at[:, gy], local)
        own.start()
        copies = []
        for d in range(1, n_gy):
            peer = lax.rem(gy + d, n_gy)
            copies.append(
                pltpu.make_async_remote_copy(
                    src_ref=middle.at[:, peer],
                    dst_ref=target.at[:, gy],
                    send_sem=send_y.at[d - 1],
                    recv_sem=recv_y.at[d - 1],
                    device_id=(gx, peer),
                    device_id_type=MESH,
                )
            )
        for copy in copies:
            copy.start()
        own.wait()
        for copy in copies:
            copy.wait()

    swap(sent, here, there, sems[0:5])
    cells = jnp.concatenate([cell[0:1], cell[1:2]], axis=1)
    cell_row, cell_col = cells // lanes, cells % lanes
    pick = (lax.broadcasted_iota(jnp.int32, (lanes, 2 * tiles), 0) == cell_col).astype(jnp.bfloat16)
    in_row = lax.broadcasted_iota(jnp.int32, (rows, 2 * tiles), 0) == cell_row
    arrived = there[...].reshape(tiles, lanes).T
    spread = []
    for comp in range(2):
        values = jnp.concatenate([arrived[2 * comp : 2 * comp + 1], arrived[2 * comp + 1 : 2 * comp + 2]], axis=1)
        spread.append(jnp.where(in_row, values, 0.0))
    forcing = lax.dot_general(
        split(jnp.concatenate(spread, axis=0)),
        pick,
        (((1,), (1,)), ((), ())),
        preferred_element_type=jnp.float32,
    )
    level = skin[...].reshape(2 * rows, lanes) + joined(forcing)
    surface[...] = level.reshape(2, rows, lanes)
    found = joined(jnp.dot(split(level), pick, preferred_element_type=jnp.float32))
    replies = []
    for comp in range(2):
        values = jnp.where(in_row, found[comp * rows : (comp + 1) * rows], 0.0)
        values = jnp.sum(values, axis=0, keepdims=True)
        replies += [values[:, :tiles], values[:, tiles:]]
    replies.append(jnp.zeros((lanes - 4, tiles), jnp.float32))
    back[...] = jnp.concatenate(replies, axis=0).T.reshape(back.shape)
    swap(back, home, current, sems[5:10])


def couple(n_gx, n_gy, sent, skin, cell):
    tiles, lanes = n_gx * n_gy, skin.shape[2]
    box = (n_gx, n_gy, 1, lanes)
    dma = pltpu.SemaphoreType.DMA
    sems = [dma((n_gx - 1,)), dma((n_gx - 1,)), dma((n_gy - 1,)), dma((n_gy - 1,)), dma]
    return pl.pallas_call(
        functools.partial(couple_kernel, n_gx, n_gy),
        out_shape=(shape(*skin.shape), shape(*box)),
        in_specs=[VMEM] * 3,
        out_specs=(VMEM,) * 2,
        scratch_shapes=[pltpu.VMEM(box, jnp.float32)] * 4 + sems + sems,
        compiler_params=grant(4, collective_id=SUB, has_side_effects=True),
        name="couple",
    )(sent.reshape(box), skin, cell)


def finish_kernel(ocean, surface, current, slots, vel, vel_out, ocean_out, sem):
    copy = pltpu.make_async_copy(surface, ocean_out.at[pl.ds(0, 2), 0], sem)
    copy.start()
    blocks, discs = vel.shape[1], vel.shape[2]
    tiles = current.shape[0]
    got = current[...].reshape(tiles, discs).T
    spots = jnp.concatenate([slots[0:1], slots[1:2]], axis=1)
    place = lax.broadcasted_iota(jnp.int32, (blocks, 2 * tiles), 0) == spots
    for comp in range(2):
        values = jnp.concatenate([got[2 * comp : 2 * comp + 1], got[2 * comp + 1 : 2 * comp + 2]], axis=1)
        values = jnp.sum(jnp.where(place, values, 0.0), axis=1, keepdims=True)
        speed = vel[comp]
        vel_out[comp] = speed + DRAG_BACK * (values - speed)
    copy.wait()


def finish(ocean, surface, current, slots, vel):
    tiles = current.shape[0] * current.shape[1]
    return pl.pallas_call(
        finish_kernel,
        out_shape=(shape(*vel.shape), shape(*ocean.shape)),
        in_specs=[ANY, VMEM, VMEM, VMEM, VMEM],
        out_specs=(VMEM, ANY),
        scratch_shapes=[pltpu.SemaphoreType.DMA],
        input_output_aliases={0: 1},
        compiler_params=grant(4),
        name="finish",
    )(ocean, surface, current.reshape(tiles, 1, current.shape[3]), slots, vel)


def body(
    disc_pos,
    disc_vel,
    radius,
    bond_list,
    contact_mask,
    remap_block,
    ocean_state,
    mix_coef,
    remap_cell,
    fold_perm,
):
    n_gx, n_gy = lax.axis_size("gx"), lax.axis_size("gy")
    rows_dev, cols_dev, discs = radius.shape
    blocks = rows_dev * cols_dev
    slots = remap_block[0].T
    cell = remap_cell[0].T
    perm = fold_perm.reshape(1, discs)
    position = disc_pos.reshape(2, blocks, discs)
    velocity = disc_vel.reshape(2, blocks, discs)
    rad = radius.reshape(blocks, discs)
    bonds = bond_list.reshape(BONDS, blocks, discs)
    sea_shape = (4, mix_coef.shape[0], discs)
    columns, bottom, top, state, edges, mask = pack(n_gy, ocean_state, position, rad, contact_mask)
    flat = (4 * mix_coef.shape[0], discs)
    halo, lon, lat, rows, perms = exchange(
        0, n_gx, n_gy, state, edges, top.reshape(flat), bottom.reshape(flat), columns, perm
    )
    first = halo
    position, velocity, edges, turned = contact_step(
        0, n_gy, position, velocity, rad, bonds, mask, halo, first, rows, perms
    )
    halo, mirror = exchange(1, n_gx, n_gy, position, edges, turned)
    position, velocity, edges = contact_step(
        1, n_gy, position, velocity, rad, bonds, mask, halo, first
    )
    (halo,) = exchange(2, n_gx, n_gy, position, edges)
    position, velocity, sent = contact_step(
        2, n_gy, position, velocity, rad, bonds, mask, halo, first, slots
    )
    ocean, skin = ocean_step(
        n_gy, ocean_state, mix_coef, lon, lat.reshape(2, *sea_shape), mirror.reshape(sea_shape)
    )
    surface, current = couple(n_gx, n_gy, sent, skin, cell)
    vel_next, ocean_next = finish(ocean, surface, current, slots, velocity)
    return (position.reshape(disc_pos.shape), vel_next.reshape(disc_vel.shape), ocean_next)


def solution(mesh):
    in_specs = (
        P(None, "gy", "gx", None),
        P(None, "gy", "gx", None),
        P("gy", "gx", None),
        P(None, "gy", "gx", None),
        P(None, "gy", "gx"),
        P(("gx", "gy"), None, None),
        P(None, None, "gy", "gx"),
        P(None, "gy", "gx"),
        P(("gx", "gy"), None, None),
        P("gx"),
    )
    out_specs = (P(None, "gy", "gx", None), P(None, "gy", "gx", None), P(None, None, "gy", "gx"))
    return jax.shard_map(body, mesh=mesh, in_specs=in_specs, out_specs=out_specs, check_vma=False)
```

```python
import functools

import jax
import jax.numpy as jnp
from jax import lax
from jax.experimental import pallas as pl
from jax.experimental.pallas import tpu as pltpu
from jax.sharding import PartitionSpec as P

BONDS = 4
SUB = 3
SOFTEN = 0.0001
STIFFNESS = 2.0
BOND_STIFF = 0.1
TIME_STEP = 0.05
DRAG_ICE = 15.0
DRAG_BACK = 0.5
VERT_MIX = 0.1
SPIN_RATE = 0.3
NEIGHBOURS = ((-1, -1), (-1, 0), (-1, 1), (0, -1), (0, 1), (1, -1), (1, 0), (1, 1))
TOGETHER = 4
STATIC = 2
ROWS = 2
GROUP = 4
ITEMS = 8
CHUNK = 8
TURNERS = 12
EARLY = 32
TURN_ROWS = 16
MESH = pl.DeviceIdType.MESH
VMEM = pl.BlockSpec(memory_space=pltpu.VMEM)
ANY = pl.BlockSpec(memory_space=pl.ANY)
HBM = pl.BlockSpec(memory_space=pltpu.HBM)


def grant(mib, **more):
    return pltpu.CompilerParams(vmem_limit_bytes=mib << 20, **more)


def shape(*dims):
    return jax.ShapeDtypeStruct(dims, jnp.float32)


def split(value):
    high = value.astype(jnp.bfloat16)
    rest = value - high.astype(jnp.float32)
    middle = rest.astype(jnp.bfloat16)
    low = (rest - middle.astype(jnp.float32)).astype(jnp.bfloat16)
    return jnp.concatenate([high, middle, low], axis=0)


def joined(value):
    rows = value.shape[0] // 3
    return value[:rows] + value[rows : 2 * rows] + value[2 * rows :]


def lane_take(rows, index):
    return jnp.take_along_axis(rows, index, axis=1, mode="promise_in_bounds")


def pair_terms(acc_x, acc_y, own_x, own_y, own_r, other_x, other_y, other_r):
    sep_x = other_x - own_x
    sep_y = other_y - own_y
    inverse = lax.rsqrt(sep_x * sep_x + sep_y * sep_y + SOFTEN)
    push = jnp.maximum((other_r + own_r) * inverse - 1.0, 0.0)
    return acc_x + push * sep_x, acc_y + push * sep_y


def turn(rows, perms, turned):
    lanes = rows.shape[2]

    def one(h, carry):
        wanted = jnp.broadcast_to(perms[h], (8, lanes))
        owner, column = wanted // lanes, wanted % lanes
        for half in range(TURN_ROWS // 8):
            at = pl.ds(8 * half, 8)
            got = jnp.zeros((8, lanes), jnp.float32)
            for source in range(rows.shape[0]):
                got = jnp.where(owner == source, lane_take(rows[source, at, :], column), got)
            turned[h, at, :] = got
        return carry

    lax.fori_loop(0, perms.shape[0], one, 0)


def own_setup(pos, rad, columns):
    for comp in range(2):
        columns[comp] = pos[comp].T
    columns[2] = rad[...].T


def gather_own(pos, rad, b):
    own = (pos[0, pl.ds(b, 1), :], pos[1, pl.ds(b, 1), :], rad[pl.ds(b, 1), :])
    return own, jnp.full((8, rad.shape[1]), b, jnp.int32)


def visit(source, at, target, acc):
    own, index = target
    return pair_terms(*acc, *own, *[lane_take(source[k, at, :], index) for k in range(3)])


def own_forces(first, count, pos, rad, columns, force):
    blocks, discs = rad.shape
    zero = jnp.zeros((8, discs), jnp.float32)

    def some(t, carry):
        for u in range(TOGETHER):
            b = first + t * TOGETHER + u
            target = gather_own(pos, rad, b)
            acc = (zero, zero)
            for c in range(discs // 8):
                acc = visit(columns, pl.ds(c * 8, 8), target, acc)
            for k in range(2):
                force[k, pl.ds(b, 1), :] = jnp.sum(acc[k], axis=0, keepdims=True)
        return carry

    lax.fori_loop(0, count // TOGETHER, some, 0)


def contact_kernel(which, n_gy, pos, vel, rad, bonds, mask, held, halo, halo_rad, *refs):
    last = which == SUB - 1
    if last:
        slots, pos_out, vel_out, sent, *scratch = refs
    elif which == 1:
        rows, perms, pos_out, vel_out, edges, turned, *scratch = refs

        @pl.when(lax.axis_index("gy") == n_gy - 1)
        def _():
            turn(rows, perms, turned)

    else:
        pos_out, vel_out, edges, *scratch = refs
    wide, found, found_t, force, tally, counts, work, sem = scratch
    rows_dev, cols_dev = wide.shape[1] - 2, pos.shape[1] // (wide.shape[1] - 2)
    blocks, discs = rad.shape
    for comp in range(3):
        source = pos.at[comp] if comp < 2 else rad

        def frame(side, first, size):
            if comp < 2:
                return halo[side, comp, pl.ds(first, size), :]
            return halo_rad[side, pl.ds(first, size), :]

        for y in range(rows_dev):
            wide[comp, y + 1, pl.ds(1, cols_dev), :] = source[pl.ds(y * cols_dev, cols_dev), :]
            wide[comp, y + 1, pl.ds(0, 1), :] = frame(3, y, 1)
            wide[comp, y + 1, pl.ds(cols_dev + 1, 1), :] = frame(4, y, 1)
        for side, y in ((0, 0), (5, rows_dev + 1)):
            wide[comp, y, pl.ds(0, 1), :] = frame(side, 7, 1)
            wide[comp, y, pl.ds(1, cols_dev), :] = frame(side + 1, 0, cols_dev)
            wide[comp, y, pl.ds(cols_dev + 1, 1), :] = frame(side + 2, 0, 1)
    lane = lax.broadcasted_iota(jnp.int32, (8, discs), 1)
    lane_f = lane.astype(jnp.float32)
    tri_row = lax.broadcasted_iota(jnp.int32, (discs, 2 * discs), 0)
    tri_col = lax.broadcasted_iota(jnp.int32, (discs, 2 * discs), 1)
    triangle = (tri_row <= tri_col).astype(jnp.bfloat16)

    def collect(start):
        def one_row(step_y, carry):
            for half in range(ROWS * cols_dev // 8):
                y = step_y * ROWS + half // (cols_dev // 8)
                x0 = half % (cols_dev // 8) * 8
                at = pl.multiple_of(y * cols_dev + x0, 8)
                own = [pos[0, pl.ds(at, 8), :], pos[1, pl.ds(at, 8), :], rad[pl.ds(at, 8), :]]
                reach = jnp.max(own[2], axis=1, keepdims=True)
                low = [jnp.min(own[c], axis=1, keepdims=True) - reach for c in range(2)]
                high = [jnp.max(own[c], axis=1, keepdims=True) + reach for c in range(2)]
                weights = mask[pl.ds(at, 8), :]
                near = []
                for k, (sy, sx) in enumerate(NEIGHBOURS):
                    where = (y + 1 + sy, pl.ds(x0 + 1 + sx, 8), slice(None))
                    nx = wide[(0,) + where] + float(sx)
                    ny = wide[(1,) + where] + float(sy)
                    nr = wide[(2,) + where]
                    close = (nx - nr < high[0]) & (nx + nr > low[0])
                    close = close & (ny - nr < high[1]) & (ny + nr > low[1])
                    close = close & (weights[:, k : k + 1] > 0.5)
                    near.append((nx, ny, nr, close))
                flags = jnp.concatenate([n[3].astype(jnp.float32) for n in near], axis=0)
                ranks = jnp.dot(
                    flags.astype(jnp.bfloat16), triangle, preferred_element_type=jnp.float32
                )
                base = jnp.zeros((8, discs), jnp.float32) - start
                gx = jnp.zeros((8, discs), jnp.float32)
                gy = jnp.zeros((8, discs), jnp.float32)
                gr = jnp.full((8, discs), -1.0, jnp.float32)
                for k in range(8):
                    nx, ny, nr, _ = near[k]
                    rank = ranks[8 * k : 8 * k + 8, :discs]
                    total = ranks[8 * k : 8 * k + 8, discs:]
                    want = lane_f - base
                    source = jnp.zeros((8, discs), jnp.int32)
                    step = discs // 2
                    while step >= 1:
                        probe = lane_take(rank, source + (step - 1))
                        source = jnp.where(probe <= want, source + step, source)
                        step //= 2
                    valid = (want >= 0.0) & (want < total)
                    gx = jnp.where(valid, lane_take(nx, source), gx)
                    gy = jnp.where(valid, lane_take(ny, source), gy)
                    gr = jnp.where(valid, lane_take(nr, source), gr)
                    base = base + total
                found[0, pl.ds(at, 8), :] = gx
                found[1, pl.ds(at, 8), :] = gy
                found[2, pl.ds(at, 8), :] = gr
                found[3, pl.ds(at, 8), :] = base
            return carry

        lax.fori_loop(0, rows_dev // ROWS, one_row, 0)
        for comp in range(3):
            found_t[comp] = found[comp].T
        left = found[3].T[0:8]
        groups = jnp.clip(jnp.ceil(left * (1.0 / 32.0)), 0.0, 4.0).astype(jnp.int32)
        passes = jnp.ceil(jnp.max(left, axis=1, keepdims=True) * (1.0 / discs)).astype(jnp.int32)
        tally[0:8] = groups
        tally[8:16] = jnp.broadcast_to(passes, (8, discs))
        copy = pltpu.make_async_copy(tally, counts, sem)
        copy.start()
        copy.wait()

    zero = jnp.zeros((8, discs), jnp.float32)
    span = 8 * GROUP

    def group(b, g, scale, target, acc):
        for c in range(GROUP):
            at = pl.ds(pl.multiple_of(g * span + c * 8, 8), 8)
            acc = visit(found_t, at, target, acc)
        return acc

    def sweep(static):
        def some(t, size):
            for u in range(TOGETHER):
                b = t * TOGETHER + u
                target = gather_own(pos, rad, b)
                acc = (zero, zero)
                for g in range(static):
                    acc = group(b, g, None, target, acc)
                if static:
                    for k in range(2):
                        force[k, pl.ds(b, 1), :] = jnp.sum(acc[k], axis=0, keepdims=True)
                for g in range(static, discs // span):
                    work[size] = b * 8 + g
                    size = size + (counts[0, b] > g).astype(jnp.int32)
            return size

        size = lax.fori_loop(0, blocks // TOGETHER, some, 0)

        def rest(i, carry):
            for u in range(ITEMS):
                slot = i * ITEMS + u
                item = jnp.where(slot < size, work[slot], 0)
                scale = jnp.where(slot < size, 1.0, 0.0)
                b, g = item // 8, item % 8
                target = gather_own(pos, rad, b)
                acc = group(b, g, scale, target, (zero, zero))
                for k in range(2):
                    total = jnp.sum(acc[k], axis=0, keepdims=True)
                    force[k, pl.ds(b, 1), :] += total * scale
            return carry

        lax.fori_loop(0, (size + ITEMS - 1) // ITEMS, rest, 0)

    collect(0.0)
    sweep(STATIC)

    def more(p, carry):
        collect(p.astype(jnp.float32) * discs)
        sweep(0)
        return carry

    lax.fori_loop(1, counts[8, 0], more, 0)

    def update(g, carry):
        at = pl.ds(pl.multiple_of(g * 8, 8), 8)
        scale = 0.06 / rad[at, :]
        scale = scale * scale
        for k in range(2):
            here = pos[k, at, :]
            bonded = lane_take(here, bonds[0, at, :])
            for p in range(1, BONDS):
                bonded = bonded + lane_take(here, bonds[p, at, :])
            total = BOND_STIFF * (bonded - BONDS * here) - STIFFNESS * (held[k, at, :] + force[k, at, :])
            speed = vel[k, at, :] + total * scale
            vel_out[k, at, :] = speed
            pos_out[k, at, :] = here + TIME_STEP * speed
        return carry

    lax.fori_loop(0, blocks // 8, update, 0)
    if last:
        spots = [jnp.broadcast_to(slots[k : k + 1], (8, blocks)) for k in range(2)]
        rows = []
        for comp in range(2):
            drag = rad[...] * rad[...] * vel_out[comp]
            total = DRAG_ICE * jnp.sum(drag.T, axis=0, keepdims=True)
            total = jnp.broadcast_to(total, (8, blocks))
            for spot in spots:
                moved = lane_take(total, jnp.maximum(spot, 0))
                rows.append(jnp.where(spot >= 0, moved, 0.0)[0:1])
        rows.append(jnp.zeros((blocks - 4, blocks), jnp.float32))
        sent[:, 0, :] = jnp.concatenate(rows, axis=0).T
    else:
        for side in range(2):
            for comp in range(2):
                at = pl.ds(side * (cols_dev - 1), rows_dev, stride=cols_dev)
                edges[side, comp] = pos_out[comp, at, :]


def contact_step(which, n_gy, pos, vel, rad, bonds, mask, held, halo, halo_rad, *extra):
    blocks, discs = rad.shape
    rows_dev = blocks // 16
    square = shape(2, blocks, discs)
    tail = shape(blocks, 1, discs) if which == SUB - 1 else shape(2, 2, rows_dev, discs)
    outs = (square, square, tail)
    if which == 1:
        outs += (shape(*extra[0].shape),)
    args = (pos, vel, rad, bonds, mask, held, halo, halo_rad) + extra
    return pl.pallas_call(
        functools.partial(contact_kernel, which, n_gy),
        out_shape=outs,
        in_specs=[VMEM] * len(args),
        out_specs=(VMEM,) * len(outs),
        scratch_shapes=[
            pltpu.VMEM((3, rows_dev + 2, 24, discs), jnp.float32),
            pltpu.VMEM((4, blocks, discs), jnp.float32),
            pltpu.VMEM((3, discs, blocks), jnp.float32),
            pltpu.VMEM((2, blocks, discs), jnp.float32),
            pltpu.VMEM((16, blocks), jnp.int32),
            pltpu.SMEM((16, blocks), jnp.int32),
            pltpu.SMEM((blocks * 4 + 2 * ITEMS,), jnp.int32),
            pltpu.SemaphoreType.DMA,
        ],
        compiler_params=grant(16),
        name=("contact_first", "contact", "contact_last")[which],
    )(*args)


def prep_kernel(n_gy, pos_in, rad_in, allowed_in, pos, rad, edges, mask, allowed, sems):
    copies = [
        pltpu.make_async_copy(allowed_in, allowed, sems.at[0]),
        pltpu.make_async_copy(pos_in, pos, sems.at[1]),
        pltpu.make_async_copy(rad_in, rad, sems.at[2]),
    ]
    for copy in copies:
        copy.start()
    copies[0].wait()
    lane = lax.broadcasted_iota(jnp.int32, (8, 128), 1)
    _, rows_dev, cols_dev = allowed.shape
    spread = jnp.zeros((8, 128), jnp.float32)
    for y in range(rows_dev):
        part = allowed[:, y, :].astype(jnp.float32)
        part = jnp.concatenate([part, jnp.zeros((8, 128 - cols_dev), jnp.float32)], axis=1)
        spread = spread + (pltpu.roll(part, y * cols_dev, 1) if y else part)
    which = lax.broadcasted_iota(jnp.int32, (8, 128), 0)
    shift_y = jnp.where(which < 3, -1, jnp.where(which < 5, 0, 1))
    row = lax.axis_index("gy") * rows_dev + lane // cols_dev + shift_y
    spread = jnp.where((row >= 0) & (row < n_gy * rows_dev), spread, 0.0)
    mask[...] = jnp.concatenate([spread, jnp.zeros((120, 128), jnp.float32)], axis=0).T
    copies[1].wait()
    copies[2].wait()
    for comp in range(3):
        source = pos.at[comp] if comp < 2 else rad
        for side in range(2):
            edges[side, comp] = source[pl.ds(side * 15, 8, stride=16), :]


def prep(n_gy, pos, rad, allowed):
    return pl.pallas_call(
        functools.partial(prep_kernel, n_gy),
        out_shape=(shape(*pos.shape), shape(*rad.shape), shape(2, 3, 8, 128), shape(*rad.shape)),
        in_specs=[HBM] * 3,
        out_specs=(VMEM,) * 4,
        scratch_shapes=[pltpu.VMEM(allowed.shape, jnp.int32), pltpu.SemaphoreType.DMA((3,))],
        compiler_params=grant(4),
        name="prep",
    )(pos, rad, allowed)


def pack_kernel(ocean, after, columns, bottom, top):
    rows = ocean.shape[2]
    lane = lax.broadcasted_iota(jnp.int32, (8, 128), 1)
    packed = [jnp.zeros((8, 128), jnp.float32)] * 2
    for field in range(4):
        for layer in range(CHUNK):
            for v in range(rows // 8):
                g = (field * CHUNK + layer) * (rows // 8) + v
                place = g % 64
                turned = pltpu.roll(ocean[field, layer, pl.ds(8 * v, 8), :], 2 * place + 1, 1)
                packed[g // 64] = jnp.where(lane // 2 == place, turned, packed[g // 64])
    columns[0] = jnp.concatenate(packed, axis=0)
    bottom[...] = ocean[:, :, 0, :]
    top[...] = ocean[:, :, rows - 1, :]


def pack(ocean, after):
    fields, layers, rows, lanes = ocean.shape
    steps = layers // CHUNK
    row = pl.BlockSpec((fields, CHUNK, lanes), lambda i: (0, i, 0))
    return pl.pallas_call(
        pack_kernel,
        grid=(steps,),
        out_shape=(
            shape(steps, 16, lanes),
            shape(fields, layers, lanes),
            shape(fields, layers, lanes),
        ),
        in_specs=[pl.BlockSpec((fields, CHUNK, rows, lanes), lambda i: (0, i, 0, 0)), ANY],
        out_specs=(pl.BlockSpec((1, 16, lanes), lambda i: (i, 0, 0)), row, row),
        compiler_params=grant(8),
        name="pack",
    )(ocean, after)


def exchange_kernel(which, n_gx, n_gy, *refs):
    if which == 0:
        pos, rad, edges, halo, held, halo_rad, columns, send_sem, recv_sem, rad_send, rad_recv = refs
    elif which == 1:
        pos, rad, edges, top, bottom, sides, perm, halo, held, lon, lat, rows, perms, *scratch = refs
        columns, send_sem, recv_sem, sea_send, sea_recv, far_send, far_recv, *scratch = scratch
        perm_send, perm_recv, own = scratch
    else:
        pos, rad, edges, turned, halo, held, mirror, columns, send_sem, recv_sem, *scratch = refs
        far_send, far_recv, own = scratch
    gx, gy = lax.axis_index("gx"), lax.axis_index("gy")
    is_top = gy == n_gy - 1

    def at(dx, dy):
        return lax.rem(gx + dx + n_gx, n_gx), lax.rem(gy + dy + n_gy, n_gy)

    barrier = pltpu.get_barrier_semaphore()
    for dy, dx in NEIGHBOURS:
        pl.semaphore_signal(barrier, inc=1, device_id=at(dx, dy), device_id_type=MESH)
    if which > 0:

        @pl.when(is_top)
        def _():
            for d in range(1, n_gx):
                pl.semaphore_signal(barrier, inc=1, device_id=at(d, 0), device_id_type=MESH)

    blocks = rad.shape[0]
    own_setup(pos, rad, columns)
    own_forces(0, EARLY, pos, rad, columns, held)
    if which > 0:

        @pl.when(is_top)
        def _():
            pl.semaphore_wait(barrier, len(NEIGHBOURS) + n_gx - 1)

        @pl.when(jnp.logical_not(is_top))
        def _():
            pl.semaphore_wait(barrier, len(NEIGHBOURS))

    else:
        pl.semaphore_wait(barrier, len(NEIGHBOURS))

    def send(source, target, sems, index, device):
        return pltpu.make_async_remote_copy(
            src_ref=source,
            dst_ref=target,
            send_sem=sems[0].at[index],
            recv_sem=sems[1].at[index],
            device_id=device,
            device_id_type=MESH,
        )

    def halo_copies(body, part, target, sems):
        copies = []
        for k, (sy, sx) in enumerate(NEIGHBOURS):
            first = 0 if sy == 1 else blocks - 16
            first = first + 8 if sx == -1 else first
            size = 16 if sx == 0 else 8
            source = part(0 if sx == 1 else 1) if sy == 0 else body(pl.ds(first, size))
            copies.append(send(source, target(k, pl.ds(0, size)), sems, k, at(-sx, -sy)))
        return copies

    copies = halo_copies(
        lambda rows: pos.at[:, rows, :],
        lambda side: edges.at[side, pl.ds(0, 2)],
        lambda k, rows: halo.at[k, :, rows, :],
        (send_sem, recv_sem),
    )
    if which == 0:
        copies += halo_copies(
            lambda rows: rad.at[rows, :],
            lambda side: edges.at[side, 2],
            lambda k, rows: halo_rad.at[k, rows, :],
            (rad_send, rad_recv),
        )
    for copy in copies:
        copy.start()
    if which == 1:
        sea = (sea_send, sea_recv)
        later = [
            send(sides, lon.at[0], sea, 0, at(1, 0)),
            send(sides, lon.at[1], sea, 1, at(-1, 0)),
            send(top, lat.at[0], sea, 2, at(0, 1)),
            send(bottom, lat.at[1], sea, 3, at(0, -1)),
        ]
        copies += later

    if which == 1:
        first = pl.multiple_of(jnp.minimum(gx, TURNERS - 1) * TURN_ROWS, TURN_ROWS)
        kept = pltpu.make_async_copy(perm, perms.at[gx], own.at[0])
        mine = pltpu.make_async_copy(top.at[pl.ds(first, TURN_ROWS), :], rows.at[gx], own.at[1])
        notes, far = [], []
        for d in range(1, n_gx):
            peer = lax.rem(gx + d, n_gx)
            start = pl.multiple_of(jnp.minimum(peer, TURNERS - 1) * TURN_ROWS, TURN_ROWS)
            notes.append(send(perm, perms.at[gx], (perm_send, perm_recv), d - 1, at(d, 0)))
            source = top.at[pl.ds(start, TURN_ROWS), :]
            far.append(send(source, rows.at[gx], (far_send, far_recv), d - 1, at(d, 0)))

        @pl.when(is_top)
        def _():
            kept.start()
            for d in range(1, n_gx):
                notes[d - 1].start()

                @pl.when(lax.rem(gx + d, n_gx) < TURNERS)
                def _(copy=far[d - 1]):
                    copy.start()

            @pl.when(gx < TURNERS)
            def _():
                mine.start()

        for copy in later:
            copy.start()

    if which == 2:
        me = jnp.minimum(gx, TURNERS - 1)
        mine = pltpu.make_async_copy(turned.at[gx], mirror.at[me], own)
        far = []
        for d in range(1, n_gx):
            source = turned.at[lax.rem(gx + d, n_gx)]
            far.append(send(source, mirror.at[me], (far_send, far_recv), d - 1, at(d, 0)))

        @pl.when(is_top & (gx < TURNERS))
        def _():
            mine.start()
            for copy in far:
                copy.start()

    own_forces(EARLY, blocks - EARLY, pos, rad, columns, held)
    for copy in copies:
        copy.wait()
    if which == 1:

        @pl.when(is_top)
        def _():
            kept.wait()
            for d in range(1, n_gx):
                notes[d - 1].wait()

                @pl.when(lax.rem(gx + d, n_gx) < TURNERS)
                def _(copy=far[d - 1]):
                    copy.wait_send()

            @pl.when(gx < TURNERS)
            def _():
                mine.wait()
                for copy in far:
                    copy.wait_recv()

    if which == 2:

        @pl.when(is_top & (gx < TURNERS))
        def _():
            mine.wait()
            for copy in far:
                copy.wait_send()

        @pl.when(is_top)
        def _():
            for d in range(1, n_gx):

                @pl.when(lax.rem(gx - d + n_gx, n_gx) < TURNERS)
                def _(copy=far[d - 1]):
                    copy.wait_recv()


def exchange(which, n_gx, n_gy, pos, rad, edges, *args):
    lanes = rad.shape[1]
    outs = [shape(8, 2, 16, lanes), shape(*pos.shape)]
    dma = pltpu.SemaphoreType.DMA
    scratch = [pltpu.VMEM((3, lanes, rad.shape[0]), jnp.float32), dma((8,)), dma((8,))]
    far = [dma((n_gx - 1,)), dma((n_gx - 1,))]
    if which == 0:
        outs += [shape(8, 16, lanes)]
        scratch += [dma((8,)), dma((8,))]
    if which == 1:
        top, bottom, sides, perm = args
        outs += [shape(2, *sides.shape), shape(2, *top.shape)]
        outs += [shape(n_gx, TURN_ROWS, lanes), jax.ShapeDtypeStruct((n_gx, 1, lanes), jnp.int32)]
        scratch += [dma((4,)), dma((4,))] + far + far + [dma((2,))]
    if which == 2:
        outs += [shape(TURNERS, TURN_ROWS, lanes)]
        scratch += far + [dma]
    return pl.pallas_call(
        functools.partial(exchange_kernel, which, n_gx, n_gy),
        out_shape=tuple(outs),
        in_specs=[VMEM] * (3 + len(args)),
        out_specs=(VMEM,) * len(outs),
        scratch_shapes=scratch,
        compiler_params=grant(8, collective_id=which, has_side_effects=True),
        name=("exchange_first", "exchange_second", "exchange_third")[which],
    )(pos, rad, edges, *args)


def ocean_kernel(n_gy, ocean, above, below, mix, lon, lat, mirror, out, skin):
    step = pl.program_id(0)
    rows, lanes = ocean.shape[2], ocean.shape[3]
    gy = lax.axis_index("gy")
    lane = lax.broadcasted_iota(jnp.int32, (rows, lanes), 1)
    sub = lax.broadcasted_iota(jnp.int32, (rows, lanes), 0)
    lane8 = lax.broadcasted_iota(jnp.int32, (8, lanes), 1)
    bands = []
    for half in range(2):
        at = pl.ds(8 * half, 8)
        west, east = pltpu.roll(lon[0, 0, at, :], 1, 1), pltpu.roll(lon[1, 0, at, :], lanes - 1, 1)
        bands.append(jnp.where(lane8 % 2 == 1, west, east))
    spin = 2.0 * ((gy * rows + sub).astype(jnp.float32) + 0.5) / (rows * n_gy) - 1.0
    spin = SPIN_RATE * spin
    is_top, is_low = gy == n_gy - 1, gy == 0
    for field in range(4):
        folded = -mirror[field] if field < 2 else mirror[field]
        upper = jnp.where(is_top, folded, lat[1, field])
        lower = jnp.where(is_low, 0.0, lat[0, field])
        for layer in range(CHUNK):
            here = ocean[field, layer]
            up = ocean[field, layer - 1] if layer > 0 else above[field, 0]
            down = ocean[field, layer + 1] if layer < CHUNK - 1 else below[field, 0]
            sides = []
            for v in range(rows // 8):
                g = (field * CHUNK + layer) * (rows // 8) + v
                sides.append(pltpu.roll(bands[g // 64], lanes - 1 - 2 * (g % 64), 1))
            sides = jnp.concatenate(sides, axis=0)
            west = jnp.where(lane == 0, sides, pltpu.roll(here, 1, 1))
            east = jnp.where(lane == lanes - 1, sides, pltpu.roll(here, lanes - 1, 1))
            south = jnp.where(sub == 0, lower[layer : layer + 1], pltpu.roll(here, 1, 0))
            north = jnp.where(sub == rows - 1, upper[layer : layer + 1], pltpu.roll(here, rows - 1, 0))
            laplace = east + west + north + south - 4.0 * here
            value = here + mix[layer] * laplace + VERT_MIX * (up + down - 2.0 * here)
            if field == 0:
                value = value + spin * ocean[1, layer]
            if field == 1:
                value = value - spin * ocean[0, layer]
            out[field, layer] = value
            if field < 2 and layer == 0:

                @pl.when(step == 0)
                def _():
                    skin[field] = value


def ocean_step(n_gy, ocean, mix, lon, lat, mirror):
    fields, layers, rows, lanes = ocean.shape
    steps = layers // CHUNK
    block = pl.BlockSpec((fields, CHUNK, rows, lanes), lambda i: (0, i, 0, 0))
    one = (fields, 1, rows, lanes)
    return pl.pallas_call(
        functools.partial(ocean_kernel, n_gy),
        grid=(steps,),
        out_shape=(shape(*ocean.shape), shape(2, rows, lanes)),
        in_specs=[
            block,
            pl.BlockSpec(one, lambda i: (0, jnp.maximum(i * CHUNK - 1, 0), 0, 0)),
            pl.BlockSpec(one, lambda i: (0, jnp.minimum(i * CHUNK + CHUNK, layers - 1), 0, 0)),
            pl.BlockSpec((CHUNK, rows, lanes), lambda i: (i, 0, 0)),
            pl.BlockSpec((2, 1, 16, lanes), lambda i: (0, i, 0, 0)),
            pl.BlockSpec((2, fields, CHUNK, lanes), lambda i: (0, 0, i, 0)),
            pl.BlockSpec((fields, CHUNK, lanes), lambda i: (0, i, 0)),
        ],
        out_specs=(block, pl.BlockSpec((2, rows, lanes), lambda i: (0, 0, 0))),
        compiler_params=grant(24),
        name="ocean",
    )(ocean, ocean, ocean, mix, lon, lat, mirror)


def couple_kernel(n_gx, n_gy, sent, skin, cell, surface, current, *refs):
    here, there, back, home, *sems = refs
    gx, gy = lax.axis_index("gx"), lax.axis_index("gy")
    tiles, lanes = n_gx * n_gy, skin.shape[2]
    rows = skin.shape[1]
    barrier = pltpu.get_barrier_semaphore()
    for d in range(1, n_gx):
        peer = (lax.rem(gx + d, n_gx), gy)
        pl.semaphore_signal(barrier, inc=1, device_id=peer, device_id_type=MESH)
    for d in range(1, n_gy):
        peer = (gx, lax.rem(gy + d, n_gy))
        pl.semaphore_signal(barrier, inc=1, device_id=peer, device_id_type=MESH)
    pl.semaphore_wait(barrier, n_gx + n_gy - 2)

    def swap(source, middle, target, sems):
        send_x, recv_x, send_y, recv_y, local = sems
        own = pltpu.make_async_copy(source.at[gx], middle.at[gx], local)
        own.start()
        copies = []
        for d in range(1, n_gx):
            peer = lax.rem(gx + d, n_gx)
            copies.append(
                pltpu.make_async_remote_copy(
                    src_ref=source.at[peer],
                    dst_ref=middle.at[gx],
                    send_sem=send_x.at[d - 1],
                    recv_sem=recv_x.at[d - 1],
                    device_id=(peer, gy),
                    device_id_type=MESH,
                )
            )
        for copy in copies:
            copy.start()
        own.wait()
        for copy in copies:
            copy.wait()
        own = pltpu.make_async_copy(middle.at[:, gy], target.at[:, gy], local)
        own.start()
        copies = []
        for d in range(1, n_gy):
            peer = lax.rem(gy + d, n_gy)
            copies.append(
                pltpu.make_async_remote_copy(
                    src_ref=middle.at[:, peer],
                    dst_ref=target.at[:, gy],
                    send_sem=send_y.at[d - 1],
                    recv_sem=recv_y.at[d - 1],
                    device_id=(gx, peer),
                    device_id_type=MESH,
                )
            )
        for copy in copies:
            copy.start()
        own.wait()
        for copy in copies:
            copy.wait()

    swap(sent, here, there, sems[0:5])
    cells = jnp.concatenate([cell[0:1], cell[1:2]], axis=1)
    cell_row, cell_col = cells // lanes, cells % lanes
    pick = (lax.broadcasted_iota(jnp.int32, (lanes, 2 * tiles), 0) == cell_col).astype(jnp.bfloat16)
    in_row = lax.broadcasted_iota(jnp.int32, (rows, 2 * tiles), 0) == cell_row
    arrived = there[...].reshape(tiles, lanes).T
    spread = []
    for comp in range(2):
        values = jnp.concatenate([arrived[2 * comp : 2 * comp + 1], arrived[2 * comp + 1 : 2 * comp + 2]], axis=1)
        spread.append(jnp.where(in_row, values, 0.0))
    forcing = lax.dot_general(
        split(jnp.concatenate(spread, axis=0)),
        pick,
        (((1,), (1,)), ((), ())),
        preferred_element_type=jnp.float32,
    )
    level = skin[...].reshape(2 * rows, lanes) + joined(forcing)
    surface[...] = level.reshape(2, rows, lanes)
    found = joined(jnp.dot(split(level), pick, preferred_element_type=jnp.float32))
    replies = []
    for comp in range(2):
        values = jnp.where(in_row, found[comp * rows : (comp + 1) * rows], 0.0)
        values = jnp.sum(values, axis=0, keepdims=True)
        replies += [values[:, :tiles], values[:, tiles:]]
    replies.append(jnp.zeros((lanes - 4, tiles), jnp.float32))
    back[...] = jnp.concatenate(replies, axis=0).T.reshape(back.shape)
    swap(back, home, current, sems[5:10])


def couple(n_gx, n_gy, sent, skin, cell):
    tiles, lanes = n_gx * n_gy, skin.shape[2]
    box = (n_gx, n_gy, 1, lanes)
    dma = pltpu.SemaphoreType.DMA
    sems = [dma((n_gx - 1,)), dma((n_gx - 1,)), dma((n_gy - 1,)), dma((n_gy - 1,)), dma]
    return pl.pallas_call(
        functools.partial(couple_kernel, n_gx, n_gy),
        out_shape=(shape(*skin.shape), shape(*box)),
        in_specs=[VMEM] * 3,
        out_specs=(VMEM,) * 2,
        scratch_shapes=[pltpu.VMEM(box, jnp.float32)] * 4 + sems + sems,
        compiler_params=grant(4, collective_id=SUB, has_side_effects=True),
        name="couple",
    )(sent.reshape(box), skin, cell)


def finish_kernel(ocean, surface, current, slots, vel, vel_out, ocean_out, sem):
    copy = pltpu.make_async_copy(surface, ocean_out.at[pl.ds(0, 2), 0], sem)
    copy.start()
    blocks, discs = vel.shape[1], vel.shape[2]
    tiles = current.shape[0]
    got = current[...].reshape(tiles, discs).T
    spots = jnp.concatenate([slots[0:1], slots[1:2]], axis=1)
    place = lax.broadcasted_iota(jnp.int32, (blocks, 2 * tiles), 0) == spots
    for comp in range(2):
        values = jnp.concatenate([got[2 * comp : 2 * comp + 1], got[2 * comp + 1 : 2 * comp + 2]], axis=1)
        values = jnp.sum(jnp.where(place, values, 0.0), axis=1, keepdims=True)
        speed = vel[comp]
        vel_out[comp] = speed + DRAG_BACK * (values - speed)
    copy.wait()


def finish(ocean, surface, current, slots, vel):
    tiles = current.shape[0] * current.shape[1]
    return pl.pallas_call(
        finish_kernel,
        out_shape=(shape(*vel.shape), shape(*ocean.shape)),
        in_specs=[ANY, VMEM, VMEM, VMEM, VMEM],
        out_specs=(VMEM, ANY),
        scratch_shapes=[pltpu.SemaphoreType.DMA],
        input_output_aliases={0: 1},
        compiler_params=grant(4),
        name="finish",
    )(ocean, surface, current.reshape(tiles, 1, current.shape[3]), slots, vel)


def body(
    disc_pos,
    disc_vel,
    radius,
    bond_list,
    contact_mask,
    remap_block,
    ocean_state,
    mix_coef,
    remap_cell,
    fold_perm,
):
    n_gx, n_gy = lax.axis_size("gx"), lax.axis_size("gy")
    rows_dev, cols_dev, discs = radius.shape
    blocks = rows_dev * cols_dev
    slots = remap_block[0].T
    cell = remap_cell[0].T
    perm = fold_perm.reshape(1, discs)
    position = disc_pos.reshape(2, blocks, discs)
    velocity = disc_vel.reshape(2, blocks, discs)
    rad = radius.reshape(blocks, discs)
    bonds = bond_list.reshape(BONDS, blocks, discs)
    sea_shape = (4, mix_coef.shape[0], discs)
    flat = (4 * mix_coef.shape[0], discs)
    position, rad, edges, mask = prep(n_gy, position, rad, contact_mask)
    halo, held, halo_rad = exchange(0, n_gx, n_gy, position, rad, edges)
    position, velocity, edges = contact_step(
        0, n_gy, position, velocity, rad, bonds, mask, held, halo, halo_rad
    )
    sides, bottom, top = pack(ocean_state, edges)
    halo, held, lon, lat, rows, perms = exchange(
        1, n_gx, n_gy, position, rad, edges, top.reshape(flat), bottom.reshape(flat), sides, perm
    )
    position, velocity, edges, turned = contact_step(
        1, n_gy, position, velocity, rad, bonds, mask, held, halo, halo_rad, rows, perms
    )
    halo, held, mirror = exchange(2, n_gx, n_gy, position, rad, edges, turned)
    position, velocity, sent = contact_step(
        2, n_gy, position, velocity, rad, bonds, mask, held, halo, halo_rad, slots
    )
    ocean, skin = ocean_step(
        n_gy, ocean_state, mix_coef, lon, lat.reshape(2, *sea_shape), mirror.reshape(sea_shape)
    )
    surface, current = couple(n_gx, n_gy, sent, skin, cell)
    vel_next, ocean_next = finish(ocean, surface, current, slots, velocity)
    return (position.reshape(disc_pos.shape), vel_next.reshape(disc_vel.shape), ocean_next)


def solution(mesh):
    in_specs = (
        P(None, "gy", "gx", None),
        P(None, "gy", "gx", None),
        P("gy", "gx", None),
        P(None, "gy", "gx", None),
        P(None, "gy", "gx"),
        P(("gx", "gy"), None, None),
        P(None, None, "gy", "gx"),
        P(None, "gy", "gx"),
        P(("gx", "gy"), None, None),
        P("gx"),
    )
    out_specs = (P(None, "gy", "gx", None), P(None, "gy", "gx", None), P(None, None, "gy", "gx"))
    return jax.shard_map(body, mesh=mesh, in_specs=in_specs, out_specs=out_specs, check_vma=False)
```

```python
import functools

import jax
import jax.numpy as jnp
from jax import lax
from jax.experimental import pallas as pl
from jax.experimental.pallas import tpu as pltpu
from jax.sharding import PartitionSpec as P

BONDS = 4
SUB = 3
SOFTEN = 0.0001
STIFFNESS = 2.0
BOND_STIFF = 0.1
TIME_STEP = 0.05
DRAG_ICE = 15.0
DRAG_BACK = 0.5
VERT_MIX = 0.1
SPIN_RATE = 0.3
NEIGHBOURS = ((-1, -1), (-1, 0), (-1, 1), (0, -1), (0, 1), (1, -1), (1, 0), (1, 1))
ROWS = 1
OWN_STEP = 8
NEAR_STEP = 16
REST_STEP = 8
HALF = 64
MARKS = 16
CHUNK = 8
TURNERS = 12
EARLY = 32
TURN_ROWS = 16
MESH = pl.DeviceIdType.MESH
VMEM = pl.BlockSpec(memory_space=pltpu.VMEM)
ANY = pl.BlockSpec(memory_space=pl.ANY)
HBM = pl.BlockSpec(memory_space=pltpu.HBM)


def grant(mib, **more):
    return pltpu.CompilerParams(vmem_limit_bytes=mib << 20, **more)


def shape(*dims):
    return jax.ShapeDtypeStruct(dims, jnp.float32)


def split(value):
    high = value.astype(jnp.bfloat16)
    rest = value - high.astype(jnp.float32)
    middle = rest.astype(jnp.bfloat16)
    low = (rest - middle.astype(jnp.float32)).astype(jnp.bfloat16)
    return jnp.concatenate([high, middle, low], axis=0)


def joined(value):
    rows = value.shape[0] // 3
    return value[:rows] + value[rows : 2 * rows] + value[2 * rows :]


def lane_take(rows, index):
    return lax.gather(
        rows,
        index[..., None],
        lax.GatherDimensionNumbers(
            offset_dims=(),
            collapsed_slice_dims=(1,),
            start_index_map=(1,),
            operand_batching_dims=(0,),
            start_indices_batching_dims=(0,),
        ),
        slice_sizes=(1, 1),
        mode=lax.GatherScatterMode.PROMISE_IN_BOUNDS,
    )


def pieces(value):
    high = value.astype(jnp.bfloat16).astype(jnp.float32)
    middle = (value - high).astype(jnp.bfloat16).astype(jnp.float32)
    return high, middle, value - high - middle


def write_marks(parts, marks):
    for comp, part in enumerate(parts):
        for i, piece in enumerate(pieces(part)):
            marks[pl.ds(3 * comp + i, part.shape[0], stride=MARKS), :] = piece


def other_side(marks):
    row = lax.broadcasted_iota(jnp.int32, marks.shape, 0)
    marks = jnp.where(row < 9, marks, jnp.where(row < 12, 1.0, 0.0))
    return marks.T.astype(jnp.bfloat16)


def own_side(marks):
    row = lax.broadcasted_iota(jnp.int32, marks.shape, 0)
    sides = []
    for comp in range(3):
        moved = pltpu.roll(marks, 9 - 3 * comp, 0)
        moved = moved if comp == 2 else -moved
        fixed = jnp.where(row // 3 == comp, 1.0, 0.0)
        sides.append(jnp.where((row >= 9) & (row < 12), moved, fixed))
    return jnp.concatenate(sides, axis=1).astype(jnp.bfloat16)


def pair_sums(other, own):
    pairs = jnp.dot(other, own, preferred_element_type=jnp.float32)
    lanes = pairs.shape[1] // 3
    acc_x = acc_y = jnp.zeros((8, lanes), jnp.float32)
    for c in range(pairs.shape[0] // 8):
        rows = pairs[8 * c : 8 * c + 8]
        sep_x, sep_y, reach = rows[:, :lanes], rows[:, lanes : 2 * lanes], rows[:, 2 * lanes :]
        inverse = lax.rsqrt(sep_x * sep_x + sep_y * sep_y + SOFTEN)
        push = jnp.maximum(reach * inverse - 1.0, 0.0)
        acc_x = acc_x + push * sep_x
        acc_y = acc_y + push * sep_y
    return acc_x, acc_y


def marks_of(marks, b):
    return marks[pl.ds(pl.multiple_of(b * MARKS, MARKS), MARKS), :]


def turn(rows, perms, turned):
    lanes = rows.shape[2]

    def one(h, carry):
        wanted = jnp.broadcast_to(perms[h], (8, lanes))
        owner, column = wanted // lanes, wanted % lanes
        for half in range(TURN_ROWS // 8):
            at = pl.ds(8 * half, 8)
            got = jnp.zeros((8, lanes), jnp.float32)
            for source in range(rows.shape[0]):
                got = jnp.where(owner == source, lane_take(rows[source, at, :], column), got)
            turned[h, at, :] = got
        return carry

    lax.fori_loop(0, perms.shape[0], one, 0)


def own_forces(first, count, marks, force):
    def some(t, carry):
        for u in range(OWN_STEP):
            b = first + t * OWN_STEP + u
            own = marks_of(marks, b)
            acc = pair_sums(other_side(own), own_side(own))
            at = pl.ds(pl.multiple_of(b * 8, 8), 8)
            for k in range(2):
                force[k, at, :] = acc[k]
        return carry

    lax.fori_loop(0, count // OWN_STEP, some, 0)


def contact_kernel(which, n_gy, pos, vel, rad, bonds, mask, marks, held, halo, halo_rad, *refs):
    last = which == SUB - 1
    if last:
        slots, pos_out, vel_out, sent, *scratch = refs
    elif which == 1:
        rows, perms, pos_out, vel_out, edges, turned, *scratch = refs

        @pl.when(lax.axis_index("gy") == n_gy - 1)
        def _():
            turn(rows, perms, turned)

    else:
        pos_out, vel_out, edges, *scratch = refs
    wide, found, seen, force, tally, work, sem = scratch
    rows_dev, cols_dev = wide.shape[1] - 2, pos.shape[1] // (wide.shape[1] - 2)
    blocks, discs = rad.shape
    for comp in range(3):
        source = pos.at[comp] if comp < 2 else rad

        def frame(side, first, size):
            if comp < 2:
                return halo[side, comp, pl.ds(first, size), :]
            return halo_rad[side, pl.ds(first, size), :]

        for y in range(rows_dev):
            wide[comp, y + 1, pl.ds(1, cols_dev), :] = source[pl.ds(y * cols_dev, cols_dev), :]
            wide[comp, y + 1, pl.ds(0, 1), :] = frame(3, y, 1)
            wide[comp, y + 1, pl.ds(cols_dev + 1, 1), :] = frame(4, y, 1)
        for side, y in ((0, 0), (5, rows_dev + 1)):
            wide[comp, y, pl.ds(0, 1), :] = frame(side, 7, 1)
            wide[comp, y, pl.ds(1, cols_dev), :] = frame(side + 1, 0, cols_dev)
            wide[comp, y, pl.ds(cols_dev + 1, 1), :] = frame(side + 2, 0, 1)
    lane = lax.broadcasted_iota(jnp.int32, (8, discs), 1)
    lane_f = lane.astype(jnp.float32)
    tri_row = lax.broadcasted_iota(jnp.int32, (discs, 2 * discs), 0)
    tri_col = lax.broadcasted_iota(jnp.int32, (discs, 2 * discs), 1)
    triangle = (tri_row <= tri_col).astype(jnp.bfloat16)
    low_row = lax.broadcasted_iota(jnp.int32, (blocks, blocks), 0)
    low_col = lax.broadcasted_iota(jnp.int32, (blocks, blocks), 1)
    lower = (low_col <= low_row).astype(jnp.bfloat16)

    def collect(start):
        def one_row(step_y, carry):
            units, totals = [], []
            for half in range(ROWS * cols_dev // 8):
                y = step_y * ROWS + half // (cols_dev // 8)
                x0 = half % (cols_dev // 8) * 8
                at = pl.ds(pl.multiple_of(y * cols_dev + x0, 8), 8)
                own = [pos[0, at, :], pos[1, at, :], rad[at, :]]
                reach = jnp.max(own[2], axis=1, keepdims=True)
                low = [jnp.min(own[c], axis=1, keepdims=True) - reach for c in range(2)]
                high = [jnp.max(own[c], axis=1, keepdims=True) + reach for c in range(2)]
                weights = mask[at, :]
                flags = []
                places = []
                for k, (sy, sx) in enumerate(NEIGHBOURS):
                    place = (y + 1 + sy, pl.ds(x0 + 1 + sx, 8), slice(None))
                    nx, ny, nr = (wide[(c,) + place] for c in range(3))
                    close = (nx - nr < high[0] - float(sx)) & (nx + nr > low[0] - float(sx))
                    close = close & (ny - nr < high[1] - float(sy)) & (ny + nr > low[1] - float(sy))
                    close = close & (weights[:, k : k + 1] > 0.5)
                    flags.append(close.astype(jnp.float32))
                    places.append(place)
                ranks = jnp.dot(
                    jnp.concatenate(flags, axis=0).astype(jnp.bfloat16),
                    triangle,
                    preferred_element_type=jnp.float32,
                )
                base = jnp.zeros((8, discs), jnp.float32) - start
                for k in range(8):
                    rank = ranks[8 * k : 8 * k + 8, :discs]
                    total = ranks[8 * k : 8 * k + 8, discs:]
                    want = lane_f - base
                    source = jnp.zeros((8, discs), jnp.int32)
                    units.append((half, k, source, places[k], rank, total, want))
                    base = base + total
                totals.append((at, base))
            sources = [u[2] for u in units]
            step = discs // 2
            while step >= 1:
                probes = [lane_take(u[4], i + (step - 1)) for u, i in zip(units, sources)]
                sources = [
                    jnp.where(probe <= u[6], i + step, i)
                    for probe, u, i in zip(probes, units, sources)
                ]
                step //= 2
            for half, (at, base) in enumerate(totals):
                mine = [(u, i) for u, i in zip(units, sources) if u[0] == half]
                for comp in range(3):
                    got = jnp.full((8, discs), -1.0 if comp == 2 else 0.0, jnp.float32)
                    for (_, k, _, place, _, total, want), source in mine:
                        valid = (want >= 0.0) & (want < total)
                        value = wide[(comp,) + place]
                        if comp < 2 and NEIGHBOURS[k][1 - comp] != 0:
                            value = value + float(NEIGHBOURS[k][1 - comp])
                        got = jnp.where(valid, lane_take(value, source), got)
                    found[comp, at, :] = got
                found[3, at, :] = base
            return carry

        lax.fori_loop(0, rows_dev // ROWS, one_row, 0)
        write_marks([found[k] for k in range(3)], seen)
        left = found[3]
        size = jnp.where(left > float(HALF), 1.0, 0.0)
        ends = jnp.dot(lower, size.astype(jnp.bfloat16), preferred_element_type=jnp.float32)
        spot = lax.broadcasted_iota(jnp.int32, (1, discs), 1).astype(jnp.float32)
        block = jnp.sum(jnp.where(ends <= spot, 1.0, 0.0), axis=0, keepdims=True)
        tally[0:1] = block.astype(jnp.int32)
        tally[1:2] = ends[blocks - 1 :].astype(jnp.int32)
        deepest = jnp.max(left, axis=0, keepdims=True)
        tally[2:3] = jnp.ceil(deepest * (1.0 / discs)).astype(jnp.int32)
        copy = pltpu.make_async_copy(tally, work, sem)
        copy.start()
        copy.wait()

    def meet(b, part, fresh):
        at = pl.ds(pl.multiple_of(b * 8, 8), 8)
        b = jnp.minimum(b, blocks - 1)
        other = other_side(marks_of(seen, b))[part * HALF : (part + 1) * HALF]
        acc = pair_sums(other, own_side(marks_of(marks, b)))
        for k in range(2):
            if fresh:
                force[k, at, :] = acc[k]
            else:
                force[k, at, :] += acc[k]

    def sweep(fresh):
        def some(t, carry):
            for u in range(NEAR_STEP):
                meet(t * NEAR_STEP + u, 0, fresh)
            return carry

        def rest(t, carry):
            for u in range(REST_STEP):
                meet(work[0, t * REST_STEP + u], 1, False)
            return carry

        lax.fori_loop(0, blocks // NEAR_STEP, some, 0)
        lax.fori_loop(0, (work[1, 0] + (REST_STEP - 1)) // REST_STEP, rest, 0)

    collect(0.0)
    sweep(True)

    def more(p, carry):
        collect(p.astype(jnp.float32) * discs)
        sweep(False)
        return carry

    lax.fori_loop(1, work[2, 0], more, 0)

    def update(g, carry):
        at = pl.ds(pl.multiple_of(g * 8, 8), 8)
        scale = 0.06 / rad[at, :]
        scale = scale * scale
        for k in range(2):
            here = pos[k, at, :]
            bonded = lane_take(here, bonds[0, at, :])
            for p in range(1, BONDS):
                bonded = bonded + lane_take(here, bonds[p, at, :])
            push = jnp.zeros((8, discs), jnp.float32)
            for r in range(8):
                rows = pl.ds(g * 64 + r, 8, stride=8)
                push = push + (held[k, rows, :] + force[k, rows, :])
            total = BOND_STIFF * (bonded - BONDS * here) - STIFFNESS * push
            speed = vel[k, at, :] + total * scale
            vel_out[k, at, :] = speed
            pos_out[k, at, :] = here + TIME_STEP * speed
        return carry

    lax.fori_loop(0, blocks // 8, update, 0)
    if last:
        spots = [jnp.broadcast_to(slots[k : k + 1], (8, blocks)) for k in range(2)]
        rows = []
        for comp in range(2):
            drag = rad[...] * rad[...] * vel_out[comp]
            total = DRAG_ICE * jnp.sum(drag.T, axis=0, keepdims=True)
            total = jnp.broadcast_to(total, (8, blocks))
            for spot in spots:
                moved = lane_take(total, jnp.maximum(spot, 0))
                rows.append(jnp.where(spot >= 0, moved, 0.0)[0:1])
        rows.append(jnp.zeros((blocks - 4, blocks), jnp.float32))
        sent[:, 0, :] = jnp.concatenate(rows, axis=0).T
    else:
        for side in range(2):
            for comp in range(2):
                at = pl.ds(side * (cols_dev - 1), rows_dev, stride=cols_dev)
                edges[side, comp] = pos_out[comp, at, :]


def contact_step(which, n_gy, pos, vel, rad, bonds, mask, marks, held, halo, halo_rad, *extra):
    blocks, discs = rad.shape
    rows_dev = blocks // 16
    square = shape(2, blocks, discs)
    tail = shape(blocks, 1, discs) if which == SUB - 1 else shape(2, 2, rows_dev, discs)
    outs = (square, square, tail)
    if which == 1:
        outs += (shape(*extra[0].shape),)
    args = (pos, vel, rad, bonds, mask, marks, held, halo, halo_rad) + extra
    return pl.pallas_call(
        functools.partial(contact_kernel, which, n_gy),
        out_shape=outs,
        in_specs=[VMEM] * len(args),
        out_specs=(VMEM,) * len(outs),
        scratch_shapes=[
            pltpu.VMEM((3, rows_dev + 2, 24, discs), jnp.float32),
            pltpu.VMEM((4, blocks, discs), jnp.float32),
            pltpu.VMEM((MARKS * blocks, discs), jnp.float32),
            pltpu.VMEM((2, 8 * blocks + 8, discs), jnp.float32),
            pltpu.VMEM((8, discs), jnp.int32),
            pltpu.SMEM((8, discs), jnp.int32),
            pltpu.SemaphoreType.DMA,
        ],
        compiler_params=grant(16),
        name=("contact_first", "contact", "contact_last")[which],
    )(*args)


def prep_kernel(n_gy, pos_in, rad_in, allowed_in, pos, rad, edges, mask, allowed, sems):
    copies = [
        pltpu.make_async_copy(allowed_in, allowed, sems.at[0]),
        pltpu.make_async_copy(pos_in, pos, sems.at[1]),
        pltpu.make_async_copy(rad_in, rad, sems.at[2]),
    ]
    for copy in copies:
        copy.start()
    copies[0].wait()
    lane = lax.broadcasted_iota(jnp.int32, (8, 128), 1)
    _, rows_dev, cols_dev = allowed.shape
    spread = jnp.zeros((8, 128), jnp.float32)
    for y in range(rows_dev):
        part = allowed[:, y, :].astype(jnp.float32)
        part = jnp.concatenate([part, jnp.zeros((8, 128 - cols_dev), jnp.float32)], axis=1)
        spread = spread + (pltpu.roll(part, y * cols_dev, 1) if y else part)
    which = lax.broadcasted_iota(jnp.int32, (8, 128), 0)
    shift_y = jnp.where(which < 3, -1, jnp.where(which < 5, 0, 1))
    row = lax.axis_index("gy") * rows_dev + lane // cols_dev + shift_y
    spread = jnp.where((row >= 0) & (row < n_gy * rows_dev), spread, 0.0)
    mask[...] = jnp.concatenate([spread, jnp.zeros((120, 128), jnp.float32)], axis=0).T
    copies[1].wait()
    copies[2].wait()
    for comp in range(3):
        source = pos.at[comp] if comp < 2 else rad
        for side in range(2):
            edges[side, comp] = source[pl.ds(side * 15, 8, stride=16), :]


def prep(n_gy, pos, rad, allowed):
    return pl.pallas_call(
        functools.partial(prep_kernel, n_gy),
        out_shape=(shape(*pos.shape), shape(*rad.shape), shape(2, 3, 8, 128), shape(*rad.shape)),
        in_specs=[HBM] * 3,
        out_specs=(VMEM,) * 4,
        scratch_shapes=[pltpu.VMEM(allowed.shape, jnp.int32), pltpu.SemaphoreType.DMA((3,))],
        compiler_params=grant(4),
        name="prep",
    )(pos, rad, allowed)


def pack_kernel(ocean, after, columns, bottom, top):
    rows = ocean.shape[2]
    lane = lax.broadcasted_iota(jnp.int32, (8, 128), 1)
    packed = [jnp.zeros((8, 128), jnp.float32)] * 2
    for field in range(4):
        for layer in range(CHUNK):
            for v in range(rows // 8):
                g = (field * CHUNK + layer) * (rows // 8) + v
                place = g % 64
                turned = pltpu.roll(ocean[field, layer, pl.ds(8 * v, 8), :], 2 * place + 1, 1)
                packed[g // 64] = jnp.where(lane // 2 == place, turned, packed[g // 64])
    columns[0] = jnp.concatenate(packed, axis=0)
    bottom[...] = ocean[:, :, 0, :]
    top[...] = ocean[:, :, rows - 1, :]


def pack(ocean, after):
    fields, layers, rows, lanes = ocean.shape
    steps = layers // CHUNK
    row = pl.BlockSpec((fields, CHUNK, lanes), lambda i: (0, i, 0))
    return pl.pallas_call(
        pack_kernel,
        grid=(steps,),
        out_shape=(
            shape(steps, 16, lanes),
            shape(fields, layers, lanes),
            shape(fields, layers, lanes),
        ),
        in_specs=[pl.BlockSpec((fields, CHUNK, rows, lanes), lambda i: (0, i, 0, 0)), ANY],
        out_specs=(pl.BlockSpec((1, 16, lanes), lambda i: (i, 0, 0)), row, row),
        compiler_params=grant(8),
        name="pack",
    )(ocean, after)


def exchange_kernel(which, n_gx, n_gy, *refs):
    if which == 0:
        pos, rad, edges, halo, held, marks, halo_rad, *scratch = refs
        send_sem, recv_sem, rad_send, rad_recv = scratch
    elif which == 1:
        pos, rad, edges, top, bottom, sides, perm, halo, held, marks, lon, lat, rows, perms, *scratch = refs
        send_sem, recv_sem, sea_send, sea_recv, *scratch = scratch
        far_send, far_recv, perm_send, perm_recv, own = scratch
    else:
        pos, rad, edges, turned, halo, held, marks, mirror, *scratch = refs
        send_sem, recv_sem, far_send, far_recv, own = scratch
    gx, gy = lax.axis_index("gx"), lax.axis_index("gy")
    is_top = gy == n_gy - 1

    def at(dx, dy):
        return lax.rem(gx + dx + n_gx, n_gx), lax.rem(gy + dy + n_gy, n_gy)

    barrier = pltpu.get_barrier_semaphore()
    for dy, dx in NEIGHBOURS:
        pl.semaphore_signal(barrier, inc=1, device_id=at(dx, dy), device_id_type=MESH)
    if which > 0:

        @pl.when(is_top)
        def _():
            for d in range(1, n_gx):
                pl.semaphore_signal(barrier, inc=1, device_id=at(d, 0), device_id_type=MESH)

    blocks = rad.shape[0]
    write_marks([pos[0], pos[1], rad[...]], marks)
    own_forces(0, EARLY, marks, held)
    if which > 0:

        @pl.when(is_top)
        def _():
            pl.semaphore_wait(barrier, len(NEIGHBOURS) + n_gx - 1)

        @pl.when(jnp.logical_not(is_top))
        def _():
            pl.semaphore_wait(barrier, len(NEIGHBOURS))

    else:
        pl.semaphore_wait(barrier, len(NEIGHBOURS))

    def send(source, target, sems, index, device):
        return pltpu.make_async_remote_copy(
            src_ref=source,
            dst_ref=target,
            send_sem=sems[0].at[index],
            recv_sem=sems[1].at[index],
            device_id=device,
            device_id_type=MESH,
        )

    def halo_copies(body, part, target, sems):
        copies = []
        for k, (sy, sx) in enumerate(NEIGHBOURS):
            first = 0 if sy == 1 else blocks - 16
            first = first + 8 if sx == -1 else first
            size = 16 if sx == 0 else 8
            source = part(0 if sx == 1 else 1) if sy == 0 else body(pl.ds(first, size))
            copies.append(send(source, target(k, pl.ds(0, size)), sems, k, at(-sx, -sy)))
        return copies

    copies = halo_copies(
        lambda rows: pos.at[:, rows, :],
        lambda side: edges.at[side, pl.ds(0, 2)],
        lambda k, rows: halo.at[k, :, rows, :],
        (send_sem, recv_sem),
    )
    if which == 0:
        copies += halo_copies(
            lambda rows: rad.at[rows, :],
            lambda side: edges.at[side, 2],
            lambda k, rows: halo_rad.at[k, rows, :],
            (rad_send, rad_recv),
        )
    for copy in copies:
        copy.start()
    if which == 1:
        sea = (sea_send, sea_recv)
        later = [
            send(sides, lon.at[0], sea, 0, at(1, 0)),
            send(sides, lon.at[1], sea, 1, at(-1, 0)),
            send(top, lat.at[0], sea, 2, at(0, 1)),
            send(bottom, lat.at[1], sea, 3, at(0, -1)),
        ]
        copies += later

    if which == 1:
        first = pl.multiple_of(jnp.minimum(gx, TURNERS - 1) * TURN_ROWS, TURN_ROWS)
        kept = pltpu.make_async_copy(perm, perms.at[gx], own.at[0])
        mine = pltpu.make_async_copy(top.at[pl.ds(first, TURN_ROWS), :], rows.at[gx], own.at[1])
        notes, far = [], []
        for d in range(1, n_gx):
            peer = lax.rem(gx + d, n_gx)
            start = pl.multiple_of(jnp.minimum(peer, TURNERS - 1) * TURN_ROWS, TURN_ROWS)
            notes.append(send(perm, perms.at[gx], (perm_send, perm_recv), d - 1, at(d, 0)))
            source = top.at[pl.ds(start, TURN_ROWS), :]
            far.append(send(source, rows.at[gx], (far_send, far_recv), d - 1, at(d, 0)))

        @pl.when(is_top)
        def _():
            kept.start()
            for d in range(1, n_gx):
                notes[d - 1].start()

                @pl.when(lax.rem(gx + d, n_gx) < TURNERS)
                def _(copy=far[d - 1]):
                    copy.start()

            @pl.when(gx < TURNERS)
            def _():
                mine.start()

        for copy in later:
            copy.start()

    if which == 2:
        me = jnp.minimum(gx, TURNERS - 1)
        mine = pltpu.make_async_copy(turned.at[gx], mirror.at[me], own)
        far = []
        for d in range(1, n_gx):
            source = turned.at[lax.rem(gx + d, n_gx)]
            far.append(send(source, mirror.at[me], (far_send, far_recv), d - 1, at(d, 0)))

        @pl.when(is_top & (gx < TURNERS))
        def _():
            mine.start()
            for copy in far:
                copy.start()

    own_forces(EARLY, blocks - EARLY, marks, held)
    for copy in copies:
        copy.wait()
    if which == 1:

        @pl.when(is_top)
        def _():
            kept.wait()
            for d in range(1, n_gx):
                notes[d - 1].wait()

                @pl.when(lax.rem(gx + d, n_gx) < TURNERS)
                def _(copy=far[d - 1]):
                    copy.wait_send()

            @pl.when(gx < TURNERS)
            def _():
                mine.wait()
                for copy in far:
                    copy.wait_recv()

    if which == 2:

        @pl.when(is_top & (gx < TURNERS))
        def _():
            mine.wait()
            for copy in far:
                copy.wait_send()

        @pl.when(is_top)
        def _():
            for d in range(1, n_gx):

                @pl.when(lax.rem(gx - d + n_gx, n_gx) < TURNERS)
                def _(copy=far[d - 1]):
                    copy.wait_recv()


def exchange(which, n_gx, n_gy, pos, rad, edges, *args):
    lanes = rad.shape[1]
    blocks = rad.shape[0]
    outs = [shape(8, 2, 16, lanes), shape(2, 8 * blocks, lanes)]
    outs += [shape(MARKS * blocks, lanes)]
    dma = pltpu.SemaphoreType.DMA
    scratch = [dma((8,)), dma((8,))]
    far = [dma((n_gx - 1,)), dma((n_gx - 1,))]
    if which == 0:
        outs += [shape(8, 16, lanes)]
        scratch += [dma((8,)), dma((8,))]
    if which == 1:
        top, bottom, sides, perm = args
        outs += [shape(2, *sides.shape), shape(2, *top.shape)]
        outs += [shape(n_gx, TURN_ROWS, lanes), jax.ShapeDtypeStruct((n_gx, 1, lanes), jnp.int32)]
        scratch += [dma((4,)), dma((4,))] + far + far + [dma((2,))]
    if which == 2:
        outs += [shape(TURNERS, TURN_ROWS, lanes)]
        scratch += far + [dma]
    return pl.pallas_call(
        functools.partial(exchange_kernel, which, n_gx, n_gy),
        out_shape=tuple(outs),
        in_specs=[VMEM] * (3 + len(args)),
        out_specs=(VMEM,) * len(outs),
        scratch_shapes=scratch,
        compiler_params=grant(8, collective_id=which, has_side_effects=True),
        name=("exchange_first", "exchange_second", "exchange_third")[which],
    )(pos, rad, edges, *args)


def ocean_kernel(n_gy, ocean, above, below, mix, lon, lat, mirror, out, skin):
    step = pl.program_id(0)
    rows, lanes = ocean.shape[2], ocean.shape[3]
    gy = lax.axis_index("gy")
    lane = lax.broadcasted_iota(jnp.int32, (rows, lanes), 1)
    sub = lax.broadcasted_iota(jnp.int32, (rows, lanes), 0)
    lane8 = lax.broadcasted_iota(jnp.int32, (8, lanes), 1)
    bands = []
    for half in range(2):
        at = pl.ds(8 * half, 8)
        west, east = pltpu.roll(lon[0, 0, at, :], 1, 1), pltpu.roll(lon[1, 0, at, :], lanes - 1, 1)
        bands.append(jnp.where(lane8 % 2 == 1, west, east))
    spin = 2.0 * ((gy * rows + sub).astype(jnp.float32) + 0.5) / (rows * n_gy) - 1.0
    spin = SPIN_RATE * spin
    is_top, is_low = gy == n_gy - 1, gy == 0
    for field in range(4):
        folded = -mirror[field] if field < 2 else mirror[field]
        upper = jnp.where(is_top, folded, lat[1, field])
        lower = jnp.where(is_low, 0.0, lat[0, field])
        for layer in range(CHUNK):
            here = ocean[field, layer]
            up = ocean[field, layer - 1] if layer > 0 else above[field, 0]
            down = ocean[field, layer + 1] if layer < CHUNK - 1 else below[field, 0]
            sides = []
            for v in range(rows // 8):
                g = (field * CHUNK + layer) * (rows // 8) + v
                sides.append(pltpu.roll(bands[g // 64], lanes - 1 - 2 * (g % 64), 1))
            sides = jnp.concatenate(sides, axis=0)
            west = jnp.where(lane == 0, sides, pltpu.roll(here, 1, 1))
            east = jnp.where(lane == lanes - 1, sides, pltpu.roll(here, lanes - 1, 1))
            south = jnp.where(sub == 0, lower[layer : layer + 1], pltpu.roll(here, 1, 0))
            north = jnp.where(sub == rows - 1, upper[layer : layer + 1], pltpu.roll(here, rows - 1, 0))
            laplace = east + west + north + south - 4.0 * here
            value = here + mix[layer] * laplace + VERT_MIX * (up + down - 2.0 * here)
            if field == 0:
                value = value + spin * ocean[1, layer]
            if field == 1:
                value = value - spin * ocean[0, layer]
            out[field, layer] = value
            if field < 2 and layer == 0:

                @pl.when(step == 0)
                def _():
                    skin[field] = value


def ocean_step(n_gy, ocean, mix, lon, lat, mirror):
    fields, layers, rows, lanes = ocean.shape
    steps = layers // CHUNK
    block = pl.BlockSpec((fields, CHUNK, rows, lanes), lambda i: (0, i, 0, 0))
    one = (fields, 1, rows, lanes)
    return pl.pallas_call(
        functools.partial(ocean_kernel, n_gy),
        grid=(steps,),
        out_shape=(shape(*ocean.shape), shape(2, rows, lanes)),
        in_specs=[
            block,
            pl.BlockSpec(one, lambda i: (0, jnp.maximum(i * CHUNK - 1, 0), 0, 0)),
            pl.BlockSpec(one, lambda i: (0, jnp.minimum(i * CHUNK + CHUNK, layers - 1), 0, 0)),
            pl.BlockSpec((CHUNK, rows, lanes), lambda i: (i, 0, 0)),
            pl.BlockSpec((2, 1, 16, lanes), lambda i: (0, i, 0, 0)),
            pl.BlockSpec((2, fields, CHUNK, lanes), lambda i: (0, 0, i, 0)),
            pl.BlockSpec((fields, CHUNK, lanes), lambda i: (0, i, 0)),
        ],
        out_specs=(block, pl.BlockSpec((2, rows, lanes), lambda i: (0, 0, 0))),
        compiler_params=grant(24),
        name="ocean",
    )(ocean, ocean, ocean, mix, lon, lat, mirror)


def couple_kernel(n_gx, n_gy, sent, skin, cell, surface, current, *refs):
    here, there, back, home, *sems = refs
    gx, gy = lax.axis_index("gx"), lax.axis_index("gy")
    tiles, lanes = n_gx * n_gy, skin.shape[2]
    rows = skin.shape[1]
    barrier = pltpu.get_barrier_semaphore()
    for d in range(1, n_gx):
        peer = (lax.rem(gx + d, n_gx), gy)
        pl.semaphore_signal(barrier, inc=1, device_id=peer, device_id_type=MESH)
    for d in range(1, n_gy):
        peer = (gx, lax.rem(gy + d, n_gy))
        pl.semaphore_signal(barrier, inc=1, device_id=peer, device_id_type=MESH)
    pl.semaphore_wait(barrier, n_gx + n_gy - 2)

    def swap(source, middle, target, sems):
        send_x, recv_x, send_y, recv_y, local = sems
        own = pltpu.make_async_copy(source.at[gx], middle.at[gx], local)
        own.start()
        copies = []
        for d in range(1, n_gx):
            peer = lax.rem(gx + d, n_gx)
            copies.append(
                pltpu.make_async_remote_copy(
                    src_ref=source.at[peer],
                    dst_ref=middle.at[gx],
                    send_sem=send_x.at[d - 1],
                    recv_sem=recv_x.at[d - 1],
                    device_id=(peer, gy),
                    device_id_type=MESH,
                )
            )
        for copy in copies:
            copy.start()
        own.wait()
        for copy in copies:
            copy.wait()
        own = pltpu.make_async_copy(middle.at[:, gy], target.at[:, gy], local)
        own.start()
        copies = []
        for d in range(1, n_gy):
            peer = lax.rem(gy + d, n_gy)
            copies.append(
                pltpu.make_async_remote_copy(
                    src_ref=middle.at[:, peer],
                    dst_ref=target.at[:, gy],
                    send_sem=send_y.at[d - 1],
                    recv_sem=recv_y.at[d - 1],
                    device_id=(gx, peer),
                    device_id_type=MESH,
                )
            )
        for copy in copies:
            copy.start()
        own.wait()
        for copy in copies:
            copy.wait()

    swap(sent, here, there, sems[0:5])
    cells = jnp.concatenate([cell[0:1], cell[1:2]], axis=1)
    cell_row, cell_col = cells // lanes, cells % lanes
    pick = (lax.broadcasted_iota(jnp.int32, (lanes, 2 * tiles), 0) == cell_col).astype(jnp.bfloat16)
    in_row = lax.broadcasted_iota(jnp.int32, (rows, 2 * tiles), 0) == cell_row
    arrived = there[...].reshape(tiles, lanes).T
    spread = []
    for comp in range(2):
        values = jnp.concatenate([arrived[2 * comp : 2 * comp + 1], arrived[2 * comp + 1 : 2 * comp + 2]], axis=1)
        spread.append(jnp.where(in_row, values, 0.0))
    forcing = lax.dot_general(
        split(jnp.concatenate(spread, axis=0)),
        pick,
        (((1,), (1,)), ((), ())),
        preferred_element_type=jnp.float32,
    )
    level = skin[...].reshape(2 * rows, lanes) + joined(forcing)
    surface[...] = level.reshape(2, rows, lanes)
    found = joined(jnp.dot(split(level), pick, preferred_element_type=jnp.float32))
    replies = []
    for comp in range(2):
        values = jnp.where(in_row, found[comp * rows : (comp + 1) * rows], 0.0)
        values = jnp.sum(values, axis=0, keepdims=True)
        replies += [values[:, :tiles], values[:, tiles:]]
    replies.append(jnp.zeros((lanes - 4, tiles), jnp.float32))
    back[...] = jnp.concatenate(replies, axis=0).T.reshape(back.shape)
    swap(back, home, current, sems[5:10])


def couple(n_gx, n_gy, sent, skin, cell):
    tiles, lanes = n_gx * n_gy, skin.shape[2]
    box = (n_gx, n_gy, 1, lanes)
    dma = pltpu.SemaphoreType.DMA
    sems = [dma((n_gx - 1,)), dma((n_gx - 1,)), dma((n_gy - 1,)), dma((n_gy - 1,)), dma]
    return pl.pallas_call(
        functools.partial(couple_kernel, n_gx, n_gy),
        out_shape=(shape(*skin.shape), shape(*box)),
        in_specs=[VMEM] * 3,
        out_specs=(VMEM,) * 2,
        scratch_shapes=[pltpu.VMEM(box, jnp.float32)] * 4 + sems + sems,
        compiler_params=grant(4, collective_id=SUB, has_side_effects=True),
        name="couple",
    )(sent.reshape(box), skin, cell)


def finish_kernel(ocean, surface, current, slots, vel, vel_out, ocean_out, sem):
    copy = pltpu.make_async_copy(surface, ocean_out.at[pl.ds(0, 2), 0], sem)
    copy.start()
    blocks, discs = vel.shape[1], vel.shape[2]
    tiles = current.shape[0]
    got = current[...].reshape(tiles, discs).T
    spots = jnp.concatenate([slots[0:1], slots[1:2]], axis=1)
    place = lax.broadcasted_iota(jnp.int32, (blocks, 2 * tiles), 0) == spots
    for comp in range(2):
        values = jnp.concatenate([got[2 * comp : 2 * comp + 1], got[2 * comp + 1 : 2 * comp + 2]], axis=1)
        values = jnp.sum(jnp.where(place, values, 0.0), axis=1, keepdims=True)
        speed = vel[comp]
        vel_out[comp] = speed + DRAG_BACK * (values - speed)
    copy.wait()


def finish(ocean, surface, current, slots, vel):
    tiles = current.shape[0] * current.shape[1]
    return pl.pallas_call(
        finish_kernel,
        out_shape=(shape(*vel.shape), shape(*ocean.shape)),
        in_specs=[ANY, VMEM, VMEM, VMEM, VMEM],
        out_specs=(VMEM, ANY),
        scratch_shapes=[pltpu.SemaphoreType.DMA],
        input_output_aliases={0: 1},
        compiler_params=grant(4),
        name="finish",
    )(ocean, surface, current.reshape(tiles, 1, current.shape[3]), slots, vel)


def body(
    disc_pos,
    disc_vel,
    radius,
    bond_list,
    contact_mask,
    remap_block,
    ocean_state,
    mix_coef,
    remap_cell,
    fold_perm,
):
    n_gx, n_gy = lax.axis_size("gx"), lax.axis_size("gy")
    rows_dev, cols_dev, discs = radius.shape
    blocks = rows_dev * cols_dev
    slots = remap_block[0].T
    cell = remap_cell[0].T
    perm = fold_perm.reshape(1, discs)
    position = disc_pos.reshape(2, blocks, discs)
    velocity = disc_vel.reshape(2, blocks, discs)
    rad = radius.reshape(blocks, discs)
    bonds = bond_list.reshape(BONDS, blocks, discs)
    sea_shape = (4, mix_coef.shape[0], discs)
    flat = (4 * mix_coef.shape[0], discs)
    position, rad, edges, mask = prep(n_gy, position, rad, contact_mask)
    halo, held, marks, halo_rad = exchange(0, n_gx, n_gy, position, rad, edges)
    position, velocity, edges = contact_step(
        0, n_gy, position, velocity, rad, bonds, mask, marks, held, halo, halo_rad
    )
    sides, bottom, top = pack(ocean_state, edges)
    halo, held, marks, lon, lat, rows, perms = exchange(
        1, n_gx, n_gy, position, rad, edges, top.reshape(flat), bottom.reshape(flat), sides, perm
    )
    position, velocity, edges, turned = contact_step(
        1, n_gy, position, velocity, rad, bonds, mask, marks, held, halo, halo_rad, rows, perms
    )
    halo, held, marks, mirror = exchange(2, n_gx, n_gy, position, rad, edges, turned)
    position, velocity, sent = contact_step(
        2, n_gy, position, velocity, rad, bonds, mask, marks, held, halo, halo_rad, slots
    )
    ocean, skin = ocean_step(
        n_gy, ocean_state, mix_coef, lon, lat.reshape(2, *sea_shape), mirror.reshape(sea_shape)
    )
    surface, current = couple(n_gx, n_gy, sent, skin, cell)
    vel_next, ocean_next = finish(ocean, surface, current, slots, velocity)
    return (position.reshape(disc_pos.shape), vel_next.reshape(disc_vel.shape), ocean_next)


def solution(mesh):
    in_specs = (
        P(None, "gy", "gx", None),
        P(None, "gy", "gx", None),
        P("gy", "gx", None),
        P(None, "gy", "gx", None),
        P(None, "gy", "gx"),
        P(("gx", "gy"), None, None),
        P(None, None, "gy", "gx"),
        P(None, "gy", "gx"),
        P(("gx", "gy"), None, None),
        P("gx"),
    )
    out_specs = (P(None, "gy", "gx", None), P(None, "gy", "gx", None), P(None, None, "gy", "gx"))
    return jax.shard_map(body, mesh=mesh, in_specs=in_specs, out_specs=out_specs, check_vma=False)
```

```python
import functools

import jax
import jax.numpy as jnp
from jax import lax
from jax.experimental import pallas as pl
from jax.experimental.pallas import tpu as pltpu
from jax.sharding import PartitionSpec as P

BONDS = 4
SUB = 3
SOFTEN = 0.0001
STIFFNESS = 2.0
BOND_STIFF = 0.1
TIME_STEP = 0.05
DRAG_ICE = 15.0
DRAG_BACK = 0.5
VERT_MIX = 0.1
SPIN_RATE = 0.3
NEIGHBOURS = ((-1, -1), (-1, 0), (-1, 1), (0, -1), (0, 1), (1, -1), (1, 0), (1, 1))
ROWS = 1
OWN_STEP = 8
NEAR_STEP = 16
REST_STEP = 8
HALF = 64
MARKS = 16
CHUNK = 8
TURNERS = 12
EARLY = 32
TURN_ROWS = 16
MESH = pl.DeviceIdType.MESH
BUSY = pl.CostEstimate(flops=1 << 32, bytes_accessed=1 << 24, transcendentals=1 << 22)
VMEM = pl.BlockSpec(memory_space=pltpu.VMEM)
ANY = pl.BlockSpec(memory_space=pl.ANY)
HBM = pl.BlockSpec(memory_space=pltpu.HBM)


def grant(mib, **more):
    return pltpu.CompilerParams(vmem_limit_bytes=mib << 20, **more)


def shape(*dims):
    return jax.ShapeDtypeStruct(dims, jnp.float32)


def split(value):
    high = value.astype(jnp.bfloat16)
    rest = value - high.astype(jnp.float32)
    middle = rest.astype(jnp.bfloat16)
    low = (rest - middle.astype(jnp.float32)).astype(jnp.bfloat16)
    return jnp.concatenate([high, middle, low], axis=0)


def joined(value):
    rows = value.shape[0] // 3
    return value[:rows] + value[rows : 2 * rows] + value[2 * rows :]


def lane_take(rows, index):
    return lax.gather(
        rows,
        index[..., None],
        lax.GatherDimensionNumbers(
            offset_dims=(),
            collapsed_slice_dims=(1,),
            start_index_map=(1,),
            operand_batching_dims=(0,),
            start_indices_batching_dims=(0,),
        ),
        slice_sizes=(1, 1),
        mode=lax.GatherScatterMode.PROMISE_IN_BOUNDS,
    )


def pieces(value):
    high = value.astype(jnp.bfloat16).astype(jnp.float32)
    middle = (value - high).astype(jnp.bfloat16).astype(jnp.float32)
    return high, middle, value - high - middle


def write_marks(parts, marks):
    for comp, part in enumerate(parts):
        for i, piece in enumerate(pieces(part)):
            marks[pl.ds(3 * comp + i, part.shape[0], stride=MARKS), :] = piece


def other_side(marks):
    row = lax.broadcasted_iota(jnp.int32, marks.shape, 0)
    marks = jnp.where(row < 9, marks, jnp.where(row < 12, 1.0, 0.0))
    return marks.T.astype(jnp.bfloat16)


def own_side(marks):
    row = lax.broadcasted_iota(jnp.int32, marks.shape, 0)
    sides = []
    for comp in range(3):
        moved = pltpu.roll(marks, 9 - 3 * comp, 0)
        moved = moved if comp == 2 else -moved
        fixed = jnp.where(row // 3 == comp, 1.0, 0.0)
        sides.append(jnp.where((row >= 9) & (row < 12), moved, fixed))
    return jnp.concatenate(sides, axis=1).astype(jnp.bfloat16)


def pair_sums(other, own):
    pairs = jnp.dot(other, own, preferred_element_type=jnp.float32)
    lanes = pairs.shape[1] // 3
    acc_x = acc_y = jnp.zeros((8, lanes), jnp.float32)
    for c in range(pairs.shape[0] // 8):
        rows = pairs[8 * c : 8 * c + 8]
        sep_x, sep_y, reach = rows[:, :lanes], rows[:, lanes : 2 * lanes], rows[:, 2 * lanes :]
        inverse = lax.rsqrt(sep_x * sep_x + sep_y * sep_y + SOFTEN)
        push = jnp.maximum(reach * inverse - 1.0, 0.0)
        acc_x = acc_x + push * sep_x
        acc_y = acc_y + push * sep_y
    return acc_x, acc_y


def marks_of(marks, b):
    return marks[pl.ds(pl.multiple_of(b * MARKS, MARKS), MARKS), :]


def turn(rows, perms, turned):
    lanes = rows.shape[2]

    def one(h, carry):
        wanted = jnp.broadcast_to(perms[h], (8, lanes))
        owner, column = wanted // lanes, wanted % lanes
        for half in range(TURN_ROWS // 8):
            at = pl.ds(8 * half, 8)
            got = jnp.zeros((8, lanes), jnp.float32)
            for source in range(rows.shape[0]):
                got = jnp.where(owner == source, lane_take(rows[source, at, :], column), got)
            turned[h, at, :] = got
        return carry

    lax.fori_loop(0, perms.shape[0], one, 0)


def own_forces(first, count, marks, force):
    def some(t, carry):
        for u in range(OWN_STEP):
            b = first + t * OWN_STEP + u
            own = marks_of(marks, b)
            acc = pair_sums(other_side(own), own_side(own))
            at = pl.ds(pl.multiple_of(b * 8, 8), 8)
            for k in range(2):
                force[k, at, :] = acc[k]
        return carry

    lax.fori_loop(0, count // OWN_STEP, some, 0)


def write_mask(n_gy, allowed, mask):
    lane = lax.broadcasted_iota(jnp.int32, (8, 128), 1)
    _, rows_dev, cols_dev = allowed.shape
    spread = jnp.zeros((8, 128), jnp.float32)
    for y in range(rows_dev):
        part = allowed[:, y, :].astype(jnp.float32)
        part = jnp.concatenate([part, jnp.zeros((8, 128 - cols_dev), jnp.float32)], axis=1)
        spread = spread + (pltpu.roll(part, y * cols_dev, 1) if y else part)
    which = lax.broadcasted_iota(jnp.int32, (8, 128), 0)
    shift_y = jnp.where(which < 3, -1, jnp.where(which < 5, 0, 1))
    row = lax.axis_index("gy") * rows_dev + lane // cols_dev + shift_y
    spread = jnp.where((row >= 0) & (row < n_gy * rows_dev), spread, 0.0)
    mask[...] = jnp.concatenate([spread, jnp.zeros((120, 128), jnp.float32)], axis=0).T


def contact_kernel(which, n_gy, pos, vel, rad, bonds, mask, marks, held, halo, halo_rad, *refs):
    last = which == SUB - 1
    if last:
        slots, pos_out, vel_out, sent, *scratch = refs
    elif which == 1:
        rows, perms, pos_out, vel_out, edges, turned, *scratch = refs

        @pl.when(lax.axis_index("gy") == n_gy - 1)
        def _():
            turn(rows, perms, turned)

    else:
        allowed, mask = mask, refs[3]
        pos_out, vel_out, edges, _, *scratch = refs
        write_mask(n_gy, allowed, mask)
    wide, found, seen, force, tally, work, sem = scratch
    rows_dev, cols_dev = wide.shape[1] - 2, pos.shape[1] // (wide.shape[1] - 2)
    blocks, discs = rad.shape
    for comp in range(3):
        source = pos.at[comp] if comp < 2 else rad

        def frame(side, first, size):
            if comp < 2:
                return halo[side, comp, pl.ds(first, size), :]
            return halo_rad[side, pl.ds(first, size), :]

        for y in range(rows_dev):
            wide[comp, y + 1, pl.ds(1, cols_dev), :] = source[pl.ds(y * cols_dev, cols_dev), :]
            wide[comp, y + 1, pl.ds(0, 1), :] = frame(3, y, 1)
            wide[comp, y + 1, pl.ds(cols_dev + 1, 1), :] = frame(4, y, 1)
        for side, y in ((0, 0), (5, rows_dev + 1)):
            wide[comp, y, pl.ds(0, 1), :] = frame(side, 7, 1)
            wide[comp, y, pl.ds(1, cols_dev), :] = frame(side + 1, 0, cols_dev)
            wide[comp, y, pl.ds(cols_dev + 1, 1), :] = frame(side + 2, 0, 1)
    lane = lax.broadcasted_iota(jnp.int32, (8, discs), 1)
    lane_f = lane.astype(jnp.float32)
    tri_row = lax.broadcasted_iota(jnp.int32, (discs, 2 * discs), 0)
    tri_col = lax.broadcasted_iota(jnp.int32, (discs, 2 * discs), 1)
    triangle = (tri_row <= tri_col).astype(jnp.bfloat16)
    low_row = lax.broadcasted_iota(jnp.int32, (blocks, blocks), 0)
    low_col = lax.broadcasted_iota(jnp.int32, (blocks, blocks), 1)
    lower = (low_col <= low_row).astype(jnp.bfloat16)

    def collect(start):
        def one_row(step_y, carry):
            units, totals = [], []
            for half in range(ROWS * cols_dev // 8):
                y = step_y * ROWS + half // (cols_dev // 8)
                x0 = half % (cols_dev // 8) * 8
                at = pl.ds(pl.multiple_of(y * cols_dev + x0, 8), 8)
                own = [pos[0, at, :], pos[1, at, :], rad[at, :]]
                reach = jnp.max(own[2], axis=1, keepdims=True)
                low = [jnp.min(own[c], axis=1, keepdims=True) - reach for c in range(2)]
                high = [jnp.max(own[c], axis=1, keepdims=True) + reach for c in range(2)]
                weights = mask[at, :]
                flags = []
                places = []
                for k, (sy, sx) in enumerate(NEIGHBOURS):
                    place = (y + 1 + sy, pl.ds(x0 + 1 + sx, 8), slice(None))
                    nx, ny, nr = (wide[(c,) + place] for c in range(3))
                    close = (nx - nr < high[0] - float(sx)) & (nx + nr > low[0] - float(sx))
                    close = close & (ny - nr < high[1] - float(sy)) & (ny + nr > low[1] - float(sy))
                    close = close & (weights[:, k : k + 1] > 0.5)
                    flags.append(close.astype(jnp.float32))
                    places.append(place)
                ranks = jnp.dot(
                    jnp.concatenate(flags, axis=0).astype(jnp.bfloat16),
                    triangle,
                    preferred_element_type=jnp.float32,
                )
                base = jnp.zeros((8, discs), jnp.float32) - start
                for k in range(8):
                    rank = ranks[8 * k : 8 * k + 8, :discs]
                    total = ranks[8 * k : 8 * k + 8, discs:]
                    want = lane_f - base
                    source = jnp.zeros((8, discs), jnp.int32)
                    units.append((half, k, source, places[k], rank, total, want))
                    base = base + total
                totals.append((at, base))
            sources = [u[2] for u in units]
            step = discs // 2
            while step >= 1:
                probes = [lane_take(u[4], i + (step - 1)) for u, i in zip(units, sources)]
                sources = [
                    jnp.where(probe <= u[6], i + step, i)
                    for probe, u, i in zip(probes, units, sources)
                ]
                step //= 2
            for half, (at, base) in enumerate(totals):
                mine = [(u, i) for u, i in zip(units, sources) if u[0] == half]
                for comp in range(3):
                    got = jnp.full((8, discs), -1.0 if comp == 2 else 0.0, jnp.float32)
                    for (_, k, _, place, _, total, want), source in mine:
                        valid = (want >= 0.0) & (want < total)
                        value = wide[(comp,) + place]
                        if comp < 2 and NEIGHBOURS[k][1 - comp] != 0:
                            value = value + float(NEIGHBOURS[k][1 - comp])
                        got = jnp.where(valid, lane_take(value, source), got)
                    found[comp, at, :] = got
                found[3, at, :] = base
            return carry

        lax.fori_loop(0, rows_dev // ROWS, one_row, 0)
        write_marks([found[k] for k in range(3)], seen)
        left = found[3]
        size = jnp.where(left > float(HALF), 1.0, 0.0)
        ends = jnp.dot(lower, size.astype(jnp.bfloat16), preferred_element_type=jnp.float32)
        spot = lax.broadcasted_iota(jnp.int32, (1, discs), 1).astype(jnp.float32)
        block = jnp.sum(jnp.where(ends <= spot, 1.0, 0.0), axis=0, keepdims=True)
        tally[0:1] = block.astype(jnp.int32)
        tally[1:2] = ends[blocks - 1 :].astype(jnp.int32)
        deepest = jnp.max(left, axis=0, keepdims=True)
        tally[2:3] = jnp.ceil(deepest * (1.0 / discs)).astype(jnp.int32)
        copy = pltpu.make_async_copy(tally, work, sem)
        copy.start()
        copy.wait()

    def meet(b, part, fresh):
        at = pl.ds(pl.multiple_of(b * 8, 8), 8)
        b = jnp.minimum(b, blocks - 1)
        other = other_side(marks_of(seen, b))[part * HALF : (part + 1) * HALF]
        acc = pair_sums(other, own_side(marks_of(marks, b)))
        for k in range(2):
            if fresh:
                force[k, at, :] = acc[k]
            else:
                force[k, at, :] += acc[k]

    def sweep(fresh):
        def some(t, carry):
            for u in range(NEAR_STEP):
                meet(t * NEAR_STEP + u, 0, fresh)
            return carry

        def rest(t, carry):
            for u in range(REST_STEP):
                meet(work[0, t * REST_STEP + u], 1, False)
            return carry

        lax.fori_loop(0, blocks // NEAR_STEP, some, 0)
        lax.fori_loop(0, (work[1, 0] + (REST_STEP - 1)) // REST_STEP, rest, 0)

    collect(0.0)
    sweep(True)

    def more(p, carry):
        collect(p.astype(jnp.float32) * discs)
        sweep(False)
        return carry

    lax.fori_loop(1, work[2, 0], more, 0)

    def update(g, carry):
        at = pl.ds(pl.multiple_of(g * 8, 8), 8)
        scale = 0.06 / rad[at, :]
        scale = scale * scale
        for k in range(2):
            here = pos[k, at, :]
            bonded = lane_take(here, bonds[0, at, :])
            for p in range(1, BONDS):
                bonded = bonded + lane_take(here, bonds[p, at, :])
            push = jnp.zeros((8, discs), jnp.float32)
            for r in range(8):
                rows = pl.ds(g * 64 + r, 8, stride=8)
                push = push + (held[k, rows, :] + force[k, rows, :])
            total = BOND_STIFF * (bonded - BONDS * here) - STIFFNESS * push
            speed = vel[k, at, :] + total * scale
            vel_out[k, at, :] = speed
            pos_out[k, at, :] = here + TIME_STEP * speed
        return carry

    lax.fori_loop(0, blocks // 8, update, 0)
    if last:
        spots = [jnp.broadcast_to(slots[k : k + 1], (8, blocks)) for k in range(2)]
        rows = []
        for comp in range(2):
            drag = rad[...] * rad[...] * vel_out[comp]
            total = DRAG_ICE * jnp.sum(drag.T, axis=0, keepdims=True)
            total = jnp.broadcast_to(total, (8, blocks))
            for spot in spots:
                moved = lane_take(total, jnp.maximum(spot, 0))
                rows.append(jnp.where(spot >= 0, moved, 0.0)[0:1])
        rows.append(jnp.zeros((blocks - 4, blocks), jnp.float32))
        sent[:, 0, :] = jnp.concatenate(rows, axis=0).T
    else:
        for side in range(2):
            for comp in range(2):
                at = pl.ds(side * (cols_dev - 1), rows_dev, stride=cols_dev)
                edges[side, comp] = pos_out[comp, at, :]


def contact_step(which, n_gy, pos, vel, rad, bonds, mask, marks, held, halo, halo_rad, *extra):
    blocks, discs = rad.shape
    rows_dev = blocks // 16
    square = shape(2, blocks, discs)
    tail = shape(blocks, 1, discs) if which == SUB - 1 else shape(2, 2, rows_dev, discs)
    outs = (square, square, tail)
    if which == 0:
        outs += (shape(*rad.shape),)
    if which == 1:
        outs += (shape(*extra[0].shape),)
    args = (pos, vel, rad, bonds, mask, marks, held, halo, halo_rad) + extra
    return pl.pallas_call(
        functools.partial(contact_kernel, which, n_gy),
        out_shape=outs,
        in_specs=[VMEM] * len(args),
        out_specs=(VMEM,) * len(outs),
        scratch_shapes=[
            pltpu.VMEM((3, rows_dev + 2, 24, discs), jnp.float32),
            pltpu.VMEM((4, blocks, discs), jnp.float32),
            pltpu.VMEM((MARKS * blocks, discs), jnp.float32),
            pltpu.VMEM((2, 8 * blocks + 8, discs), jnp.float32),
            pltpu.VMEM((8, discs), jnp.int32),
            pltpu.SMEM((8, discs), jnp.int32),
            pltpu.SemaphoreType.DMA,
        ],
        compiler_params=grant(16),
        cost_estimate=BUSY,
        name=("contact_first", "contact", "contact_last")[which],
    )(*args)


def prep_kernel(pos_in, rad_in, pos, rad, edges, sems):
    copies = [
        pltpu.make_async_copy(pos_in, pos, sems.at[0]),
        pltpu.make_async_copy(rad_in, rad, sems.at[1]),
    ]
    for copy in copies:
        copy.start()
    for copy in copies:
        copy.wait()
    for comp in range(3):
        source = pos.at[comp] if comp < 2 else rad
        for side in range(2):
            edges[side, comp] = source[pl.ds(side * 15, 8, stride=16), :]


def prep(pos, rad):
    return pl.pallas_call(
        prep_kernel,
        out_shape=(shape(*pos.shape), shape(*rad.shape), shape(2, 3, 8, 128)),
        in_specs=[HBM] * 2,
        out_specs=(VMEM,) * 3,
        scratch_shapes=[pltpu.SemaphoreType.DMA((2,))],
        compiler_params=grant(4),
        name="prep",
    )(pos, rad)


def pack_kernel(ocean, after, columns, bottom, top):
    rows = ocean.shape[2]
    lane = lax.broadcasted_iota(jnp.int32, (8, 128), 1)
    packed = [jnp.zeros((8, 128), jnp.float32)] * 2
    for field in range(4):
        for layer in range(CHUNK):
            for v in range(rows // 8):
                g = (field * CHUNK + layer) * (rows // 8) + v
                place = g % 64
                turned = pltpu.roll(ocean[field, layer, pl.ds(8 * v, 8), :], 2 * place + 1, 1)
                packed[g // 64] = jnp.where(lane // 2 == place, turned, packed[g // 64])
    columns[0] = jnp.concatenate(packed, axis=0)
    bottom[...] = ocean[:, :, 0, :]
    top[...] = ocean[:, :, rows - 1, :]


def pack(ocean, after):
    fields, layers, rows, lanes = ocean.shape
    steps = layers // CHUNK
    row = pl.BlockSpec((fields, CHUNK, lanes), lambda i: (0, i, 0))
    return pl.pallas_call(
        pack_kernel,
        grid=(steps,),
        out_shape=(
            shape(steps, 16, lanes),
            shape(fields, layers, lanes),
            shape(fields, layers, lanes),
        ),
        in_specs=[pl.BlockSpec((fields, CHUNK, rows, lanes), lambda i: (0, i, 0, 0)), ANY],
        out_specs=(pl.BlockSpec((1, 16, lanes), lambda i: (i, 0, 0)), row, row),
        compiler_params=grant(8),
        name="pack",
    )(ocean, after)


def exchange_kernel(which, n_gx, n_gy, *refs):
    if which == 0:
        pos, rad, edges, halo, held, marks, halo_rad, *scratch = refs
        send_sem, recv_sem, rad_send, rad_recv = scratch
    elif which == 1:
        pos, rad, edges, top, bottom, sides, perm, halo, held, marks, lon, lat, rows, perms, *scratch = refs
        send_sem, recv_sem, sea_send, sea_recv, *scratch = scratch
        far_send, far_recv, perm_send, perm_recv, own = scratch
    else:
        pos, rad, edges, turned, halo, held, marks, mirror, *scratch = refs
        send_sem, recv_sem, far_send, far_recv, own = scratch
    gx, gy = lax.axis_index("gx"), lax.axis_index("gy")
    is_top = gy == n_gy - 1

    def at(dx, dy):
        return lax.rem(gx + dx + n_gx, n_gx), lax.rem(gy + dy + n_gy, n_gy)

    barrier = pltpu.get_barrier_semaphore()
    for dy, dx in NEIGHBOURS:
        pl.semaphore_signal(barrier, inc=1, device_id=at(dx, dy), device_id_type=MESH)
    if which > 0:

        @pl.when(is_top)
        def _():
            for d in range(1, n_gx):
                pl.semaphore_signal(barrier, inc=1, device_id=at(d, 0), device_id_type=MESH)

    blocks = rad.shape[0]
    write_marks([pos[0], pos[1], rad[...]], marks)
    own_forces(0, EARLY, marks, held)
    if which > 0:

        @pl.when(is_top)
        def _():
            pl.semaphore_wait(barrier, len(NEIGHBOURS) + n_gx - 1)

        @pl.when(jnp.logical_not(is_top))
        def _():
            pl.semaphore_wait(barrier, len(NEIGHBOURS))

    else:
        pl.semaphore_wait(barrier, len(NEIGHBOURS))

    def send(source, target, sems, index, device):
        return pltpu.make_async_remote_copy(
            src_ref=source,
            dst_ref=target,
            send_sem=sems[0].at[index],
            recv_sem=sems[1].at[index],
            device_id=device,
            device_id_type=MESH,
        )

    def halo_copies(body, part, target, sems):
        copies = []
        for k, (sy, sx) in enumerate(NEIGHBOURS):
            first = 0 if sy == 1 else blocks - 16
            first = first + 8 if sx == -1 else first
            size = 16 if sx == 0 else 8
            source = part(0 if sx == 1 else 1) if sy == 0 else body(pl.ds(first, size))
            copies.append(send(source, target(k, pl.ds(0, size)), sems, k, at(-sx, -sy)))
        return copies

    copies = halo_copies(
        lambda rows: pos.at[:, rows, :],
        lambda side: edges.at[side, pl.ds(0, 2)],
        lambda k, rows: halo.at[k, :, rows, :],
        (send_sem, recv_sem),
    )
    if which == 0:
        copies += halo_copies(
            lambda rows: rad.at[rows, :],
            lambda side: edges.at[side, 2],
            lambda k, rows: halo_rad.at[k, rows, :],
            (rad_send, rad_recv),
        )
    for copy in copies:
        copy.start()
    if which == 1:
        sea = (sea_send, sea_recv)
        later = [
            send(sides, lon.at[0], sea, 0, at(1, 0)),
            send(sides, lon.at[1], sea, 1, at(-1, 0)),
            send(top, lat.at[0], sea, 2, at(0, 1)),
            send(bottom, lat.at[1], sea, 3, at(0, -1)),
        ]
        copies += later

    if which == 1:
        first = pl.multiple_of(jnp.minimum(gx, TURNERS - 1) * TURN_ROWS, TURN_ROWS)
        kept = pltpu.make_async_copy(perm, perms.at[gx], own.at[0])
        mine = pltpu.make_async_copy(top.at[pl.ds(first, TURN_ROWS), :], rows.at[gx], own.at[1])
        notes, far = [], []
        for d in range(1, n_gx):
            peer = lax.rem(gx + d, n_gx)
            start = pl.multiple_of(jnp.minimum(peer, TURNERS - 1) * TURN_ROWS, TURN_ROWS)
            notes.append(send(perm, perms.at[gx], (perm_send, perm_recv), d - 1, at(d, 0)))
            source = top.at[pl.ds(start, TURN_ROWS), :]
            far.append(send(source, rows.at[gx], (far_send, far_recv), d - 1, at(d, 0)))

        @pl.when(is_top)
        def _():
            kept.start()
            for d in range(1, n_gx):
                notes[d - 1].start()

                @pl.when(lax.rem(gx + d, n_gx) < TURNERS)
                def _(copy=far[d - 1]):
                    copy.start()

            @pl.when(gx < TURNERS)
            def _():
                mine.start()

        for copy in later:
            copy.start()

    if which == 2:
        me = jnp.minimum(gx, TURNERS - 1)
        mine = pltpu.make_async_copy(turned.at[gx], mirror.at[me], own)
        far = []
        for d in range(1, n_gx):
            source = turned.at[lax.rem(gx + d, n_gx)]
            far.append(send(source, mirror.at[me], (far_send, far_recv), d - 1, at(d, 0)))

        @pl.when(is_top & (gx < TURNERS))
        def _():
            mine.start()
            for copy in far:
                copy.start()

    own_forces(EARLY, blocks - EARLY, marks, held)
    for copy in copies:
        copy.wait()
    if which == 1:

        @pl.when(is_top)
        def _():
            kept.wait()
            for d in range(1, n_gx):
                notes[d - 1].wait()

                @pl.when(lax.rem(gx + d, n_gx) < TURNERS)
                def _(copy=far[d - 1]):
                    copy.wait_send()

            @pl.when(gx < TURNERS)
            def _():
                mine.wait()
                for copy in far:
                    copy.wait_recv()

    if which == 2:

        @pl.when(is_top & (gx < TURNERS))
        def _():
            mine.wait()
            for copy in far:
                copy.wait_send()

        @pl.when(is_top)
        def _():
            for d in range(1, n_gx):

                @pl.when(lax.rem(gx - d + n_gx, n_gx) < TURNERS)
                def _(copy=far[d - 1]):
                    copy.wait_recv()


def exchange(which, n_gx, n_gy, pos, rad, edges, *args):
    lanes = rad.shape[1]
    blocks = rad.shape[0]
    outs = [shape(8, 2, 16, lanes), shape(2, 8 * blocks, lanes)]
    outs += [shape(MARKS * blocks, lanes)]
    dma = pltpu.SemaphoreType.DMA
    scratch = [dma((8,)), dma((8,))]
    far = [dma((n_gx - 1,)), dma((n_gx - 1,))]
    if which == 0:
        outs += [shape(8, 16, lanes)]
        scratch += [dma((8,)), dma((8,))]
    if which == 1:
        top, bottom, sides, perm = args
        outs += [shape(2, *sides.shape), shape(2, *top.shape)]
        outs += [shape(n_gx, TURN_ROWS, lanes), jax.ShapeDtypeStruct((n_gx, 1, lanes), jnp.int32)]
        scratch += [dma((4,)), dma((4,))] + far + far + [dma((2,))]
    if which == 2:
        outs += [shape(TURNERS, TURN_ROWS, lanes)]
        scratch += far + [dma]
    return pl.pallas_call(
        functools.partial(exchange_kernel, which, n_gx, n_gy),
        out_shape=tuple(outs),
        in_specs=[VMEM] * (3 + len(args)),
        out_specs=(VMEM,) * len(outs),
        scratch_shapes=scratch,
        compiler_params=grant(8, collective_id=which, has_side_effects=True),
        cost_estimate=BUSY,
        name=("exchange_first", "exchange_second", "exchange_third")[which],
    )(pos, rad, edges, *args)


def stencil(step, n_gy, ocean, mix, lon, lat, mirror, out):
    layers, rows, lanes = ocean.shape[1:]
    gy = lax.axis_index("gy")
    first = step * CHUNK
    lane = lax.broadcasted_iota(jnp.int32, (rows, lanes), 1)
    sub = lax.broadcasted_iota(jnp.int32, (rows, lanes), 0)
    lane8 = lax.broadcasted_iota(jnp.int32, (8, lanes), 1)
    bands = []
    for half in range(2):
        at = pl.ds(8 * half, 8)
        west = pltpu.roll(lon[0, step, at, :], 1, 1)
        east = pltpu.roll(lon[1, step, at, :], lanes - 1, 1)
        bands.append(jnp.where(lane8 % 2 == 1, west, east))
    spin = 2.0 * ((gy * rows + sub).astype(jnp.float32) + 0.5) / (rows * n_gy) - 1.0
    spin = SPIN_RATE * spin
    is_top, is_low = gy == n_gy - 1, gy == 0
    level = pl.ds(pl.multiple_of(first, CHUNK), CHUNK)
    for field in range(4):
        folded = -mirror[field, level, :] if field < 2 else mirror[field, level, :]
        upper = jnp.where(is_top, folded, lat[1, field, level, :])
        lower = jnp.where(is_low, 0.0, lat[0, field, level, :])
        for layer in range(CHUNK):
            at = first + layer
            here = ocean[field, at]
            up = ocean[field, jnp.maximum(at - 1, 0)]
            down = ocean[field, jnp.minimum(at + 1, layers - 1)]
            sides = []
            for v in range(rows // 8):
                g = (field * CHUNK + layer) * (rows // 8) + v
                sides.append(pltpu.roll(bands[g // 64], lanes - 1 - 2 * (g % 64), 1))
            sides = jnp.concatenate(sides, axis=0)
            west = jnp.where(lane == 0, sides, pltpu.roll(here, 1, 1))
            east = jnp.where(lane == lanes - 1, sides, pltpu.roll(here, lanes - 1, 1))
            south = jnp.where(sub == 0, lower[layer : layer + 1], pltpu.roll(here, 1, 0))
            north = jnp.where(sub == rows - 1, upper[layer : layer + 1], pltpu.roll(here, rows - 1, 0))
            laplace = east + west + north + south - 4.0 * here
            value = here + mix[at] * laplace + VERT_MIX * (up + down - 2.0 * here)
            if field == 0:
                value = value + spin * ocean[1, at]
            if field == 1:
                value = value - spin * ocean[0, at]
            out[field, at] = value


def couple_kernel(n_gx, n_gy, sent, cell, ocean, mix, lon, lat, mirror, *refs):
    surface, current, plain, here, there, back, home, *sems = refs
    gx, gy = lax.axis_index("gx"), lax.axis_index("gy")
    tiles = n_gx * n_gy
    rows, lanes = ocean.shape[2:]
    steps = ocean.shape[1] // CHUNK

    def work(first, last):
        def one(step, carry):
            stencil(step, n_gy, ocean, mix, lon, lat, mirror, plain)
            return carry

        lax.fori_loop(first, last, one, 0)

    barrier = pltpu.get_barrier_semaphore()
    for d in range(1, n_gx):
        peer = (lax.rem(gx + d, n_gx), gy)
        pl.semaphore_signal(barrier, inc=1, device_id=peer, device_id_type=MESH)
    for d in range(1, n_gy):
        peer = (gx, lax.rem(gy + d, n_gy))
        pl.semaphore_signal(barrier, inc=1, device_id=peer, device_id_type=MESH)
    pl.semaphore_wait(barrier, n_gx + n_gy - 2)

    def swap(source, middle, target, sems, marks):
        send_x, recv_x, send_y, recv_y, local = sems
        own = pltpu.make_async_copy(source.at[gx], middle.at[gx], local)
        own.start()
        copies = []
        for d in range(1, n_gx):
            peer = lax.rem(gx + d, n_gx)
            copies.append(
                pltpu.make_async_remote_copy(
                    src_ref=source.at[peer],
                    dst_ref=middle.at[gx],
                    send_sem=send_x.at[d - 1],
                    recv_sem=recv_x.at[d - 1],
                    device_id=(peer, gy),
                    device_id_type=MESH,
                )
            )
        for copy in copies:
            copy.start()
        work(marks[0], marks[1])
        own.wait()
        for copy in copies:
            copy.wait()
        own = pltpu.make_async_copy(middle.at[:, gy], target.at[:, gy], local)
        own.start()
        copies = []
        for d in range(1, n_gy):
            peer = lax.rem(gy + d, n_gy)
            copies.append(
                pltpu.make_async_remote_copy(
                    src_ref=middle.at[:, peer],
                    dst_ref=target.at[:, gy],
                    send_sem=send_y.at[d - 1],
                    recv_sem=recv_y.at[d - 1],
                    device_id=(gx, peer),
                    device_id_type=MESH,
                )
            )
        for copy in copies:
            copy.start()
        work(marks[1], marks[2])
        own.wait()
        for copy in copies:
            copy.wait()

    swap(sent, here, there, sems[0:5], (0, steps // 3, steps // 2))
    cells = jnp.concatenate([cell[0:1], cell[1:2]], axis=1)
    cell_row, cell_col = cells // lanes, cells % lanes
    pick = (lax.broadcasted_iota(jnp.int32, (lanes, 2 * tiles), 0) == cell_col).astype(jnp.bfloat16)
    in_row = lax.broadcasted_iota(jnp.int32, (rows, 2 * tiles), 0) == cell_row
    arrived = there[...].reshape(tiles, lanes).T
    spread = []
    for comp in range(2):
        values = jnp.concatenate([arrived[2 * comp : 2 * comp + 1], arrived[2 * comp + 1 : 2 * comp + 2]], axis=1)
        spread.append(jnp.where(in_row, values, 0.0))
    forcing = lax.dot_general(
        split(jnp.concatenate(spread, axis=0)),
        pick,
        (((1,), (1,)), ((), ())),
        preferred_element_type=jnp.float32,
    )
    skin = jnp.concatenate([plain[0, 0], plain[1, 0]], axis=0)
    level = skin + joined(forcing)
    surface[...] = level.reshape(2, rows, lanes)
    found = joined(jnp.dot(split(level), pick, preferred_element_type=jnp.float32))
    replies = []
    for comp in range(2):
        values = jnp.where(in_row, found[comp * rows : (comp + 1) * rows], 0.0)
        values = jnp.sum(values, axis=0, keepdims=True)
        replies += [values[:, :tiles], values[:, tiles:]]
    replies.append(jnp.zeros((lanes - 4, tiles), jnp.float32))
    back[...] = jnp.concatenate(replies, axis=0).T.reshape(back.shape)
    swap(back, home, current, sems[5:10], (steps // 2, steps - 1, steps))


def couple(n_gx, n_gy, sent, cell, ocean, *sea):
    tiles = n_gx * n_gy
    rows, lanes = ocean.shape[2:]
    box = (n_gx, n_gy, 1, lanes)
    dma = pltpu.SemaphoreType.DMA
    sems = [dma((n_gx - 1,)), dma((n_gx - 1,)), dma((n_gy - 1,)), dma((n_gy - 1,)), dma]
    return pl.pallas_call(
        functools.partial(couple_kernel, n_gx, n_gy),
        out_shape=(shape(2, rows, lanes), shape(*box), shape(*ocean.shape)),
        in_specs=[VMEM] * (3 + len(sea)),
        out_specs=(VMEM,) * 3,
        scratch_shapes=[pltpu.VMEM(box, jnp.float32)] * 4 + sems + sems,
        compiler_params=grant(16, collective_id=SUB, has_side_effects=True),
        name="couple",
    )(sent.reshape(box), cell, ocean, *sea)


def finish_kernel(plain, surface, current, slots, vel, vel_out, ocean_out, sems):
    layers = plain.shape[1]
    copies = [
        pltpu.make_async_copy(surface, ocean_out.at[pl.ds(0, 2), 0], sems.at[0]),
        pltpu.make_async_copy(plain.at[pl.ds(2, 2)], ocean_out.at[pl.ds(2, 2)], sems.at[1]),
    ]
    for field in range(2):
        deep = pl.ds(1, layers - 1)
        copies.append(
            pltpu.make_async_copy(plain.at[field, deep], ocean_out.at[field, deep], sems.at[2 + field])
        )
    for copy in copies:
        copy.start()
    blocks, discs = vel.shape[1], vel.shape[2]
    tiles = current.shape[0]
    got = current[...].reshape(tiles, discs).T
    spots = jnp.concatenate([slots[0:1], slots[1:2]], axis=1)
    place = lax.broadcasted_iota(jnp.int32, (blocks, 2 * tiles), 0) == spots
    for comp in range(2):
        values = jnp.concatenate([got[2 * comp : 2 * comp + 1], got[2 * comp + 1 : 2 * comp + 2]], axis=1)
        values = jnp.sum(jnp.where(place, values, 0.0), axis=1, keepdims=True)
        speed = vel[comp]
        vel_out[comp] = speed + DRAG_BACK * (values - speed)
    for copy in copies:
        copy.wait()


def finish(plain, surface, current, slots, vel):
    tiles = current.shape[0] * current.shape[1]
    return pl.pallas_call(
        finish_kernel,
        out_shape=(shape(*vel.shape), shape(*plain.shape)),
        in_specs=[VMEM] * 5,
        out_specs=(VMEM, ANY),
        scratch_shapes=[pltpu.SemaphoreType.DMA((4,))],
        compiler_params=grant(4),
        name="finish",
    )(plain, surface, current.reshape(tiles, 1, current.shape[3]), slots, vel)


def body(
    disc_pos,
    disc_vel,
    radius,
    bond_list,
    contact_mask,
    remap_block,
    ocean_state,
    mix_coef,
    remap_cell,
    fold_perm,
):
    n_gx, n_gy = lax.axis_size("gx"), lax.axis_size("gy")
    rows_dev, cols_dev, discs = radius.shape
    blocks = rows_dev * cols_dev
    slots = remap_block[0].T
    cell = remap_cell[0].T
    perm = fold_perm.reshape(1, discs)
    position = disc_pos.reshape(2, blocks, discs)
    velocity = disc_vel.reshape(2, blocks, discs)
    rad = radius.reshape(blocks, discs)
    bonds = bond_list.reshape(BONDS, blocks, discs)
    sea_shape = (4, mix_coef.shape[0], discs)
    flat = (4 * mix_coef.shape[0], discs)
    position, rad, edges = prep(position, rad)
    halo, held, marks, halo_rad = exchange(0, n_gx, n_gy, position, rad, edges)
    position, velocity, edges, mask = contact_step(
        0, n_gy, position, velocity, rad, bonds, contact_mask, marks, held, halo, halo_rad
    )
    sides, bottom, top = pack(ocean_state, edges)
    halo, held, marks, lon, lat, rows, perms = exchange(
        1, n_gx, n_gy, position, rad, edges, top.reshape(flat), bottom.reshape(flat), sides, perm
    )
    position, velocity, edges, turned = contact_step(
        1, n_gy, position, velocity, rad, bonds, mask, marks, held, halo, halo_rad, rows, perms
    )
    halo, held, marks, mirror = exchange(2, n_gx, n_gy, position, rad, edges, turned)
    position, velocity, sent = contact_step(
        2, n_gy, position, velocity, rad, bonds, mask, marks, held, halo, halo_rad, slots
    )
    sea = (mix_coef, lon, lat.reshape(2, *sea_shape), mirror.reshape(sea_shape))
    surface, current, plain = couple(n_gx, n_gy, sent, cell, ocean_state, *sea)
    vel_next, ocean_next = finish(plain, surface, current, slots, velocity)
    return (position.reshape(disc_pos.shape), vel_next.reshape(disc_vel.shape), ocean_next)


def solution(mesh):
    in_specs = (
        P(None, "gy", "gx", None),
        P(None, "gy", "gx", None),
        P("gy", "gx", None),
        P(None, "gy", "gx", None),
        P(None, "gy", "gx"),
        P(("gx", "gy"), None, None),
        P(None, None, "gy", "gx"),
        P(None, "gy", "gx"),
        P(("gx", "gy"), None, None),
        P("gx"),
    )
    out_specs = (P(None, "gy", "gx", None), P(None, "gy", "gx", None), P(None, None, "gy", "gx"))
    return jax.shard_map(body, mesh=mesh, in_specs=in_specs, out_specs=out_specs, check_vma=False)
```

```python
import functools

import jax
import jax.numpy as jnp
from jax import lax
from jax.experimental import pallas as pl
from jax.experimental.pallas import tpu as pltpu
from jax.sharding import PartitionSpec as P

BONDS = 4
SUB = 3
SOFTEN = 0.0001
STIFFNESS = 2.0
BOND_STIFF = 0.1
TIME_STEP = 0.05
DRAG_ICE = 15.0
DRAG_BACK = 0.5
VERT_MIX = 0.1
SPIN_RATE = 0.3
NEIGHBOURS = ((-1, -1), (-1, 0), (-1, 1), (0, -1), (0, 1), (1, -1), (1, 0), (1, 1))
ROWS = 1
OWN_STEP = 16
NEAR_STEP = 32
REST_STEP = 16
HALF = 64
MARKS = 16
CHUNK = 8
TURNERS = 12
EARLY = 32
TURN_ROWS = 16
MESH = pl.DeviceIdType.MESH
BUSY = pl.CostEstimate(flops=1 << 32, bytes_accessed=1 << 24, transcendentals=1 << 22)
VMEM = pl.BlockSpec(memory_space=pltpu.VMEM)
ANY = pl.BlockSpec(memory_space=pl.ANY)
HBM = pl.BlockSpec(memory_space=pltpu.HBM)


def grant(mib, **more):
    return pltpu.CompilerParams(vmem_limit_bytes=mib << 20, **more)


def shape(*dims):
    return jax.ShapeDtypeStruct(dims, jnp.float32)


def split(value):
    high = value.astype(jnp.bfloat16)
    rest = value - high.astype(jnp.float32)
    middle = rest.astype(jnp.bfloat16)
    low = (rest - middle.astype(jnp.float32)).astype(jnp.bfloat16)
    return jnp.concatenate([high, middle, low], axis=0)


def joined(value):
    rows = value.shape[0] // 3
    return value[:rows] + value[rows : 2 * rows] + value[2 * rows :]


def lane_take(rows, index):
    return lax.gather(
        rows,
        index[..., None],
        lax.GatherDimensionNumbers(
            offset_dims=(),
            collapsed_slice_dims=(1,),
            start_index_map=(1,),
            operand_batching_dims=(0,),
            start_indices_batching_dims=(0,),
        ),
        slice_sizes=(1, 1),
        mode=lax.GatherScatterMode.PROMISE_IN_BOUNDS,
    )


def pieces(value):
    high = value.astype(jnp.bfloat16).astype(jnp.float32)
    middle = (value - high).astype(jnp.bfloat16).astype(jnp.float32)
    return high, middle, value - high - middle


def write_marks(parts, marks):
    for comp, part in enumerate(parts):
        for i, piece in enumerate(pieces(part)):
            marks[pl.ds(3 * comp + i, part.shape[0], stride=MARKS), :] = piece


def other_side(marks):
    row = lax.broadcasted_iota(jnp.int32, marks.shape, 0)
    marks = jnp.where(row < 9, marks, jnp.where(row < 12, 1.0, 0.0))
    return marks.T.astype(jnp.bfloat16)


def own_side(marks):
    row = lax.broadcasted_iota(jnp.int32, marks.shape, 0)
    sides = []
    for comp in range(3):
        moved = pltpu.roll(marks, 9 - 3 * comp, 0)
        moved = moved if comp == 2 else -moved
        fixed = jnp.where(row // 3 == comp, 1.0, 0.0)
        sides.append(jnp.where((row >= 9) & (row < 12), moved, fixed))
    return jnp.concatenate(sides, axis=1).astype(jnp.bfloat16)


def pair_sums(other, own):
    pairs = jnp.dot(other, own, preferred_element_type=jnp.float32)
    lanes = pairs.shape[1] // 3
    acc_x = acc_y = jnp.zeros((8, lanes), jnp.float32)
    for c in range(pairs.shape[0] // 8):
        rows = pairs[8 * c : 8 * c + 8]
        sep_x, sep_y, reach = rows[:, :lanes], rows[:, lanes : 2 * lanes], rows[:, 2 * lanes :]
        inverse = lax.rsqrt(sep_x * sep_x + sep_y * sep_y + SOFTEN)
        push = jnp.maximum(reach * inverse - 1.0, 0.0)
        acc_x = acc_x + push * sep_x
        acc_y = acc_y + push * sep_y
    return acc_x, acc_y


def marks_of(marks, b):
    return marks[pl.ds(pl.multiple_of(b * MARKS, MARKS), MARKS), :]


def turn(rows, perms, turned):
    lanes = rows.shape[2]

    def one(h, carry):
        wanted = jnp.broadcast_to(perms[h], (8, lanes))
        owner, column = wanted // lanes, wanted % lanes
        for half in range(TURN_ROWS // 8):
            at = pl.ds(8 * half, 8)
            got = jnp.zeros((8, lanes), jnp.float32)
            for source in range(rows.shape[0]):
                got = jnp.where(owner == source, lane_take(rows[source, at, :], column), got)
            turned[h, at, :] = got
        return carry

    lax.fori_loop(0, perms.shape[0], one, 0)


def own_forces(first, count, marks, force):
    def some(t, carry):
        for u in range(OWN_STEP):
            b = first + t * OWN_STEP + u
            own = marks_of(marks, b)
            acc = pair_sums(other_side(own), own_side(own))
            at = pl.ds(pl.multiple_of(b * 8, 8), 8)
            for k in range(2):
                force[k, at, :] = acc[k]
        return carry

    lax.fori_loop(0, count // OWN_STEP, some, 0)


def write_mask(n_gy, allowed, mask):
    lane = lax.broadcasted_iota(jnp.int32, (8, 128), 1)
    _, rows_dev, cols_dev = allowed.shape
    spread = jnp.zeros((8, 128), jnp.float32)
    for y in range(rows_dev):
        part = allowed[:, y, :].astype(jnp.float32)
        part = jnp.concatenate([part, jnp.zeros((8, 128 - cols_dev), jnp.float32)], axis=1)
        spread = spread + (pltpu.roll(part, y * cols_dev, 1) if y else part)
    which = lax.broadcasted_iota(jnp.int32, (8, 128), 0)
    shift_y = jnp.where(which < 3, -1, jnp.where(which < 5, 0, 1))
    row = lax.axis_index("gy") * rows_dev + lane // cols_dev + shift_y
    spread = jnp.where((row >= 0) & (row < n_gy * rows_dev), spread, 0.0)
    mask[...] = jnp.concatenate([spread, jnp.zeros((120, 128), jnp.float32)], axis=0).T


def contact_kernel(which, n_gy, pos, vel, rad, bonds, mask, marks, held, halo, halo_rad, *refs):
    last = which == SUB - 1
    if last:
        slots, pos_out, vel_out, sent, *scratch = refs
    elif which == 1:
        rows, perms, pos_out, vel_out, edges, turned, *scratch = refs

        @pl.when(lax.axis_index("gy") == n_gy - 1)
        def _():
            turn(rows, perms, turned)

    else:
        allowed, mask = mask, refs[3]
        pos_out, vel_out, edges, _, *scratch = refs
        write_mask(n_gy, allowed, mask)
    wide, found, seen, force, tally, work, sem = scratch
    rows_dev, cols_dev = wide.shape[1] - 2, pos.shape[1] // (wide.shape[1] - 2)
    blocks, discs = rad.shape
    for comp in range(3):
        source = pos.at[comp] if comp < 2 else rad

        def frame(side, first, size):
            if comp < 2:
                return halo[side, comp, pl.ds(first, size), :]
            return halo_rad[side, pl.ds(first, size), :]

        for y in range(rows_dev):
            wide[comp, y + 1, pl.ds(1, cols_dev), :] = source[pl.ds(y * cols_dev, cols_dev), :]
            wide[comp, y + 1, pl.ds(0, 1), :] = frame(3, y, 1)
            wide[comp, y + 1, pl.ds(cols_dev + 1, 1), :] = frame(4, y, 1)
        for side, y in ((0, 0), (5, rows_dev + 1)):
            wide[comp, y, pl.ds(0, 1), :] = frame(side, 7, 1)
            wide[comp, y, pl.ds(1, cols_dev), :] = frame(side + 1, 0, cols_dev)
            wide[comp, y, pl.ds(cols_dev + 1, 1), :] = frame(side + 2, 0, 1)
    lane = lax.broadcasted_iota(jnp.int32, (8, discs), 1)
    lane_f = lane.astype(jnp.float32)
    tri_row = lax.broadcasted_iota(jnp.int32, (discs, 2 * discs), 0)
    tri_col = lax.broadcasted_iota(jnp.int32, (discs, 2 * discs), 1)
    triangle = (tri_row <= tri_col).astype(jnp.bfloat16)
    low_row = lax.broadcasted_iota(jnp.int32, (blocks, blocks), 0)
    low_col = lax.broadcasted_iota(jnp.int32, (blocks, blocks), 1)
    lower = (low_col <= low_row).astype(jnp.bfloat16)

    def collect(start):
        def one_row(step_y, carry):
            units, totals = [], []
            for half in range(ROWS * cols_dev // 8):
                y = step_y * ROWS + half // (cols_dev // 8)
                x0 = half % (cols_dev // 8) * 8
                at = pl.ds(pl.multiple_of(y * cols_dev + x0, 8), 8)
                own = [pos[0, at, :], pos[1, at, :], rad[at, :]]
                reach = jnp.max(own[2], axis=1, keepdims=True)
                low = [jnp.min(own[c], axis=1, keepdims=True) - reach for c in range(2)]
                high = [jnp.max(own[c], axis=1, keepdims=True) + reach for c in range(2)]
                weights = mask[at, :]
                flags = []
                places = []
                for k, (sy, sx) in enumerate(NEIGHBOURS):
                    place = (y + 1 + sy, pl.ds(x0 + 1 + sx, 8), slice(None))
                    nx, ny, nr = (wide[(c,) + place] for c in range(3))
                    close = (nx - nr < high[0] - float(sx)) & (nx + nr > low[0] - float(sx))
                    close = close & (ny - nr < high[1] - float(sy)) & (ny + nr > low[1] - float(sy))
                    close = close & (weights[:, k : k + 1] > 0.5)
                    flags.append(close.astype(jnp.float32))
                    places.append(place)
                ranks = jnp.dot(
                    jnp.concatenate(flags, axis=0).astype(jnp.bfloat16),
                    triangle,
                    preferred_element_type=jnp.float32,
                )
                base = jnp.zeros((8, discs), jnp.float32) - start
                for k in range(8):
                    rank = ranks[8 * k : 8 * k + 8, :discs]
                    total = ranks[8 * k : 8 * k + 8, discs:]
                    want = lane_f - base
                    source = jnp.zeros((8, discs), jnp.int32)
                    units.append((half, k, source, places[k], rank, total, want))
                    base = base + total
                totals.append((at, base))
            sources = [u[2] for u in units]
            step = discs // 2
            while step >= 1:
                probes = [lane_take(u[4], i + (step - 1)) for u, i in zip(units, sources)]
                sources = [
                    jnp.where(probe <= u[6], i + step, i)
                    for probe, u, i in zip(probes, units, sources)
                ]
                step //= 2
            for half, (at, base) in enumerate(totals):
                mine = [(u, i) for u, i in zip(units, sources) if u[0] == half]
                for comp in range(3):
                    got = jnp.full((8, discs), -1.0 if comp == 2 else 0.0, jnp.float32)
                    for (_, k, _, place, _, total, want), source in mine:
                        valid = (want >= 0.0) & (want < total)
                        value = wide[(comp,) + place]
                        if comp < 2 and NEIGHBOURS[k][1 - comp] != 0:
                            value = value + float(NEIGHBOURS[k][1 - comp])
                        got = jnp.where(valid, lane_take(value, source), got)
                    found[comp, at, :] = got
                found[3, at, :] = base
            return carry

        lax.fori_loop(0, rows_dev // ROWS, one_row, 0)
        write_marks([found[k] for k in range(3)], seen)
        left = found[3]
        size = jnp.where(left > float(HALF), 1.0, 0.0)
        ends = jnp.dot(lower, size.astype(jnp.bfloat16), preferred_element_type=jnp.float32)
        spot = lax.broadcasted_iota(jnp.int32, (1, discs), 1).astype(jnp.float32)
        block = jnp.sum(jnp.where(ends <= spot, 1.0, 0.0), axis=0, keepdims=True)
        tally[0:1] = block.astype(jnp.int32)
        tally[1:2] = ends[blocks - 1 :].astype(jnp.int32)
        deepest = jnp.max(left, axis=0, keepdims=True)
        tally[2:3] = jnp.ceil(deepest * (1.0 / discs)).astype(jnp.int32)
        copy = pltpu.make_async_copy(tally, work, sem)
        copy.start()
        copy.wait()

    def meet(b, part, fresh):
        at = pl.ds(pl.multiple_of(b * 8, 8), 8)
        b = jnp.minimum(b, blocks - 1)
        other = other_side(marks_of(seen, b))[part * HALF : (part + 1) * HALF]
        acc = pair_sums(other, own_side(marks_of(marks, b)))
        for k in range(2):
            if fresh:
                force[k, at, :] = acc[k]
            else:
                force[k, at, :] += acc[k]

    def sweep(fresh):
        def some(t, carry):
            for u in range(NEAR_STEP):
                meet(t * NEAR_STEP + u, 0, fresh)
            return carry

        def rest(t, carry):
            for u in range(REST_STEP):
                meet(work[0, t * REST_STEP + u], 1, False)
            return carry

        lax.fori_loop(0, blocks // NEAR_STEP, some, 0)
        lax.fori_loop(0, (work[1, 0] + (REST_STEP - 1)) // REST_STEP, rest, 0)

    collect(0.0)
    sweep(True)

    def more(p, carry):
        collect(p.astype(jnp.float32) * discs)
        sweep(False)
        return carry

    lax.fori_loop(1, work[2, 0], more, 0)

    def update(g, carry):
        at = pl.ds(pl.multiple_of(g * 8, 8), 8)
        scale = 0.06 / rad[at, :]
        scale = scale * scale
        for k in range(2):
            here = pos[k, at, :]
            bonded = lane_take(here, bonds[0, at, :])
            for p in range(1, BONDS):
                bonded = bonded + lane_take(here, bonds[p, at, :])
            push = jnp.zeros((8, discs), jnp.float32)
            for r in range(8):
                rows = pl.ds(g * 64 + r, 8, stride=8)
                push = push + (held[k, rows, :] + force[k, rows, :])
            total = BOND_STIFF * (bonded - BONDS * here) - STIFFNESS * push
            speed = vel[k, at, :] + total * scale
            vel_out[k, at, :] = speed
            pos_out[k, at, :] = here + TIME_STEP * speed
        return carry

    lax.fori_loop(0, blocks // 8, update, 0)
    if last:
        spots = [jnp.broadcast_to(slots[k : k + 1], (8, blocks)) for k in range(2)]
        rows = []
        for comp in range(2):
            drag = rad[...] * rad[...] * vel_out[comp]
            total = DRAG_ICE * jnp.sum(drag.T, axis=0, keepdims=True)
            total = jnp.broadcast_to(total, (8, blocks))
            for spot in spots:
                moved = lane_take(total, jnp.maximum(spot, 0))
                rows.append(jnp.where(spot >= 0, moved, 0.0)[0:1])
        rows.append(jnp.zeros((blocks - 4, blocks), jnp.float32))
        sent[:, 0, :] = jnp.concatenate(rows, axis=0).T
    else:
        for side in range(2):
            for comp in range(2):
                at = pl.ds(side * (cols_dev - 1), rows_dev, stride=cols_dev)
                edges[side, comp] = pos_out[comp, at, :]


def contact_step(which, n_gy, pos, vel, rad, bonds, mask, marks, held, halo, halo_rad, *extra):
    blocks, discs = rad.shape
    rows_dev = blocks // 16
    square = shape(2, blocks, discs)
    tail = shape(blocks, 1, discs) if which == SUB - 1 else shape(2, 2, rows_dev, discs)
    outs = (square, square, tail)
    if which == 0:
        outs += (shape(*rad.shape),)
    if which == 1:
        outs += (shape(*extra[0].shape),)
    args = (pos, vel, rad, bonds, mask, marks, held, halo, halo_rad) + extra
    return pl.pallas_call(
        functools.partial(contact_kernel, which, n_gy),
        out_shape=outs,
        in_specs=[VMEM] * len(args),
        out_specs=(VMEM,) * len(outs),
        scratch_shapes=[
            pltpu.VMEM((3, rows_dev + 2, 24, discs), jnp.float32),
            pltpu.VMEM((4, blocks, discs), jnp.float32),
            pltpu.VMEM((MARKS * blocks, discs), jnp.float32),
            pltpu.VMEM((2, 8 * blocks + 8, discs), jnp.float32),
            pltpu.VMEM((8, discs), jnp.int32),
            pltpu.SMEM((8, discs), jnp.int32),
            pltpu.SemaphoreType.DMA,
        ],
        compiler_params=grant(16),
        cost_estimate=BUSY,
        name=("contact_first", "contact", "contact_last")[which],
    )(*args)


def prep_kernel(pos_in, rad_in, pos, rad, edges, sems):
    copies = [
        pltpu.make_async_copy(pos_in, pos, sems.at[0]),
        pltpu.make_async_copy(rad_in, rad, sems.at[1]),
    ]
    for copy in copies:
        copy.start()
    for copy in copies:
        copy.wait()
    for comp in range(3):
        source = pos.at[comp] if comp < 2 else rad
        for side in range(2):
            edges[side, comp] = source[pl.ds(side * 15, 8, stride=16), :]


def prep(pos, rad):
    return pl.pallas_call(
        prep_kernel,
        out_shape=(shape(*pos.shape), shape(*rad.shape), shape(2, 3, 8, 128)),
        in_specs=[HBM] * 2,
        out_specs=(VMEM,) * 3,
        scratch_shapes=[pltpu.SemaphoreType.DMA((2,))],
        compiler_params=grant(4),
        name="prep",
    )(pos, rad)


def pack_kernel(ocean, after, columns, bottom, top):
    rows = ocean.shape[2]
    lane = lax.broadcasted_iota(jnp.int32, (8, 128), 1)
    packed = [jnp.zeros((8, 128), jnp.float32)] * 2
    for field in range(4):
        for layer in range(CHUNK):
            for v in range(rows // 8):
                g = (field * CHUNK + layer) * (rows // 8) + v
                place = g % 64
                turned = pltpu.roll(ocean[field, layer, pl.ds(8 * v, 8), :], 2 * place + 1, 1)
                packed[g // 64] = jnp.where(lane // 2 == place, turned, packed[g // 64])
    columns[0] = jnp.concatenate(packed, axis=0)
    bottom[...] = ocean[:, :, 0, :]
    top[...] = ocean[:, :, rows - 1, :]


def pack(ocean, after):
    fields, layers, rows, lanes = ocean.shape
    steps = layers // CHUNK
    row = pl.BlockSpec((fields, CHUNK, lanes), lambda i: (0, i, 0))
    return pl.pallas_call(
        pack_kernel,
        grid=(steps,),
        out_shape=(
            shape(steps, 16, lanes),
            shape(fields, layers, lanes),
            shape(fields, layers, lanes),
        ),
        in_specs=[pl.BlockSpec((fields, CHUNK, rows, lanes), lambda i: (0, i, 0, 0)), ANY],
        out_specs=(pl.BlockSpec((1, 16, lanes), lambda i: (i, 0, 0)), row, row),
        compiler_params=grant(8),
        name="pack",
    )(ocean, after)


def exchange_kernel(which, n_gx, n_gy, *refs):
    if which == 0:
        pos, rad, edges, halo, held, marks, halo_rad, *scratch = refs
        send_sem, recv_sem, rad_send, rad_recv = scratch
    elif which == 1:
        pos, rad, edges, top, bottom, sides, perm, halo, held, marks, lon, lat, rows, perms, *scratch = refs
        send_sem, recv_sem, sea_send, sea_recv, *scratch = scratch
        far_send, far_recv, perm_send, perm_recv, own = scratch
    else:
        pos, rad, edges, turned, halo, held, marks, mirror, *scratch = refs
        send_sem, recv_sem, far_send, far_recv, own = scratch
    gx, gy = lax.axis_index("gx"), lax.axis_index("gy")
    is_top = gy == n_gy - 1

    def at(dx, dy):
        return lax.rem(gx + dx + n_gx, n_gx), lax.rem(gy + dy + n_gy, n_gy)

    barrier = pltpu.get_barrier_semaphore()
    for dy, dx in NEIGHBOURS:
        pl.semaphore_signal(barrier, inc=1, device_id=at(dx, dy), device_id_type=MESH)
    if which > 0:

        @pl.when(is_top)
        def _():
            for d in range(1, n_gx):
                pl.semaphore_signal(barrier, inc=1, device_id=at(d, 0), device_id_type=MESH)

    blocks = rad.shape[0]
    write_marks([pos[0], pos[1], rad[...]], marks)
    own_forces(0, EARLY, marks, held)
    if which > 0:

        @pl.when(is_top)
        def _():
            pl.semaphore_wait(barrier, len(NEIGHBOURS) + n_gx - 1)

        @pl.when(jnp.logical_not(is_top))
        def _():
            pl.semaphore_wait(barrier, len(NEIGHBOURS))

    else:
        pl.semaphore_wait(barrier, len(NEIGHBOURS))

    def send(source, target, sems, index, device):
        return pltpu.make_async_remote_copy(
            src_ref=source,
            dst_ref=target,
            send_sem=sems[0].at[index],
            recv_sem=sems[1].at[index],
            device_id=device,
            device_id_type=MESH,
        )

    def halo_copies(body, part, target, sems):
        copies = []
        for k, (sy, sx) in enumerate(NEIGHBOURS):
            first = 0 if sy == 1 else blocks - 16
            first = first + 8 if sx == -1 else first
            size = 16 if sx == 0 else 8
            source = part(0 if sx == 1 else 1) if sy == 0 else body(pl.ds(first, size))
            copies.append(send(source, target(k, pl.ds(0, size)), sems, k, at(-sx, -sy)))
        return copies

    copies = halo_copies(
        lambda rows: pos.at[:, rows, :],
        lambda side: edges.at[side, pl.ds(0, 2)],
        lambda k, rows: halo.at[k, :, rows, :],
        (send_sem, recv_sem),
    )
    if which == 0:
        copies += halo_copies(
            lambda rows: rad.at[rows, :],
            lambda side: edges.at[side, 2],
            lambda k, rows: halo_rad.at[k, rows, :],
            (rad_send, rad_recv),
        )
    for copy in copies:
        copy.start()
    if which == 1:
        sea = (sea_send, sea_recv)
        later = [
            send(sides, lon.at[0], sea, 0, at(1, 0)),
            send(sides, lon.at[1], sea, 1, at(-1, 0)),
            send(top, lat.at[0], sea, 2, at(0, 1)),
            send(bottom, lat.at[1], sea, 3, at(0, -1)),
        ]
        copies += later

    if which == 1:
        first = pl.multiple_of(jnp.minimum(gx, TURNERS - 1) * TURN_ROWS, TURN_ROWS)
        kept = pltpu.make_async_copy(perm, perms.at[gx], own.at[0])
        mine = pltpu.make_async_copy(top.at[pl.ds(first, TURN_ROWS), :], rows.at[gx], own.at[1])
        notes, far = [], []
        for d in range(1, n_gx):
            peer = lax.rem(gx + d, n_gx)
            start = pl.multiple_of(jnp.minimum(peer, TURNERS - 1) * TURN_ROWS, TURN_ROWS)
            notes.append(send(perm, perms.at[gx], (perm_send, perm_recv), d - 1, at(d, 0)))
            source = top.at[pl.ds(start, TURN_ROWS), :]
            far.append(send(source, rows.at[gx], (far_send, far_recv), d - 1, at(d, 0)))

        @pl.when(is_top)
        def _():
            kept.start()
            for d in range(1, n_gx):
                notes[d - 1].start()

                @pl.when(lax.rem(gx + d, n_gx) < TURNERS)
                def _(copy=far[d - 1]):
                    copy.start()

            @pl.when(gx < TURNERS)
            def _():
                mine.start()

        for copy in later:
            copy.start()

    if which == 2:
        me = jnp.minimum(gx, TURNERS - 1)
        mine = pltpu.make_async_copy(turned.at[gx], mirror.at[me], own)
        far = []
        for d in range(1, n_gx):
            source = turned.at[lax.rem(gx + d, n_gx)]
            far.append(send(source, mirror.at[me], (far_send, far_recv), d - 1, at(d, 0)))

        @pl.when(is_top & (gx < TURNERS))
        def _():
            mine.start()
            for copy in far:
                copy.start()

    own_forces(EARLY, blocks - EARLY, marks, held)
    for copy in copies:
        copy.wait()
    if which == 1:

        @pl.when(is_top)
        def _():
            kept.wait()
            for d in range(1, n_gx):
                notes[d - 1].wait()

                @pl.when(lax.rem(gx + d, n_gx) < TURNERS)
                def _(copy=far[d - 1]):
                    copy.wait_send()

            @pl.when(gx < TURNERS)
            def _():
                mine.wait()
                for copy in far:
                    copy.wait_recv()

    if which == 2:

        @pl.when(is_top & (gx < TURNERS))
        def _():
            mine.wait()
            for copy in far:
                copy.wait_send()

        @pl.when(is_top)
        def _():
            for d in range(1, n_gx):

                @pl.when(lax.rem(gx - d + n_gx, n_gx) < TURNERS)
                def _(copy=far[d - 1]):
                    copy.wait_recv()


def exchange(which, n_gx, n_gy, pos, rad, edges, *args):
    lanes = rad.shape[1]
    blocks = rad.shape[0]
    outs = [shape(8, 2, 16, lanes), shape(2, 8 * blocks, lanes)]
    outs += [shape(MARKS * blocks, lanes)]
    dma = pltpu.SemaphoreType.DMA
    scratch = [dma((8,)), dma((8,))]
    far = [dma((n_gx - 1,)), dma((n_gx - 1,))]
    if which == 0:
        outs += [shape(8, 16, lanes)]
        scratch += [dma((8,)), dma((8,))]
    if which == 1:
        top, bottom, sides, perm = args
        outs += [shape(2, *sides.shape), shape(2, *top.shape)]
        outs += [shape(n_gx, TURN_ROWS, lanes), jax.ShapeDtypeStruct((n_gx, 1, lanes), jnp.int32)]
        scratch += [dma((4,)), dma((4,))] + far + far + [dma((2,))]
    if which == 2:
        outs += [shape(TURNERS, TURN_ROWS, lanes)]
        scratch += far + [dma]
    return pl.pallas_call(
        functools.partial(exchange_kernel, which, n_gx, n_gy),
        out_shape=tuple(outs),
        in_specs=[VMEM] * (3 + len(args)),
        out_specs=(VMEM,) * len(outs),
        scratch_shapes=scratch,
        compiler_params=grant(8, collective_id=which, has_side_effects=True),
        cost_estimate=BUSY,
        name=("exchange_first", "exchange_second", "exchange_third")[which],
    )(pos, rad, edges, *args)


def stencil(step, n_gy, ocean, mix, lon, lat, mirror, out):
    layers, rows, lanes = ocean.shape[1:]
    gy = lax.axis_index("gy")
    first = step * CHUNK
    lane = lax.broadcasted_iota(jnp.int32, (rows, lanes), 1)
    sub = lax.broadcasted_iota(jnp.int32, (rows, lanes), 0)
    lane8 = lax.broadcasted_iota(jnp.int32, (8, lanes), 1)
    bands = []
    for half in range(2):
        at = pl.ds(8 * half, 8)
        west = pltpu.roll(lon[0, step, at, :], 1, 1)
        east = pltpu.roll(lon[1, step, at, :], lanes - 1, 1)
        bands.append(jnp.where(lane8 % 2 == 1, west, east))
    spin = 2.0 * ((gy * rows + sub).astype(jnp.float32) + 0.5) / (rows * n_gy) - 1.0
    spin = SPIN_RATE * spin
    is_top, is_low = gy == n_gy - 1, gy == 0
    level = pl.ds(pl.multiple_of(first, CHUNK), CHUNK)
    for field in range(4):
        folded = -mirror[field, level, :] if field < 2 else mirror[field, level, :]
        upper = jnp.where(is_top, folded, lat[1, field, level, :])
        lower = jnp.where(is_low, 0.0, lat[0, field, level, :])
        for layer in range(CHUNK):
            at = first + layer
            here = ocean[field, at]
            up = ocean[field, jnp.maximum(at - 1, 0)]
            down = ocean[field, jnp.minimum(at + 1, layers - 1)]
            sides = []
            for v in range(rows // 8):
                g = (field * CHUNK + layer) * (rows // 8) + v
                sides.append(pltpu.roll(bands[g // 64], lanes - 1 - 2 * (g % 64), 1))
            sides = jnp.concatenate(sides, axis=0)
            west = jnp.where(lane == 0, sides, pltpu.roll(here, 1, 1))
            east = jnp.where(lane == lanes - 1, sides, pltpu.roll(here, lanes - 1, 1))
            south = jnp.where(sub == 0, lower[layer : layer + 1], pltpu.roll(here, 1, 0))
            north = jnp.where(sub == rows - 1, upper[layer : layer + 1], pltpu.roll(here, rows - 1, 0))
            laplace = east + west + north + south - 4.0 * here
            value = here + mix[at] * laplace + VERT_MIX * (up + down - 2.0 * here)
            if field == 0:
                value = value + spin * ocean[1, at]
            if field == 1:
                value = value - spin * ocean[0, at]
            out[field, at] = value


def couple_kernel(n_gx, n_gy, sent, cell, ocean, mix, lon, lat, mirror, *refs):
    surface, current, plain, here, there, back, home, *sems = refs
    gx, gy = lax.axis_index("gx"), lax.axis_index("gy")
    tiles = n_gx * n_gy
    rows, lanes = ocean.shape[2:]
    steps = ocean.shape[1] // CHUNK

    def work(first, last):
        def one(step, carry):
            stencil(step, n_gy, ocean, mix, lon, lat, mirror, plain)
            return carry

        lax.fori_loop(first, last, one, 0)

    barrier = pltpu.get_barrier_semaphore()
    for d in range(1, n_gx):
        peer = (lax.rem(gx + d, n_gx), gy)
        pl.semaphore_signal(barrier, inc=1, device_id=peer, device_id_type=MESH)
    for d in range(1, n_gy):
        peer = (gx, lax.rem(gy + d, n_gy))
        pl.semaphore_signal(barrier, inc=1, device_id=peer, device_id_type=MESH)
    pl.semaphore_wait(barrier, n_gx + n_gy - 2)

    def swap(source, middle, target, sems, marks):
        send_x, recv_x, send_y, recv_y, local = sems
        own = pltpu.make_async_copy(source.at[gx], middle.at[gx], local)
        own.start()
        copies = []
        for d in range(1, n_gx):
            peer = lax.rem(gx + d, n_gx)
            copies.append(
                pltpu.make_async_remote_copy(
                    src_ref=source.at[peer],
                    dst_ref=middle.at[gx],
                    send_sem=send_x.at[d - 1],
                    recv_sem=recv_x.at[d - 1],
                    device_id=(peer, gy),
                    device_id_type=MESH,
                )
            )
        for copy in copies:
            copy.start()
        work(marks[0], marks[1])
        own.wait()
        for copy in copies:
            copy.wait()
        own = pltpu.make_async_copy(middle.at[:, gy], target.at[:, gy], local)
        own.start()
        copies = []
        for d in range(1, n_gy):
            peer = lax.rem(gy + d, n_gy)
            copies.append(
                pltpu.make_async_remote_copy(
                    src_ref=middle.at[:, peer],
                    dst_ref=target.at[:, gy],
                    send_sem=send_y.at[d - 1],
                    recv_sem=recv_y.at[d - 1],
                    device_id=(gx, peer),
                    device_id_type=MESH,
                )
            )
        for copy in copies:
            copy.start()
        work(marks[1], marks[2])
        own.wait()
        for copy in copies:
            copy.wait()

    swap(sent, here, there, sems[0:5], (0, steps // 3, steps // 2))
    cells = jnp.concatenate([cell[0:1], cell[1:2]], axis=1)
    cell_row, cell_col = cells // lanes, cells % lanes
    pick = (lax.broadcasted_iota(jnp.int32, (lanes, 2 * tiles), 0) == cell_col).astype(jnp.bfloat16)
    in_row = lax.broadcasted_iota(jnp.int32, (rows, 2 * tiles), 0) == cell_row
    arrived = there[...].reshape(tiles, lanes).T
    spread = []
    for comp in range(2):
        values = jnp.concatenate([arrived[2 * comp : 2 * comp + 1], arrived[2 * comp + 1 : 2 * comp + 2]], axis=1)
        spread.append(jnp.where(in_row, values, 0.0))
    forcing = lax.dot_general(
        split(jnp.concatenate(spread, axis=0)),
        pick,
        (((1,), (1,)), ((), ())),
        preferred_element_type=jnp.float32,
    )
    skin = jnp.concatenate([plain[0, 0], plain[1, 0]], axis=0)
    level = skin + joined(forcing)
    surface[...] = level.reshape(2, rows, lanes)
    found = joined(jnp.dot(split(level), pick, preferred_element_type=jnp.float32))
    replies = []
    for comp in range(2):
        values = jnp.where(in_row, found[comp * rows : (comp + 1) * rows], 0.0)
        values = jnp.sum(values, axis=0, keepdims=True)
        replies += [values[:, :tiles], values[:, tiles:]]
    replies.append(jnp.zeros((lanes - 4, tiles), jnp.float32))
    back[...] = jnp.concatenate(replies, axis=0).T.reshape(back.shape)
    swap(back, home, current, sems[5:10], (steps // 2, steps - 1, steps))


def couple(n_gx, n_gy, sent, cell, ocean, *sea):
    tiles = n_gx * n_gy
    rows, lanes = ocean.shape[2:]
    box = (n_gx, n_gy, 1, lanes)
    dma = pltpu.SemaphoreType.DMA
    sems = [dma((n_gx - 1,)), dma((n_gx - 1,)), dma((n_gy - 1,)), dma((n_gy - 1,)), dma]
    return pl.pallas_call(
        functools.partial(couple_kernel, n_gx, n_gy),
        out_shape=(shape(2, rows, lanes), shape(*box), shape(*ocean.shape)),
        in_specs=[VMEM] * (3 + len(sea)),
        out_specs=(VMEM,) * 3,
        scratch_shapes=[pltpu.VMEM(box, jnp.float32)] * 4 + sems + sems,
        compiler_params=grant(16, collective_id=SUB, has_side_effects=True),
        name="couple",
    )(sent.reshape(box), cell, ocean, *sea)


def finish_kernel(plain, surface, current, slots, vel, vel_out, ocean_out, sems):
    layers = plain.shape[1]
    copies = [
        pltpu.make_async_copy(surface, ocean_out.at[pl.ds(0, 2), 0], sems.at[0]),
        pltpu.make_async_copy(plain.at[pl.ds(2, 2)], ocean_out.at[pl.ds(2, 2)], sems.at[1]),
    ]
    for field in range(2):
        deep = pl.ds(1, layers - 1)
        copies.append(
            pltpu.make_async_copy(plain.at[field, deep], ocean_out.at[field, deep], sems.at[2 + field])
        )
    for copy in copies:
        copy.start()
    blocks, discs = vel.shape[1], vel.shape[2]
    tiles = current.shape[0]
    got = current[...].reshape(tiles, discs).T
    spots = jnp.concatenate([slots[0:1], slots[1:2]], axis=1)
    place = lax.broadcasted_iota(jnp.int32, (blocks, 2 * tiles), 0) == spots
    for comp in range(2):
        values = jnp.concatenate([got[2 * comp : 2 * comp + 1], got[2 * comp + 1 : 2 * comp + 2]], axis=1)
        values = jnp.sum(jnp.where(place, values, 0.0), axis=1, keepdims=True)
        speed = vel[comp]
        vel_out[comp] = speed + DRAG_BACK * (values - speed)
    for copy in copies:
        copy.wait()


def finish(plain, surface, current, slots, vel):
    tiles = current.shape[0] * current.shape[1]
    return pl.pallas_call(
        finish_kernel,
        out_shape=(shape(*vel.shape), shape(*plain.shape)),
        in_specs=[VMEM] * 5,
        out_specs=(VMEM, ANY),
        scratch_shapes=[pltpu.SemaphoreType.DMA((4,))],
        compiler_params=grant(4),
        name="finish",
    )(plain, surface, current.reshape(tiles, 1, current.shape[3]), slots, vel)


def body(
    disc_pos,
    disc_vel,
    radius,
    bond_list,
    contact_mask,
    remap_block,
    ocean_state,
    mix_coef,
    remap_cell,
    fold_perm,
):
    n_gx, n_gy = lax.axis_size("gx"), lax.axis_size("gy")
    rows_dev, cols_dev, discs = radius.shape
    blocks = rows_dev * cols_dev
    slots = remap_block[0].T
    cell = remap_cell[0].T
    perm = fold_perm.reshape(1, discs)
    position = disc_pos.reshape(2, blocks, discs)
    velocity = disc_vel.reshape(2, blocks, discs)
    rad = radius.reshape(blocks, discs)
    bonds = bond_list.reshape(BONDS, blocks, discs)
    sea_shape = (4, mix_coef.shape[0], discs)
    flat = (4 * mix_coef.shape[0], discs)
    position, rad, edges = prep(position, rad)
    halo, held, marks, halo_rad = exchange(0, n_gx, n_gy, position, rad, edges)
    position, velocity, edges, mask = contact_step(
        0, n_gy, position, velocity, rad, bonds, contact_mask, marks, held, halo, halo_rad
    )
    sides, bottom, top = pack(ocean_state, edges)
    halo, held, marks, lon, lat, rows, perms = exchange(
        1, n_gx, n_gy, position, rad, edges, top.reshape(flat), bottom.reshape(flat), sides, perm
    )
    position, velocity, edges, turned = contact_step(
        1, n_gy, position, velocity, rad, bonds, mask, marks, held, halo, halo_rad, rows, perms
    )
    halo, held, marks, mirror = exchange(2, n_gx, n_gy, position, rad, edges, turned)
    position, velocity, sent = contact_step(
        2, n_gy, position, velocity, rad, bonds, mask, marks, held, halo, halo_rad, slots
    )
    sea = (mix_coef, lon, lat.reshape(2, *sea_shape), mirror.reshape(sea_shape))
    surface, current, plain = couple(n_gx, n_gy, sent, cell, ocean_state, *sea)
    vel_next, ocean_next = finish(plain, surface, current, slots, velocity)
    return (position.reshape(disc_pos.shape), vel_next.reshape(disc_vel.shape), ocean_next)


def solution(mesh):
    in_specs = (
        P(None, "gy", "gx", None),
        P(None, "gy", "gx", None),
        P("gy", "gx", None),
        P(None, "gy", "gx", None),
        P(None, "gy", "gx"),
        P(("gx", "gy"), None, None),
        P(None, None, "gy", "gx"),
        P(None, "gy", "gx"),
        P(("gx", "gy"), None, None),
        P("gx"),
    )
    out_specs = (P(None, "gy", "gx", None), P(None, "gy", "gx", None), P(None, None, "gy", "gx"))
    return jax.shard_map(body, mesh=mesh, in_specs=in_specs, out_specs=out_specs, check_vma=False)
```

```python
import functools

import jax
import jax.numpy as jnp
from jax import lax
from jax.experimental import pallas as pl
from jax.experimental.pallas import tpu as pltpu
from jax.sharding import PartitionSpec as P

BONDS = 4
SUB = 3
SOFTEN = 0.0001
STIFFNESS = 2.0
BOND_STIFF = 0.1
TIME_STEP = 0.05
DRAG_ICE = 15.0
DRAG_BACK = 0.5
VERT_MIX = 0.1
SPIN_RATE = 0.3
NEIGHBOURS = ((-1, -1), (-1, 0), (-1, 1), (0, -1), (0, 1), (1, -1), (1, 0), (1, 1))
OWN_STEP = 16
NEAR_STEP = 32
REST_STEP = 16
HALF = 64
MARKS = 16
CHUNK = 8
TURNERS = 12
EARLY = 32
TURN_ROWS = 16
MESH = pl.DeviceIdType.MESH
BUSY = pl.CostEstimate(flops=1 << 32, bytes_accessed=1 << 24, transcendentals=1 << 22)
VMEM = pl.BlockSpec(memory_space=pltpu.VMEM)
ANY = pl.BlockSpec(memory_space=pl.ANY)
HBM = pl.BlockSpec(memory_space=pltpu.HBM)


def grant(mib, **more):
    return pltpu.CompilerParams(vmem_limit_bytes=mib << 20, **more)


def shape(*dims):
    return jax.ShapeDtypeStruct(dims, jnp.float32)


def split(value):
    high = value.astype(jnp.bfloat16)
    rest = value - high.astype(jnp.float32)
    middle = rest.astype(jnp.bfloat16)
    low = (rest - middle.astype(jnp.float32)).astype(jnp.bfloat16)
    return jnp.concatenate([high, middle, low], axis=0)


def joined(value):
    rows = value.shape[0] // 3
    return value[:rows] + value[rows : 2 * rows] + value[2 * rows :]


def lane_take(rows, index):
    return lax.gather(
        rows,
        index[..., None],
        lax.GatherDimensionNumbers(
            offset_dims=(),
            collapsed_slice_dims=(1,),
            start_index_map=(1,),
            operand_batching_dims=(0,),
            start_indices_batching_dims=(0,),
        ),
        slice_sizes=(1, 1),
        mode=lax.GatherScatterMode.PROMISE_IN_BOUNDS,
    )


def pieces(value):
    high = value.astype(jnp.bfloat16).astype(jnp.float32)
    middle = (value - high).astype(jnp.bfloat16).astype(jnp.float32)
    return high, middle, value - high - middle


def write_marks(parts, marks):
    for comp, part in enumerate(parts):
        for i, piece in enumerate(pieces(part)):
            marks[pl.ds(3 * comp + i, part.shape[0], stride=MARKS), :] = piece


def other_side(marks):
    row = lax.broadcasted_iota(jnp.int32, marks.shape, 0)
    marks = jnp.where(row < 9, marks, jnp.where(row < 12, 1.0, 0.0))
    return marks.T.astype(jnp.bfloat16)


def own_side(marks):
    row = lax.broadcasted_iota(jnp.int32, marks.shape, 0)
    sides = []
    for comp in range(3):
        moved = pltpu.roll(marks, 9 - 3 * comp, 0)
        moved = moved if comp == 2 else -moved
        fixed = jnp.where(row // 3 == comp, 1.0, 0.0)
        sides.append(jnp.where((row >= 9) & (row < 12), moved, fixed))
    return jnp.concatenate(sides, axis=1).astype(jnp.bfloat16)


def pair_sums(other, own):
    pairs = jnp.dot(other, own, preferred_element_type=jnp.float32)
    lanes = pairs.shape[1] // 3
    acc_x = acc_y = jnp.zeros((8, lanes), jnp.float32)
    for c in range(pairs.shape[0] // 8):
        rows = pairs[8 * c : 8 * c + 8]
        sep_x, sep_y, reach = rows[:, :lanes], rows[:, lanes : 2 * lanes], rows[:, 2 * lanes :]
        inverse = lax.rsqrt(sep_x * sep_x + sep_y * sep_y + SOFTEN)
        push = jnp.maximum(reach * inverse - 1.0, 0.0)
        acc_x = acc_x + push * sep_x
        acc_y = acc_y + push * sep_y
    return acc_x, acc_y


def marks_of(marks, b):
    return marks[pl.ds(pl.multiple_of(b * MARKS, MARKS), MARKS), :]


def turn(rows, perms, turned):
    lanes = rows.shape[2]

    def one(h, carry):
        wanted = jnp.broadcast_to(perms[h], (8, lanes))
        owner, column = wanted // lanes, wanted % lanes
        for half in range(TURN_ROWS // 8):
            at = pl.ds(8 * half, 8)
            got = jnp.zeros((8, lanes), jnp.float32)
            for source in range(rows.shape[0]):
                got = jnp.where(owner == source, lane_take(rows[source, at, :], column), got)
            turned[h, at, :] = got
        return carry

    lax.fori_loop(0, perms.shape[0], one, 0)


def own_forces(first, count, marks, force):
    def some(t, carry):
        for u in range(OWN_STEP):
            b = first + t * OWN_STEP + u
            own = marks_of(marks, b)
            acc = pair_sums(other_side(own), own_side(own))
            at = pl.ds(pl.multiple_of(b * 8, 8), 8)
            for k in range(2):
                force[k, at, :] = acc[k]
        return carry

    lax.fori_loop(0, count // OWN_STEP, some, 0)


def write_mask(n_gy, allowed, mask):
    lane = lax.broadcasted_iota(jnp.int32, (8, 128), 1)
    _, rows_dev, cols_dev = allowed.shape
    spread = jnp.zeros((8, 128), jnp.float32)
    for y in range(rows_dev):
        part = allowed[:, y, :].astype(jnp.float32)
        part = jnp.concatenate([part, jnp.zeros((8, 128 - cols_dev), jnp.float32)], axis=1)
        spread = spread + (pltpu.roll(part, y * cols_dev, 1) if y else part)
    which = lax.broadcasted_iota(jnp.int32, (8, 128), 0)
    shift_y = jnp.where(which < 3, -1, jnp.where(which < 5, 0, 1))
    row = lax.axis_index("gy") * rows_dev + lane // cols_dev + shift_y
    spread = jnp.where((row >= 0) & (row < n_gy * rows_dev), spread, 0.0)
    mask[...] = jnp.concatenate([spread, jnp.zeros((120, 128), jnp.float32)], axis=0).T


def contact_kernel(which, n_gy, pos, vel, rad, bonds, mask, marks, held, halo, halo_rad, *refs):
    last = which == SUB - 1
    if last:
        slots, pos_out, vel_out, sent, *scratch = refs
    elif which == 1:
        rows, perms, pos_out, vel_out, edges, turned, *scratch = refs

        @pl.when(lax.axis_index("gy") == n_gy - 1)
        def _():
            turn(rows, perms, turned)

    else:
        allowed, mask = mask, refs[3]
        pos_out, vel_out, edges, _, *scratch = refs
        write_mask(n_gy, allowed, mask)
    wide, found, seen, force, tally, work, sem = scratch
    rows_dev, cols_dev = wide.shape[1] - 2, pos.shape[1] // (wide.shape[1] - 2)
    blocks, discs = rad.shape
    for comp in range(3):
        source = pos.at[comp] if comp < 2 else rad

        def frame(side, first, size):
            if comp < 2:
                return halo[side, comp, pl.ds(first, size), :]
            return halo_rad[side, pl.ds(first, size), :]

        for y in range(rows_dev):
            wide[comp, y + 1, pl.ds(1, cols_dev), :] = source[pl.ds(y * cols_dev, cols_dev), :]
            wide[comp, y + 1, pl.ds(0, 1), :] = frame(3, y, 1)
            wide[comp, y + 1, pl.ds(cols_dev + 1, 1), :] = frame(4, y, 1)
        for side, y in ((0, 0), (5, rows_dev + 1)):
            wide[comp, y, pl.ds(0, 1), :] = frame(side, 7, 1)
            wide[comp, y, pl.ds(1, cols_dev), :] = frame(side + 1, 0, cols_dev)
            wide[comp, y, pl.ds(cols_dev + 1, 1), :] = frame(side + 2, 0, 1)
    lane = lax.broadcasted_iota(jnp.int32, (8, discs), 1)
    lane_f = lane.astype(jnp.float32)
    tri_row = lax.broadcasted_iota(jnp.int32, (discs, 2 * discs), 0)
    tri_col = lax.broadcasted_iota(jnp.int32, (discs, 2 * discs), 1)
    triangle = (tri_row <= tri_col).astype(jnp.bfloat16)
    low_row = lax.broadcasted_iota(jnp.int32, (blocks, blocks), 0)
    low_col = lax.broadcasted_iota(jnp.int32, (blocks, blocks), 1)
    lower = (low_col <= low_row).astype(jnp.bfloat16)

    def collect_row(y, start):
        units, totals = [], []
        for half in range(cols_dev // 8):
            x0 = half * 8
            at = pl.ds(pl.multiple_of(y * cols_dev + x0, 8), 8)
            own = [pos[0, at, :], pos[1, at, :], rad[at, :]]
            reach = jnp.max(own[2], axis=1, keepdims=True)
            low = [jnp.min(own[c], axis=1, keepdims=True) - reach for c in range(2)]
            high = [jnp.max(own[c], axis=1, keepdims=True) + reach for c in range(2)]
            weights = mask[at, :]
            flags = []
            places = []
            for k, (sy, sx) in enumerate(NEIGHBOURS):
                place = (y + 1 + sy, pl.ds(x0 + 1 + sx, 8), slice(None))
                nx, ny, nr = (wide[(c,) + place] for c in range(3))
                close = (nx - nr < high[0] - float(sx)) & (nx + nr > low[0] - float(sx))
                close = close & (ny - nr < high[1] - float(sy)) & (ny + nr > low[1] - float(sy))
                close = close & (weights[:, k : k + 1] > 0.5)
                flags.append(close.astype(jnp.float32))
                places.append(place)
            ranks = jnp.dot(
                jnp.concatenate(flags, axis=0).astype(jnp.bfloat16),
                triangle,
                preferred_element_type=jnp.float32,
            )
            base = jnp.zeros((8, discs), jnp.float32) - start
            for k in range(8):
                rank = ranks[8 * k : 8 * k + 8, :discs]
                total = ranks[8 * k : 8 * k + 8, discs:]
                want = lane_f - base
                source = jnp.zeros((8, discs), jnp.int32)
                units.append((half, k, source, places[k], rank, total, want))
                base = base + total
            totals.append((at, base))
        sources = [u[2] for u in units]
        step = discs // 2
        while step >= 1:
            probes = [lane_take(u[4], i + (step - 1)) for u, i in zip(units, sources)]
            sources = [
                jnp.where(probe <= u[6], i + step, i)
                for probe, u, i in zip(probes, units, sources)
            ]
            step //= 2
        for half, (at, base) in enumerate(totals):
            mine = [(u, i) for u, i in zip(units, sources) if u[0] == half]
            for comp in range(3):
                got = jnp.full((8, discs), -1.0 if comp == 2 else 0.0, jnp.float32)
                for (_, k, _, place, _, total, want), source in mine:
                    valid = (want >= 0.0) & (want < total)
                    value = wide[(comp,) + place]
                    if comp < 2 and NEIGHBOURS[k][1 - comp] != 0:
                        value = value + float(NEIGHBOURS[k][1 - comp])
                    got = jnp.where(valid, lane_take(value, source), got)
                found[comp, at, :] = got
            found[3, at, :] = base

    def collect():
        def one_row(y, carry):
            collect_row(y, 0.0)
            return carry

        lax.fori_loop(0, rows_dev, one_row, 0)
        write_marks([found[k] for k in range(3)], seen)
        left = found[3]
        spot = lax.broadcasted_iota(jnp.int32, (1, discs), 1).astype(jnp.float32)
        for row, bound in ((0, HALF), (3, discs)):
            size = jnp.where(left > float(bound), 1.0, 0.0)
            ends = jnp.dot(lower, size.astype(jnp.bfloat16), preferred_element_type=jnp.float32)
            block = jnp.sum(jnp.where(ends <= spot, 1.0, 0.0), axis=0, keepdims=True)
            tally[row : row + 1] = block.astype(jnp.int32)
            tally[row + 1 : row + 2] = ends[blocks - 1 :].astype(jnp.int32)
        deepest = jnp.max(left, axis=0, keepdims=True)
        tally[2:3] = jnp.ceil(deepest * (1.0 / discs)).astype(jnp.int32)
        copy = pltpu.make_async_copy(tally, work, sem)
        copy.start()
        copy.wait()

    def meet(b, part, fresh):
        at = pl.ds(pl.multiple_of(b * 8, 8), 8)
        b = jnp.minimum(b, blocks - 1)
        other = other_side(marks_of(seen, b))[part * HALF : (part + 1) * HALF]
        acc = pair_sums(other, own_side(marks_of(marks, b)))
        for k in range(2):
            if fresh:
                force[k, at, :] = acc[k]
            else:
                force[k, at, :] += acc[k]

    def some(t, carry):
        for u in range(NEAR_STEP):
            meet(t * NEAR_STEP + u, 0, True)
        return carry

    def rest(t, carry):
        for u in range(REST_STEP):
            meet(work[0, t * REST_STEP + u], 1, False)
        return carry

    def crowded(i, carry):
        b = work[3, i]
        y = b // cols_dev
        at = pl.ds(pl.multiple_of(y * cols_dev, cols_dev), cols_dev)
        first = pl.multiple_of(y * (cols_dev * MARKS), cols_dev * MARKS)
        near = seen.at[pl.ds(first, cols_dev * MARKS), :]

        def deeper(p, carry):
            collect_row(y, p.astype(jnp.float32) * discs)
            write_marks([found[k, at, :] for k in range(3)], near)
            for part in range(2):
                meet(b, part, False)
            return carry

        return lax.fori_loop(1, work[2, 0], deeper, carry)

    collect()
    lax.fori_loop(0, blocks // NEAR_STEP, some, 0)
    lax.fori_loop(0, (work[1, 0] + (REST_STEP - 1)) // REST_STEP, rest, 0)
    lax.fori_loop(0, work[4, 0], crowded, 0)

    def update(g, carry):
        at = pl.ds(pl.multiple_of(g * 8, 8), 8)
        scale = 0.06 / rad[at, :]
        scale = scale * scale
        for k in range(2):
            here = pos[k, at, :]
            bonded = lane_take(here, bonds[0, at, :])
            for p in range(1, BONDS):
                bonded = bonded + lane_take(here, bonds[p, at, :])
            push = jnp.zeros((8, discs), jnp.float32)
            for r in range(8):
                rows = pl.ds(g * 64 + r, 8, stride=8)
                push = push + (held[k, rows, :] + force[k, rows, :])
            total = BOND_STIFF * (bonded - BONDS * here) - STIFFNESS * push
            speed = vel[k, at, :] + total * scale
            vel_out[k, at, :] = speed
            pos_out[k, at, :] = here + TIME_STEP * speed
        return carry

    lax.fori_loop(0, blocks // 8, update, 0)
    if last:
        spots = [jnp.broadcast_to(slots[k : k + 1], (8, blocks)) for k in range(2)]
        rows = []
        for comp in range(2):
            drag = rad[...] * rad[...] * vel_out[comp]
            total = DRAG_ICE * jnp.sum(drag.T, axis=0, keepdims=True)
            total = jnp.broadcast_to(total, (8, blocks))
            for spot in spots:
                moved = lane_take(total, jnp.maximum(spot, 0))
                rows.append(jnp.where(spot >= 0, moved, 0.0)[0:1])
        rows.append(jnp.zeros((blocks - 4, blocks), jnp.float32))
        sent[:, 0, :] = jnp.concatenate(rows, axis=0).T
    else:
        for side in range(2):
            for comp in range(2):
                at = pl.ds(side * (cols_dev - 1), rows_dev, stride=cols_dev)
                edges[side, comp] = pos_out[comp, at, :]


def contact_step(which, n_gy, pos, vel, rad, bonds, mask, marks, held, halo, halo_rad, *extra):
    blocks, discs = rad.shape
    rows_dev = blocks // 16
    square = shape(2, blocks, discs)
    tail = shape(blocks, 1, discs) if which == SUB - 1 else shape(2, 2, rows_dev, discs)
    outs = (square, square, tail)
    if which == 0:
        outs += (shape(*rad.shape),)
    if which == 1:
        outs += (shape(*extra[0].shape),)
    args = (pos, vel, rad, bonds, mask, marks, held, halo, halo_rad) + extra
    return pl.pallas_call(
        functools.partial(contact_kernel, which, n_gy),
        out_shape=outs,
        in_specs=[VMEM] * len(args),
        out_specs=(VMEM,) * len(outs),
        scratch_shapes=[
            pltpu.VMEM((3, rows_dev + 2, 24, discs), jnp.float32),
            pltpu.VMEM((4, blocks, discs), jnp.float32),
            pltpu.VMEM((MARKS * blocks, discs), jnp.float32),
            pltpu.VMEM((2, 8 * blocks + 8, discs), jnp.float32),
            pltpu.VMEM((8, discs), jnp.int32),
            pltpu.SMEM((8, discs), jnp.int32),
            pltpu.SemaphoreType.DMA,
        ],
        compiler_params=grant(16),
        cost_estimate=BUSY,
        name=("contact_first", "contact", "contact_last")[which],
    )(*args)


def prep_kernel(pos_in, rad_in, pos, rad, edges, sems):
    copies = [
        pltpu.make_async_copy(pos_in, pos, sems.at[0]),
        pltpu.make_async_copy(rad_in, rad, sems.at[1]),
    ]
    for copy in copies:
        copy.start()
    for copy in copies:
        copy.wait()
    for comp in range(3):
        source = pos.at[comp] if comp < 2 else rad
        for side in range(2):
            edges[side, comp] = source[pl.ds(side * 15, 8, stride=16), :]


def prep(pos, rad):
    return pl.pallas_call(
        prep_kernel,
        out_shape=(shape(*pos.shape), shape(*rad.shape), shape(2, 3, 8, 128)),
        in_specs=[HBM] * 2,
        out_specs=(VMEM,) * 3,
        scratch_shapes=[pltpu.SemaphoreType.DMA((2,))],
        compiler_params=grant(4),
        name="prep",
    )(pos, rad)


def pack_kernel(ocean, after, columns, bottom, top):
    rows = ocean.shape[2]
    lane = lax.broadcasted_iota(jnp.int32, (8, 128), 1)
    packed = [jnp.zeros((8, 128), jnp.float32)] * 2
    for field in range(4):
        for layer in range(CHUNK):
            for v in range(rows // 8):
                g = (field * CHUNK + layer) * (rows // 8) + v
                place = g % 64
                turned = pltpu.roll(ocean[field, layer, pl.ds(8 * v, 8), :], 2 * place + 1, 1)
                packed[g // 64] = jnp.where(lane // 2 == place, turned, packed[g // 64])
    columns[0] = jnp.concatenate(packed, axis=0)
    bottom[...] = ocean[:, :, 0, :]
    top[...] = ocean[:, :, rows - 1, :]


def pack(ocean, after):
    fields, layers, rows, lanes = ocean.shape
    steps = layers // CHUNK
    row = pl.BlockSpec((fields, CHUNK, lanes), lambda i: (0, i, 0))
    return pl.pallas_call(
        pack_kernel,
        grid=(steps,),
        out_shape=(
            shape(steps, 16, lanes),
            shape(fields, layers, lanes),
            shape(fields, layers, lanes),
        ),
        in_specs=[pl.BlockSpec((fields, CHUNK, rows, lanes), lambda i: (0, i, 0, 0)), ANY],
        out_specs=(pl.BlockSpec((1, 16, lanes), lambda i: (i, 0, 0)), row, row),
        compiler_params=grant(8),
        name="pack",
    )(ocean, after)


def exchange_kernel(which, n_gx, n_gy, *refs):
    if which == 0:
        pos, rad, edges, halo, held, marks, halo_rad, *scratch = refs
        send_sem, recv_sem, rad_send, rad_recv = scratch
    elif which == 1:
        pos, rad, edges, top, bottom, sides, perm, halo, held, marks, lon, lat, rows, perms, *scratch = refs
        send_sem, recv_sem, sea_send, sea_recv, *scratch = scratch
        far_send, far_recv, perm_send, perm_recv, own = scratch
    else:
        pos, rad, edges, turned, halo, held, marks, mirror, *scratch = refs
        send_sem, recv_sem, far_send, far_recv, own = scratch
    gx, gy = lax.axis_index("gx"), lax.axis_index("gy")
    is_top = gy == n_gy - 1

    def at(dx, dy):
        return lax.rem(gx + dx + n_gx, n_gx), lax.rem(gy + dy + n_gy, n_gy)

    barrier = pltpu.get_barrier_semaphore()
    for dy, dx in NEIGHBOURS:
        pl.semaphore_signal(barrier, inc=1, device_id=at(dx, dy), device_id_type=MESH)
    if which > 0:

        @pl.when(is_top)
        def _():
            for d in range(1, n_gx):
                pl.semaphore_signal(barrier, inc=1, device_id=at(d, 0), device_id_type=MESH)

    blocks = rad.shape[0]
    write_marks([pos[0], pos[1], rad[...]], marks)
    own_forces(0, EARLY, marks, held)
    if which > 0:

        @pl.when(is_top)
        def _():
            pl.semaphore_wait(barrier, len(NEIGHBOURS) + n_gx - 1)

        @pl.when(jnp.logical_not(is_top))
        def _():
            pl.semaphore_wait(barrier, len(NEIGHBOURS))

    else:
        pl.semaphore_wait(barrier, len(NEIGHBOURS))

    def send(source, target, sems, index, device):
        return pltpu.make_async_remote_copy(
            src_ref=source,
            dst_ref=target,
            send_sem=sems[0].at[index],
            recv_sem=sems[1].at[index],
            device_id=device,
            device_id_type=MESH,
        )

    def halo_copies(body, part, target, sems):
        copies = []
        for k, (sy, sx) in enumerate(NEIGHBOURS):
            first = 0 if sy == 1 else blocks - 16
            first = first + 8 if sx == -1 else first
            size = 16 if sx == 0 else 8
            source = part(0 if sx == 1 else 1) if sy == 0 else body(pl.ds(first, size))
            copies.append(send(source, target(k, pl.ds(0, size)), sems, k, at(-sx, -sy)))
        return copies

    copies = halo_copies(
        lambda rows: pos.at[:, rows, :],
        lambda side: edges.at[side, pl.ds(0, 2)],
        lambda k, rows: halo.at[k, :, rows, :],
        (send_sem, recv_sem),
    )
    if which == 0:
        copies += halo_copies(
            lambda rows: rad.at[rows, :],
            lambda side: edges.at[side, 2],
            lambda k, rows: halo_rad.at[k, rows, :],
            (rad_send, rad_recv),
        )
    for copy in copies:
        copy.start()
    if which == 1:
        sea = (sea_send, sea_recv)
        later = [
            send(sides, lon.at[0], sea, 0, at(1, 0)),
            send(sides, lon.at[1], sea, 1, at(-1, 0)),
            send(top, lat.at[0], sea, 2, at(0, 1)),
            send(bottom, lat.at[1], sea, 3, at(0, -1)),
        ]
        copies += later

    if which == 1:
        first = pl.multiple_of(jnp.minimum(gx, TURNERS - 1) * TURN_ROWS, TURN_ROWS)
        kept = pltpu.make_async_copy(perm, perms.at[gx], own.at[0])
        mine = pltpu.make_async_copy(top.at[pl.ds(first, TURN_ROWS), :], rows.at[gx], own.at[1])
        notes, far = [], []
        for d in range(1, n_gx):
            peer = lax.rem(gx + d, n_gx)
            start = pl.multiple_of(jnp.minimum(peer, TURNERS - 1) * TURN_ROWS, TURN_ROWS)
            notes.append(send(perm, perms.at[gx], (perm_send, perm_recv), d - 1, at(d, 0)))
            source = top.at[pl.ds(start, TURN_ROWS), :]
            far.append(send(source, rows.at[gx], (far_send, far_recv), d - 1, at(d, 0)))

        @pl.when(is_top)
        def _():
            kept.start()
            for d in range(1, n_gx):
                notes[d - 1].start()

                @pl.when(lax.rem(gx + d, n_gx) < TURNERS)
                def _(copy=far[d - 1]):
                    copy.start()

            @pl.when(gx < TURNERS)
            def _():
                mine.start()

        for copy in later:
            copy.start()

    if which == 2:
        me = jnp.minimum(gx, TURNERS - 1)
        mine = pltpu.make_async_copy(turned.at[gx], mirror.at[me], own)
        far = []
        for d in range(1, n_gx):
            source = turned.at[lax.rem(gx + d, n_gx)]
            far.append(send(source, mirror.at[me], (far_send, far_recv), d - 1, at(d, 0)))

        @pl.when(is_top & (gx < TURNERS))
        def _():
            mine.start()
            for copy in far:
                copy.start()

    own_forces(EARLY, blocks - EARLY, marks, held)
    for copy in copies:
        copy.wait()
    if which == 1:

        @pl.when(is_top)
        def _():
            kept.wait()
            for d in range(1, n_gx):
                notes[d - 1].wait()

                @pl.when(lax.rem(gx + d, n_gx) < TURNERS)
                def _(copy=far[d - 1]):
                    copy.wait_send()

            @pl.when(gx < TURNERS)
            def _():
                mine.wait()
                for copy in far:
                    copy.wait_recv()

    if which == 2:

        @pl.when(is_top & (gx < TURNERS))
        def _():
            mine.wait()
            for copy in far:
                copy.wait_send()

        @pl.when(is_top)
        def _():
            for d in range(1, n_gx):

                @pl.when(lax.rem(gx - d + n_gx, n_gx) < TURNERS)
                def _(copy=far[d - 1]):
                    copy.wait_recv()


def exchange(which, n_gx, n_gy, pos, rad, edges, *args):
    lanes = rad.shape[1]
    blocks = rad.shape[0]
    outs = [shape(8, 2, 16, lanes), shape(2, 8 * blocks, lanes)]
    outs += [shape(MARKS * blocks, lanes)]
    dma = pltpu.SemaphoreType.DMA
    scratch = [dma((8,)), dma((8,))]
    far = [dma((n_gx - 1,)), dma((n_gx - 1,))]
    if which == 0:
        outs += [shape(8, 16, lanes)]
        scratch += [dma((8,)), dma((8,))]
    if which == 1:
        top, bottom, sides, perm = args
        outs += [shape(2, *sides.shape), shape(2, *top.shape)]
        outs += [shape(n_gx, TURN_ROWS, lanes), jax.ShapeDtypeStruct((n_gx, 1, lanes), jnp.int32)]
        scratch += [dma((4,)), dma((4,))] + far + far + [dma((2,))]
    if which == 2:
        outs += [shape(TURNERS, TURN_ROWS, lanes)]
        scratch += far + [dma]
    return pl.pallas_call(
        functools.partial(exchange_kernel, which, n_gx, n_gy),
        out_shape=tuple(outs),
        in_specs=[VMEM] * (3 + len(args)),
        out_specs=(VMEM,) * len(outs),
        scratch_shapes=scratch,
        compiler_params=grant(8, collective_id=which, has_side_effects=True),
        cost_estimate=BUSY,
        name=("exchange_first", "exchange_second", "exchange_third")[which],
    )(pos, rad, edges, *args)


def stencil(step, n_gy, ocean, mix, lon, lat, mirror, out):
    layers, rows, lanes = ocean.shape[1:]
    gy = lax.axis_index("gy")
    first = step * CHUNK
    lane = lax.broadcasted_iota(jnp.int32, (rows, lanes), 1)
    sub = lax.broadcasted_iota(jnp.int32, (rows, lanes), 0)
    lane8 = lax.broadcasted_iota(jnp.int32, (8, lanes), 1)
    bands = []
    for half in range(2):
        at = pl.ds(8 * half, 8)
        west = pltpu.roll(lon[0, step, at, :], 1, 1)
        east = pltpu.roll(lon[1, step, at, :], lanes - 1, 1)
        bands.append(jnp.where(lane8 % 2 == 1, west, east))
    spin = 2.0 * ((gy * rows + sub).astype(jnp.float32) + 0.5) / (rows * n_gy) - 1.0
    spin = SPIN_RATE * spin
    is_top, is_low = gy == n_gy - 1, gy == 0
    level = pl.ds(pl.multiple_of(first, CHUNK), CHUNK)
    for field in range(4):
        folded = -mirror[field, level, :] if field < 2 else mirror[field, level, :]
        upper = jnp.where(is_top, folded, lat[1, field, level, :])
        lower = jnp.where(is_low, 0.0, lat[0, field, level, :])
        for layer in range(CHUNK):
            at = first + layer
            here = ocean[field, at]
            up = ocean[field, jnp.maximum(at - 1, 0)]
            down = ocean[field, jnp.minimum(at + 1, layers - 1)]
            sides = []
            for v in range(rows // 8):
                g = (field * CHUNK + layer) * (rows // 8) + v
                sides.append(pltpu.roll(bands[g // 64], lanes - 1 - 2 * (g % 64), 1))
            sides = jnp.concatenate(sides, axis=0)
            west = jnp.where(lane == 0, sides, pltpu.roll(here, 1, 1))
            east = jnp.where(lane == lanes - 1, sides, pltpu.roll(here, lanes - 1, 1))
            south = jnp.where(sub == 0, lower[layer : layer + 1], pltpu.roll(here, 1, 0))
            north = jnp.where(sub == rows - 1, upper[layer : layer + 1], pltpu.roll(here, rows - 1, 0))
            laplace = east + west + north + south - 4.0 * here
            value = here + mix[at] * laplace + VERT_MIX * (up + down - 2.0 * here)
            if field == 0:
                value = value + spin * ocean[1, at]
            if field == 1:
                value = value - spin * ocean[0, at]
            out[field, at] = value


def couple_kernel(n_gx, n_gy, sent, cell, ocean, mix, lon, lat, mirror, *refs):
    surface, current, plain, here, there, back, home, *sems = refs
    gx, gy = lax.axis_index("gx"), lax.axis_index("gy")
    tiles = n_gx * n_gy
    rows, lanes = ocean.shape[2:]
    steps = ocean.shape[1] // CHUNK

    def work(first, last):
        def one(step, carry):
            stencil(step, n_gy, ocean, mix, lon, lat, mirror, plain)
            return carry

        lax.fori_loop(first, last, one, 0)

    barrier = pltpu.get_barrier_semaphore()
    for d in range(1, n_gx):
        peer = (lax.rem(gx + d, n_gx), gy)
        pl.semaphore_signal(barrier, inc=1, device_id=peer, device_id_type=MESH)
    for d in range(1, n_gy):
        peer = (gx, lax.rem(gy + d, n_gy))
        pl.semaphore_signal(barrier, inc=1, device_id=peer, device_id_type=MESH)
    pl.semaphore_wait(barrier, n_gx + n_gy - 2)

    def swap(source, middle, target, sems, marks):
        send_x, recv_x, send_y, recv_y, local = sems
        own = pltpu.make_async_copy(source.at[gx], middle.at[gx], local)
        own.start()
        copies = []
        for d in range(1, n_gx):
            peer = lax.rem(gx + d, n_gx)
            copies.append(
                pltpu.make_async_remote_copy(
                    src_ref=source.at[peer],
                    dst_ref=middle.at[gx],
                    send_sem=send_x.at[d - 1],
                    recv_sem=recv_x.at[d - 1],
                    device_id=(peer, gy),
                    device_id_type=MESH,
                )
            )
        for copy in copies:
            copy.start()
        work(marks[0], marks[1])
        own.wait()
        for copy in copies:
            copy.wait()
        own = pltpu.make_async_copy(middle.at[:, gy], target.at[:, gy], local)
        own.start()
        copies = []
        for d in range(1, n_gy):
            peer = lax.rem(gy + d, n_gy)
            copies.append(
                pltpu.make_async_remote_copy(
                    src_ref=middle.at[:, peer],
                    dst_ref=target.at[:, gy],
                    send_sem=send_y.at[d - 1],
                    recv_sem=recv_y.at[d - 1],
                    device_id=(gx, peer),
                    device_id_type=MESH,
                )
            )
        for copy in copies:
            copy.start()
        work(marks[1], marks[2])
        own.wait()
        for copy in copies:
            copy.wait()

    swap(sent, here, there, sems[0:5], (0, steps // 3, steps // 2))
    cells = jnp.concatenate([cell[0:1], cell[1:2]], axis=1)
    cell_row, cell_col = cells // lanes, cells % lanes
    pick = (lax.broadcasted_iota(jnp.int32, (lanes, 2 * tiles), 0) == cell_col).astype(jnp.bfloat16)
    in_row = lax.broadcasted_iota(jnp.int32, (rows, 2 * tiles), 0) == cell_row
    arrived = there[...].reshape(tiles, lanes).T
    spread = []
    for comp in range(2):
        values = jnp.concatenate([arrived[2 * comp : 2 * comp + 1], arrived[2 * comp + 1 : 2 * comp + 2]], axis=1)
        spread.append(jnp.where(in_row, values, 0.0))
    forcing = lax.dot_general(
        split(jnp.concatenate(spread, axis=0)),
        pick,
        (((1,), (1,)), ((), ())),
        preferred_element_type=jnp.float32,
    )
    skin = jnp.concatenate([plain[0, 0], plain[1, 0]], axis=0)
    level = skin + joined(forcing)
    surface[...] = level.reshape(2, rows, lanes)
    found = joined(jnp.dot(split(level), pick, preferred_element_type=jnp.float32))
    replies = []
    for comp in range(2):
        values = jnp.where(in_row, found[comp * rows : (comp + 1) * rows], 0.0)
        values = jnp.sum(values, axis=0, keepdims=True)
        replies += [values[:, :tiles], values[:, tiles:]]
    replies.append(jnp.zeros((lanes - 4, tiles), jnp.float32))
    back[...] = jnp.concatenate(replies, axis=0).T.reshape(back.shape)
    swap(back, home, current, sems[5:10], (steps // 2, steps - 1, steps))


def couple(n_gx, n_gy, sent, cell, ocean, *sea):
    tiles = n_gx * n_gy
    rows, lanes = ocean.shape[2:]
    box = (n_gx, n_gy, 1, lanes)
    dma = pltpu.SemaphoreType.DMA
    sems = [dma((n_gx - 1,)), dma((n_gx - 1,)), dma((n_gy - 1,)), dma((n_gy - 1,)), dma]
    return pl.pallas_call(
        functools.partial(couple_kernel, n_gx, n_gy),
        out_shape=(shape(2, rows, lanes), shape(*box), shape(*ocean.shape)),
        in_specs=[VMEM] * (3 + len(sea)),
        out_specs=(VMEM,) * 3,
        scratch_shapes=[pltpu.VMEM(box, jnp.float32)] * 4 + sems + sems,
        compiler_params=grant(16, collective_id=SUB, has_side_effects=True),
        name="couple",
    )(sent.reshape(box), cell, ocean, *sea)


def finish_kernel(plain, surface, current, slots, vel, vel_out, ocean_out, sems):
    layers = plain.shape[1]
    copies = [
        pltpu.make_async_copy(surface, ocean_out.at[pl.ds(0, 2), 0], sems.at[0]),
        pltpu.make_async_copy(plain.at[pl.ds(2, 2)], ocean_out.at[pl.ds(2, 2)], sems.at[1]),
    ]
    for field in range(2):
        deep = pl.ds(1, layers - 1)
        copies.append(
            pltpu.make_async_copy(plain.at[field, deep], ocean_out.at[field, deep], sems.at[2 + field])
        )
    for copy in copies:
        copy.start()
    blocks, discs = vel.shape[1], vel.shape[2]
    tiles = current.shape[0]
    got = current[...].reshape(tiles, discs).T
    spots = jnp.concatenate([slots[0:1], slots[1:2]], axis=1)
    place = lax.broadcasted_iota(jnp.int32, (blocks, 2 * tiles), 0) == spots
    for comp in range(2):
        values = jnp.concatenate([got[2 * comp : 2 * comp + 1], got[2 * comp + 1 : 2 * comp + 2]], axis=1)
        values = jnp.sum(jnp.where(place, values, 0.0), axis=1, keepdims=True)
        speed = vel[comp]
        vel_out[comp] = speed + DRAG_BACK * (values - speed)
    for copy in copies:
        copy.wait()


def finish(plain, surface, current, slots, vel):
    tiles = current.shape[0] * current.shape[1]
    return pl.pallas_call(
        finish_kernel,
        out_shape=(shape(*vel.shape), shape(*plain.shape)),
        in_specs=[VMEM] * 5,
        out_specs=(VMEM, ANY),
        scratch_shapes=[pltpu.SemaphoreType.DMA((4,))],
        compiler_params=grant(4),
        name="finish",
    )(plain, surface, current.reshape(tiles, 1, current.shape[3]), slots, vel)


def body(
    disc_pos,
    disc_vel,
    radius,
    bond_list,
    contact_mask,
    remap_block,
    ocean_state,
    mix_coef,
    remap_cell,
    fold_perm,
):
    n_gx, n_gy = lax.axis_size("gx"), lax.axis_size("gy")
    rows_dev, cols_dev, discs = radius.shape
    blocks = rows_dev * cols_dev
    slots = remap_block[0].T
    cell = remap_cell[0].T
    perm = fold_perm.reshape(1, discs)
    position = disc_pos.reshape(2, blocks, discs)
    velocity = disc_vel.reshape(2, blocks, discs)
    rad = radius.reshape(blocks, discs)
    bonds = bond_list.reshape(BONDS, blocks, discs)
    sea_shape = (4, mix_coef.shape[0], discs)
    flat = (4 * mix_coef.shape[0], discs)
    position, rad, edges = prep(position, rad)
    halo, held, marks, halo_rad = exchange(0, n_gx, n_gy, position, rad, edges)
    position, velocity, edges, mask = contact_step(
        0, n_gy, position, velocity, rad, bonds, contact_mask, marks, held, halo, halo_rad
    )
    sides, bottom, top = pack(ocean_state, edges)
    halo, held, marks, lon, lat, rows, perms = exchange(
        1, n_gx, n_gy, position, rad, edges, top.reshape(flat), bottom.reshape(flat), sides, perm
    )
    position, velocity, edges, turned = contact_step(
        1, n_gy, position, velocity, rad, bonds, mask, marks, held, halo, halo_rad, rows, perms
    )
    halo, held, marks, mirror = exchange(2, n_gx, n_gy, position, rad, edges, turned)
    position, velocity, sent = contact_step(
        2, n_gy, position, velocity, rad, bonds, mask, marks, held, halo, halo_rad, slots
    )
    sea = (mix_coef, lon, lat.reshape(2, *sea_shape), mirror.reshape(sea_shape))
    surface, current, plain = couple(n_gx, n_gy, sent, cell, ocean_state, *sea)
    vel_next, ocean_next = finish(plain, surface, current, slots, velocity)
    return (position.reshape(disc_pos.shape), vel_next.reshape(disc_vel.shape), ocean_next)


def solution(mesh):
    in_specs = (
        P(None, "gy", "gx", None),
        P(None, "gy", "gx", None),
        P("gy", "gx", None),
        P(None, "gy", "gx", None),
        P(None, "gy", "gx"),
        P(("gx", "gy"), None, None),
        P(None, None, "gy", "gx"),
        P(None, "gy", "gx"),
        P(("gx", "gy"), None, None),
        P("gx"),
    )
    out_specs = (P(None, "gy", "gx", None), P(None, "gy", "gx", None), P(None, None, "gy", "gx"))
    return jax.shard_map(body, mesh=mesh, in_specs=in_specs, out_specs=out_specs, check_vma=False)
```

```python
import functools

import jax
import jax.numpy as jnp
from jax import lax
from jax.experimental import pallas as pl
from jax.experimental.pallas import tpu as pltpu
from jax.sharding import PartitionSpec as P

BONDS = 4
SUB = 3
SOFTEN = 0.0001
STIFFNESS = 2.0
BOND_STIFF = 0.1
TIME_STEP = 0.05
DRAG_ICE = 15.0
DRAG_BACK = 0.5
VERT_MIX = 0.1
SPIN_RATE = 0.3
NEIGHBOURS = ((-1, -1), (-1, 0), (-1, 1), (0, -1), (0, 1), (1, -1), (1, 0), (1, 1))
OWN_STEP = 16
NEAR_STEP = 32
REST_STEP = 16
HALF = 64
MARKS = 16
CHUNK = 8
TURNERS = 12
EARLY = 32
TURN_ROWS = 16
MESH = pl.DeviceIdType.MESH
BUSY = pl.CostEstimate(flops=1 << 32, bytes_accessed=1 << 24, transcendentals=1 << 22)
VMEM = pl.BlockSpec(memory_space=pltpu.VMEM)
ANY = pl.BlockSpec(memory_space=pl.ANY)
HBM = pl.BlockSpec(memory_space=pltpu.HBM)


def grant(mib, **more):
    return pltpu.CompilerParams(vmem_limit_bytes=mib << 20, **more)


def shape(*dims):
    return jax.ShapeDtypeStruct(dims, jnp.float32)


def split(value):
    high = value.astype(jnp.bfloat16)
    rest = value - high.astype(jnp.float32)
    middle = rest.astype(jnp.bfloat16)
    low = (rest - middle.astype(jnp.float32)).astype(jnp.bfloat16)
    return jnp.concatenate([high, middle, low], axis=0)


def joined(value):
    rows = value.shape[0] // 3
    return value[:rows] + value[rows : 2 * rows] + value[2 * rows :]


def lane_take(rows, index):
    return lax.gather(
        rows,
        index[..., None],
        lax.GatherDimensionNumbers(
            offset_dims=(),
            collapsed_slice_dims=(1,),
            start_index_map=(1,),
            operand_batching_dims=(0,),
            start_indices_batching_dims=(0,),
        ),
        slice_sizes=(1, 1),
        mode=lax.GatherScatterMode.PROMISE_IN_BOUNDS,
    )


def pieces(value):
    high = value.astype(jnp.bfloat16).astype(jnp.float32)
    middle = (value - high).astype(jnp.bfloat16).astype(jnp.float32)
    return high, middle, value - high - middle


def write_marks(parts, marks):
    for comp, part in enumerate(parts):
        for i, piece in enumerate(pieces(part)):
            marks[pl.ds(3 * comp + i, part.shape[0], stride=MARKS), :] = piece


def other_side(marks):
    row = lax.broadcasted_iota(jnp.int32, marks.shape, 0)
    marks = jnp.where(row < 9, marks, jnp.where(row < 12, 1.0, 0.0))
    return marks.T.astype(jnp.bfloat16)


def own_side(marks):
    row = lax.broadcasted_iota(jnp.int32, marks.shape, 0)
    sides = []
    for comp in range(3):
        moved = pltpu.roll(marks, 9 - 3 * comp, 0)
        moved = moved if comp == 2 else -moved
        fixed = jnp.where(row // 3 == comp, 1.0, 0.0)
        sides.append(jnp.where((row >= 9) & (row < 12), moved, fixed))
    return jnp.concatenate(sides, axis=1).astype(jnp.bfloat16)


def pair_sums(other, own):
    pairs = jnp.dot(other, own, preferred_element_type=jnp.float32)
    lanes = pairs.shape[1] // 3
    acc_x = acc_y = jnp.zeros((8, lanes), jnp.float32)
    for c in range(pairs.shape[0] // 8):
        rows = pairs[8 * c : 8 * c + 8]
        sep_x, sep_y, reach = rows[:, :lanes], rows[:, lanes : 2 * lanes], rows[:, 2 * lanes :]
        inverse = lax.rsqrt(sep_x * sep_x + sep_y * sep_y + SOFTEN)
        push = jnp.maximum(reach * inverse - 1.0, 0.0)
        acc_x = acc_x + push * sep_x
        acc_y = acc_y + push * sep_y
    return acc_x, acc_y


def marks_of(marks, b):
    return marks[pl.ds(pl.multiple_of(b * MARKS, MARKS), MARKS), :]


def turn(rows, perms, turned):
    lanes = rows.shape[2]

    def one(step, carry):
        for u in range(4):
            h = step * 4 + u
            wanted = jnp.broadcast_to(perms[h], (8, lanes))
            owner, column = wanted // lanes, wanted % lanes
            for half in range(TURN_ROWS // 8):
                at = pl.ds(8 * half, 8)
                got = jnp.zeros((8, lanes), jnp.float32)
                for source in range(rows.shape[0]):
                    got = jnp.where(owner == source, lane_take(rows[source, at, :], column), got)
                turned[h, at, :] = got
        return carry

    lax.fori_loop(0, perms.shape[0] // 4, one, 0)


def own_forces(first, count, marks, force):
    def some(t, carry):
        for u in range(OWN_STEP):
            b = first + t * OWN_STEP + u
            own = marks_of(marks, b)
            acc = pair_sums(other_side(own), own_side(own))
            at = pl.ds(pl.multiple_of(b * 8, 8), 8)
            for k in range(2):
                force[k, at, :] = acc[k]
        return carry

    lax.fori_loop(0, count // OWN_STEP, some, 0)


def write_mask(n_gy, allowed, mask):
    lane = lax.broadcasted_iota(jnp.int32, (8, 128), 1)
    _, rows_dev, cols_dev = allowed.shape
    spread = jnp.zeros((8, 128), jnp.float32)
    for y in range(rows_dev):
        part = allowed[:, y, :].astype(jnp.float32)
        part = jnp.concatenate([part, jnp.zeros((8, 128 - cols_dev), jnp.float32)], axis=1)
        spread = spread + (pltpu.roll(part, y * cols_dev, 1) if y else part)
    which = lax.broadcasted_iota(jnp.int32, (8, 128), 0)
    shift_y = jnp.where(which < 3, -1, jnp.where(which < 5, 0, 1))
    row = lax.axis_index("gy") * rows_dev + lane // cols_dev + shift_y
    spread = jnp.where((row >= 0) & (row < n_gy * rows_dev), spread, 0.0)
    mask[...] = jnp.concatenate([spread, jnp.zeros((120, 128), jnp.float32)], axis=0).T


def contact_kernel(which, n_gy, pos, vel, rad, bonds, mask, marks, held, halo, halo_rad, *refs):
    last = which == SUB - 1
    if last:
        slots, pos_out, vel_out, sent, *scratch = refs
    elif which == 1:
        rows, perms, pos_out, vel_out, edges, turned, *scratch = refs

        @pl.when(lax.axis_index("gy") == n_gy - 1)
        def _():
            turn(rows, perms, turned)

    else:
        allowed, mask = mask, refs[3]
        pos_out, vel_out, edges, _, *scratch = refs
        write_mask(n_gy, allowed, mask)
    wide, found, seen, force, tally, work, sem = scratch
    rows_dev, cols_dev = wide.shape[1] - 2, pos.shape[1] // (wide.shape[1] - 2)
    blocks, discs = rad.shape
    for comp in range(3):
        source = pos.at[comp] if comp < 2 else rad

        def frame(side, first, size):
            if comp < 2:
                return halo[side, comp, pl.ds(first, size), :]
            return halo_rad[side, pl.ds(first, size), :]

        for y in range(rows_dev):
            wide[comp, y + 1, pl.ds(1, cols_dev), :] = source[pl.ds(y * cols_dev, cols_dev), :]
            wide[comp, y + 1, pl.ds(0, 1), :] = frame(3, y, 1)
            wide[comp, y + 1, pl.ds(cols_dev + 1, 1), :] = frame(4, y, 1)
        for side, y in ((0, 0), (5, rows_dev + 1)):
            wide[comp, y, pl.ds(0, 1), :] = frame(side, 7, 1)
            wide[comp, y, pl.ds(1, cols_dev), :] = frame(side + 1, 0, cols_dev)
            wide[comp, y, pl.ds(cols_dev + 1, 1), :] = frame(side + 2, 0, 1)
    lane = lax.broadcasted_iota(jnp.int32, (8, discs), 1)
    lane_f = lane.astype(jnp.float32)
    tri_row = lax.broadcasted_iota(jnp.int32, (discs, 2 * discs), 0)
    tri_col = lax.broadcasted_iota(jnp.int32, (discs, 2 * discs), 1)
    triangle = (tri_row <= tri_col).astype(jnp.bfloat16)
    low_row = lax.broadcasted_iota(jnp.int32, (blocks, blocks), 0)
    low_col = lax.broadcasted_iota(jnp.int32, (blocks, blocks), 1)
    lower = (low_col <= low_row).astype(jnp.bfloat16)

    def collect_row(y, start):
        units, totals = [], []
        for half in range(cols_dev // 8):
            x0 = half * 8
            at = pl.ds(pl.multiple_of(y * cols_dev + x0, 8), 8)
            own = [pos[0, at, :], pos[1, at, :], rad[at, :]]
            reach = jnp.max(own[2], axis=1, keepdims=True)
            low = [jnp.min(own[c], axis=1, keepdims=True) - reach for c in range(2)]
            high = [jnp.max(own[c], axis=1, keepdims=True) + reach for c in range(2)]
            weights = mask[at, :]
            flags = []
            places = []
            for k, (sy, sx) in enumerate(NEIGHBOURS):
                place = (y + 1 + sy, pl.ds(x0 + 1 + sx, 8), slice(None))
                nx, ny, nr = (wide[(c,) + place] for c in range(3))
                close = (nx - nr < high[0] - float(sx)) & (nx + nr > low[0] - float(sx))
                close = close & (ny - nr < high[1] - float(sy)) & (ny + nr > low[1] - float(sy))
                close = close & (weights[:, k : k + 1] > 0.5)
                flags.append(close.astype(jnp.float32))
                places.append(place)
            ranks = jnp.dot(
                jnp.concatenate(flags, axis=0).astype(jnp.bfloat16),
                triangle,
                preferred_element_type=jnp.float32,
            )
            base = jnp.zeros((8, discs), jnp.float32) - start
            for k in range(8):
                rank = ranks[8 * k : 8 * k + 8, :discs]
                total = ranks[8 * k : 8 * k + 8, discs:]
                want = lane_f - base
                source = jnp.zeros((8, discs), jnp.int32)
                units.append((half, k, source, places[k], rank, total, want))
                base = base + total
            totals.append((at, base))
        sources = [u[2] for u in units]
        step = discs // 2
        while step >= 1:
            probes = [lane_take(u[4], i + (step - 1)) for u, i in zip(units, sources)]
            sources = [
                jnp.where(probe <= u[6], i + step, i)
                for probe, u, i in zip(probes, units, sources)
            ]
            step //= 2
        for half, (at, base) in enumerate(totals):
            mine = [(u, i) for u, i in zip(units, sources) if u[0] == half]
            for comp in range(3):
                got = jnp.full((8, discs), -1.0 if comp == 2 else 0.0, jnp.float32)
                for (_, k, _, place, _, total, want), source in mine:
                    valid = (want >= 0.0) & (want < total)
                    value = wide[(comp,) + place]
                    if comp < 2 and NEIGHBOURS[k][1 - comp] != 0:
                        value = value + float(NEIGHBOURS[k][1 - comp])
                    got = jnp.where(valid, lane_take(value, source), got)
                found[comp, at, :] = got
            found[3, at, :] = base

    def collect():
        def one_row(y, carry):
            collect_row(y, 0.0)
            return carry

        lax.fori_loop(0, rows_dev, one_row, 0)
        write_marks([found[k] for k in range(3)], seen)
        left = found[3]
        spot = lax.broadcasted_iota(jnp.int32, (1, discs), 1).astype(jnp.float32)
        for row, bound in ((0, HALF), (3, discs)):
            size = jnp.where(left > float(bound), 1.0, 0.0)
            ends = jnp.dot(lower, size.astype(jnp.bfloat16), preferred_element_type=jnp.float32)
            block = jnp.sum(jnp.where(ends <= spot, 1.0, 0.0), axis=0, keepdims=True)
            tally[row : row + 1] = block.astype(jnp.int32)
            tally[row + 1 : row + 2] = ends[blocks - 1 :].astype(jnp.int32)
        deepest = jnp.max(left, axis=0, keepdims=True)
        tally[2:3] = jnp.ceil(deepest * (1.0 / discs)).astype(jnp.int32)
        copy = pltpu.make_async_copy(tally, work, sem)
        copy.start()
        copy.wait()

    def meet(b, part, fresh):
        at = pl.ds(pl.multiple_of(b * 8, 8), 8)
        b = jnp.minimum(b, blocks - 1)
        other = other_side(marks_of(seen, b))[part * HALF : (part + 1) * HALF]
        acc = pair_sums(other, own_side(marks_of(marks, b)))
        for k in range(2):
            if fresh:
                force[k, at, :] = acc[k]
            else:
                force[k, at, :] += acc[k]

    def some(t, carry):
        for u in range(NEAR_STEP):
            meet(t * NEAR_STEP + u, 0, True)
        return carry

    def rest(t, carry):
        for u in range(REST_STEP):
            meet(work[0, t * REST_STEP + u], 1, False)
        return carry

    def crowded(i, carry):
        b = work[3, i]
        y = b // cols_dev
        at = pl.ds(pl.multiple_of(y * cols_dev, cols_dev), cols_dev)
        first = pl.multiple_of(y * (cols_dev * MARKS), cols_dev * MARKS)
        near = seen.at[pl.ds(first, cols_dev * MARKS), :]

        def deeper(p, carry):
            collect_row(y, p.astype(jnp.float32) * discs)
            write_marks([found[k, at, :] for k in range(3)], near)
            for part in range(2):
                meet(b, part, False)
            return carry

        return lax.fori_loop(1, work[2, 0], deeper, carry)

    collect()
    lax.fori_loop(0, blocks // NEAR_STEP, some, 0)
    lax.fori_loop(0, (work[1, 0] + (REST_STEP - 1)) // REST_STEP, rest, 0)
    lax.fori_loop(0, work[4, 0], crowded, 0)

    def update(g, carry):
        at = pl.ds(pl.multiple_of(g * 8, 8), 8)
        scale = 0.06 / rad[at, :]
        scale = scale * scale
        for k in range(2):
            here = pos[k, at, :]
            bonded = lane_take(here, bonds[0, at, :])
            for p in range(1, BONDS):
                bonded = bonded + lane_take(here, bonds[p, at, :])
            push = jnp.zeros((8, discs), jnp.float32)
            for r in range(8):
                rows = pl.ds(g * 64 + r, 8, stride=8)
                push = push + (held[k, rows, :] + force[k, rows, :])
            total = BOND_STIFF * (bonded - BONDS * here) - STIFFNESS * push
            speed = vel[k, at, :] + total * scale
            vel_out[k, at, :] = speed
            pos_out[k, at, :] = here + TIME_STEP * speed
        return carry

    lax.fori_loop(0, blocks // 8, update, 0)
    if last:
        spots = [jnp.broadcast_to(slots[k : k + 1], (8, blocks)) for k in range(2)]
        rows = []
        for comp in range(2):
            drag = rad[...] * rad[...] * vel_out[comp]
            total = DRAG_ICE * jnp.sum(drag.T, axis=0, keepdims=True)
            total = jnp.broadcast_to(total, (8, blocks))
            for spot in spots:
                moved = lane_take(total, jnp.maximum(spot, 0))
                rows.append(jnp.where(spot >= 0, moved, 0.0)[0:1])
        rows.append(jnp.zeros((blocks - 4, blocks), jnp.float32))
        sent[:, 0, :] = jnp.concatenate(rows, axis=0).T
    else:
        for side in range(2):
            for comp in range(2):
                at = pl.ds(side * (cols_dev - 1), rows_dev, stride=cols_dev)
                edges[side, comp] = pos_out[comp, at, :]


def contact_step(which, n_gy, pos, vel, rad, bonds, mask, marks, held, halo, halo_rad, *extra):
    blocks, discs = rad.shape
    rows_dev = blocks // 16
    square = shape(2, blocks, discs)
    tail = shape(blocks, 1, discs) if which == SUB - 1 else shape(2, 2, rows_dev, discs)
    outs = (square, square, tail)
    if which == 0:
        outs += (shape(*rad.shape),)
    if which == 1:
        outs += (shape(*extra[0].shape),)
    args = (pos, vel, rad, bonds, mask, marks, held, halo, halo_rad) + extra
    return pl.pallas_call(
        functools.partial(contact_kernel, which, n_gy),
        out_shape=outs,
        in_specs=[VMEM] * len(args),
        out_specs=(VMEM,) * len(outs),
        scratch_shapes=[
            pltpu.VMEM((3, rows_dev + 2, 24, discs), jnp.float32),
            pltpu.VMEM((4, blocks, discs), jnp.float32),
            pltpu.VMEM((MARKS * blocks, discs), jnp.float32),
            pltpu.VMEM((2, 8 * blocks + 8, discs), jnp.float32),
            pltpu.VMEM((8, discs), jnp.int32),
            pltpu.SMEM((8, discs), jnp.int32),
            pltpu.SemaphoreType.DMA,
        ],
        compiler_params=grant(16),
        cost_estimate=BUSY,
        name=("contact_first", "contact", "contact_last")[which],
    )(*args)


def prep_kernel(pos_in, rad_in, pos, rad, edges, sems):
    copies = [
        pltpu.make_async_copy(pos_in, pos, sems.at[0]),
        pltpu.make_async_copy(rad_in, rad, sems.at[1]),
    ]
    for copy in copies:
        copy.start()
    for copy in copies:
        copy.wait()
    for comp in range(3):
        source = pos.at[comp] if comp < 2 else rad
        for side in range(2):
            edges[side, comp] = source[pl.ds(side * 15, 8, stride=16), :]


def prep(pos, rad):
    return pl.pallas_call(
        prep_kernel,
        out_shape=(shape(*pos.shape), shape(*rad.shape), shape(2, 3, 8, 128)),
        in_specs=[HBM] * 2,
        out_specs=(VMEM,) * 3,
        scratch_shapes=[pltpu.SemaphoreType.DMA((2,))],
        compiler_params=grant(4),
        name="prep",
    )(pos, rad)


def pack_kernel(ocean, after, columns, bottom, top):
    rows = ocean.shape[2]
    lane = lax.broadcasted_iota(jnp.int32, (8, 128), 1)
    packed = [jnp.zeros((8, 128), jnp.float32)] * 2
    for field in range(4):
        for layer in range(CHUNK):
            for v in range(rows // 8):
                g = (field * CHUNK + layer) * (rows // 8) + v
                place = g % 64
                turned = pltpu.roll(ocean[field, layer, pl.ds(8 * v, 8), :], 2 * place + 1, 1)
                packed[g // 64] = jnp.where(lane // 2 == place, turned, packed[g // 64])
    columns[0] = jnp.concatenate(packed, axis=0)
    bottom[...] = ocean[:, :, 0, :]
    top[...] = ocean[:, :, rows - 1, :]


def pack(ocean, after):
    fields, layers, rows, lanes = ocean.shape
    steps = layers // CHUNK
    row = pl.BlockSpec((fields, CHUNK, lanes), lambda i: (0, i, 0))
    return pl.pallas_call(
        pack_kernel,
        grid=(steps,),
        out_shape=(
            shape(steps, 16, lanes),
            shape(fields, layers, lanes),
            shape(fields, layers, lanes),
        ),
        in_specs=[pl.BlockSpec((fields, CHUNK, rows, lanes), lambda i: (0, i, 0, 0)), ANY],
        out_specs=(pl.BlockSpec((1, 16, lanes), lambda i: (i, 0, 0)), row, row),
        compiler_params=grant(8),
        name="pack",
    )(ocean, after)


def exchange_kernel(which, n_gx, n_gy, *refs):
    if which == 0:
        pos, rad, edges, halo, held, marks, halo_rad, *scratch = refs
        send_sem, recv_sem, rad_send, rad_recv = scratch
    elif which == 1:
        pos, rad, edges, top, bottom, perm, halo, held, marks, lat, rows, perms, *scratch = refs
        send_sem, recv_sem, sea_send, sea_recv, *scratch = scratch
        far_send, far_recv, perm_send, perm_recv, own = scratch
    else:
        pos, rad, edges, turned, sides, halo, held, marks, mirror, lon, *scratch = refs
        send_sem, recv_sem, sea_send, sea_recv, far_send, far_recv, own = scratch
    gx, gy = lax.axis_index("gx"), lax.axis_index("gy")
    is_top = gy == n_gy - 1

    def at(dx, dy):
        return lax.rem(gx + dx + n_gx, n_gx), lax.rem(gy + dy + n_gy, n_gy)

    barrier = pltpu.get_barrier_semaphore()
    for dy, dx in NEIGHBOURS:
        pl.semaphore_signal(barrier, inc=1, device_id=at(dx, dy), device_id_type=MESH)
    if which > 0:

        @pl.when(is_top)
        def _():
            for d in range(1, n_gx):
                pl.semaphore_signal(barrier, inc=1, device_id=at(d, 0), device_id_type=MESH)

    blocks = rad.shape[0]
    write_marks([pos[0], pos[1], rad[...]], marks)
    own_forces(0, EARLY, marks, held)
    if which > 0:

        @pl.when(is_top)
        def _():
            pl.semaphore_wait(barrier, len(NEIGHBOURS) + n_gx - 1)

        @pl.when(jnp.logical_not(is_top))
        def _():
            pl.semaphore_wait(barrier, len(NEIGHBOURS))

    else:
        pl.semaphore_wait(barrier, len(NEIGHBOURS))

    def send(source, target, sems, index, device):
        return pltpu.make_async_remote_copy(
            src_ref=source,
            dst_ref=target,
            send_sem=sems[0].at[index],
            recv_sem=sems[1].at[index],
            device_id=device,
            device_id_type=MESH,
        )

    def halo_copies(body, part, target, sems):
        copies = []
        for k, (sy, sx) in enumerate(NEIGHBOURS):
            first = 0 if sy == 1 else blocks - 16
            first = first + 8 if sx == -1 else first
            size = 16 if sx == 0 else 8
            source = part(0 if sx == 1 else 1) if sy == 0 else body(pl.ds(first, size))
            copies.append(send(source, target(k, pl.ds(0, size)), sems, k, at(-sx, -sy)))
        return copies

    copies = halo_copies(
        lambda rows: pos.at[:, rows, :],
        lambda side: edges.at[side, pl.ds(0, 2)],
        lambda k, rows: halo.at[k, :, rows, :],
        (send_sem, recv_sem),
    )
    if which == 0:
        copies += halo_copies(
            lambda rows: rad.at[rows, :],
            lambda side: edges.at[side, 2],
            lambda k, rows: halo_rad.at[k, rows, :],
            (rad_send, rad_recv),
        )
    for copy in copies:
        copy.start()
    if which > 0:
        sea = (sea_send, sea_recv)
        if which == 1:
            pairs = ((top, lat.at[0], at(0, 1)), (bottom, lat.at[1], at(0, -1)))
        else:
            pairs = ((sides, lon.at[0], at(1, 0)), (sides, lon.at[1], at(-1, 0)))
        later = [send(pair[0], pair[1], sea, n, pair[2]) for n, pair in enumerate(pairs)]
        copies += later

    if which == 1:
        first = pl.multiple_of(jnp.minimum(gx, TURNERS - 1) * TURN_ROWS, TURN_ROWS)
        kept = pltpu.make_async_copy(perm, perms.at[gx], own.at[0])
        mine = pltpu.make_async_copy(top.at[pl.ds(first, TURN_ROWS), :], rows.at[gx], own.at[1])
        notes, far = [], []
        for d in range(1, n_gx):
            peer = lax.rem(gx + d, n_gx)
            start = pl.multiple_of(jnp.minimum(peer, TURNERS - 1) * TURN_ROWS, TURN_ROWS)
            notes.append(send(perm, perms.at[gx], (perm_send, perm_recv), d - 1, at(d, 0)))
            source = top.at[pl.ds(start, TURN_ROWS), :]
            far.append(send(source, rows.at[gx], (far_send, far_recv), d - 1, at(d, 0)))

        @pl.when(is_top)
        def _():
            kept.start()
            for d in range(1, n_gx):
                notes[d - 1].start()

                @pl.when(lax.rem(gx + d, n_gx) < TURNERS)
                def _(copy=far[d - 1]):
                    copy.start()

            @pl.when(gx < TURNERS)
            def _():
                mine.start()

        for copy in later:
            copy.start()

    if which == 2:
        for copy in later:
            copy.start()
        me = jnp.minimum(gx, TURNERS - 1)
        mine = pltpu.make_async_copy(turned.at[gx], mirror.at[me], own)
        far = []
        for d in range(1, n_gx):
            source = turned.at[lax.rem(gx + d, n_gx)]
            far.append(send(source, mirror.at[me], (far_send, far_recv), d - 1, at(d, 0)))

        @pl.when(is_top & (gx < TURNERS))
        def _():
            mine.start()
            for copy in far:
                copy.start()

    own_forces(EARLY, blocks - EARLY, marks, held)
    for copy in copies:
        copy.wait()
    if which == 1:

        @pl.when(is_top)
        def _():
            kept.wait()
            for d in range(1, n_gx):
                notes[d - 1].wait()

                @pl.when(lax.rem(gx + d, n_gx) < TURNERS)
                def _(copy=far[d - 1]):
                    copy.wait_send()

            @pl.when(gx < TURNERS)
            def _():
                mine.wait()
                for copy in far:
                    copy.wait_recv()

    if which == 2:

        @pl.when(is_top & (gx < TURNERS))
        def _():
            mine.wait()
            for copy in far:
                copy.wait_send()

        @pl.when(is_top)
        def _():
            for d in range(1, n_gx):

                @pl.when(lax.rem(gx - d + n_gx, n_gx) < TURNERS)
                def _(copy=far[d - 1]):
                    copy.wait_recv()


def exchange(which, n_gx, n_gy, pos, rad, edges, *args):
    lanes = rad.shape[1]
    blocks = rad.shape[0]
    outs = [shape(8, 2, 16, lanes), shape(2, 8 * blocks, lanes)]
    outs += [shape(MARKS * blocks, lanes)]
    dma = pltpu.SemaphoreType.DMA
    scratch = [dma((8,)), dma((8,))]
    far = [dma((n_gx - 1,)), dma((n_gx - 1,))]
    if which == 0:
        outs += [shape(8, 16, lanes)]
        scratch += [dma((8,)), dma((8,))]
    if which == 1:
        top, bottom, perm = args
        outs += [shape(2, *top.shape)]
        outs += [shape(n_gx, TURN_ROWS, lanes), jax.ShapeDtypeStruct((n_gx, 1, lanes), jnp.int32)]
        scratch += [dma((2,)), dma((2,))] + far + far + [dma((2,))]
    if which == 2:
        outs += [shape(TURNERS, TURN_ROWS, lanes), shape(2, *args[1].shape)]
        scratch += [dma((2,)), dma((2,))] + far + [dma]
    return pl.pallas_call(
        functools.partial(exchange_kernel, which, n_gx, n_gy),
        out_shape=tuple(outs),
        in_specs=[VMEM] * (3 + len(args)),
        out_specs=(VMEM,) * len(outs),
        scratch_shapes=scratch,
        compiler_params=grant(8, collective_id=which, has_side_effects=True),
        cost_estimate=BUSY,
        name=("exchange_first", "exchange_second", "exchange_third")[which],
    )(pos, rad, edges, *args)


def stencil(step, n_gy, ocean, mix, lon, lat, mirror, out):
    layers, rows, lanes = ocean.shape[1:]
    gy = lax.axis_index("gy")
    first = step * CHUNK
    lane = lax.broadcasted_iota(jnp.int32, (rows, lanes), 1)
    sub = lax.broadcasted_iota(jnp.int32, (rows, lanes), 0)
    lane8 = lax.broadcasted_iota(jnp.int32, (8, lanes), 1)
    bands = []
    for half in range(2):
        at = pl.ds(8 * half, 8)
        west = pltpu.roll(lon[0, step, at, :], 1, 1)
        east = pltpu.roll(lon[1, step, at, :], lanes - 1, 1)
        bands.append(jnp.where(lane8 % 2 == 1, west, east))
    spin = 2.0 * ((gy * rows + sub).astype(jnp.float32) + 0.5) / (rows * n_gy) - 1.0
    spin = SPIN_RATE * spin
    is_top, is_low = gy == n_gy - 1, gy == 0
    level = pl.ds(pl.multiple_of(first, CHUNK), CHUNK)
    for field in range(4):
        folded = -mirror[field, level, :] if field < 2 else mirror[field, level, :]
        upper = jnp.where(is_top, folded, lat[1, field, level, :])
        lower = jnp.where(is_low, 0.0, lat[0, field, level, :])
        for layer in range(CHUNK):
            at = first + layer
            here = ocean[field, at]
            up = ocean[field, jnp.maximum(at - 1, 0)]
            down = ocean[field, jnp.minimum(at + 1, layers - 1)]
            sides = []
            for v in range(rows // 8):
                g = (field * CHUNK + layer) * (rows // 8) + v
                sides.append(pltpu.roll(bands[g // 64], lanes - 1 - 2 * (g % 64), 1))
            sides = jnp.concatenate(sides, axis=0)
            west = jnp.where(lane == 0, sides, pltpu.roll(here, 1, 1))
            east = jnp.where(lane == lanes - 1, sides, pltpu.roll(here, lanes - 1, 1))
            south = jnp.where(sub == 0, lower[layer : layer + 1], pltpu.roll(here, 1, 0))
            north = jnp.where(sub == rows - 1, upper[layer : layer + 1], pltpu.roll(here, rows - 1, 0))
            laplace = east + west + north + south - 4.0 * here
            value = here + mix[at] * laplace + VERT_MIX * (up + down - 2.0 * here)
            if field == 0:
                value = value + spin * ocean[1, at]
            if field == 1:
                value = value - spin * ocean[0, at]
            out[field, at] = value


def couple_kernel(n_gx, n_gy, sent, cell, ocean, mix, lon, lat, mirror, *refs):
    surface, current, plain, here, there, back, home, *sems = refs
    gx, gy = lax.axis_index("gx"), lax.axis_index("gy")
    tiles = n_gx * n_gy
    rows, lanes = ocean.shape[2:]
    steps = ocean.shape[1] // CHUNK

    def work(first, last):
        def one(step, carry):
            stencil(step, n_gy, ocean, mix, lon, lat, mirror, plain)
            return carry

        lax.fori_loop(first, last, one, 0)

    barrier = pltpu.get_barrier_semaphore()
    for d in range(1, n_gx):
        peer = (lax.rem(gx + d, n_gx), gy)
        pl.semaphore_signal(barrier, inc=1, device_id=peer, device_id_type=MESH)
    for d in range(1, n_gy):
        peer = (gx, lax.rem(gy + d, n_gy))
        pl.semaphore_signal(barrier, inc=1, device_id=peer, device_id_type=MESH)
    pl.semaphore_wait(barrier, n_gx + n_gy - 2)

    def swap(source, middle, target, sems, marks):
        send_x, recv_x, send_y, recv_y, local = sems
        own = pltpu.make_async_copy(source.at[gx], middle.at[gx], local)
        own.start()
        copies = []
        for d in range(1, n_gx):
            peer = lax.rem(gx + d, n_gx)
            copies.append(
                pltpu.make_async_remote_copy(
                    src_ref=source.at[peer],
                    dst_ref=middle.at[gx],
                    send_sem=send_x.at[d - 1],
                    recv_sem=recv_x.at[d - 1],
                    device_id=(peer, gy),
                    device_id_type=MESH,
                )
            )
        for copy in copies:
            copy.start()
        work(marks[0], marks[1])
        own.wait()
        for copy in copies:
            copy.wait()
        own = pltpu.make_async_copy(middle.at[:, gy], target.at[:, gy], local)
        own.start()
        copies = []
        for d in range(1, n_gy):
            peer = lax.rem(gy + d, n_gy)
            copies.append(
                pltpu.make_async_remote_copy(
                    src_ref=middle.at[:, peer],
                    dst_ref=target.at[:, gy],
                    send_sem=send_y.at[d - 1],
                    recv_sem=recv_y.at[d - 1],
                    device_id=(gx, peer),
                    device_id_type=MESH,
                )
            )
        for copy in copies:
            copy.start()
        work(marks[1], marks[2])
        own.wait()
        for copy in copies:
            copy.wait()

    swap(sent, here, there, sems[0:5], (0, steps // 3, steps // 2))
    cells = jnp.concatenate([cell[0:1], cell[1:2]], axis=1)
    cell_row, cell_col = cells // lanes, cells % lanes
    pick = (lax.broadcasted_iota(jnp.int32, (lanes, 2 * tiles), 0) == cell_col).astype(jnp.bfloat16)
    in_row = lax.broadcasted_iota(jnp.int32, (rows, 2 * tiles), 0) == cell_row
    arrived = there[...].reshape(tiles, lanes).T
    spread = []
    for comp in range(2):
        values = jnp.concatenate([arrived[2 * comp : 2 * comp + 1], arrived[2 * comp + 1 : 2 * comp + 2]], axis=1)
        spread.append(jnp.where(in_row, values, 0.0))
    forcing = lax.dot_general(
        split(jnp.concatenate(spread, axis=0)),
        pick,
        (((1,), (1,)), ((), ())),
        preferred_element_type=jnp.float32,
    )
    skin = jnp.concatenate([plain[0, 0], plain[1, 0]], axis=0)
    level = skin + joined(forcing)
    surface[...] = level.reshape(2, rows, lanes)
    found = joined(jnp.dot(split(level), pick, preferred_element_type=jnp.float32))
    replies = []
    for comp in range(2):
        values = jnp.where(in_row, found[comp * rows : (comp + 1) * rows], 0.0)
        values = jnp.sum(values, axis=0, keepdims=True)
        replies += [values[:, :tiles], values[:, tiles:]]
    replies.append(jnp.zeros((lanes - 4, tiles), jnp.float32))
    back[...] = jnp.concatenate(replies, axis=0).T.reshape(back.shape)
    swap(back, home, current, sems[5:10], (steps // 2, steps - 1, steps))


def couple(n_gx, n_gy, sent, cell, ocean, *sea):
    tiles = n_gx * n_gy
    rows, lanes = ocean.shape[2:]
    box = (n_gx, n_gy, 1, lanes)
    dma = pltpu.SemaphoreType.DMA
    sems = [dma((n_gx - 1,)), dma((n_gx - 1,)), dma((n_gy - 1,)), dma((n_gy - 1,)), dma]
    return pl.pallas_call(
        functools.partial(couple_kernel, n_gx, n_gy),
        out_shape=(shape(2, rows, lanes), shape(*box), shape(*ocean.shape)),
        in_specs=[VMEM] * (3 + len(sea)),
        out_specs=(VMEM,) * 3,
        scratch_shapes=[pltpu.VMEM(box, jnp.float32)] * 4 + sems + sems,
        compiler_params=grant(16, collective_id=SUB, has_side_effects=True),
        name="couple",
    )(sent.reshape(box), cell, ocean, *sea)


def finish_kernel(plain, surface, current, slots, vel, vel_out, ocean_out, sems):
    layers = plain.shape[1]
    copies = [
        pltpu.make_async_copy(surface, ocean_out.at[pl.ds(0, 2), 0], sems.at[0]),
        pltpu.make_async_copy(plain.at[pl.ds(2, 2)], ocean_out.at[pl.ds(2, 2)], sems.at[1]),
    ]
    for field in range(2):
        deep = pl.ds(1, layers - 1)
        copies.append(
            pltpu.make_async_copy(plain.at[field, deep], ocean_out.at[field, deep], sems.at[2 + field])
        )
    for copy in copies:
        copy.start()
    blocks, discs = vel.shape[1], vel.shape[2]
    tiles = current.shape[0]
    got = current[...].reshape(tiles, discs).T
    spots = jnp.concatenate([slots[0:1], slots[1:2]], axis=1)
    place = lax.broadcasted_iota(jnp.int32, (blocks, 2 * tiles), 0) == spots
    for comp in range(2):
        values = jnp.concatenate([got[2 * comp : 2 * comp + 1], got[2 * comp + 1 : 2 * comp + 2]], axis=1)
        values = jnp.sum(jnp.where(place, values, 0.0), axis=1, keepdims=True)
        speed = vel[comp]
        vel_out[comp] = speed + DRAG_BACK * (values - speed)
    for copy in copies:
        copy.wait()


def finish(plain, surface, current, slots, vel):
    tiles = current.shape[0] * current.shape[1]
    return pl.pallas_call(
        finish_kernel,
        out_shape=(shape(*vel.shape), shape(*plain.shape)),
        in_specs=[VMEM] * 5,
        out_specs=(VMEM, ANY),
        scratch_shapes=[pltpu.SemaphoreType.DMA((4,))],
        compiler_params=grant(4),
        name="finish",
    )(plain, surface, current.reshape(tiles, 1, current.shape[3]), slots, vel)


def body(
    disc_pos,
    disc_vel,
    radius,
    bond_list,
    contact_mask,
    remap_block,
    ocean_state,
    mix_coef,
    remap_cell,
    fold_perm,
):
    n_gx, n_gy = lax.axis_size("gx"), lax.axis_size("gy")
    rows_dev, cols_dev, discs = radius.shape
    blocks = rows_dev * cols_dev
    slots = remap_block[0].T
    cell = remap_cell[0].T
    perm = fold_perm.reshape(1, discs)
    position = disc_pos.reshape(2, blocks, discs)
    velocity = disc_vel.reshape(2, blocks, discs)
    rad = radius.reshape(blocks, discs)
    bonds = bond_list.reshape(BONDS, blocks, discs)
    sea_shape = (4, mix_coef.shape[0], discs)
    flat = (4 * mix_coef.shape[0], discs)
    position, rad, edges = prep(position, rad)
    halo, held, marks, halo_rad = exchange(0, n_gx, n_gy, position, rad, edges)
    position, velocity, edges, mask = contact_step(
        0, n_gy, position, velocity, rad, bonds, contact_mask, marks, held, halo, halo_rad
    )
    sides, bottom, top = pack(ocean_state, edges)
    halo, held, marks, lat, rows, perms = exchange(
        1, n_gx, n_gy, position, rad, edges, top.reshape(flat), bottom.reshape(flat), perm
    )
    position, velocity, edges, turned = contact_step(
        1, n_gy, position, velocity, rad, bonds, mask, marks, held, halo, halo_rad, rows, perms
    )
    halo, held, marks, mirror, lon = exchange(2, n_gx, n_gy, position, rad, edges, turned, sides)
    position, velocity, sent = contact_step(
        2, n_gy, position, velocity, rad, bonds, mask, marks, held, halo, halo_rad, slots
    )
    sea = (mix_coef, lon, lat.reshape(2, *sea_shape), mirror.reshape(sea_shape))
    surface, current, plain = couple(n_gx, n_gy, sent, cell, ocean_state, *sea)
    vel_next, ocean_next = finish(plain, surface, current, slots, velocity)
    return (position.reshape(disc_pos.shape), vel_next.reshape(disc_vel.shape), ocean_next)


def solution(mesh):
    in_specs = (
        P(None, "gy", "gx", None),
        P(None, "gy", "gx", None),
        P("gy", "gx", None),
        P(None, "gy", "gx", None),
        P(None, "gy", "gx"),
        P(("gx", "gy"), None, None),
        P(None, None, "gy", "gx"),
        P(None, "gy", "gx"),
        P(("gx", "gy"), None, None),
        P("gx"),
    )
    out_specs = (P(None, "gy", "gx", None), P(None, "gy", "gx", None), P(None, None, "gy", "gx"))
    return jax.shard_map(body, mesh=mesh, in_specs=in_specs, out_specs=out_specs, check_vma=False)
```

```python
import functools

import jax
import jax.numpy as jnp
from jax import lax
from jax.experimental import pallas as pl
from jax.experimental.pallas import tpu as pltpu
from jax.sharding import PartitionSpec as P

BONDS = 4
SUB = 3
SOFTEN = 0.0001
STIFFNESS = 2.0
BOND_STIFF = 0.1
TIME_STEP = 0.05
DRAG_ICE = 15.0
DRAG_BACK = 0.5
VERT_MIX = 0.1
SPIN_RATE = 0.3
NEIGHBOURS = ((-1, -1), (-1, 0), (-1, 1), (0, -1), (0, 1), (1, -1), (1, 0), (1, 1))
OWN_STEP = 16
NEAR_STEP = 32
REST_STEP = 16
HALF = 64
MARKS = 16
CHUNK = 8
TURNERS = 12
EARLY = 32
TURN_ROWS = 16
MESH = pl.DeviceIdType.MESH
BUSY = pl.CostEstimate(flops=1 << 32, bytes_accessed=1 << 24, transcendentals=1 << 22)
VMEM = pl.BlockSpec(memory_space=pltpu.VMEM)
ANY = pl.BlockSpec(memory_space=pl.ANY)
HBM = pl.BlockSpec(memory_space=pltpu.HBM)


def grant(mib, **more):
    return pltpu.CompilerParams(vmem_limit_bytes=mib << 20, **more)


def shape(*dims):
    return jax.ShapeDtypeStruct(dims, jnp.float32)


def split(value):
    high = value.astype(jnp.bfloat16)
    rest = value - high.astype(jnp.float32)
    middle = rest.astype(jnp.bfloat16)
    low = (rest - middle.astype(jnp.float32)).astype(jnp.bfloat16)
    return jnp.concatenate([high, middle, low], axis=0)


def joined(value):
    rows = value.shape[0] // 3
    return value[:rows] + value[rows : 2 * rows] + value[2 * rows :]


def lane_take(rows, index):
    return lax.gather(
        rows,
        index[..., None],
        lax.GatherDimensionNumbers(
            offset_dims=(),
            collapsed_slice_dims=(1,),
            start_index_map=(1,),
            operand_batching_dims=(0,),
            start_indices_batching_dims=(0,),
        ),
        slice_sizes=(1, 1),
        mode=lax.GatherScatterMode.PROMISE_IN_BOUNDS,
    )


def pieces(value):
    high = value.astype(jnp.bfloat16).astype(jnp.float32)
    middle = (value - high).astype(jnp.bfloat16).astype(jnp.float32)
    return high, middle, value - high - middle


def write_marks(parts, marks):
    for comp, part in enumerate(parts):
        for i, piece in enumerate(pieces(part)):
            marks[pl.ds(3 * comp + i, part.shape[0], stride=MARKS), :] = piece


def other_side(marks):
    row = lax.broadcasted_iota(jnp.int32, marks.shape, 0)
    marks = jnp.where(row < 9, marks, jnp.where(row < 12, 1.0, 0.0))
    return marks.T.astype(jnp.bfloat16)


def own_side(marks):
    row = lax.broadcasted_iota(jnp.int32, marks.shape, 0)
    sides = []
    for comp in range(3):
        moved = pltpu.roll(marks, 9 - 3 * comp, 0)
        moved = moved if comp == 2 else -moved
        fixed = jnp.where(row // 3 == comp, 1.0, 0.0)
        sides.append(jnp.where((row >= 9) & (row < 12), moved, fixed))
    return jnp.concatenate(sides, axis=1).astype(jnp.bfloat16)


def pair_sums(other, own):
    pairs = jnp.dot(other, own, preferred_element_type=jnp.float32)
    lanes = pairs.shape[1] // 3
    acc_x = acc_y = jnp.zeros((8, lanes), jnp.float32)
    for c in range(pairs.shape[0] // 8):
        rows = pairs[8 * c : 8 * c + 8]
        sep_x, sep_y, reach = rows[:, :lanes], rows[:, lanes : 2 * lanes], rows[:, 2 * lanes :]
        inverse = lax.rsqrt(sep_x * sep_x + sep_y * sep_y + SOFTEN)
        push = jnp.maximum(reach * inverse - 1.0, 0.0)
        acc_x = acc_x + push * sep_x
        acc_y = acc_y + push * sep_y
    return acc_x, acc_y


def marks_of(marks, b):
    return marks[pl.ds(pl.multiple_of(b * MARKS, MARKS), MARKS), :]


def turn(rows, perms, turned):
    lanes = rows.shape[2]

    def one(step, carry):
        for u in range(4):
            h = step * 4 + u
            wanted = jnp.broadcast_to(perms[h], (8, lanes))
            owner, column = wanted // lanes, wanted % lanes
            for half in range(TURN_ROWS // 8):
                at = pl.ds(8 * half, 8)
                got = jnp.zeros((8, lanes), jnp.float32)
                for source in range(rows.shape[0]):
                    got = jnp.where(owner == source, lane_take(rows[source, at, :], column), got)
                turned[h, at, :] = got
        return carry

    lax.fori_loop(0, perms.shape[0] // 4, one, 0)


def own_forces(first, count, marks, force):
    def some(t, carry):
        for u in range(OWN_STEP):
            b = first + t * OWN_STEP + u
            own = marks_of(marks, b)
            acc = pair_sums(other_side(own), own_side(own))
            at = pl.ds(pl.multiple_of(b * 8, 8), 8)
            for k in range(2):
                force[k, at, :] = acc[k]
        return carry

    lax.fori_loop(0, count // OWN_STEP, some, 0)


def write_mask(n_gy, allowed, mask):
    lane = lax.broadcasted_iota(jnp.int32, (8, 128), 1)
    _, rows_dev, cols_dev = allowed.shape
    spread = jnp.zeros((8, 128), jnp.float32)
    for y in range(rows_dev):
        part = allowed[:, y, :].astype(jnp.float32)
        part = jnp.concatenate([part, jnp.zeros((8, 128 - cols_dev), jnp.float32)], axis=1)
        spread = spread + (pltpu.roll(part, y * cols_dev, 1) if y else part)
    which = lax.broadcasted_iota(jnp.int32, (8, 128), 0)
    shift_y = jnp.where(which < 3, -1, jnp.where(which < 5, 0, 1))
    row = lax.axis_index("gy") * rows_dev + lane // cols_dev + shift_y
    spread = jnp.where((row >= 0) & (row < n_gy * rows_dev), spread, 0.0)
    mask[...] = jnp.concatenate([spread, jnp.zeros((120, 128), jnp.float32)], axis=0).T


def contact_kernel(which, n_gy, pos, vel, rad, bonds, mask, marks, held, halo, halo_rad, *refs):
    last = which == SUB - 1
    if last:
        slots, pos_out, vel_out, sent, *scratch = refs
    elif which == 1:
        rows, perms, pos_out, vel_out, edges, turned, *scratch = refs

        @pl.when(lax.axis_index("gy") == n_gy - 1)
        def _():
            turn(rows, perms, turned)

    else:
        allowed, mask = mask, refs[3]
        pos_out, vel_out, edges, _, *scratch = refs
        write_mask(n_gy, allowed, mask)
    wide, found, seen, force, tally, work, sem = scratch
    rows_dev, cols_dev = wide.shape[1] - 2, pos.shape[1] // (wide.shape[1] - 2)
    blocks, discs = rad.shape
    for comp in range(3):
        source = pos.at[comp] if comp < 2 else rad

        def frame(side, first, size):
            if comp < 2:
                return halo[side, comp, pl.ds(first, size), :]
            return halo_rad[side, pl.ds(first, size), :]

        for y in range(rows_dev):
            wide[comp, y + 1, pl.ds(1, cols_dev), :] = source[pl.ds(y * cols_dev, cols_dev), :]
            wide[comp, y + 1, pl.ds(0, 1), :] = frame(3, y, 1)
            wide[comp, y + 1, pl.ds(cols_dev + 1, 1), :] = frame(4, y, 1)
        for side, y in ((0, 0), (5, rows_dev + 1)):
            wide[comp, y, pl.ds(0, 1), :] = frame(side, 7, 1)
            wide[comp, y, pl.ds(1, cols_dev), :] = frame(side + 1, 0, cols_dev)
            wide[comp, y, pl.ds(cols_dev + 1, 1), :] = frame(side + 2, 0, 1)
    lane = lax.broadcasted_iota(jnp.int32, (8, discs), 1)
    lane_f = lane.astype(jnp.float32)
    tri_row = lax.broadcasted_iota(jnp.int32, (discs, 2 * discs), 0)
    tri_col = lax.broadcasted_iota(jnp.int32, (discs, 2 * discs), 1)
    triangle = (tri_row <= tri_col).astype(jnp.bfloat16)
    low_row = lax.broadcasted_iota(jnp.int32, (blocks, blocks), 0)
    low_col = lax.broadcasted_iota(jnp.int32, (blocks, blocks), 1)
    lower = (low_col <= low_row).astype(jnp.bfloat16)

    def collect_row(y, start):
        units, totals = [], []
        for half in range(cols_dev // 8):
            x0 = half * 8
            at = pl.ds(pl.multiple_of(y * cols_dev + x0, 8), 8)
            own = [pos[0, at, :], pos[1, at, :], rad[at, :]]
            reach = jnp.max(own[2], axis=1, keepdims=True)
            low = [jnp.min(own[c], axis=1, keepdims=True) - reach for c in range(2)]
            high = [jnp.max(own[c], axis=1, keepdims=True) + reach for c in range(2)]
            weights = mask[at, :]
            flags = []
            places = []
            for k, (sy, sx) in enumerate(NEIGHBOURS):
                place = (y + 1 + sy, pl.ds(x0 + 1 + sx, 8), slice(None))
                nx, ny, nr = (wide[(c,) + place] for c in range(3))
                close = (nx - nr < high[0] - float(sx)) & (nx + nr > low[0] - float(sx))
                close = close & (ny - nr < high[1] - float(sy)) & (ny + nr > low[1] - float(sy))
                close = close & (weights[:, k : k + 1] > 0.5)
                flags.append(close.astype(jnp.float32))
                places.append(place)
            ranks = jnp.dot(
                jnp.concatenate(flags, axis=0).astype(jnp.bfloat16),
                triangle,
                preferred_element_type=jnp.float32,
            )
            base = jnp.zeros((8, discs), jnp.float32) - start
            for k in range(8):
                rank = ranks[8 * k : 8 * k + 8, :discs]
                total = ranks[8 * k : 8 * k + 8, discs:]
                want = lane_f - base
                source = jnp.zeros((8, discs), jnp.int32)
                units.append((half, k, source, places[k], rank, total, want))
                base = base + total
            totals.append((at, base))
        sources = [u[2] for u in units]
        step = discs // 2
        while step >= 1:
            probes = [lane_take(u[4], i + (step - 1)) for u, i in zip(units, sources)]
            sources = [
                jnp.where(probe <= u[6], i + step, i)
                for probe, u, i in zip(probes, units, sources)
            ]
            step //= 2
        for half, (at, base) in enumerate(totals):
            mine = [(u, i) for u, i in zip(units, sources) if u[0] == half]
            for comp in range(3):
                got = jnp.full((8, discs), -1.0 if comp == 2 else 0.0, jnp.float32)
                for (_, k, _, place, _, total, want), source in mine:
                    valid = (want >= 0.0) & (want < total)
                    value = wide[(comp,) + place]
                    if comp < 2 and NEIGHBOURS[k][1 - comp] != 0:
                        value = value + float(NEIGHBOURS[k][1 - comp])
                    got = jnp.where(valid, lane_take(value, source), got)
                found[comp, at, :] = got
            found[3, at, :] = base

    def collect():
        def one_row(y, carry):
            collect_row(y, 0.0)
            return carry

        lax.fori_loop(0, rows_dev, one_row, 0)
        write_marks([found[k] for k in range(3)], seen)
        left = found[3]
        spot = lax.broadcasted_iota(jnp.int32, (1, discs), 1).astype(jnp.float32)
        for row, bound in ((0, HALF), (3, discs)):
            size = jnp.where(left > float(bound), 1.0, 0.0)
            ends = jnp.dot(lower, size.astype(jnp.bfloat16), preferred_element_type=jnp.float32)
            block = jnp.sum(jnp.where(ends <= spot, 1.0, 0.0), axis=0, keepdims=True)
            tally[row : row + 1] = block.astype(jnp.int32)
            tally[row + 1 : row + 2] = ends[blocks - 1 :].astype(jnp.int32)
        deepest = jnp.max(left, axis=0, keepdims=True)
        tally[2:3] = jnp.ceil(deepest * (1.0 / discs)).astype(jnp.int32)
        copy = pltpu.make_async_copy(tally, work, sem)
        copy.start()
        copy.wait()

    def meet(b, part, fresh):
        at = pl.ds(pl.multiple_of(b * 8, 8), 8)
        b = jnp.minimum(b, blocks - 1)
        other = other_side(marks_of(seen, b))[part * HALF : (part + 1) * HALF]
        acc = pair_sums(other, own_side(marks_of(marks, b)))
        for k in range(2):
            if fresh:
                force[k, at, :] = acc[k]
            else:
                force[k, at, :] += acc[k]

    def some(t, carry):
        for u in range(NEAR_STEP):
            meet(t * NEAR_STEP + u, 0, True)
        return carry

    def rest(t, carry):
        for u in range(REST_STEP):
            meet(work[0, t * REST_STEP + u], 1, False)
        return carry

    def crowded(i, carry):
        b = work[3, i]
        y = b // cols_dev
        at = pl.ds(pl.multiple_of(y * cols_dev, cols_dev), cols_dev)
        first = pl.multiple_of(y * (cols_dev * MARKS), cols_dev * MARKS)
        near = seen.at[pl.ds(first, cols_dev * MARKS), :]

        def deeper(p, carry):
            collect_row(y, p.astype(jnp.float32) * discs)
            write_marks([found[k, at, :] for k in range(3)], near)
            for part in range(2):
                meet(b, part, False)
            return carry

        return lax.fori_loop(1, work[2, 0], deeper, carry)

    collect()
    lax.fori_loop(0, blocks // NEAR_STEP, some, 0)
    lax.fori_loop(0, (work[1, 0] + (REST_STEP - 1)) // REST_STEP, rest, 0)
    lax.fori_loop(0, work[4, 0], crowded, 0)

    def update(g, carry):
        at = pl.ds(pl.multiple_of(g * 8, 8), 8)
        scale = 0.06 / rad[at, :]
        scale = scale * scale
        for k in range(2):
            here = pos[k, at, :]
            bonded = lane_take(here, bonds[0, at, :])
            for p in range(1, BONDS):
                bonded = bonded + lane_take(here, bonds[p, at, :])
            push = jnp.zeros((8, discs), jnp.float32)
            for r in range(8):
                rows = pl.ds(g * 64 + r, 8, stride=8)
                push = push + (held[k, rows, :] + force[k, rows, :])
            total = BOND_STIFF * (bonded - BONDS * here) - STIFFNESS * push
            speed = vel[k, at, :] + total * scale
            vel_out[k, at, :] = speed
            pos_out[k, at, :] = here + TIME_STEP * speed
        return carry

    lax.fori_loop(0, blocks // 8, update, 0)
    if last:
        spots = [jnp.broadcast_to(slots[k : k + 1], (8, blocks)) for k in range(2)]
        rows = []
        for comp in range(2):
            drag = rad[...] * rad[...] * vel_out[comp]
            total = DRAG_ICE * jnp.sum(drag.T, axis=0, keepdims=True)
            total = jnp.broadcast_to(total, (8, blocks))
            for spot in spots:
                moved = lane_take(total, jnp.maximum(spot, 0))
                rows.append(jnp.where(spot >= 0, moved, 0.0)[0:1])
        rows.append(jnp.zeros((blocks - 4, blocks), jnp.float32))
        sent[:, 0, :] = jnp.concatenate(rows, axis=0).T
    else:
        for side in range(2):
            for comp in range(2):
                at = pl.ds(side * (cols_dev - 1), rows_dev, stride=cols_dev)
                edges[side, comp] = pos_out[comp, at, :]


def contact_step(which, n_gy, pos, vel, rad, bonds, mask, marks, held, halo, halo_rad, *extra):
    blocks, discs = rad.shape
    rows_dev = blocks // 16
    square = shape(2, blocks, discs)
    tail = shape(blocks, 1, discs) if which == SUB - 1 else shape(2, 2, rows_dev, discs)
    outs = (square, square, tail)
    if which == 0:
        outs += (shape(*rad.shape),)
    if which == 1:
        outs += (shape(*extra[0].shape),)
    args = (pos, vel, rad, bonds, mask, marks, held, halo, halo_rad) + extra
    return pl.pallas_call(
        functools.partial(contact_kernel, which, n_gy),
        out_shape=outs,
        in_specs=[VMEM] * len(args),
        out_specs=(VMEM,) * len(outs),
        scratch_shapes=[
            pltpu.VMEM((3, rows_dev + 2, 24, discs), jnp.float32),
            pltpu.VMEM((4, blocks, discs), jnp.float32),
            pltpu.VMEM((MARKS * blocks, discs), jnp.float32),
            pltpu.VMEM((2, 8 * blocks + 8, discs), jnp.float32),
            pltpu.VMEM((8, discs), jnp.int32),
            pltpu.SMEM((8, discs), jnp.int32),
            pltpu.SemaphoreType.DMA,
        ],
        compiler_params=grant(16),
        cost_estimate=BUSY,
        name=("contact_first", "contact", "contact_last")[which],
    )(*args)


def prep_kernel(pos_in, rad_in, pos, rad, edges, sems):
    copies = [
        pltpu.make_async_copy(pos_in, pos, sems.at[0]),
        pltpu.make_async_copy(rad_in, rad, sems.at[1]),
    ]
    for copy in copies:
        copy.start()
    for copy in copies:
        copy.wait()
    for comp in range(3):
        source = pos.at[comp] if comp < 2 else rad
        for side in range(2):
            edges[side, comp] = source[pl.ds(side * 15, 8, stride=16), :]


def prep(pos, rad):
    return pl.pallas_call(
        prep_kernel,
        out_shape=(shape(*pos.shape), shape(*rad.shape), shape(2, 3, 8, 128)),
        in_specs=[HBM] * 2,
        out_specs=(VMEM,) * 3,
        scratch_shapes=[pltpu.SemaphoreType.DMA((2,))],
        compiler_params=grant(4),
        name="prep",
    )(pos, rad)


def pack(ocean, sides, bottom, top):
    layers, rows, lanes = ocean.shape[1:]
    lane = lax.broadcasted_iota(jnp.int32, (8, lanes), 1)

    def one(step, carry):
        first = pl.multiple_of(step * CHUNK, CHUNK)
        packed = [jnp.zeros((8, lanes), jnp.float32)] * 2
        for field in range(4):
            at = pl.ds(pl.multiple_of(field * layers + first, CHUNK), CHUNK)
            bottom[at, :] = ocean[field, pl.ds(first, CHUNK), 0, :]
            top[at, :] = ocean[field, pl.ds(first, CHUNK), rows - 1, :]
            for layer in range(CHUNK):
                for v in range(rows // 8):
                    g = (field * CHUNK + layer) * (rows // 8) + v
                    here = ocean[field, first + layer, pl.ds(8 * v, 8), :]
                    turned = pltpu.roll(here, 2 * (g % 64) + 1, 1)
                    packed[g // 64] = jnp.where(lane // 2 == g % 64, turned, packed[g // 64])
        sides[step] = jnp.concatenate(packed, axis=0)
        return carry

    lax.fori_loop(0, layers // CHUNK, one, 0)


def exchange_kernel(which, n_gx, n_gy, *refs):
    if which == 0:
        pos, rad, edges, halo, held, marks, halo_rad, *scratch = refs
        send_sem, recv_sem, rad_send, rad_recv = scratch
    elif which == 1:
        pos, rad, edges, ocean, perm, halo, held, marks, lat, rows, perms, sides, *scratch = refs
        top, bottom, *scratch = scratch
        send_sem, recv_sem, sea_send, sea_recv, *scratch = scratch
        far_send, far_recv, perm_send, perm_recv, own = scratch
    else:
        pos, rad, edges, turned, sides, halo, held, marks, mirror, lon, *scratch = refs
        send_sem, recv_sem, sea_send, sea_recv, far_send, far_recv, own = scratch
    gx, gy = lax.axis_index("gx"), lax.axis_index("gy")
    is_top = gy == n_gy - 1

    def at(dx, dy):
        return lax.rem(gx + dx + n_gx, n_gx), lax.rem(gy + dy + n_gy, n_gy)

    barrier = pltpu.get_barrier_semaphore()
    for dy, dx in NEIGHBOURS:
        pl.semaphore_signal(barrier, inc=1, device_id=at(dx, dy), device_id_type=MESH)
    if which > 0:

        @pl.when(is_top)
        def _():
            for d in range(1, n_gx):
                pl.semaphore_signal(barrier, inc=1, device_id=at(d, 0), device_id_type=MESH)

    if which == 1:
        pack(ocean, sides, bottom, top)
    blocks = rad.shape[0]
    write_marks([pos[0], pos[1], rad[...]], marks)
    own_forces(0, EARLY, marks, held)
    if which > 0:

        @pl.when(is_top)
        def _():
            pl.semaphore_wait(barrier, len(NEIGHBOURS) + n_gx - 1)

        @pl.when(jnp.logical_not(is_top))
        def _():
            pl.semaphore_wait(barrier, len(NEIGHBOURS))

    else:
        pl.semaphore_wait(barrier, len(NEIGHBOURS))

    def send(source, target, sems, index, device):
        return pltpu.make_async_remote_copy(
            src_ref=source,
            dst_ref=target,
            send_sem=sems[0].at[index],
            recv_sem=sems[1].at[index],
            device_id=device,
            device_id_type=MESH,
        )

    def halo_copies(body, part, target, sems):
        copies = []
        for k, (sy, sx) in enumerate(NEIGHBOURS):
            first = 0 if sy == 1 else blocks - 16
            first = first + 8 if sx == -1 else first
            size = 16 if sx == 0 else 8
            source = part(0 if sx == 1 else 1) if sy == 0 else body(pl.ds(first, size))
            copies.append(send(source, target(k, pl.ds(0, size)), sems, k, at(-sx, -sy)))
        return copies

    copies = halo_copies(
        lambda rows: pos.at[:, rows, :],
        lambda side: edges.at[side, pl.ds(0, 2)],
        lambda k, rows: halo.at[k, :, rows, :],
        (send_sem, recv_sem),
    )
    if which == 0:
        copies += halo_copies(
            lambda rows: rad.at[rows, :],
            lambda side: edges.at[side, 2],
            lambda k, rows: halo_rad.at[k, rows, :],
            (rad_send, rad_recv),
        )
    for copy in copies:
        copy.start()
    if which > 0:
        sea = (sea_send, sea_recv)
        if which == 1:
            pairs = ((top, lat.at[0], at(0, 1)), (bottom, lat.at[1], at(0, -1)))
        else:
            pairs = ((sides, lon.at[0], at(1, 0)), (sides, lon.at[1], at(-1, 0)))
        later = [send(pair[0], pair[1], sea, n, pair[2]) for n, pair in enumerate(pairs)]
        copies += later

    if which == 1:
        first = pl.multiple_of(jnp.minimum(gx, TURNERS - 1) * TURN_ROWS, TURN_ROWS)
        kept = pltpu.make_async_copy(perm, perms.at[gx], own.at[0])
        mine = pltpu.make_async_copy(top.at[pl.ds(first, TURN_ROWS), :], rows.at[gx], own.at[1])
        notes, far = [], []
        for d in range(1, n_gx):
            peer = lax.rem(gx + d, n_gx)
            start = pl.multiple_of(jnp.minimum(peer, TURNERS - 1) * TURN_ROWS, TURN_ROWS)
            notes.append(send(perm, perms.at[gx], (perm_send, perm_recv), d - 1, at(d, 0)))
            source = top.at[pl.ds(start, TURN_ROWS), :]
            far.append(send(source, rows.at[gx], (far_send, far_recv), d - 1, at(d, 0)))

        @pl.when(is_top)
        def _():
            kept.start()
            for d in range(1, n_gx):
                notes[d - 1].start()

                @pl.when(lax.rem(gx + d, n_gx) < TURNERS)
                def _(copy=far[d - 1]):
                    copy.start()

            @pl.when(gx < TURNERS)
            def _():
                mine.start()

        for copy in later:
            copy.start()

    if which == 2:
        for copy in later:
            copy.start()
        me = jnp.minimum(gx, TURNERS - 1)
        mine = pltpu.make_async_copy(turned.at[gx], mirror.at[me], own)
        far = []
        for d in range(1, n_gx):
            source = turned.at[lax.rem(gx + d, n_gx)]
            far.append(send(source, mirror.at[me], (far_send, far_recv), d - 1, at(d, 0)))

        @pl.when(is_top & (gx < TURNERS))
        def _():
            mine.start()
            for copy in far:
                copy.start()

    own_forces(EARLY, blocks - EARLY, marks, held)
    for copy in copies:
        copy.wait()
    if which == 1:

        @pl.when(is_top)
        def _():
            kept.wait()
            for d in range(1, n_gx):
                notes[d - 1].wait()

                @pl.when(lax.rem(gx + d, n_gx) < TURNERS)
                def _(copy=far[d - 1]):
                    copy.wait_send()

            @pl.when(gx < TURNERS)
            def _():
                mine.wait()
                for copy in far:
                    copy.wait_recv()

    if which == 2:

        @pl.when(is_top & (gx < TURNERS))
        def _():
            mine.wait()
            for copy in far:
                copy.wait_send()

        @pl.when(is_top)
        def _():
            for d in range(1, n_gx):

                @pl.when(lax.rem(gx - d + n_gx, n_gx) < TURNERS)
                def _(copy=far[d - 1]):
                    copy.wait_recv()


def exchange(which, n_gx, n_gy, pos, rad, edges, *args):
    lanes = rad.shape[1]
    blocks = rad.shape[0]
    outs = [shape(8, 2, 16, lanes), shape(2, 8 * blocks, lanes)]
    outs += [shape(MARKS * blocks, lanes)]
    dma = pltpu.SemaphoreType.DMA
    scratch = [dma((8,)), dma((8,))]
    far = [dma((n_gx - 1,)), dma((n_gx - 1,))]
    if which == 0:
        outs += [shape(8, 16, lanes)]
        scratch += [dma((8,)), dma((8,))]
    if which == 1:
        layers = args[0].shape[1]
        outs += [shape(2, 4 * layers, lanes)]
        outs += [shape(n_gx, TURN_ROWS, lanes), jax.ShapeDtypeStruct((n_gx, 1, lanes), jnp.int32)]
        outs += [shape(layers // CHUNK, 16, lanes)]
        scratch = [pltpu.VMEM((4 * layers, lanes), jnp.float32)] * 2 + scratch
        scratch += [dma((2,)), dma((2,))] + far + far + [dma((2,))]
    if which == 2:
        outs += [shape(TURNERS, TURN_ROWS, lanes), shape(2, *args[1].shape)]
        scratch += [dma((2,)), dma((2,))] + far + [dma]
    return pl.pallas_call(
        functools.partial(exchange_kernel, which, n_gx, n_gy),
        out_shape=tuple(outs),
        in_specs=[VMEM] * (3 + len(args)),
        out_specs=(VMEM,) * len(outs),
        scratch_shapes=scratch,
        compiler_params=grant(8, collective_id=which, has_side_effects=True),
        cost_estimate=BUSY,
        name=("exchange_first", "exchange_second", "exchange_third")[which],
    )(pos, rad, edges, *args)


def stencil(step, n_gy, ocean, mix, lon, lat, mirror, out):
    layers, rows, lanes = ocean.shape[1:]
    gy = lax.axis_index("gy")
    first = step * CHUNK
    lane = lax.broadcasted_iota(jnp.int32, (rows, lanes), 1)
    sub = lax.broadcasted_iota(jnp.int32, (rows, lanes), 0)
    lane8 = lax.broadcasted_iota(jnp.int32, (8, lanes), 1)
    bands = []
    for half in range(2):
        at = pl.ds(8 * half, 8)
        west = pltpu.roll(lon[0, step, at, :], 1, 1)
        east = pltpu.roll(lon[1, step, at, :], lanes - 1, 1)
        bands.append(jnp.where(lane8 % 2 == 1, west, east))
    spin = 2.0 * ((gy * rows + sub).astype(jnp.float32) + 0.5) / (rows * n_gy) - 1.0
    spin = SPIN_RATE * spin
    is_top, is_low = gy == n_gy - 1, gy == 0
    level = pl.ds(pl.multiple_of(first, CHUNK), CHUNK)
    for field in range(4):
        folded = -mirror[field, level, :] if field < 2 else mirror[field, level, :]
        upper = jnp.where(is_top, folded, lat[1, field, level, :])
        lower = jnp.where(is_low, 0.0, lat[0, field, level, :])
        for layer in range(CHUNK):
            at = first + layer
            here = ocean[field, at]
            up = ocean[field, jnp.maximum(at - 1, 0)]
            down = ocean[field, jnp.minimum(at + 1, layers - 1)]
            sides = []
            for v in range(rows // 8):
                g = (field * CHUNK + layer) * (rows // 8) + v
                sides.append(pltpu.roll(bands[g // 64], lanes - 1 - 2 * (g % 64), 1))
            sides = jnp.concatenate(sides, axis=0)
            west = jnp.where(lane == 0, sides, pltpu.roll(here, 1, 1))
            east = jnp.where(lane == lanes - 1, sides, pltpu.roll(here, lanes - 1, 1))
            south = jnp.where(sub == 0, lower[layer : layer + 1], pltpu.roll(here, 1, 0))
            north = jnp.where(sub == rows - 1, upper[layer : layer + 1], pltpu.roll(here, rows - 1, 0))
            laplace = east + west + north + south - 4.0 * here
            value = here + mix[at] * laplace + VERT_MIX * (up + down - 2.0 * here)
            if field == 0:
                value = value + spin * ocean[1, at]
            if field == 1:
                value = value - spin * ocean[0, at]
            out[field, at] = value


def couple_kernel(n_gx, n_gy, sent, cell, ocean, mix, lon, lat, mirror, *refs):
    surface, current, plain, here, there, back, home, *sems = refs
    gx, gy = lax.axis_index("gx"), lax.axis_index("gy")
    tiles = n_gx * n_gy
    rows, lanes = ocean.shape[2:]
    steps = ocean.shape[1] // CHUNK

    def work(first, last):
        def one(step, carry):
            stencil(step, n_gy, ocean, mix, lon, lat, mirror, plain)
            return carry

        lax.fori_loop(first, last, one, 0)

    barrier = pltpu.get_barrier_semaphore()
    for d in range(1, n_gx):
        peer = (lax.rem(gx + d, n_gx), gy)
        pl.semaphore_signal(barrier, inc=1, device_id=peer, device_id_type=MESH)
    for d in range(1, n_gy):
        peer = (gx, lax.rem(gy + d, n_gy))
        pl.semaphore_signal(barrier, inc=1, device_id=peer, device_id_type=MESH)
    pl.semaphore_wait(barrier, n_gx + n_gy - 2)

    def swap(source, middle, target, sems, marks):
        send_x, recv_x, send_y, recv_y, local = sems
        own = pltpu.make_async_copy(source.at[gx], middle.at[gx], local)
        own.start()
        copies = []
        for d in range(1, n_gx):
            peer = lax.rem(gx + d, n_gx)
            copies.append(
                pltpu.make_async_remote_copy(
                    src_ref=source.at[peer],
                    dst_ref=middle.at[gx],
                    send_sem=send_x.at[d - 1],
                    recv_sem=recv_x.at[d - 1],
                    device_id=(peer, gy),
                    device_id_type=MESH,
                )
            )
        for copy in copies:
            copy.start()
        work(marks[0], marks[1])
        own.wait()
        for copy in copies:
            copy.wait()
        own = pltpu.make_async_copy(middle.at[:, gy], target.at[:, gy], local)
        own.start()
        copies = []
        for d in range(1, n_gy):
            peer = lax.rem(gy + d, n_gy)
            copies.append(
                pltpu.make_async_remote_copy(
                    src_ref=middle.at[:, peer],
                    dst_ref=target.at[:, gy],
                    send_sem=send_y.at[d - 1],
                    recv_sem=recv_y.at[d - 1],
                    device_id=(gx, peer),
                    device_id_type=MESH,
                )
            )
        for copy in copies:
            copy.start()
        work(marks[1], marks[2])
        own.wait()
        for copy in copies:
            copy.wait()

    swap(sent, here, there, sems[0:5], (0, steps // 3, steps // 2))
    cells = jnp.concatenate([cell[0:1], cell[1:2]], axis=1)
    cell_row, cell_col = cells // lanes, cells % lanes
    pick = (lax.broadcasted_iota(jnp.int32, (lanes, 2 * tiles), 0) == cell_col).astype(jnp.bfloat16)
    in_row = lax.broadcasted_iota(jnp.int32, (rows, 2 * tiles), 0) == cell_row
    arrived = there[...].reshape(tiles, lanes).T
    spread = []
    for comp in range(2):
        values = jnp.concatenate([arrived[2 * comp : 2 * comp + 1], arrived[2 * comp + 1 : 2 * comp + 2]], axis=1)
        spread.append(jnp.where(in_row, values, 0.0))
    forcing = lax.dot_general(
        split(jnp.concatenate(spread, axis=0)),
        pick,
        (((1,), (1,)), ((), ())),
        preferred_element_type=jnp.float32,
    )
    skin = jnp.concatenate([plain[0, 0], plain[1, 0]], axis=0)
    level = skin + joined(forcing)
    surface[...] = level.reshape(2, rows, lanes)
    found = joined(jnp.dot(split(level), pick, preferred_element_type=jnp.float32))
    replies = []
    for comp in range(2):
        values = jnp.where(in_row, found[comp * rows : (comp + 1) * rows], 0.0)
        values = jnp.sum(values, axis=0, keepdims=True)
        replies += [values[:, :tiles], values[:, tiles:]]
    replies.append(jnp.zeros((lanes - 4, tiles), jnp.float32))
    back[...] = jnp.concatenate(replies, axis=0).T.reshape(back.shape)
    swap(back, home, current, sems[5:10], (steps // 2, steps - 1, steps))


def couple(n_gx, n_gy, sent, cell, ocean, *sea):
    tiles = n_gx * n_gy
    rows, lanes = ocean.shape[2:]
    box = (n_gx, n_gy, 1, lanes)
    dma = pltpu.SemaphoreType.DMA
    sems = [dma((n_gx - 1,)), dma((n_gx - 1,)), dma((n_gy - 1,)), dma((n_gy - 1,)), dma]
    return pl.pallas_call(
        functools.partial(couple_kernel, n_gx, n_gy),
        out_shape=(shape(2, rows, lanes), shape(*box), shape(*ocean.shape)),
        in_specs=[VMEM] * (3 + len(sea)),
        out_specs=(VMEM,) * 3,
        scratch_shapes=[pltpu.VMEM(box, jnp.float32)] * 4 + sems + sems,
        compiler_params=grant(16, collective_id=SUB, has_side_effects=True),
        name="couple",
    )(sent.reshape(box), cell, ocean, *sea)


def finish_kernel(plain, surface, current, slots, vel, vel_out, ocean_out, sems):
    layers = plain.shape[1]
    copies = [
        pltpu.make_async_copy(surface, ocean_out.at[pl.ds(0, 2), 0], sems.at[0]),
        pltpu.make_async_copy(plain.at[pl.ds(2, 2)], ocean_out.at[pl.ds(2, 2)], sems.at[1]),
    ]
    for field in range(2):
        deep = pl.ds(1, layers - 1)
        copies.append(
            pltpu.make_async_copy(plain.at[field, deep], ocean_out.at[field, deep], sems.at[2 + field])
        )
    for copy in copies:
        copy.start()
    blocks, discs = vel.shape[1], vel.shape[2]
    tiles = current.shape[0]
    got = current[...].reshape(tiles, discs).T
    spots = jnp.concatenate([slots[0:1], slots[1:2]], axis=1)
    place = lax.broadcasted_iota(jnp.int32, (blocks, 2 * tiles), 0) == spots
    for comp in range(2):
        values = jnp.concatenate([got[2 * comp : 2 * comp + 1], got[2 * comp + 1 : 2 * comp + 2]], axis=1)
        values = jnp.sum(jnp.where(place, values, 0.0), axis=1, keepdims=True)
        speed = vel[comp]
        vel_out[comp] = speed + DRAG_BACK * (values - speed)
    for copy in copies:
        copy.wait()


def finish(plain, surface, current, slots, vel):
    tiles = current.shape[0] * current.shape[1]
    return pl.pallas_call(
        finish_kernel,
        out_shape=(shape(*vel.shape), shape(*plain.shape)),
        in_specs=[VMEM] * 5,
        out_specs=(VMEM, ANY),
        scratch_shapes=[pltpu.SemaphoreType.DMA((4,))],
        compiler_params=grant(4),
        name="finish",
    )(plain, surface, current.reshape(tiles, 1, current.shape[3]), slots, vel)


def body(
    disc_pos,
    disc_vel,
    radius,
    bond_list,
    contact_mask,
    remap_block,
    ocean_state,
    mix_coef,
    remap_cell,
    fold_perm,
):
    n_gx, n_gy = lax.axis_size("gx"), lax.axis_size("gy")
    rows_dev, cols_dev, discs = radius.shape
    blocks = rows_dev * cols_dev
    slots = remap_block[0].T
    cell = remap_cell[0].T
    perm = fold_perm.reshape(1, discs)
    position = disc_pos.reshape(2, blocks, discs)
    velocity = disc_vel.reshape(2, blocks, discs)
    rad = radius.reshape(blocks, discs)
    bonds = bond_list.reshape(BONDS, blocks, discs)
    sea_shape = (4, mix_coef.shape[0], discs)
    position, rad, edges = prep(position, rad)
    halo, held, marks, halo_rad = exchange(0, n_gx, n_gy, position, rad, edges)
    position, velocity, edges, mask = contact_step(
        0, n_gy, position, velocity, rad, bonds, contact_mask, marks, held, halo, halo_rad
    )
    halo, held, marks, lat, rows, perms, sides = exchange(
        1, n_gx, n_gy, position, rad, edges, ocean_state, perm
    )
    position, velocity, edges, turned = contact_step(
        1, n_gy, position, velocity, rad, bonds, mask, marks, held, halo, halo_rad, rows, perms
    )
    halo, held, marks, mirror, lon = exchange(2, n_gx, n_gy, position, rad, edges, turned, sides)
    position, velocity, sent = contact_step(
        2, n_gy, position, velocity, rad, bonds, mask, marks, held, halo, halo_rad, slots
    )
    sea = (mix_coef, lon, lat.reshape(2, *sea_shape), mirror.reshape(sea_shape))
    surface, current, plain = couple(n_gx, n_gy, sent, cell, ocean_state, *sea)
    vel_next, ocean_next = finish(plain, surface, current, slots, velocity)
    return (position.reshape(disc_pos.shape), vel_next.reshape(disc_vel.shape), ocean_next)


def solution(mesh):
    in_specs = (
        P(None, "gy", "gx", None),
        P(None, "gy", "gx", None),
        P("gy", "gx", None),
        P(None, "gy", "gx", None),
        P(None, "gy", "gx"),
        P(("gx", "gy"), None, None),
        P(None, None, "gy", "gx"),
        P(None, "gy", "gx"),
        P(("gx", "gy"), None, None),
        P("gx"),
    )
    out_specs = (P(None, "gy", "gx", None), P(None, "gy", "gx", None), P(None, None, "gy", "gx"))
    return jax.shard_map(body, mesh=mesh, in_specs=in_specs, out_specs=out_specs, check_vma=False)
```

```python
import functools

import jax
import jax.numpy as jnp
from jax import lax
from jax.experimental import pallas as pl
from jax.experimental.pallas import tpu as pltpu
from jax.sharding import PartitionSpec as P

BONDS = 4
SUB = 3
SOFTEN = 0.0001
STIFFNESS = 2.0
BOND_STIFF = 0.1
TIME_STEP = 0.05
DRAG_ICE = 15.0
DRAG_BACK = 0.5
VERT_MIX = 0.1
SPIN_RATE = 0.3
NEIGHBOURS = ((-1, -1), (-1, 0), (-1, 1), (0, -1), (0, 1), (1, -1), (1, 0), (1, 1))
OWN_STEP = 16
NEAR_STEP = 32
REST_STEP = 16
HALF = 64
MARKS = 16
CHUNK = 8
TURNERS = 12
EARLY = 48
TURN_ROWS = 16
MESH = pl.DeviceIdType.MESH
BUSY = pl.CostEstimate(flops=1 << 32, bytes_accessed=1 << 24, transcendentals=1 << 22)
VMEM = pl.BlockSpec(memory_space=pltpu.VMEM)
ANY = pl.BlockSpec(memory_space=pl.ANY)
HBM = pl.BlockSpec(memory_space=pltpu.HBM)


def grant(mib, **more):
    return pltpu.CompilerParams(vmem_limit_bytes=mib << 20, **more)


def shape(*dims):
    return jax.ShapeDtypeStruct(dims, jnp.float32)


def split(value):
    high = value.astype(jnp.bfloat16)
    rest = value - high.astype(jnp.float32)
    middle = rest.astype(jnp.bfloat16)
    low = (rest - middle.astype(jnp.float32)).astype(jnp.bfloat16)
    return jnp.concatenate([high, middle, low], axis=0)


def joined(value):
    rows = value.shape[0] // 3
    return value[:rows] + value[rows : 2 * rows] + value[2 * rows :]


def lane_take(rows, index):
    return lax.gather(
        rows,
        index[..., None],
        lax.GatherDimensionNumbers(
            offset_dims=(),
            collapsed_slice_dims=(1,),
            start_index_map=(1,),
            operand_batching_dims=(0,),
            start_indices_batching_dims=(0,),
        ),
        slice_sizes=(1, 1),
        mode=lax.GatherScatterMode.PROMISE_IN_BOUNDS,
    )


def pieces(value):
    high = value.astype(jnp.bfloat16).astype(jnp.float32)
    middle = (value - high).astype(jnp.bfloat16).astype(jnp.float32)
    return high, middle, value - high - middle


def write_marks(parts, marks):
    for comp, part in enumerate(parts):
        for i, piece in enumerate(pieces(part)):
            marks[pl.ds(3 * comp + i, part.shape[0], stride=MARKS), :] = piece


def other_side(marks):
    row = lax.broadcasted_iota(jnp.int32, marks.shape, 0)
    marks = jnp.where(row < 9, marks, jnp.where(row < 12, 1.0, 0.0))
    return marks.T.astype(jnp.bfloat16)


def own_side(marks):
    row = lax.broadcasted_iota(jnp.int32, marks.shape, 0)
    sides = []
    for comp in range(3):
        moved = pltpu.roll(marks, 9 - 3 * comp, 0)
        moved = moved if comp == 2 else -moved
        fixed = jnp.where(row // 3 == comp, 1.0, 0.0)
        sides.append(jnp.where((row >= 9) & (row < 12), moved, fixed))
    return jnp.concatenate(sides, axis=1).astype(jnp.bfloat16)


def pair_sums(other, own):
    pairs = jnp.dot(other, own, preferred_element_type=jnp.float32)
    lanes = pairs.shape[1] // 3
    acc_x = acc_y = jnp.zeros((8, lanes), jnp.float32)
    for c in range(pairs.shape[0] // 8):
        rows = pairs[8 * c : 8 * c + 8]
        sep_x, sep_y, reach = rows[:, :lanes], rows[:, lanes : 2 * lanes], rows[:, 2 * lanes :]
        inverse = lax.rsqrt(sep_x * sep_x + sep_y * sep_y + SOFTEN)
        push = jnp.maximum(reach * inverse - 1.0, 0.0)
        acc_x = acc_x + push * sep_x
        acc_y = acc_y + push * sep_y
    return acc_x, acc_y


def marks_of(marks, b):
    return marks[pl.ds(pl.multiple_of(b * MARKS, MARKS), MARKS), :]


def turn(rows, perms, turned):
    lanes = rows.shape[2]

    def one(step, carry):
        for u in range(4):
            h = step * 4 + u
            wanted = jnp.broadcast_to(perms[h], (8, lanes))
            owner, column = wanted // lanes, wanted % lanes
            for half in range(TURN_ROWS // 8):
                at = pl.ds(8 * half, 8)
                got = jnp.zeros((8, lanes), jnp.float32)
                for source in range(rows.shape[0]):
                    got = jnp.where(owner == source, lane_take(rows[source, at, :], column), got)
                turned[h, at, :] = got
        return carry

    lax.fori_loop(0, perms.shape[0] // 4, one, 0)


def own_forces(first, count, marks, force):
    def some(t, carry):
        for u in range(OWN_STEP):
            b = first + t * OWN_STEP + u
            own = marks_of(marks, b)
            acc = pair_sums(other_side(own), own_side(own))
            at = pl.ds(pl.multiple_of(b * 8, 8), 8)
            for k in range(2):
                force[k, at, :] = acc[k]
        return carry

    lax.fori_loop(0, count // OWN_STEP, some, 0)


def write_mask(n_gy, allowed, mask):
    lane = lax.broadcasted_iota(jnp.int32, (8, 128), 1)
    _, rows_dev, cols_dev = allowed.shape
    spread = jnp.zeros((8, 128), jnp.float32)
    for y in range(rows_dev):
        part = allowed[:, y, :].astype(jnp.float32)
        part = jnp.concatenate([part, jnp.zeros((8, 128 - cols_dev), jnp.float32)], axis=1)
        spread = spread + (pltpu.roll(part, y * cols_dev, 1) if y else part)
    which = lax.broadcasted_iota(jnp.int32, (8, 128), 0)
    shift_y = jnp.where(which < 3, -1, jnp.where(which < 5, 0, 1))
    row = lax.axis_index("gy") * rows_dev + lane // cols_dev + shift_y
    spread = jnp.where((row >= 0) & (row < n_gy * rows_dev), spread, 0.0)
    mask[...] = jnp.concatenate([spread, jnp.zeros((120, 128), jnp.float32)], axis=0).T


def contact_kernel(which, n_gy, pos, vel, rad, bonds, mask, marks, held, halo, halo_rad, *refs):
    last = which == SUB - 1
    if last:
        slots, pos_out, vel_out, sent, *scratch = refs
    elif which == 1:
        rows, perms, pos_out, vel_out, edges, turned, *scratch = refs

        @pl.when(lax.axis_index("gy") == n_gy - 1)
        def _():
            turn(rows, perms, turned)

    else:
        allowed, mask = mask, refs[3]
        pos_out, vel_out, edges, _, *scratch = refs
        write_mask(n_gy, allowed, mask)
    wide, found, seen, force, tally, work, sem = scratch
    rows_dev, cols_dev = wide.shape[1] - 2, pos.shape[1] // (wide.shape[1] - 2)
    blocks, discs = rad.shape
    for comp in range(3):
        source = pos.at[comp] if comp < 2 else rad

        def frame(side, first, size):
            if comp < 2:
                return halo[side, comp, pl.ds(first, size), :]
            return halo_rad[side, pl.ds(first, size), :]

        for y in range(rows_dev):
            wide[comp, y + 1, pl.ds(1, cols_dev), :] = source[pl.ds(y * cols_dev, cols_dev), :]
            wide[comp, y + 1, pl.ds(0, 1), :] = frame(3, y, 1)
            wide[comp, y + 1, pl.ds(cols_dev + 1, 1), :] = frame(4, y, 1)
        for side, y in ((0, 0), (5, rows_dev + 1)):
            wide[comp, y, pl.ds(0, 1), :] = frame(side, 7, 1)
            wide[comp, y, pl.ds(1, cols_dev), :] = frame(side + 1, 0, cols_dev)
            wide[comp, y, pl.ds(cols_dev + 1, 1), :] = frame(side + 2, 0, 1)
    lane = lax.broadcasted_iota(jnp.int32, (8, discs), 1)
    lane_f = lane.astype(jnp.float32)
    tri_row = lax.broadcasted_iota(jnp.int32, (discs, 2 * discs), 0)
    tri_col = lax.broadcasted_iota(jnp.int32, (discs, 2 * discs), 1)
    triangle = (tri_row <= tri_col).astype(jnp.bfloat16)
    low_row = lax.broadcasted_iota(jnp.int32, (blocks, blocks), 0)
    low_col = lax.broadcasted_iota(jnp.int32, (blocks, blocks), 1)
    lower = (low_col <= low_row).astype(jnp.bfloat16)

    def collect_row(y, start):
        units, totals = [], []
        for half in range(cols_dev // 8):
            x0 = half * 8
            at = pl.ds(pl.multiple_of(y * cols_dev + x0, 8), 8)
            own = [pos[0, at, :], pos[1, at, :], rad[at, :]]
            reach = jnp.max(own[2], axis=1, keepdims=True)
            low = [jnp.min(own[c], axis=1, keepdims=True) - reach for c in range(2)]
            high = [jnp.max(own[c], axis=1, keepdims=True) + reach for c in range(2)]
            weights = mask[at, :]
            flags = []
            places = []
            for k, (sy, sx) in enumerate(NEIGHBOURS):
                place = (y + 1 + sy, pl.ds(x0 + 1 + sx, 8), slice(None))
                nx, ny, nr = (wide[(c,) + place] for c in range(3))
                close = (nx - nr < high[0] - float(sx)) & (nx + nr > low[0] - float(sx))
                close = close & (ny - nr < high[1] - float(sy)) & (ny + nr > low[1] - float(sy))
                close = close & (weights[:, k : k + 1] > 0.5)
                flags.append(close.astype(jnp.float32))
                places.append(place)
            ranks = jnp.dot(
                jnp.concatenate(flags, axis=0).astype(jnp.bfloat16),
                triangle,
                preferred_element_type=jnp.float32,
            )
            base = jnp.zeros((8, discs), jnp.float32) - start
            for k in range(8):
                rank = ranks[8 * k : 8 * k + 8, :discs]
                total = ranks[8 * k : 8 * k + 8, discs:]
                want = lane_f - base
                source = jnp.zeros((8, discs), jnp.int32)
                units.append((half, k, source, places[k], rank, total, want))
                base = base + total
            totals.append((at, base))
        sources = [u[2] for u in units]
        step = discs // 2
        while step >= 1:
            probes = [lane_take(u[4], i + (step - 1)) for u, i in zip(units, sources)]
            sources = [
                jnp.where(probe <= u[6], i + step, i)
                for probe, u, i in zip(probes, units, sources)
            ]
            step //= 2
        for half, (at, base) in enumerate(totals):
            mine = [(u, i) for u, i in zip(units, sources) if u[0] == half]
            for comp in range(3):
                got = jnp.full((8, discs), -1.0 if comp == 2 else 0.0, jnp.float32)
                for (_, k, _, place, _, total, want), source in mine:
                    valid = (want >= 0.0) & (want < total)
                    value = wide[(comp,) + place]
                    if comp < 2 and NEIGHBOURS[k][1 - comp] != 0:
                        value = value + float(NEIGHBOURS[k][1 - comp])
                    got = jnp.where(valid, lane_take(value, source), got)
                found[comp, at, :] = got
            found[3, at, :] = base

    def collect():
        def one_row(y, carry):
            collect_row(y, 0.0)
            return carry

        lax.fori_loop(0, rows_dev, one_row, 0)
        write_marks([found[k] for k in range(3)], seen)
        left = found[3]
        spot = lax.broadcasted_iota(jnp.int32, (1, discs), 1).astype(jnp.float32)
        for row, bound in ((0, HALF), (3, discs)):
            size = jnp.where(left > float(bound), 1.0, 0.0)
            ends = jnp.dot(lower, size.astype(jnp.bfloat16), preferred_element_type=jnp.float32)
            block = jnp.sum(jnp.where(ends <= spot, 1.0, 0.0), axis=0, keepdims=True)
            tally[row : row + 1] = block.astype(jnp.int32)
            tally[row + 1 : row + 2] = ends[blocks - 1 :].astype(jnp.int32)
        deepest = jnp.max(left, axis=0, keepdims=True)
        tally[2:3] = jnp.ceil(deepest * (1.0 / discs)).astype(jnp.int32)
        copy = pltpu.make_async_copy(tally, work, sem)
        copy.start()
        copy.wait()

    def meet(b, part, fresh):
        at = pl.ds(pl.multiple_of(b * 8, 8), 8)
        b = jnp.minimum(b, blocks - 1)
        other = other_side(marks_of(seen, b))[part * HALF : (part + 1) * HALF]
        acc = pair_sums(other, own_side(marks_of(marks, b)))
        for k in range(2):
            if fresh:
                force[k, at, :] = acc[k]
            else:
                force[k, at, :] += acc[k]

    def some(t, carry):
        for u in range(NEAR_STEP):
            meet(t * NEAR_STEP + u, 0, True)
        return carry

    def rest(t, carry):
        for u in range(REST_STEP):
            meet(work[0, t * REST_STEP + u], 1, False)
        return carry

    def crowded(i, carry):
        b = work[3, i]
        y = b // cols_dev
        at = pl.ds(pl.multiple_of(y * cols_dev, cols_dev), cols_dev)
        first = pl.multiple_of(y * (cols_dev * MARKS), cols_dev * MARKS)
        near = seen.at[pl.ds(first, cols_dev * MARKS), :]

        def deeper(p, carry):
            collect_row(y, p.astype(jnp.float32) * discs)
            write_marks([found[k, at, :] for k in range(3)], near)
            for part in range(2):
                meet(b, part, False)
            return carry

        return lax.fori_loop(1, work[2, 0], deeper, carry)

    collect()
    lax.fori_loop(0, blocks // NEAR_STEP, some, 0)
    lax.fori_loop(0, (work[1, 0] + (REST_STEP - 1)) // REST_STEP, rest, 0)
    lax.fori_loop(0, work[4, 0], crowded, 0)

    def update(g, carry):
        at = pl.ds(pl.multiple_of(g * 8, 8), 8)
        scale = 0.06 / rad[at, :]
        scale = scale * scale
        for k in range(2):
            here = pos[k, at, :]
            bonded = lane_take(here, bonds[0, at, :])
            for p in range(1, BONDS):
                bonded = bonded + lane_take(here, bonds[p, at, :])
            push = jnp.zeros((8, discs), jnp.float32)
            for r in range(8):
                rows = pl.ds(g * 64 + r, 8, stride=8)
                push = push + (held[k, rows, :] + force[k, rows, :])
            total = BOND_STIFF * (bonded - BONDS * here) - STIFFNESS * push
            speed = vel[k, at, :] + total * scale
            vel_out[k, at, :] = speed
            pos_out[k, at, :] = here + TIME_STEP * speed
        return carry

    lax.fori_loop(0, blocks // 8, update, 0)
    if last:
        spots = [jnp.broadcast_to(slots[k : k + 1], (8, blocks)) for k in range(2)]
        rows = []
        for comp in range(2):
            drag = rad[...] * rad[...] * vel_out[comp]
            total = DRAG_ICE * jnp.sum(drag.T, axis=0, keepdims=True)
            total = jnp.broadcast_to(total, (8, blocks))
            for spot in spots:
                moved = lane_take(total, jnp.maximum(spot, 0))
                rows.append(jnp.where(spot >= 0, moved, 0.0)[0:1])
        rows.append(jnp.zeros((blocks - 4, blocks), jnp.float32))
        sent[:, 0, :] = jnp.concatenate(rows, axis=0).T
    else:
        for side in range(2):
            for comp in range(2):
                at = pl.ds(side * (cols_dev - 1), rows_dev, stride=cols_dev)
                edges[side, comp] = pos_out[comp, at, :]


def contact_step(which, n_gy, pos, vel, rad, bonds, mask, marks, held, halo, halo_rad, *extra):
    blocks, discs = rad.shape
    rows_dev = blocks // 16
    square = shape(2, blocks, discs)
    tail = shape(blocks, 1, discs) if which == SUB - 1 else shape(2, 2, rows_dev, discs)
    outs = (square, square, tail)
    if which == 0:
        outs += (shape(*rad.shape),)
    if which == 1:
        outs += (shape(*extra[0].shape),)
    args = (pos, vel, rad, bonds, mask, marks, held, halo, halo_rad) + extra
    return pl.pallas_call(
        functools.partial(contact_kernel, which, n_gy),
        out_shape=outs,
        in_specs=[VMEM] * len(args),
        out_specs=(VMEM,) * len(outs),
        scratch_shapes=[
            pltpu.VMEM((3, rows_dev + 2, 24, discs), jnp.float32),
            pltpu.VMEM((4, blocks, discs), jnp.float32),
            pltpu.VMEM((MARKS * blocks, discs), jnp.float32),
            pltpu.VMEM((2, 8 * blocks + 8, discs), jnp.float32),
            pltpu.VMEM((8, discs), jnp.int32),
            pltpu.SMEM((8, discs), jnp.int32),
            pltpu.SemaphoreType.DMA,
        ],
        compiler_params=grant(16),
        cost_estimate=BUSY,
        name=("contact_first", "contact", "contact_last")[which],
    )(*args)


def prep_kernel(pos_in, rad_in, pos, rad, edges, sems):
    copies = [
        pltpu.make_async_copy(pos_in, pos, sems.at[0]),
        pltpu.make_async_copy(rad_in, rad, sems.at[1]),
    ]
    for copy in copies:
        copy.start()
    for copy in copies:
        copy.wait()
    for comp in range(3):
        source = pos.at[comp] if comp < 2 else rad
        for side in range(2):
            edges[side, comp] = source[pl.ds(side * 15, 8, stride=16), :]


def prep(pos, rad):
    return pl.pallas_call(
        prep_kernel,
        out_shape=(shape(*pos.shape), shape(*rad.shape), shape(2, 3, 8, 128)),
        in_specs=[HBM] * 2,
        out_specs=(VMEM,) * 3,
        scratch_shapes=[pltpu.SemaphoreType.DMA((2,))],
        compiler_params=grant(4),
        name="prep",
    )(pos, rad)


def pack(ocean, sides, bottom, top):
    layers, rows, lanes = ocean.shape[1:]
    lane = lax.broadcasted_iota(jnp.int32, (8, lanes), 1)

    def one(step, carry):
        first = pl.multiple_of(step * CHUNK, CHUNK)
        packed = [jnp.zeros((8, lanes), jnp.float32)] * 2
        for field in range(4):
            at = pl.ds(pl.multiple_of(field * layers + first, CHUNK), CHUNK)
            bottom[at, :] = ocean[field, pl.ds(first, CHUNK), 0, :]
            top[at, :] = ocean[field, pl.ds(first, CHUNK), rows - 1, :]
            for layer in range(CHUNK):
                for v in range(rows // 8):
                    g = (field * CHUNK + layer) * (rows // 8) + v
                    here = ocean[field, first + layer, pl.ds(8 * v, 8), :]
                    turned = pltpu.roll(here, 2 * (g % 64) + 1, 1)
                    packed[g // 64] = jnp.where(lane // 2 == g % 64, turned, packed[g // 64])
        sides[step] = jnp.concatenate(packed, axis=0)
        return carry

    lax.fori_loop(0, layers // CHUNK, one, 0)


def exchange_kernel(which, n_gx, n_gy, *refs):
    if which == 0:
        pos, rad, edges, halo, held, marks, halo_rad, *scratch = refs
        send_sem, recv_sem, rad_send, rad_recv = scratch
    elif which == 1:
        pos, rad, edges, ocean, perm, halo, held, marks, lat, rows, perms, sides, *scratch = refs
        top, bottom, *scratch = scratch
        send_sem, recv_sem, sea_send, sea_recv, *scratch = scratch
        far_send, far_recv, perm_send, perm_recv, own = scratch
    else:
        pos, rad, edges, turned, sides, halo, held, marks, mirror, lon, *scratch = refs
        send_sem, recv_sem, sea_send, sea_recv, far_send, far_recv, own = scratch
    gx, gy = lax.axis_index("gx"), lax.axis_index("gy")
    is_top = gy == n_gy - 1

    def at(dx, dy):
        return lax.rem(gx + dx + n_gx, n_gx), lax.rem(gy + dy + n_gy, n_gy)

    barrier = pltpu.get_barrier_semaphore()
    for dy, dx in NEIGHBOURS:
        pl.semaphore_signal(barrier, inc=1, device_id=at(dx, dy), device_id_type=MESH)
    if which > 0:

        @pl.when(is_top)
        def _():
            for d in range(1, n_gx):
                pl.semaphore_signal(barrier, inc=1, device_id=at(d, 0), device_id_type=MESH)

    if which == 1:
        pack(ocean, sides, bottom, top)
    blocks = rad.shape[0]
    write_marks([pos[0], pos[1], rad[...]], marks)
    own_forces(0, EARLY, marks, held)
    if which > 0:

        @pl.when(is_top)
        def _():
            pl.semaphore_wait(barrier, len(NEIGHBOURS) + n_gx - 1)

        @pl.when(jnp.logical_not(is_top))
        def _():
            pl.semaphore_wait(barrier, len(NEIGHBOURS))

    else:
        pl.semaphore_wait(barrier, len(NEIGHBOURS))

    def send(source, target, sems, index, device):
        return pltpu.make_async_remote_copy(
            src_ref=source,
            dst_ref=target,
            send_sem=sems[0].at[index],
            recv_sem=sems[1].at[index],
            device_id=device,
            device_id_type=MESH,
        )

    def halo_copies(body, part, target, sems):
        copies = []
        for k, (sy, sx) in enumerate(NEIGHBOURS):
            first = 0 if sy == 1 else blocks - 16
            first = first + 8 if sx == -1 else first
            size = 16 if sx == 0 else 8
            source = part(0 if sx == 1 else 1) if sy == 0 else body(pl.ds(first, size))
            copies.append(send(source, target(k, pl.ds(0, size)), sems, k, at(-sx, -sy)))
        return copies

    copies = halo_copies(
        lambda rows: pos.at[:, rows, :],
        lambda side: edges.at[side, pl.ds(0, 2)],
        lambda k, rows: halo.at[k, :, rows, :],
        (send_sem, recv_sem),
    )
    if which == 0:
        copies += halo_copies(
            lambda rows: rad.at[rows, :],
            lambda side: edges.at[side, 2],
            lambda k, rows: halo_rad.at[k, rows, :],
            (rad_send, rad_recv),
        )
    for copy in copies:
        copy.start()
    if which > 0:
        sea = (sea_send, sea_recv)
        if which == 1:
            pairs = ((top, lat.at[0], at(0, 1)), (bottom, lat.at[1], at(0, -1)))
        else:
            pairs = ((sides, lon.at[0], at(1, 0)), (sides, lon.at[1], at(-1, 0)))
        later = [send(pair[0], pair[1], sea, n, pair[2]) for n, pair in enumerate(pairs)]
        copies += later

    if which == 1:
        first = pl.multiple_of(jnp.minimum(gx, TURNERS - 1) * TURN_ROWS, TURN_ROWS)
        kept = pltpu.make_async_copy(perm, perms.at[gx], own.at[0])
        mine = pltpu.make_async_copy(top.at[pl.ds(first, TURN_ROWS), :], rows.at[gx], own.at[1])
        notes, far = [], []
        for d in range(1, n_gx):
            peer = lax.rem(gx + d, n_gx)
            start = pl.multiple_of(jnp.minimum(peer, TURNERS - 1) * TURN_ROWS, TURN_ROWS)
            notes.append(send(perm, perms.at[gx], (perm_send, perm_recv), d - 1, at(d, 0)))
            source = top.at[pl.ds(start, TURN_ROWS), :]
            far.append(send(source, rows.at[gx], (far_send, far_recv), d - 1, at(d, 0)))

        @pl.when(is_top)
        def _():
            kept.start()
            for d in range(1, n_gx):
                notes[d - 1].start()

                @pl.when(lax.rem(gx + d, n_gx) < TURNERS)
                def _(copy=far[d - 1]):
                    copy.start()

            @pl.when(gx < TURNERS)
            def _():
                mine.start()

        for copy in later:
            copy.start()

    if which == 2:
        for copy in later:
            copy.start()
        me = jnp.minimum(gx, TURNERS - 1)
        mine = pltpu.make_async_copy(turned.at[gx], mirror.at[me], own)
        far = []
        for d in range(1, n_gx):
            source = turned.at[lax.rem(gx + d, n_gx)]
            far.append(send(source, mirror.at[me], (far_send, far_recv), d - 1, at(d, 0)))

        @pl.when(is_top & (gx < TURNERS))
        def _():
            mine.start()
            for copy in far:
                copy.start()

    own_forces(EARLY, blocks - EARLY, marks, held)
    for copy in copies:
        copy.wait()
    if which == 1:

        @pl.when(is_top)
        def _():
            kept.wait()
            for d in range(1, n_gx):
                notes[d - 1].wait()

                @pl.when(lax.rem(gx + d, n_gx) < TURNERS)
                def _(copy=far[d - 1]):
                    copy.wait_send()

            @pl.when(gx < TURNERS)
            def _():
                mine.wait()
                for copy in far:
                    copy.wait_recv()

    if which == 2:

        @pl.when(is_top & (gx < TURNERS))
        def _():
            mine.wait()
            for copy in far:
                copy.wait_send()

        @pl.when(is_top)
        def _():
            for d in range(1, n_gx):

                @pl.when(lax.rem(gx - d + n_gx, n_gx) < TURNERS)
                def _(copy=far[d - 1]):
                    copy.wait_recv()


def exchange(which, n_gx, n_gy, pos, rad, edges, *args):
    lanes = rad.shape[1]
    blocks = rad.shape[0]
    outs = [shape(8, 2, 16, lanes), shape(2, 8 * blocks, lanes)]
    outs += [shape(MARKS * blocks, lanes)]
    dma = pltpu.SemaphoreType.DMA
    scratch = [dma((8,)), dma((8,))]
    far = [dma((n_gx - 1,)), dma((n_gx - 1,))]
    if which == 0:
        outs += [shape(8, 16, lanes)]
        scratch += [dma((8,)), dma((8,))]
    if which == 1:
        layers = args[0].shape[1]
        outs += [shape(2, 4 * layers, lanes)]
        outs += [shape(n_gx, TURN_ROWS, lanes), jax.ShapeDtypeStruct((n_gx, 1, lanes), jnp.int32)]
        outs += [shape(layers // CHUNK, 16, lanes)]
        scratch = [pltpu.VMEM((4 * layers, lanes), jnp.float32)] * 2 + scratch
        scratch += [dma((2,)), dma((2,))] + far + far + [dma((2,))]
    if which == 2:
        outs += [shape(TURNERS, TURN_ROWS, lanes), shape(2, *args[1].shape)]
        scratch += [dma((2,)), dma((2,))] + far + [dma]
    return pl.pallas_call(
        functools.partial(exchange_kernel, which, n_gx, n_gy),
        out_shape=tuple(outs),
        in_specs=[VMEM] * (3 + len(args)),
        out_specs=(VMEM,) * len(outs),
        scratch_shapes=scratch,
        compiler_params=grant(8, collective_id=which, has_side_effects=True),
        cost_estimate=BUSY,
        name=("exchange_first", "exchange_second", "exchange_third")[which],
    )(pos, rad, edges, *args)


def stencil(step, n_gy, ocean, mix, lon, lat, mirror, out):
    layers, rows, lanes = ocean.shape[1:]
    gy = lax.axis_index("gy")
    first = step * CHUNK
    lane = lax.broadcasted_iota(jnp.int32, (rows, lanes), 1)
    sub = lax.broadcasted_iota(jnp.int32, (rows, lanes), 0)
    lane8 = lax.broadcasted_iota(jnp.int32, (8, lanes), 1)
    bands = []
    for half in range(2):
        at = pl.ds(8 * half, 8)
        west = pltpu.roll(lon[0, step, at, :], 1, 1)
        east = pltpu.roll(lon[1, step, at, :], lanes - 1, 1)
        bands.append(jnp.where(lane8 % 2 == 1, west, east))
    spin = 2.0 * ((gy * rows + sub).astype(jnp.float32) + 0.5) / (rows * n_gy) - 1.0
    spin = SPIN_RATE * spin
    is_top, is_low = gy == n_gy - 1, gy == 0
    level = pl.ds(pl.multiple_of(first, CHUNK), CHUNK)
    for field in range(4):
        folded = -mirror[field, level, :] if field < 2 else mirror[field, level, :]
        upper = jnp.where(is_top, folded, lat[1, field, level, :])
        lower = jnp.where(is_low, 0.0, lat[0, field, level, :])
        for layer in range(CHUNK):
            at = first + layer
            here = ocean[field, at]
            up = ocean[field, jnp.maximum(at - 1, 0)]
            down = ocean[field, jnp.minimum(at + 1, layers - 1)]
            sides = []
            for v in range(rows // 8):
                g = (field * CHUNK + layer) * (rows // 8) + v
                sides.append(pltpu.roll(bands[g // 64], lanes - 1 - 2 * (g % 64), 1))
            sides = jnp.concatenate(sides, axis=0)
            west = jnp.where(lane == 0, sides, pltpu.roll(here, 1, 1))
            east = jnp.where(lane == lanes - 1, sides, pltpu.roll(here, lanes - 1, 1))
            south = jnp.where(sub == 0, lower[layer : layer + 1], pltpu.roll(here, 1, 0))
            north = jnp.where(sub == rows - 1, upper[layer : layer + 1], pltpu.roll(here, rows - 1, 0))
            laplace = east + west + north + south - 4.0 * here
            value = here + mix[at] * laplace + VERT_MIX * (up + down - 2.0 * here)
            if field == 0:
                value = value + spin * ocean[1, at]
            if field == 1:
                value = value - spin * ocean[0, at]
            out[field, at] = value


def couple_kernel(n_gx, n_gy, sent, cell, ocean, mix, lon, lat, mirror, *refs):
    surface, current, plain, here, there, back, home, *sems = refs
    gx, gy = lax.axis_index("gx"), lax.axis_index("gy")
    tiles = n_gx * n_gy
    rows, lanes = ocean.shape[2:]
    steps = ocean.shape[1] // CHUNK

    def work(first, last):
        def one(step, carry):
            stencil(step, n_gy, ocean, mix, lon, lat, mirror, plain)
            return carry

        lax.fori_loop(first, last, one, 0)

    barrier = pltpu.get_barrier_semaphore()
    for d in range(1, n_gx):
        peer = (lax.rem(gx + d, n_gx), gy)
        pl.semaphore_signal(barrier, inc=1, device_id=peer, device_id_type=MESH)
    for d in range(1, n_gy):
        peer = (gx, lax.rem(gy + d, n_gy))
        pl.semaphore_signal(barrier, inc=1, device_id=peer, device_id_type=MESH)
    pl.semaphore_wait(barrier, n_gx + n_gy - 2)

    def swap(source, middle, target, sems, marks):
        send_x, recv_x, send_y, recv_y, local = sems
        own = pltpu.make_async_copy(source.at[gx], middle.at[gx], local)
        own.start()
        copies = []
        for d in range(1, n_gx):
            peer = lax.rem(gx + d, n_gx)
            copies.append(
                pltpu.make_async_remote_copy(
                    src_ref=source.at[peer],
                    dst_ref=middle.at[gx],
                    send_sem=send_x.at[d - 1],
                    recv_sem=recv_x.at[d - 1],
                    device_id=(peer, gy),
                    device_id_type=MESH,
                )
            )
        for copy in copies:
            copy.start()
        work(marks[0], marks[1])
        own.wait()
        for copy in copies:
            copy.wait()
        own = pltpu.make_async_copy(middle.at[:, gy], target.at[:, gy], local)
        own.start()
        copies = []
        for d in range(1, n_gy):
            peer = lax.rem(gy + d, n_gy)
            copies.append(
                pltpu.make_async_remote_copy(
                    src_ref=middle.at[:, peer],
                    dst_ref=target.at[:, gy],
                    send_sem=send_y.at[d - 1],
                    recv_sem=recv_y.at[d - 1],
                    device_id=(gx, peer),
                    device_id_type=MESH,
                )
            )
        for copy in copies:
            copy.start()
        work(marks[1], marks[2])
        own.wait()
        for copy in copies:
            copy.wait()

    swap(sent, here, there, sems[0:5], (0, steps // 3, steps // 2))
    cells = jnp.concatenate([cell[0:1], cell[1:2]], axis=1)
    cell_row, cell_col = cells // lanes, cells % lanes
    pick = (lax.broadcasted_iota(jnp.int32, (lanes, 2 * tiles), 0) == cell_col).astype(jnp.bfloat16)
    in_row = lax.broadcasted_iota(jnp.int32, (rows, 2 * tiles), 0) == cell_row
    arrived = there[...].reshape(tiles, lanes).T
    spread = []
    for comp in range(2):
        values = jnp.concatenate([arrived[2 * comp : 2 * comp + 1], arrived[2 * comp + 1 : 2 * comp + 2]], axis=1)
        spread.append(jnp.where(in_row, values, 0.0))
    forcing = lax.dot_general(
        split(jnp.concatenate(spread, axis=0)),
        pick,
        (((1,), (1,)), ((), ())),
        preferred_element_type=jnp.float32,
    )
    skin = jnp.concatenate([plain[0, 0], plain[1, 0]], axis=0)
    level = skin + joined(forcing)
    surface[...] = level.reshape(2, rows, lanes)
    found = joined(jnp.dot(split(level), pick, preferred_element_type=jnp.float32))
    replies = []
    for comp in range(2):
        values = jnp.where(in_row, found[comp * rows : (comp + 1) * rows], 0.0)
        values = jnp.sum(values, axis=0, keepdims=True)
        replies += [values[:, :tiles], values[:, tiles:]]
    replies.append(jnp.zeros((lanes - 4, tiles), jnp.float32))
    back[...] = jnp.concatenate(replies, axis=0).T.reshape(back.shape)
    swap(back, home, current, sems[5:10], (steps // 2, steps - 1, steps))


def couple(n_gx, n_gy, sent, cell, ocean, *sea):
    tiles = n_gx * n_gy
    rows, lanes = ocean.shape[2:]
    box = (n_gx, n_gy, 1, lanes)
    dma = pltpu.SemaphoreType.DMA
    sems = [dma((n_gx - 1,)), dma((n_gx - 1,)), dma((n_gy - 1,)), dma((n_gy - 1,)), dma]
    return pl.pallas_call(
        functools.partial(couple_kernel, n_gx, n_gy),
        out_shape=(shape(2, rows, lanes), shape(*box), shape(*ocean.shape)),
        in_specs=[VMEM] * (3 + len(sea)),
        out_specs=(VMEM,) * 3,
        scratch_shapes=[pltpu.VMEM(box, jnp.float32)] * 4 + sems + sems,
        compiler_params=grant(16, collective_id=SUB, has_side_effects=True),
        name="couple",
    )(sent.reshape(box), cell, ocean, *sea)


def finish_kernel(plain, surface, current, slots, vel, vel_out, ocean_out, sems):
    layers = plain.shape[1]
    copies = [
        pltpu.make_async_copy(surface, ocean_out.at[pl.ds(0, 2), 0], sems.at[0]),
        pltpu.make_async_copy(plain.at[pl.ds(2, 2)], ocean_out.at[pl.ds(2, 2)], sems.at[1]),
    ]
    for field in range(2):
        deep = pl.ds(1, layers - 1)
        copies.append(
            pltpu.make_async_copy(plain.at[field, deep], ocean_out.at[field, deep], sems.at[2 + field])
        )
    for copy in copies:
        copy.start()
    blocks, discs = vel.shape[1], vel.shape[2]
    tiles = current.shape[0]
    got = current[...].reshape(tiles, discs).T
    spots = jnp.concatenate([slots[0:1], slots[1:2]], axis=1)
    place = lax.broadcasted_iota(jnp.int32, (blocks, 2 * tiles), 0) == spots
    for comp in range(2):
        values = jnp.concatenate([got[2 * comp : 2 * comp + 1], got[2 * comp + 1 : 2 * comp + 2]], axis=1)
        values = jnp.sum(jnp.where(place, values, 0.0), axis=1, keepdims=True)
        speed = vel[comp]
        vel_out[comp] = speed + DRAG_BACK * (values - speed)
    for copy in copies:
        copy.wait()


def finish(plain, surface, current, slots, vel):
    tiles = current.shape[0] * current.shape[1]
    return pl.pallas_call(
        finish_kernel,
        out_shape=(shape(*vel.shape), shape(*plain.shape)),
        in_specs=[VMEM] * 5,
        out_specs=(VMEM, ANY),
        scratch_shapes=[pltpu.SemaphoreType.DMA((4,))],
        compiler_params=grant(4),
        name="finish",
    )(plain, surface, current.reshape(tiles, 1, current.shape[3]), slots, vel)


def body(
    disc_pos,
    disc_vel,
    radius,
    bond_list,
    contact_mask,
    remap_block,
    ocean_state,
    mix_coef,
    remap_cell,
    fold_perm,
):
    n_gx, n_gy = lax.axis_size("gx"), lax.axis_size("gy")
    rows_dev, cols_dev, discs = radius.shape
    blocks = rows_dev * cols_dev
    slots = remap_block[0].T
    cell = remap_cell[0].T
    perm = fold_perm.reshape(1, discs)
    position = disc_pos.reshape(2, blocks, discs)
    velocity = disc_vel.reshape(2, blocks, discs)
    rad = radius.reshape(blocks, discs)
    bonds = bond_list.reshape(BONDS, blocks, discs)
    sea_shape = (4, mix_coef.shape[0], discs)
    position, rad, edges = prep(position, rad)
    halo, held, marks, halo_rad = exchange(0, n_gx, n_gy, position, rad, edges)
    position, velocity, edges, mask = contact_step(
        0, n_gy, position, velocity, rad, bonds, contact_mask, marks, held, halo, halo_rad
    )
    halo, held, marks, lat, rows, perms, sides = exchange(
        1, n_gx, n_gy, position, rad, edges, ocean_state, perm
    )
    position, velocity, edges, turned = contact_step(
        1, n_gy, position, velocity, rad, bonds, mask, marks, held, halo, halo_rad, rows, perms
    )
    halo, held, marks, mirror, lon = exchange(2, n_gx, n_gy, position, rad, edges, turned, sides)
    position, velocity, sent = contact_step(
        2, n_gy, position, velocity, rad, bonds, mask, marks, held, halo, halo_rad, slots
    )
    sea = (mix_coef, lon, lat.reshape(2, *sea_shape), mirror.reshape(sea_shape))
    surface, current, plain = couple(n_gx, n_gy, sent, cell, ocean_state, *sea)
    vel_next, ocean_next = finish(plain, surface, current, slots, velocity)
    return (position.reshape(disc_pos.shape), vel_next.reshape(disc_vel.shape), ocean_next)


def solution(mesh):
    in_specs = (
        P(None, "gy", "gx", None),
        P(None, "gy", "gx", None),
        P("gy", "gx", None),
        P(None, "gy", "gx", None),
        P(None, "gy", "gx"),
        P(("gx", "gy"), None, None),
        P(None, None, "gy", "gx"),
        P(None, "gy", "gx"),
        P(("gx", "gy"), None, None),
        P("gx"),
    )
    out_specs = (P(None, "gy", "gx", None), P(None, "gy", "gx", None), P(None, None, "gy", "gx"))
    return jax.shard_map(body, mesh=mesh, in_specs=in_specs, out_specs=out_specs, check_vma=False)
```
